32 devices in a mesh: ctx: 16 (over z, x, core), tp: 2 (over y).
Axes of the slice: x: 2, y: 2, z: 4, core: 2. Of those that a mesh axis runs over, the one named last changes fastest.
Arguments:
- inner_input: bfloat16 [2048, 8192], P('ctx', 'tp'), may hold values from -6 to 6
- gate_input: bfloat16 [2048, 8192], P('ctx', 'tp'), may hold values from -6 to 6
- state_inputs: bfloat16 [2, 2048, 1024], P(None, 'ctx', 'tp'), may hold values from -6 to 6
- step_size: float32 [128, 2048], P('tp', 'ctx'), may hold values from 0.5 to 2
- resets: int32 [2048], P('ctx'), may hold values 0 or 1
- decay_rate: float32 [128], P('tp'), may hold values from 0 to 0.04
- skip_gain: float32 [128], P('tp'), may hold values from 0.5 to 1.5
- conv_inner: float32 [4, 8192], P(None, 'tp'), may hold values from -3 to 3
- conv_state: float32 [2, 4, 1024], P(None, None, 'tp'), may hold values from -3 to 3
- norm_gain: float32 [8192], P('tp'), may hold values from 0.5 to 1.5
- out_weight: bfloat16 [8192, 4096], P('tp', 'ctx'), may hold values from -0.0625 to 0.0625
- residual: bfloat16 [2048, 4096], P('ctx', 'tp'), may hold values from -6 to 6
- final_gain: float32 [4096], replicated, may hold values from 0.5 to 1.5
- head_weight: bfloat16 [4096, 65536], P(None, ('ctx', 'tp')), may hold values from -8 to 8
- scored: int32 [128], P('ctx'), may hold values from 0 to 2047, as said below
- targets: int32 [128], replicated, may hold values from 0 to 65535
- policy_logprob: float32 [128], replicated, may hold values from -20 to -10
Outputs:
- ref_logprob: float32 [128], replicated
- token_kl: float32 [128], replicated
The draws below stay inside these ranges and needn't reach their ends.
Inputs may be any that keep to these rules, and one draw needn't show every extreme that they name: `scored`: entries j * 8 to (j + 1) * 8 - 1 are distinct positions in j * 128 to (j + 1) * 128 - 1.
All inputs are finite; a program needn't handle non-finite values. No bound on the sum of `resets` on one device may be relied on, other than what follows from the above.
Results may differ from the reference program's by a relative error of at most 0.00215.
The reference program's roundings to bfloat16 on the way (of `inner_conv`, `normed`, `hidden`, `chosen` and `features`) count: a program that leaves them out, or rounds other values in their place, can miss the bound.
Values may be sent and summed in bfloat16 or wider, within the bound.
A program may use at most 128 MiB of HBM per device.

```python
import math
import jax
import jax.numpy as jnp
from jax import lax

D = 4096
HEADS = 128
HEAD_DIM = 64
STATE = 128
GROUPS = 8
VOCAB = 65536
CONV = 4
SPAN = 128
TOK_DEV = 128
SC_DEV = 8
INNER = 8192
TOKENS = 2048
SCORED = 128


def draw_decay_rate(key, part):
    pick_key, slow_key, fast_key = jax.random.split(key, 3)
    share = 0.5
    slow_heads = jax.random.uniform(pick_key, (HEADS,), jnp.float32) < share
    slow_rate = jnp.exp(jax.random.uniform(slow_key, (HEADS,), jnp.float32, math.log(0.1 / TOKENS), math.log(1.0 / TOKENS)))
    fast_rate = jnp.exp(jax.random.uniform(fast_key, (HEADS,), jnp.float32, math.log(0.02), math.log(0.04)))
    return jnp.where(slow_heads, slow_rate, fast_rate)


def draw_head_weight(key, part):
    base_key = jax.random.fold_in(key, 0)
    weights = jnp.clip(jax.random.normal(base_key, (D, VOCAB), jnp.float32), -6.0, 6.0) * (3.0 / D ** 0.5)
    return weights.astype(jnp.bfloat16)


def draw_scored(key, part):
    blocks = SCORED // SC_DEV

    def one_block(index):
        order = jax.random.permutation(jax.random.fold_in(key, index), TOK_DEV)
        return order[:SC_DEV] + index * TOK_DEV
    return jax.vmap(one_block)(jnp.arange(blocks)).reshape(SCORED).astype(jnp.int32)


def with_ends(entries, own_key, low, top_value):
    longest = entries.shape.index(max(entries.shape))
    spots = []
    for shift in (0, 1):
        where = [jax.random.randint(jax.random.fold_in(own_key, axis), (), 0, length) for axis, length in enumerate(entries.shape)]
        where[longest] = (where[longest] + shift) % entries.shape[longest]
        spots.append(tuple(where))
    return entries.at[spots[0]].set(low).at[spots[1]].set(top_value)


def block_levels(key, shape, cuts, low, high):
    def one(position, parts):
        draws = jax.random.uniform(jax.random.fold_in(jax.random.fold_in(key, 6), position), (parts,), jnp.float32, low / len(cuts), high / len(cuts))
        return jnp.repeat(jnp.exp(draws), shape[position] // parts).reshape((-1,) + (1,) * (len(shape) - position - 1))

    factor_of = one(*cuts[0])
    for cut in cuts[1:]:
        factor_of = factor_of * one(*cut)
    return factor_of


def centred(key, shape, deviation, bound, cuts=(), held_as=jnp.bfloat16):
    factor_of = block_levels(key, shape, cuts, -0.22, 0.18) if cuts else 1.0
    values = jax.random.normal(key, shape, jnp.float32) * deviation * factor_of
    return jnp.minimum(jnp.maximum(values, -bound), bound).astype(held_as)


def setup_inputs(seed: int = 0) -> dict:
    keys = jax.random.split(jax.random.key(seed), 18)
    inner_input = centred(keys[0], (TOKENS, INNER), 1.0, 6.0, ((0, 16), (1, 2)))
    gate_input = centred(keys[1], (TOKENS, INNER), 1.0, 6.0, ((0, 16), (1, 2)))
    state_inputs = centred(keys[2], (2, TOKENS, GROUPS * STATE), 1.0, 6.0, ((1, 16), (2, 2)))
    step_size = jnp.clip(jnp.exp(math.log(2.0) - 1.3862944 * jax.random.uniform(keys[3], (HEADS, TOKENS), jnp.float32) ** block_levels(keys[3], (HEADS, TOKENS), ((0, 2), (1, 16)), -0.2, 0.2)), 0.5, 2.0)
    resets = with_ends((jax.random.randint(keys[4], (TOKENS,), 0, TOKENS // 4) < 1).astype(jnp.int32), jax.random.fold_in(keys[4], 1), 0, 1)
    decay_rate = draw_decay_rate(jax.random.fold_in(keys[17], 71), 0)
    skip_gain = jnp.clip(0.5 + 1.0 * jax.random.uniform(keys[6], (HEADS,), jnp.float32) ** block_levels(keys[6], (HEADS,), ((0, 2),), -0.2, 0.2), 0.5, 1.5)
    conv_inner = centred(keys[7], (CONV, INNER), CONV ** -0.5, 3.0, ((1, 2),), jnp.float32)
    conv_state = centred(keys[8], (2, CONV, GROUPS * STATE), CONV ** -0.5, 3.0, ((2, 2),), jnp.float32)
    norm_gain = jnp.clip(1.0 + 0.1 * jax.random.normal(keys[9], (INNER,), jnp.float32), 0.5, 1.5)
    out_weight = centred(keys[10], (INNER, D), INNER ** -0.5, 0.0625, ((0, 2), (1, 16)))
    residual = centred(keys[11], (TOKENS, D), 1.0, 6.0, ((0, 16), (1, 2)))
    final_gain = jnp.clip(1.0 + 0.1 * jax.random.normal(keys[12], (D,), jnp.float32), 0.5, 1.5)
    head_weight = draw_head_weight(jax.random.fold_in(keys[17], 71), 0)
    scored = draw_scored(jax.random.fold_in(keys[17], 71), 0)
    targets = with_ends(jax.random.randint(keys[15], (SCORED,), 0, VOCAB), jax.random.fold_in(keys[15], 1), 0, VOCAB - 1).astype(jnp.int32)
    policy_logprob = jnp.clip(jax.random.uniform(keys[16], (SCORED,), jnp.float32, -20.0, -10.0), -20.0, -10.0)
    return dict(inner_input=inner_input, gate_input=gate_input, state_inputs=state_inputs, step_size=step_size, resets=resets, decay_rate=decay_rate, skip_gain=skip_gain, conv_inner=conv_inner, conv_state=conv_state, norm_gain=norm_gain, out_weight=out_weight, residual=residual, final_gain=final_gain, head_weight=head_weight, scored=scored, targets=targets, policy_logprob=policy_logprob)


epsilon = 1e-05
precise = lax.Precision.HIGHEST

def causal_filter(stream, kernel, counted):
    kernel_taps = kernel.shape[0]
    rows_total = stream.shape[0]
    values = stream.astype(jnp.float32)
    summed = jnp.zeros_like(values)
    for offset in range(kernel_taps):
        shifted = jnp.concatenate([jnp.zeros((offset, values.shape[1]), jnp.float32), values[:rows_total - offset]], axis=0)
        earlier = jnp.concatenate([jnp.zeros((offset,), counted.dtype), counted[:rows_total - offset]])
        keeping = (counted - earlier == 0).astype(jnp.float32)
        summed = summed + keeping[:, None] * kernel[offset][None, :] * shifted
    return jax.nn.silu(summed).astype(jnp.bfloat16)

def reference(inner_input, gate_input, state_inputs, step_size, resets, decay_rate, skip_gain, conv_inner, conv_state, norm_gain, out_weight, residual, final_gain, head_weight, scored, targets, policy_logprob):
    counted = jnp.cumsum(resets)
    inner_conv = causal_filter(inner_input, conv_inner, counted)
    write_map = causal_filter(state_inputs[0], conv_state[0], counted)
    read_map = causal_filter(state_inputs[1], conv_state[1], counted)
    spans = TOKENS // SPAN
    per_group = HEADS // GROUPS
    values = inner_conv.reshape(spans, SPAN, HEADS, HEAD_DIM).astype(jnp.float32)
    writes = jnp.repeat(write_map.reshape(spans, SPAN, GROUPS, STATE), per_group, axis=2).astype(jnp.float32)
    reads = jnp.repeat(read_map.reshape(spans, SPAN, GROUPS, STATE), per_group, axis=2).astype(jnp.float32)
    steps_blocked = step_size.reshape(HEADS, spans, SPAN).transpose(1, 0, 2)
    segments = resets.reshape(spans, SPAN)
    positions = jnp.arange(SPAN)
    lower = positions[:, None] >= positions[None, :]

    def span_update(states, item):
        value_block, write_block, read_block, step_block, reset_block = item
        cumulated = jnp.cumsum(-decay_rate[:, None] * step_block, axis=1)
        segment = jnp.cumsum(reset_block)
        causal = lower & (segment[:, None] == segment[None, :])
        gaps = cumulated[:, :, None] - cumulated[:, None, :]
        decay_matrix = jnp.where(causal[None], jnp.exp(jnp.where(causal[None], gaps, 0.0)), 0.0)
        scores = jnp.einsum('ihn,jhn->hij', read_block, write_block, precision=precise)
        mixing = scores * decay_matrix * step_block[:, None, :]
        within = jnp.einsum('hij,jhp->ihp', mixing, value_block, precision=precise)
        from_start = jnp.exp(cumulated) * (segment == 0)[None, :]
        across = jnp.einsum('ihn,hpn->ihp', read_block, states, precision=precise) * from_start.T[:, :, None]
        to_end = jnp.exp(cumulated[:, -1:] - cumulated) * (segment == segment[-1])[None, :] * step_block
        weighted = value_block * to_end.T[:, :, None]
        span_decay = jnp.exp(cumulated[:, -1]) * (segment[-1] == 0)
        updated = span_decay[:, None, None] * states + jnp.einsum('jhp,jhn->hpn', weighted, write_block, precision=precise)
        return (updated, within + across)
    empty_state = jnp.zeros((HEADS, HEAD_DIM, STATE), jnp.float32)
    _, outputs = lax.scan(span_update, empty_state, (values, writes, reads, steps_blocked, segments))
    mixed_out = outputs.reshape(TOKENS, HEADS * HEAD_DIM) + jnp.repeat(skip_gain, HEAD_DIM)[None, :] * values.reshape(TOKENS, HEADS * HEAD_DIM)
    gated = mixed_out * jax.nn.silu(gate_input.astype(jnp.float32))
    grouped = gated.reshape(TOKENS, GROUPS, -1)
    inverse_rms = lax.rsqrt(lax.optimization_barrier(jnp.mean(grouped * grouped, axis=2, keepdims=True)) + epsilon)
    normed = ((grouped * inverse_rms).reshape(TOKENS, -1) * norm_gain[None, :]).astype(jnp.bfloat16)
    branch = jnp.dot(normed, out_weight, preferred_element_type=jnp.float32)
    hidden = (residual.astype(jnp.float32) + branch).astype(jnp.bfloat16)
    chosen = hidden[scored]
    squares = lax.optimization_barrier(jnp.sum(jnp.square(chosen.astype(jnp.float32)), axis=1))
    features = (chosen.astype(jnp.float32) * lax.rsqrt(squares / D + epsilon)[:, None] * final_gain[None, :]).astype(jnp.bfloat16)
    logits = jnp.dot(features, head_weight, preferred_element_type=jnp.float32)
    row_top = lax.optimization_barrier(jnp.max(logits, axis=1))
    summed = lax.optimization_barrier(jnp.sum(jnp.exp(logits - row_top[:, None]), axis=1))
    picked = jnp.take_along_axis(logits, targets[:, None], axis=1)[:, 0]
    ref_logprob = picked - row_top - jnp.log(summed)
    token_kl = 0.5 * jnp.square(ref_logprob - policy_logprob)
    return (ref_logprob, token_kl)
```

```python
import functools
import jax
import jax.numpy as jnp
from jax import lax
from jax.experimental import pallas as pl
from jax.experimental.pallas import tpu as pltpu
from jax.sharding import PartitionSpec as P

HEAD_DIM = 64
STATE = 128
EDGE = 16

epsilon = 1e-05
precise = lax.Precision.HIGHEST
MESH = pl.DeviceIdType.MESH
VMEM = pl.BlockSpec(memory_space=pltpu.VMEM)
ANY = pl.BlockSpec(memory_space=pl.ANY)


def remote(src, dst, send, recv, device):
    return pltpu.make_async_remote_copy(
        src_ref=src, dst_ref=dst, send_sem=send, recv_sem=recv, device_id=device, device_id_type=MESH
    )


def greet(devices):
    barrier = pltpu.get_barrier_semaphore()
    for device in devices:
        pl.semaphore_signal(barrier, inc=1, device_id=device, device_id_type=MESH)
    pl.semaphore_wait(barrier, len(devices))


def spread_kernel(n, tp, q_count, z_count, x_ref, s_ref, d_ref, g_ref, m_ref, r_ref,
                  xo, so, do, go, mo, xh, sh, mh, ro,
                  send, recv, own, edge_send, edge_recv, res_send, res_recv):
    c, t = lax.axis_index("ctx"), lax.axis_index("tp")
    z, q = c // q_count, c % q_count
    total = n * tp
    me = c * tp + t
    barrier = pltpu.get_barrier_semaphore()

    def hello(k, carry):
        other = (me + k) % total
        pl.semaphore_signal(
            barrier, inc=1, device_id=(other // tp, other % tp), device_id_type=MESH
        )
        return carry

    lax.fori_loop(1, total, hello, 0)
    pl.semaphore_wait(barrier, total - 1)
    width = xo.shape[2]
    heads = do.shape[1]
    rows = x_ref.shape[0]

    def cols(ref, k, size):
        return ref.at[:, pl.ds(pl.multiple_of(k * size, 128), size)]

    def parts(k):
        return (
            cols(x_ref, k, width),
            s_ref.at[:, :, pl.ds(pl.multiple_of(k * STATE, 128), STATE)],
            d_ref.at[pl.ds(pl.multiple_of(k * heads, 8), heads), :],
            cols(g_ref, k, width),
            m_ref,
        )

    def slots(k):
        return (xo.at[k], so.at[k], do.at[k], go.at[k], mo.at[k])

    started = []
    tail = pl.ds(rows - EDGE, EDGE)
    next_z = jnp.minimum(z + 1, z_count - 1)

    def edges(k, dst_c):
        wide = pl.ds(pl.multiple_of(k * width, 128), width)
        thin = pl.ds(pl.multiple_of(k * STATE, 128), STATE)
        triple = ((x_ref.at[tail, wide], xh), (s_ref.at[:, tail, thin], sh), (m_ref, mh))
        return [
            remote(a, b, edge_send.at[k, i], edge_recv.at[i], (dst_c, t))
            for i, (a, b) in enumerate(triple)
        ]

    sends_edge = (q == q_count - 1) & (z < z_count - 1)
    gets_edge = z > 0
    if z_count > 1:
        @pl.when(sends_edge)
        def _():
            for k in range(q_count):
                for copy in edges(k, (z + 1) * q_count + k):
                    copy.start()

    for d in range(1, q_count):
        k = (q + d) % q_count
        for i, (a, b) in enumerate(zip(parts(k), slots(q))):
            copy = remote(a, b, send.at[d - 1, i], recv.at[d - 1, i], (z * q_count + k, t))
            copy.start()
            started.append(copy)
    per = n // tp

    def res_copy(j, to_t):
        return remote(
            r_ref.at[j], ro.at[c],
            res_send.at[j * tp + to_t], res_recv.at[c], (t * per + j, to_t)
        )

    for j in range(per):
        for to_t in range(tp):
            mine = (t * per + j == c) & (to_t == t)

            @pl.when(jnp.logical_not(mine))
            def _():
                res_copy(j, to_t).start()

            @pl.when(mine)
            def _():
                pltpu.make_async_copy(r_ref.at[j], ro.at[c], res_recv.at[c]).start()
    locals_ = [
        pltpu.make_async_copy(a, b, own.at[i]) for i, (a, b) in enumerate(zip(parts(q), slots(q)))
    ]
    for copy in locals_:
        copy.start()
    for copy in locals_:
        copy.wait()
    for j in range(per):
        for to_t in range(tp):
            mine = (t * per + j == c) & (to_t == t)

            @pl.when(jnp.logical_not(mine))
            def _():
                res_copy(j, to_t).wait_send()
    for k in range(n):
        pltpu.make_async_copy(ro.at[k], ro.at[k], res_recv.at[k]).wait()
    for copy in started:
        copy.wait_send()
    for d in range(1, q_count):
        k = (q + q_count - d) % q_count
        for i, (a, b) in enumerate(zip(parts(q), slots(k))):
            remote(a, b, send.at[d - 1, i], recv.at[d - 1, i], (z * q_count + k, t)).wait_recv()
    if z_count > 1:
        @pl.when(sends_edge)
        def _():
            for k in range(q_count):
                for copy in edges(k, (z + 1) * q_count + k):
                    copy.wait_send()

        @pl.when(gets_edge)
        def _():
            for i, ref in enumerate((xh, sh, mh)):
                pltpu.make_async_copy(ref, ref, edge_recv.at[i]).wait()


def spread(n, tp, q_count, x, s, d, g, m, r):
    z_count = n // q_count
    rows, all_width = x.shape
    width = all_width // q_count
    heads = d.shape[0] // q_count
    block = r.shape[1] * tp // n
    r = r.reshape(r.shape[0], n // tp, block).transpose(1, 0, 2)
    shape = jax.ShapeDtypeStruct
    outs = (
        shape((q_count, rows, width), x.dtype),
        shape((q_count, 2, rows, STATE), s.dtype),
        shape((q_count, heads, rows), d.dtype),
        shape((q_count, g.shape[0], width), g.dtype),
        shape((q_count,) + m.shape, m.dtype),
        shape((EDGE, width), x.dtype),
        shape((2, EDGE, STATE), s.dtype),
        shape(m.shape, m.dtype),
        shape((n,) + r.shape[1:], r.dtype),
    )
    dma = pltpu.SemaphoreType.DMA
    peers = max(q_count - 1, 1)
    return pl.pallas_call(
        functools.partial(spread_kernel, n, tp, q_count, z_count),
        out_shape=outs,
        in_specs=[ANY, ANY, ANY, VMEM, VMEM, VMEM],
        out_specs=[VMEM] * len(outs),
        scratch_shapes=[
            dma((peers, 5)), dma((peers, 5)), dma((5,)), dma((q_count, 3)), dma((3,)),
            dma((n,)), dma((n,)),
        ],
        compiler_params=pltpu.CompilerParams(collective_id=0, has_side_effects=True),
    )(x, s, d, g, m, r)


def staged(kernel, skip, count, shapes):
    def run(*refs):
        ins, rest, held, sems = (
            refs[:count], refs[count : -len(shapes) - 1], refs[-len(shapes) - 1 : -1], refs[-1]
        )
        held = iter(held)
        views, copies = [], []
        for i, ref in enumerate(ins):
            if i in skip:
                views.append(ref)
                continue
            local = next(held)
            copy = pltpu.make_async_copy(ref, local, sems.at[len(copies)])
            copy.start()
            copies.append(copy)
            views.append(local)
        for copy in copies:
            copy.wait()
        kernel(*views, *rest)

    extra = [pltpu.VMEM(a.shape, a.dtype) for a in shapes]
    return run, extra + [pltpu.SemaphoreType.DMA((len(shapes),))]


def mid_kernel(q_count, z_count, x_ref, xe_ref, s_ref, se_ref, k_ref, d_ref, f_ref, spot_ref,
               gate_ref, tx_ref, ts_ref, rate_ref, skip_ref, gain_ref, out,
               pad_x, pad_s, values, writes, reads, mine_r, all_r, y, far, pd, far_pd, mixed, carried,
               r_send, r_recv, y_send, y_recv, p_send, p_recv):
    f32, bf16 = jnp.float32, jnp.bfloat16
    c, t = lax.axis_index("ctx"), lax.axis_index("tp")
    z, q = c // q_count, c % q_count
    barrier = pltpu.get_barrier_semaphore()

    def peer(d):
        return (((z + d) % z_count) * q_count + q, t)

    for d in range(1, z_count):
        pl.semaphore_signal(barrier, inc=1, device_id=peer(d), device_id_type=MESH)
    tokens, width = values.shape
    piece = tokens // q_count
    heads = d_ref.shape[1]
    rows = mine_r.shape[0]
    taps = tx_ref.shape[0]
    has_edge = (z > 0).astype(f32)
    keep = k_ref[...].T

    def filtered(pad, kernel, start, target):
        total = jnp.zeros((piece, pad.shape[1]), f32)
        for off in range(taps):
            total = total + (
                keep[start : start + piece, off : off + 1]
                * kernel[off : off + 1]
                * pad[EDGE - off + start : EDGE - off + start + piece, :]
            )
        target[start : start + piece, :] = jax.nn.silu(total).astype(bf16)

    thin = pl.ds(pl.multiple_of(q * STATE, 128), STATE)
    for which, target in ((1, reads), (0, writes)):
        edge = se_ref[which].astype(f32)
        pad_s[:EDGE, :] = jnp.where(has_edge > 0.0, edge, 0.0)
        for k in range(q_count):
            pad_s[EDGE + k * piece : EDGE + (k + 1) * piece, :] = s_ref[k, which].astype(f32)
        kernel = ts_ref[which, :, thin]
        for k in range(q_count):
            filtered(pad_s, kernel, k * piece, target)
    spots = spot_ref[...]
    lanes = lax.broadcasted_iota(jnp.int32, (rows, tokens), 1)
    pick_f = jnp.where(spots == lanes, 1.0, 0.0)
    pick = pick_f.astype(bf16)
    mine_r[...] = jnp.dot(pick, reads[...], preferred_element_type=f32).astype(bf16)
    pl.semaphore_wait(barrier, z_count - 1)
    sent = []
    for d in range(1, z_count):
        copy = remote(mine_r, all_r.at[z], r_send.at[d], r_recv.at[d], peer(d))
        copy.start()
        sent.append(copy)
    all_r[z] = mine_r[...]
    wide = pl.ds(pl.multiple_of(q * width, 128), width)
    kernel_x = tx_ref[:, wide]
    pad_x[:EDGE, :] = jnp.where(has_edge > 0.0, xe_ref[...].astype(f32), 0.0)
    for k in range(q_count):
        pad_x[EDGE + k * piece : EDGE + (k + 1) * piece, :] = x_ref[k].astype(f32)
    for k in range(q_count):
        filtered(pad_x, kernel_x, k * piece, values)
    steps = jnp.concatenate([d_ref[k] for k in range(q_count)], axis=1)
    lower = jnp.where(
        lax.broadcasted_iota(jnp.int32, (tokens, tokens), 0)
        <= lax.broadcasted_iota(jnp.int32, (tokens, tokens), 1),
        1.0, 0.0,
    )
    runs = jnp.concatenate([-rate_ref[q] * steps, f_ref[...]], axis=0)
    sums = jnp.dot(runs, lower, precision=precise, preferred_element_type=f32)
    cumulated = sums[:heads]
    segment = sums[heads : heads + 1]
    at_rows = lax.dot_general(
        pick_f, sums, (((1,), (1,)), ((), ())), precision=precise, preferred_element_type=f32
    )
    row_cum = at_rows[:, :heads]
    row_seg = at_rows[:, heads : heads + 1]
    last = cumulated[:, tokens - 1 : tokens]
    last_seg = segment[:, tokens - 1 : tokens]
    to_end = jnp.exp(last - cumulated) * jnp.where(segment == last_seg, 1.0, 0.0) * steps
    spread_heads = jnp.where(
        lax.broadcasted_iota(jnp.int32, (heads, width), 0)
        == lax.broadcasted_iota(jnp.int32, (heads, width), 1) // HEAD_DIM,
        1.0, 0.0,
    )

    def widen(a):
        return jnp.dot(a, spread_heads, precision=precise, preferred_element_type=f32)

    plane = jnp.broadcast_to(jnp.exp(last) * jnp.where(last_seg == 0.0, 1.0, 0.0), (heads, 128))
    pd[...] = widen(plane.T[:8])
    weighted = values[...].astype(f32) * widen(to_end.T)
    state = jnp.dot(
        writes[...].astype(f32).T, weighted, precision=precise, preferred_element_type=f32
    )
    for d in range(1, z_count):
        here = all_r.at[(z + z_count - d) % z_count]
        remote(mine_r, here, r_send.at[d], r_recv.at[d], peer(d)).wait_recv()
    for k in range(z_count):
        y[k] = jnp.dot(
            all_r[k].astype(f32), state, precision=precise, preferred_element_type=f32
        )

    def outgoing(d):
        return (
            remote(y.at[(z + d) % z_count], far.at[z], y_send.at[d], y_recv.at[d], peer(d)),
            remote(pd, far_pd.at[z], p_send.at[d], p_recv.at[d], peer(d)),
        )

    for d in range(1, z_count):
        @pl.when(z + d < z_count)
        def _():
            for copy in outgoing(d):
                copy.start()
    scores = lax.dot_general(
        mine_r[...], writes[...], (((1,), (1,)), ((), ())), preferred_element_type=f32
    )
    causal = (spots >= lanes) & (row_seg == segment)
    half = lax.broadcasted_iota(jnp.int32, (rows, 2 * HEAD_DIM), 1) < HEAD_DIM
    for pair in range(heads // 2):
        mixes = []
        for h in (2 * pair, 2 * pair + 1):
            gaps = row_cum[:, h : h + 1] - cumulated[h : h + 1]
            decay = jnp.where(causal, jnp.exp(jnp.where(causal, gaps, 0.0)), 0.0)
            mixes.append(scores * decay * steps[h : h + 1])
        span = slice(pair * 2 * HEAD_DIM, (pair + 1) * 2 * HEAD_DIM)
        product = jnp.dot(
            jnp.concatenate(mixes, axis=0), values[:, span].astype(f32),
            precision=precise, preferred_element_type=f32,
        )
        mixed[:, span] = jnp.where(half, product[:rows], product[rows:])
    own_values = jnp.dot(pick, values[...], preferred_element_type=f32)
    from_start = jnp.exp(row_cum) * jnp.where(row_seg == 0.0, 1.0, 0.0)
    factors = widen(
        jnp.concatenate([from_start, jnp.broadcast_to(skip_ref[q], (8, heads))], axis=0)
    )
    gate = jax.nn.silu(gate_ref[...].astype(f32))
    carried[...] = jnp.zeros((rows, width), f32)
    for d in range(z_count - 1, 0, -1):
        @pl.when(z - d >= 0)
        def _():
            k = z - d + jnp.where(z - d < 0, z_count, 0)
            here, there = far.at[k], far_pd.at[k]
            remote(here, here, y_send.at[d], y_recv.at[d], peer(d)).wait_recv()
            remote(there, there, p_send.at[d], p_recv.at[d], peer(d)).wait_recv()
            carried[...] = carried[...] * far_pd[k][0:1] + far[k]
    gated = (
        mixed[...] + carried[...] * factors[:rows] + factors[rows : rows + 1] * own_values
    ) * gate
    scale = lax.rsqrt(jnp.mean(gated * gated, axis=1, keepdims=True) + epsilon)
    out[...] = (gated * scale * gain_ref[:, wide]).astype(bf16)
    for copy in sent:
        copy.wait_send()
    for d in range(1, z_count):
        @pl.when(z + d < z_count)
        def _():
            for copy in outgoing(d):
                copy.wait_send()


def middle(xs, x_edge, ss, s_edge, keeps, steps, flags, spots, gate, taps_x, taps_s, rate, skip, gain,
           q_count, z_count):
    f32, bf16 = jnp.float32, jnp.bfloat16
    tokens = steps.shape[0] * steps.shape[2]
    rows, width = gate.shape
    operands = (
        xs, x_edge, ss, s_edge, keeps, steps, flags, spots, gate, taps_x, taps_s, rate, skip, gain
    )
    run, extra = staged(
        functools.partial(mid_kernel, q_count, z_count), (), len(operands), operands
    )
    dma, vmem = pltpu.SemaphoreType.DMA, pltpu.VMEM
    return pl.pallas_call(
        run,
        out_shape=jax.ShapeDtypeStruct((rows, width), bf16),
        in_specs=[ANY] * len(operands),
        out_specs=VMEM,
        scratch_shapes=[
            vmem((EDGE + tokens, width), f32),
            vmem((EDGE + tokens, STATE), f32),
            vmem((tokens, width), bf16),
            vmem((tokens, STATE), bf16),
            vmem((tokens, STATE), bf16),
            vmem((rows, STATE), bf16),
            vmem((z_count, rows, STATE), bf16),
            vmem((z_count, rows, width), f32),
            vmem((z_count, rows, width), f32),
            vmem((8, width), f32),
            vmem((z_count, 8, width), f32),
            vmem((rows, width), f32),
            vmem((rows, width), f32),
        ] + [dma((z_count,))] * 6 + extra,
        compiler_params=pltpu.CompilerParams(
            collective_id=1, has_side_effects=True, vmem_limit_bytes=58 * 1024 * 1024
        ),
    )(*operands)


def tail_kernel(n, tp, q_count, z_count, n_ref, ow_ref, hw_ref, r_ref, g_ref, t_ref, p_ref, out,
                ow, hw, nrm, both, hid, feat, logit, stat, every,
                own, tp_send, tp_recv, st_send, st_recv, *gather_sems):
    c, t = lax.axis_index("ctx"), lax.axis_index("tp")
    z, q = c // q_count, c % q_count
    total = n * tp
    me = c * tp + t
    get_ow = pltpu.make_async_copy(ow_ref, ow, own.at[0])
    get_hw = pltpu.make_async_copy(hw_ref, hw, own.at[1])
    barrier = pltpu.get_barrier_semaphore()

    def device(k):
        return (k // tp, k % tp)

    def hello(d, carry):
        pl.semaphore_signal(
            barrier, inc=1, device_id=device((me + d) % total), device_id_type=MESH
        )
        return carry

    lax.fori_loop(1, total, hello, 0)
    get_ow.start()
    get_hw.start()
    pl.semaphore_wait(barrier, total - 1)
    core_n = 2 if q_count % 2 == 0 else 1
    x_n = q_count // core_n
    x, core = q // core_n, q % core_n

    def at_x(k):
        return (z * q_count + k * core_n + core, t)

    at_core = (z * q_count + x * core_n + (core_n - 1) - core, t)

    def gathered(slot, mine, sems):
        z_send, z_recv, x_send, x_recv, c_send, c_recv = sems
        sent = []

        def push(copy):
            copy.start()
            sent.append(copy)

        def to_x(ref, dst, d):
            for e in range(1, x_n):
                push(remote(ref, dst, x_send.at[e - 1, d], x_recv.at[e - 1, d], at_x((x + e) % x_n)))

        def to_core(ref, dst, e, d):
            if core_n > 1:
                push(remote(ref, dst, c_send.at[e, d], c_recv.at[e, d], at_core))

        home = slot(q, z)
        for d in range(1, z_count):
            push(remote(mine, home, z_send.at[d], z_recv.at[d], (((z + d) % z_count) * q_count + q, t)))
        to_x(mine, home, 0)
        to_core(mine, home, 0, 0)
        for d in range(z_count):
            k = (z + z_count - d) % z_count
            if d:
                here = slot(q, k)
                remote(here, here, z_send.at[d], z_recv.at[d], at_core).wait_recv()
                to_x(here, here, d)
                to_core(here, here, 0, d)
            for e in range(1, x_n):
                here = slot(((x + x_n - e) % x_n) * core_n + core, k)
                remote(here, here, x_send.at[e - 1, d], x_recv.at[e - 1, d], at_core).wait_recv()
                to_core(here, here, e, d)
        if core_n > 1:
            for d in range(z_count):
                k = (z + z_count - d) % z_count
                for e in range(x_n):
                    here = slot(((x + x_n - e) % x_n) * core_n + 1 - core, k)
                    remote(here, here, c_send.at[e, d], c_recv.at[e, d], at_core).wait_recv()
        return sent

    rows = n_ref.shape[0]
    width = n_ref.shape[1]

    def normed_slot(a, b):
        return nrm.at[a, b]

    pending = gathered(normed_slot, n_ref, gather_sems[:6])
    nrm[q, z] = n_ref[...]
    get_ow.wait()
    partial = jnp.zeros(both.shape[1:], jnp.float32)
    for k in range(q_count):
        partial = partial + jnp.dot(
            nrm[k].reshape(z_count * rows, width),
            ow[k * width : (k + 1) * width, :],
            preferred_element_type=jnp.float32,
        )
    both[t] = partial
    tp_copies = []
    for d in range(1, tp):
        copy = remote(both.at[t], both.at[t], tp_send.at[d], tp_recv.at[d], (c, (t + d) % tp))
        copy.start()
        tp_copies.append(copy)
    for d in range(1, tp):
        here = both.at[(t + tp - d) % tp]
        remote(here, here, tp_send.at[d], tp_recv.at[d], (c, (t + d) % tp)).wait_recv()
    summed = both[0]
    for k in range(1, tp):
        summed = summed + both[k]
    hid[q, z] = (r_ref[...].astype(jnp.float32) + summed).astype(jnp.bfloat16)

    def hidden_slot(a, b):
        return hid.at[a, b]

    pending = pending + tp_copies + gathered(hidden_slot, hid.at[q, z], gather_sems[6:])
    block = hid.shape[3]
    all_rows = hid.shape[2]
    squares = jnp.zeros((all_rows, 1), jnp.float32)
    for k in range(z_count):
        for a in range(q_count):
            piece = hid[a, k].astype(jnp.float32)
            squares = squares + jnp.sum(piece * piece, axis=1, keepdims=True)
    inverse = lax.rsqrt(squares / (n * block) + epsilon)
    for k in range(z_count):
        for a in range(q_count):
            first = (k * q_count + a) * block
            span = slice(first, first + block)
            feat[:, span] = (
                hid[a, k].astype(jnp.float32) * inverse * g_ref[:, span]
            ).astype(jnp.bfloat16)
    get_hw.wait()
    vocab = hw.shape[1]
    tile = min(256, vocab)

    def one_tile(i, carry):
        cols = pl.ds(pl.multiple_of(i * tile, 128), tile)
        logit[:, cols] = jnp.dot(feat[...], hw[:, cols], preferred_element_type=jnp.float32)
        return carry

    lax.fori_loop(0, vocab // tile, one_tile, 0)
    values = logit[...]
    top = jnp.max(values, axis=1, keepdims=True)
    added = jnp.sum(jnp.exp(values - top), axis=1, keepdims=True)
    column = t_ref[...] - me * vocab
    places = lax.broadcasted_iota(jnp.int32, values.shape, 1)
    hit = jnp.sum(jnp.where(places == column, values, 0.0), axis=1, keepdims=True)
    lane = lax.broadcasted_iota(jnp.int32, (all_rows, 128), 1)
    packed = jnp.where(lane == 0, top, jnp.where(lane == 1, added, jnp.where(lane == 2, hit, 0.0)))
    turned = packed.T[:8]
    stat[...] = turned

    def go(d, carry):
        remote(
            stat, every.at[me], st_send.at[d], st_recv.at[d], device((me + d) % total)
        ).start()
        return carry

    lax.fori_loop(1, total, go, 0)
    every[me] = turned

    def done(d, carry):
        here = every.at[(me + total - d) % total]
        copy = remote(stat, here, st_send.at[d], st_recv.at[d], device((me + d) % total))
        copy.wait_send()
        copy.wait_recv()
        return carry

    lax.fori_loop(1, total, done, 0)
    for copy in pending:
        copy.wait_send()
    found = every[...]
    tops = found[:, 0, :]
    row_top = jnp.max(tops, axis=0, keepdims=True)
    full = jnp.sum(found[:, 1, :] * jnp.exp(tops - row_top), axis=0, keepdims=True)
    picked = jnp.sum(found[:, 2, :], axis=0, keepdims=True)
    log_prob = picked - row_top - jnp.log(full)
    out[0:1, :] = log_prob
    out[1:2, :] = 0.5 * jnp.square(log_prob - p_ref[...])


def tail(normed, out_weight, head_weight, res, gain, targets, policy, n, tp, q_count, z_count):
    dma = pltpu.SemaphoreType.DMA
    total = n * tp
    rows, width = normed.shape
    all_rows = z_count * rows
    block = out_weight.shape[1]
    core_n = 2 if q_count % 2 == 0 else 1
    x_n = q_count // core_n
    vmem = pltpu.VMEM
    bf16, f32 = jnp.bfloat16, jnp.float32
    e_n = max(x_n - 1, 1)
    sems = [
        dma((z_count,)), dma((z_count,)), dma((e_n, z_count)), dma((e_n, z_count)),
        dma((x_n, z_count)), dma((x_n, z_count)),
    ]
    operands = (
        normed, out_weight, head_weight, res, gain[None], targets[:, None], policy[None]
    )
    run, extra = staged(
        functools.partial(tail_kernel, n, tp, q_count, z_count), (1, 2), len(operands),
        operands[:1] + operands[3:],
    )
    result = pl.pallas_call(
        run,
        out_shape=jax.ShapeDtypeStruct((2, all_rows), f32),
        in_specs=[ANY] * len(operands),
        out_specs=VMEM,
        scratch_shapes=[
            vmem(out_weight.shape, bf16),
            vmem(head_weight.shape, bf16),
            vmem((q_count, z_count, rows, width), bf16),
            vmem((tp, all_rows, block), f32),
            vmem((q_count, z_count, all_rows, block), bf16),
            vmem((all_rows, n * block), bf16),
            vmem((all_rows, head_weight.shape[1]), f32),
            vmem((8, all_rows), f32),
            vmem((total, 8, all_rows), f32),
            dma((2,)), dma((tp,)), dma((tp,)), dma((total,)), dma((total,)),
        ] + sems + sems + extra,
        compiler_params=pltpu.CompilerParams(
            collective_id=3, has_side_effects=True, vmem_limit_bytes=58 * 1024 * 1024
        ),
    )(*operands)
    return result[0], result[1]


def halves(a):
    hi = a.astype(jnp.bfloat16)
    return hi, (a - hi.astype(jnp.float32)).astype(jnp.bfloat16)


def thirds(a):
    hi = a.astype(jnp.bfloat16)
    rest = a - hi.astype(jnp.float32)
    mid = rest.astype(jnp.bfloat16)
    return hi, mid, (rest - mid.astype(jnp.float32)).astype(jnp.bfloat16)


def column(row, first, count):
    lanes = row.shape[1]
    spot = lax.broadcasted_iota(jnp.int32, (count, lanes), 0) + first
    hit = lax.broadcasted_iota(jnp.int32, (count, lanes), 1) == spot
    return jnp.sum(jnp.where(hit, jnp.broadcast_to(row, (count, lanes)), 0.0), axis=1, keepdims=True)


def one_kernel(n, tp, *refs):
    names, refs = refs[0], refs[1:]
    r = dict(zip(names, refs))
    f32, bf16 = jnp.float32, jnp.bfloat16
    c, t = lax.axis_index("ctx"), lax.axis_index("tp")
    total = n * tp
    me = c * tp + t
    chips = n // 2
    z_n = chips // 2
    k, p = c % 2, c // 2
    x, z = p % 2, p // 2

    def dev(z_, x_, k_):
        return ((z_ * 2 + x_) * 2 + k_, t)

    core_peer, x_peer, y_peer = dev(z, x, 1 - k), dev(z, 1 - x, k), (c, 1 - t)
    T, C = r["x"].shape
    W = C // 2
    S = r["s"].shape[2] // 2
    G = S // STATE
    GW = W // G
    H = r["d"].shape[0]
    HC = H // 2
    Tc = 2 * T
    r8 = r["scored"].shape[0]
    RC = 2 * r8
    R = chips * RC
    taps = r["tx"].shape[0]
    blk = r["ow"].shape[1] // tp
    D = n * tp * blk
    V = r["hw"].shape[1]
    per = n // tp

    barrier = pltpu.get_barrier_semaphore()

    def hello(d, carry):
        other = (me + d) % total
        pl.semaphore_signal(
            barrier, inc=1, device_id=(other // tp, other % tp), device_id_type=MESH
        )
        return carry

    lax.fori_loop(1, total, hello, 0)

    def lanes(a, size):
        return pl.ds(pl.multiple_of(a * size, 128), size)

    local = {}

    def fetch(name, src, dst):
        copy = pltpu.make_async_copy(src, dst, r["own"].at[len(local)])
        local[name] = copy
        copy.start()

    def arrived(ref, sem):
        pltpu.make_async_copy(ref, ref, sem).wait()

    sent = []

    def push(copy, when=None):
        sent.append((copy, when))
        if when is None:
            copy.start()
        else:
            pl.when(when)(copy.start)

    fetch("resets", r["resets"], r["resv"])
    fetch("scored", r["scored"], r["spot"])
    fetch("s", r["s"].at[:, :, lanes(k, S)], r["sc"].at[k])
    fetch("ts", r["ts"].at[:, :, lanes(k, S)], r["tsv"])
    half_heads = pl.ds(pl.multiple_of(k * HC, 8), HC)
    fetch("d", r["d"].at[half_heads], r["dc"].at[k])
    fetch("rate", r["rate"], r["ratev"])
    fetch("x", r["x"].at[:, lanes(k, W)], r["xc"].at[k])
    fetch("tx", r["tx"].at[:, lanes(k, W)], r["txv"])
    fetch("g", r["g"], r["gv"])
    fetch("res", r["res"], r["rv"])
    fetch("skip", r["skip"], r["skipv"])
    fetch("gain", r["gain"].at[:, lanes(k, W)], r["gainv"])
    fetch("fg", r["fg"], r["fgv"])
    fetch("tgt", r["tgt"], r["tgtv"])
    fetch("pol", r["pol"], r["polv"])
    fetch("ow", r["ow"], r["oww"])

    first = p == 0

    @pl.when(first)
    def _():
        r["xh"][...] = jnp.zeros(r["xh"].shape, bf16)
        r["sh"][...] = jnp.zeros(r["sh"].shape, bf16)
        r["mh"][...] = jnp.zeros(r["mh"].shape, f32)

    local["resets"].wait()
    local["scored"].wait()
    lane8 = lax.broadcasted_iota(jnp.int32, (8, T), 1)
    row8 = lax.broadcasted_iota(jnp.int32, (8, T), 0)
    places = jnp.zeros((8, T), f32)
    for i in range(r8):
        places = jnp.where(lane8 == i, (r["spot"][i] - c * T).astype(f32), places)
    flags_here = jnp.broadcast_to(r["resv"][...].astype(f32), (8, T))
    r["meta"][...] = jnp.where(row8 == 0, flags_here, places)

    pl.semaphore_wait(barrier, total - 1)

    send, recv = r["core_send"], r["core_recv"]
    edge_send, edge_recv = r["edge_send"], r["edge_recv"]
    swap = (
        (r["s"].at[:, :, lanes(1 - k, S)], r["sc"].at[k]),
        (r["meta"], r["mc"].at[k]),
        (r["d"].at[pl.ds(pl.multiple_of((1 - k) * HC, 8), HC)], r["dc"].at[k]),
        (r["x"].at[:, lanes(1 - k, W)], r["xc"].at[k]),
    )
    for i, (a, b) in enumerate(swap):
        push(remote(a, b, send.at[i], recv.at[i], core_peer))
    last_core = (k == 1) & (p < chips - 1)
    tail = pl.ds(T - EDGE, EDGE)
    nxt = jnp.minimum(p + 1, chips - 1)
    for j in range(2):
        triple = (
            (r["s"].at[:, tail, j * S : (j + 1) * S], r["sh"]),
            (r["meta"], r["mh"]),
            (r["x"].at[tail, j * W : (j + 1) * W], r["xh"]),
        )
        for i, (a, b) in enumerate(triple):
            push(remote(a, b, edge_send.at[j, i], edge_recv.at[i], (nxt * 2 + j, t)), last_core)
    r["mc"][k] = r["meta"][...]

    def from_core(i, buf):
        arrived(buf.at[1 - k], recv.at[i])

    def from_edge(i, ref):
        @pl.when(jnp.logical_not(first))
        def _():
            arrived(ref, edge_recv.at[i])

    from_core(1, r["mc"])
    from_edge(1, r["mh"])
    flags = jnp.concatenate([r["mh"][...], r["mc"][0], r["mc"][1]], axis=1)
    clear = 1.0 - flags
    keeping = jnp.ones((8, 3 * T), f32)
    columns = [keeping]
    for off in range(1, taps):
        shifted = clear if off == 1 else pltpu.roll(clear, off - 1, 1)
        keeping = keeping * shifted
        columns.append(keeping)
    keep_rows = jnp.zeros((8, 3 * T), f32)
    row8w = lax.broadcasted_iota(jnp.int32, (8, 3 * T), 0)
    for off in range(taps):
        keep_rows = jnp.where(row8w == off, jnp.broadcast_to(columns[off][0:1], (8, 3 * T)), keep_rows)
    keep = keep_rows[:, T:].T
    for off in range(1, taps):
        r["kb"][off] = jnp.broadcast_to(keep[:, off : off + 1], (Tc, 128))
    wide_keep = [None] + [r["kb"].at[off] for off in range(1, taps)]

    spots = jnp.concatenate(
        [column(r["mc"][j][1:2], 0, r8) + j * T for j in range(2)], axis=0
    ).astype(jnp.int32)
    lane_t = lax.broadcasted_iota(jnp.int32, (RC, Tc), 1)
    pick_f = jnp.where(spots == lane_t, 1.0, 0.0)
    pick = pick_f.astype(bf16)

    def filtered(pad, kernel, start, size):
        width = pad.shape[1]
        acc = kernel[0:1] * pad[EDGE + start : EDGE + start + size, :]
        for off in range(1, taps):
            kept = wide_keep[off][start : start + size, :]
            kept = jnp.concatenate([kept] * (width // 128), axis=1)
            acc = acc + kept * (
                kernel[off : off + 1] * pad[EDGE - off + start : EDGE - off + start + size, :]
            )
        return jax.nn.silu(acc).astype(bf16)

    local["s"].wait()
    local["ts"].wait()
    from_core(0, r["sc"])
    from_edge(0, r["sh"])
    pad = r["pad"]
    band = 64
    for which, target in ((1, r["reads"]), (0, r["writes"])):
        for g in range(G):
            cols = slice(g * STATE, (g + 1) * STATE)
            pad_s = r["pad_s"]
            pad_s[:EDGE, :] = r["sh"][which, :, cols].astype(f32)
            for j in range(2):
                pad_s[EDGE + j * T : EDGE + (j + 1) * T, :] = r["sc"][j, which, :, cols].astype(f32)
            kernel = r["tsv"][which, :, cols]
            for b in range(Tc // band):
                target[b * band : (b + 1) * band, cols] = filtered(pad_s, kernel, b * band, band)
        if which == 1:
            r["mine_r"][...] = jnp.dot(
                pick, r["reads"][...], preferred_element_type=f32
            ).astype(bf16)
            for d in range(1, chips):
                push(remote(
                    r["mine_r"], r["all_r"].at[p], r["r_send"].at[d], r["r_recv"].at[d],
                    (((p + d) % chips) * 2 + k, t),
                ))
            r["all_r"][p] = r["mine_r"][...]

    local["d"].wait()
    local["rate"].wait()
    from_core(2, r["dc"])
    steps = jnp.concatenate([r["dc"][0], r["dc"][1]], axis=1)
    lower = jnp.where(
        lax.broadcasted_iota(jnp.int32, (Tc, Tc), 0) <= lax.broadcasted_iota(jnp.int32, (Tc, Tc), 1),
        1.0, 0.0,
    ).astype(bf16)
    rate_col = column(r["ratev"][...], k * HC, HC)
    runs = jnp.concatenate([-rate_col * steps, flags[:, T:]], axis=0)
    sums3 = jnp.dot(jnp.concatenate(thirds(runs), axis=0), lower, preferred_element_type=f32)
    count = HC + 8
    sums = sums3[:count] + sums3[count : 2 * count] + sums3[2 * count :]
    cumulated = sums[:HC]
    segment = sums[HC : HC + 1]
    last = cumulated[:, Tc - 1 : Tc]
    last_seg = segment[:, Tc - 1 : Tc]
    plane = jnp.broadcast_to(jnp.exp(last) * jnp.where(last_seg == 0.0, 1.0, 0.0), (HC, 128))
    r["mine_pd"][...] = jnp.concatenate([plane.T[:8], jnp.zeros((8, 128 - HC), f32)], axis=1)
    for d in range(1, chips):
        push(remote(
            r["mine_pd"], r["all_pd"].at[p], r["pd_send"].at[d], r["pd_recv"].at[d],
            (((p + d) % chips) * 2 + k, t),
        ))
    r["all_pd"][p] = r["mine_pd"][...]
    at_rows = lax.dot_general(
        pick_f, sums, (((1,), (1,)), ((), ())), precision=precise, preferred_element_type=f32
    )
    row_cum = at_rows[:, :HC]
    row_seg = at_rows[:, HC : HC + 1]
    to_end = jnp.exp(last - cumulated) * jnp.where(segment == last_seg, 1.0, 0.0) * steps
    r["te"][...] = jnp.concatenate(halves(to_end.T), axis=1)
    for g in range(G):
        r["wT"][g] = r["writes"][:, g * STATE : (g + 1) * STATE].astype(f32).T.astype(bf16)

    chunk = 256

    def spread_cols(j, size, offset):
        head = lax.broadcasted_iota(jnp.int32, (size, chunk), 0) % (size // 2)
        lane = lax.broadcasted_iota(jnp.int32, (size, chunk), 1)
        return jnp.where(head == offset + (j * chunk + lane) // HEAD_DIM, 1.0, 0.0).astype(bf16)

    local["x"].wait()
    local["tx"].wait()
    from_core(3, r["xc"])
    from_edge(2, r["xh"])

    def conv_step(j, carry):
        cols = lanes(j, chunk)
        pad[:EDGE, :] = r["xh"][:, cols].astype(f32)
        for i in range(2):
            pad[EDGE + i * T : EDGE + (i + 1) * T, :] = r["xc"][i, :, cols].astype(f32)
        kernel = r["txv"][:, cols]
        for b in range(Tc // band):
            r["values"][b * band : (b + 1) * band, cols] = filtered(pad, kernel, b * band, band)
        grown = jnp.dot(r["te"][...], spread_cols(j, 2 * HC, 0), preferred_element_type=f32)
        hi, lo = halves(r["values"][:, cols].astype(f32) * grown)
        w_t = r["wT"][(j * chunk) // GW]
        state = jnp.dot(w_t, hi, preferred_element_type=f32) + jnp.dot(
            w_t, lo, preferred_element_type=f32
        )
        s_hi, s_lo = halves(state)
        r["S2"][:STATE, cols] = s_hi
        r["S2"][STATE:, cols] = s_lo
        return carry

    lax.fori_loop(0, W // chunk, conv_step, 0)

    fetch("hw", r["hw"], r["hww"])

    for d in range(1, chips):
        here = (p + chips - d) % chips
        arrived(r["all_r"].at[here], r["r_recv"].at[d])
        arrived(r["all_pd"].at[here], r["pd_recv"].at[d])
    for g in range(G):
        rows_g = r["all_r"][:, :, g * STATE : (g + 1) * STATE].reshape(R, STATE)
        r["rr"][g, :, :STATE] = rows_g
        r["rr"][g, :, STATE:] = rows_g
    run_w = jnp.ones((1, 128), f32)
    weights = []
    for d in range(chips):
        weights.append(jnp.broadcast_to(run_w, (RC, 128)))
        run_w = jnp.where(d > p, run_w * r["all_pd"][d][0:1], run_w)
    far = jnp.concatenate(weights, axis=0)[:, :HC]
    r["ww"][...] = jnp.concatenate(halves(far), axis=1)

    def y_step(j, carry):
        cols = lanes(j, chunk)
        y = jnp.dot(r["rr"][(j * chunk) // GW], r["S2"][:, cols], preferred_element_type=f32)
        grown = jnp.dot(r["ww"][...], spread_cols(j, 2 * HC, 0), preferred_element_type=f32)
        r["yf"][:, cols] = y * grown
        return carry

    lax.fori_loop(0, W // chunk, y_step, 0)

    def y_rows(zd, xd):
        return r["yf"][pl.ds(pl.multiple_of((zd * 2 + xd) * RC, 16), RC), :]

    for zd in range(z_n - 1, -1, -1):
        goes = (zd > z) | ((zd == z) & (x == 0))

        @pl.when(goes)
        def _():
            r["xsend"][zd] = y_rows(zd, 1 - x)

        push(
            remote(r["xsend"].at[zd], r["xr"].at[zd], r["x_send"].at[zd], r["x_recv"].at[zd], x_peer),
            goes,
        )

    local["g"].wait()
    local["res"].wait()
    own_pick = jnp.where(
        column(r["meta"][1:2], 0, r8) == lax.broadcasted_iota(jnp.int32, (r8, T), 1).astype(f32),
        1.0, 0.0,
    ).astype(bf16)
    r["gc"][k] = jnp.dot(
        own_pick, r["gv"][:, lanes(k, W)], preferred_element_type=f32
    ).astype(bf16)
    r["gsend"][...] = jnp.dot(
        own_pick, r["gv"][:, lanes(1 - k, W)], preferred_element_type=f32
    ).astype(bf16)
    push(remote(r["gsend"], r["gc"].at[k], send.at[4], recv.at[4], core_peer))
    res_rows = jnp.dot(own_pick, r["rv"][...], preferred_element_type=f32).astype(bf16)

    for j in range(per * tp):
        r["rsend"][j] = res_rows[:, j * blk : (j + 1) * blk]

    def res_copy(j, to_t):
        i = j * tp + to_t
        return remote(
            r["rsend"].at[i], r["ro"].at[c], r["res_send"].at[i], r["res_recv"].at[c],
            (t * per + j, to_t),
        )

    for j in range(per):
        for to_t in range(tp):
            mine = (t * per + j == c) & (to_t == t)
            push(res_copy(j, to_t), jnp.logical_not(mine))

            @pl.when(mine)
            def _():
                pltpu.make_async_copy(
                    r["rsend"].at[j * tp + to_t], r["ro"].at[c], r["res_recv"].at[c]
                ).start()

    mine_r = r["mine_r"][...]
    scores = [
        lax.dot_general(
            mine_r[:, g * STATE : (g + 1) * STATE], r["writes"][:, g * STATE : (g + 1) * STATE],
            (((1,), (1,)), ((), ())), preferred_element_type=f32,
        )
        for g in range(G)
    ]
    causal = (spots >= lane_t) & (row_seg == segment)
    quad = 4
    quad_w = quad * HEAD_DIM
    which_head = lax.broadcasted_iota(jnp.int32, (RC, quad_w), 1) // HEAD_DIM

    def within(q):
        mixes = []
        for i in range(quad):
            h = q * quad + i
            gaps = row_cum[:, h : h + 1] - cumulated[h : h + 1]
            decay = jnp.where(causal, jnp.exp(jnp.where(causal, gaps, 0.0)), 0.0)
            mixes.append(scores[h * HEAD_DIM // GW] * decay * steps[h : h + 1])
        both = jnp.concatenate(halves(jnp.concatenate(mixes, axis=0)), axis=0)
        span = slice(q * quad_w, (q + 1) * quad_w)
        product = jnp.dot(both, r["values"][:, span], preferred_element_type=f32)
        product = product[: quad * RC] + product[quad * RC :]
        out = product[:RC]
        for i in range(1, quad):
            out = jnp.where(which_head == i, product[i * RC : (i + 1) * RC], out)
        r["mixed"][:, span] = out

    quads = HC // quad
    for q in range(quads // 2):
        within(q)
    for zd in range(z_n - 1, 0, -1):
        goes = zd > z

        @pl.when(goes)
        def _():
            arrived(r["xr"].at[zd], r["x_recv"].at[zd])
            r["zsend"][zd] = y_rows(zd, x) + r["xr"][zd]

        push(
            remote(
                r["zsend"].at[zd], r["zr"].at[z], r["z_send"].at[zd], r["z_recv"].at[z],
                dev(zd, x, k),
            ),
            goes,
        )
    for q in range(quads // 2, quads):
        within(q)

    local["skip"].wait()
    local["gain"].wait()
    from_start = jnp.exp(row_cum) * jnp.where(row_seg == 0.0, 1.0, 0.0)
    starts = jnp.concatenate(halves(from_start), axis=1)
    skip3 = jnp.concatenate(
        [jnp.broadcast_to(a, (8, H)) for a in thirds(jnp.broadcast_to(r["skipv"][...], (8, H)))], axis=0
    )
    from_core(4, r["gc"])
    gate = jnp.concatenate([r["gc"][0].astype(f32), r["gc"][1].astype(f32)], axis=0)

    def widen_step(j, carry):
        cols = lanes(j, chunk)
        own_values = jnp.dot(pick, r["values"][:, cols], preferred_element_type=f32)
        head = lax.broadcasted_iota(jnp.int32, (H, chunk), 0)
        lane = lax.broadcasted_iota(jnp.int32, (H, chunk), 1)
        all_heads = jnp.where(head == k * HC + (j * chunk + lane) // HEAD_DIM, 1.0, 0.0).astype(bf16)
        grown = jnp.dot(skip3, all_heads, preferred_element_type=f32)
        skip_row = grown[0:1] + grown[8:9] + grown[16:17]
        r["mixed"][:, cols] = r["mixed"][:, cols] + skip_row * own_values
        r["starts"][:, cols] = jnp.dot(starts, spread_cols(j, 2 * HC, 0), preferred_element_type=f32)
        return carry

    lax.fori_loop(0, W // chunk, widen_step, 0)
    gate = jax.nn.silu(gate)

    carried = r["carried"]
    carried[...] = jnp.zeros((RC, W), f32)

    @pl.when(x == 1)
    def _():
        here = r["xr"].at[z]
        pltpu.make_async_copy(here, here, r["x_recv"].at[z]).wait()
        carried[...] = r["xr"][z].astype(f32)

    for zs in range(z_n - 1):
        @pl.when(zs < z)
        def _():
            arrived(r["zr"].at[zs], r["z_recv"].at[zs])
            carried[...] = carried[...] + r["zr"][zs].astype(f32)

    gated = (r["mixed"][...] + carried[...] * r["starts"][...]) * gate
    for g in range(G):
        span = slice(g * GW, (g + 1) * GW)
        part = gated[:, span]
        scale = lax.rsqrt(jnp.mean(part * part, axis=1, keepdims=True) + epsilon)
        r["normed"][:, span] = (part * scale * r["gainv"][:, span]).astype(bf16)

    nrm = r["nrm"]
    mine = r["normed"]
    z_send, z_recv, x_send, x_recv, c_send, c_recv = r["gather1"]

    def slot(z_, x_, k_):
        return nrm.at[k_, z_ * 2 + x_]

    home = slot(z, x, k)
    for d in range(1, z_n):
        push(remote(mine, home, z_send.at[d], z_recv.at[d], dev((z + d) % z_n, x, k)))
    push(remote(mine, home, x_send.at[0], x_recv.at[0], x_peer))
    push(remote(mine, home, c_send.at[0, 0], c_recv.at[0, 0], core_peer))
    nrm[k, p] = mine[...]
    for d in range(z_n):
        from_z = (z + z_n - d) % z_n
        if d:
            here = slot(from_z, x, k)
            arrived(here, z_recv.at[d])
            push(remote(here, here, x_send.at[d], x_recv.at[d], x_peer))
            push(remote(here, here, c_send.at[0, d], c_recv.at[0, d], core_peer))
        here = slot(from_z, 1 - x, k)
        arrived(here, x_recv.at[d])
        push(remote(here, here, c_send.at[1, d], c_recv.at[1, d], core_peer))
    for d in range(z_n):
        from_z = (z + z_n - d) % z_n
        for e, x_ in ((0, x), (1, 1 - x)):
            arrived(slot(from_z, x_, 1 - k), c_recv.at[e, d])
    local["ow"].wait()
    partial = jnp.zeros((R, tp * blk), f32)
    for j in range(2):
        partial = partial + jnp.dot(
            nrm[j].reshape(R, W), r["oww"][j * W : (j + 1) * W, :], preferred_element_type=f32
        )
    for j in range(tp):
        r["pt"][j] = partial[:, j * blk : (j + 1) * blk]
    push(remote(r["pt"].at[1 - t], r["pr"], r["t_send"], r["t_recv"], y_peer))
    for j in range(n):
        arrived(r["ro"].at[j], r["res_recv"].at[j])
    res_all = r["ro"][...].astype(f32).reshape(R, blk)
    arrived(r["pr"], r["t_recv"])
    hid = r["hid"]
    hid[c, t] = (res_all + (r["pt"][t] + r["pr"][...])).astype(bf16)

    z_send, z_recv, a_send, a_recv, b_send, b_recv, c_send, c_recv = r["gather2"]
    even = k == 0
    a0, b0 = jnp.where(even, t, x), jnp.where(even, x, t)

    def place(z_, a_, b_, k_):
        y_, x_ = jnp.where(k_ == 0, a_, b_), jnp.where(k_ == 0, b_, a_)
        return hid.at[(z_ * 2 + x_) * 2 + k_, y_]

    a_peer = (jnp.where(even, c, x_peer[0]), jnp.where(even, 1 - t, t))
    b_peer = (jnp.where(even, x_peer[0], c), jnp.where(even, t, 1 - t))

    def to_a(here, d):
        push(remote(here, here, a_send.at[d], a_recv.at[d], a_peer))

    def to_b(here, e, d):
        push(remote(here, here, b_send.at[e, d], b_recv.at[e, d], b_peer))

    def to_core(here, e, d):
        push(remote(here, here, c_send.at[e, d], c_recv.at[e, d], core_peer))

    home = place(z, a0, b0, k)
    for d in range(1, z_n):
        push(remote(home, home, z_send.at[d], z_recv.at[d], dev((z + d) % z_n, x, k)))
    to_a(home, 0)
    to_b(home, 0, 0)
    to_core(home, 0, 0)
    for d in range(z_n):
        from_z = (z + z_n - d) % z_n
        if d:
            here = place(from_z, a0, b0, k)
            arrived(here, z_recv.at[d])
            to_a(here, d)
            to_b(here, 0, d)
            to_core(here, 0, d)
        here = place(from_z, 1 - a0, b0, k)
        arrived(here, a_recv.at[d])
        to_b(here, 1, d)
        to_core(here, 1, d)
        if d:
            for e, a_ in ((0, a0), (1, 1 - a0)):
                here = place((z + z_n - d + 1) % z_n, a_, 1 - b0, k)
                arrived(here, b_recv.at[e, d - 1])
                to_core(here, 2 + e, d - 1)
    for e, a_ in ((0, a0), (1, 1 - a0)):
        here = place((z + 1) % z_n, a_, 1 - b0, k)
        arrived(here, b_recv.at[e, z_n - 1])
        to_core(here, 2 + e, z_n - 1)
    oa, ob = jnp.where(even, x, t), jnp.where(even, t, x)
    for d in range(z_n):
        from_z = (z + z_n - d) % z_n
        for e, (a_, b_) in enumerate(((oa, ob), (1 - oa, ob), (oa, 1 - ob), (1 - oa, 1 - ob))):
            arrived(place(from_z, a_, b_, 1 - k), c_recv.at[e, d])

    squares = jnp.zeros((R, 1), f32)
    for a in range(n):
        for b in range(tp):
            piece = hid[a, b].astype(f32)
            squares = squares + jnp.sum(piece * piece, axis=1, keepdims=True)
    inverse = lax.rsqrt(squares / D + epsilon)
    local["fg"].wait()
    feat = r["feat"]
    for a in range(n):
        for b in range(tp):
            start = (a * tp + b) * blk
            span = slice(start, start + blk)
            feat[:, span] = (hid[a, b].astype(f32) * inverse * r["fgv"][:, span]).astype(bf16)
    local["hw"].wait()
    tile = min(256, V)
    logit = r["logit"]

    def one_tile(i, carry):
        cols = lanes(i, tile)
        logit[:, cols] = jnp.dot(feat[...], r["hww"][:, cols], preferred_element_type=f32)
        return carry

    lax.fori_loop(0, V // tile, one_tile, 0)
    values = logit[...]
    top = jnp.max(values, axis=1, keepdims=True)
    added = jnp.sum(jnp.exp(values - top), axis=1, keepdims=True)
    local["tgt"].wait()
    local["pol"].wait()
    target = column(r["tgtv"][...].astype(f32), 0, R).astype(jnp.int32) - me * V
    hit = jnp.sum(
        jnp.where(lax.broadcasted_iota(jnp.int32, values.shape, 1) == target, values, 0.0),
        axis=1, keepdims=True,
    )
    lane = lax.broadcasted_iota(jnp.int32, (R, 128), 1)
    packed = jnp.where(lane == 0, top, jnp.where(lane == 1, added, jnp.where(lane == 2, hit, 0.0)))
    turned = packed.T[:8]
    stat, every = r["stat"], r["every"]
    stat[...] = turned
    st_send, st_recv = r["st_send"], r["st_recv"]

    def device(a):
        return (a // tp, a % tp)

    def go(d, carry):
        remote(
            stat, every.at[me], st_send.at[d], st_recv.at[d], device((me + d) % total)
        ).start()
        return carry

    lax.fori_loop(1, total, go, 0)
    every[me] = turned

    for copy, when in sent:
        if when is None:
            copy.wait_send()
        else:
            pl.when(when)(copy.wait_send)

    def done(d, carry):
        here = every.at[(me + total - d) % total]
        copy = remote(stat, here, st_send.at[d], st_recv.at[d], device((me + d) % total))
        copy.wait_send()
        copy.wait_recv()
        return carry

    lax.fori_loop(1, total, done, 0)
    found = every[...]
    tops = found[:, 0, :]
    row_top = jnp.max(tops, axis=0, keepdims=True)
    full = jnp.sum(found[:, 1, :] * jnp.exp(tops - row_top), axis=0, keepdims=True)
    picked = jnp.sum(found[:, 2, :], axis=0, keepdims=True)
    log_prob = picked - row_top - jnp.log(full)
    r["out_a"][...] = log_prob
    r["out_b"][...] = 0.5 * jnp.square(log_prob - r["polv"][...])


def fused(n, tp, x, g, s, d, resets, rate, skip, tx, ts, gain, ow, res, fg, hw, scored, tgt, pol):
    f32, bf16, i32 = jnp.float32, jnp.bfloat16, jnp.int32
    dma, vmem = pltpu.SemaphoreType.DMA, pltpu.VMEM
    chips = n // 2
    z_n = chips // 2
    T, C = x.shape
    W, Tc = C // 2, 2 * T
    S = s.shape[2] // 2
    G = S // STATE
    H = d.shape[0]
    HC = H // 2
    r8 = scored.shape[0]
    RC = 2 * r8
    R = chips * RC
    blk = ow.shape[1] // tp
    taps = tx.shape[0]
    total = n * tp
    inputs = dict(
        x=x, g=g, s=s, d=d, resets=resets[None], rate=rate[None], skip=skip[None], tx=tx, ts=ts,
        gain=gain[None], ow=ow, res=res, fg=fg[None], hw=hw, scored=scored, tgt=tgt[None], pol=pol[None],
    )
    scratch = dict(
        resv=vmem((1, T), i32), spot=pltpu.SMEM((r8,), i32), meta=vmem((8, T), f32),
        xc=vmem((2, T, W), bf16), xh=vmem((EDGE, W), bf16),
        sc=vmem((2, 2, T, S), bf16), sh=vmem((2, EDGE, S), bf16),
        dc=vmem((2, HC, T), f32), mc=vmem((2, 8, T), f32), mh=vmem((8, T), f32),
        gv=vmem(g.shape, bf16), rv=vmem(res.shape, bf16),
        gc=vmem((2, r8, W), bf16), gsend=vmem((r8, W), bf16),
        rsend=vmem((n, r8, blk), bf16), ro=vmem((n, r8, blk), bf16),
        txv=vmem((taps, W), f32), tsv=vmem((2, taps, S), f32), gainv=vmem((1, W), f32),
        ratev=vmem((1, H), f32), skipv=vmem((1, H), f32), fgv=vmem((1, n * tp * blk), f32),
        tgtv=vmem((1, R), i32), polv=vmem((1, R), f32),
        pad=vmem((EDGE + Tc, 256), f32), pad_s=vmem((EDGE + Tc, STATE), f32),
        kb=vmem((taps, Tc, 128), f32),
        reads=vmem((Tc, S), bf16), writes=vmem((Tc, S), bf16),
        mine_r=vmem((RC, S), bf16), all_r=vmem((chips, RC, S), bf16),
        mine_pd=vmem((8, 128), f32), all_pd=vmem((chips, 8, 128), f32),
        te=vmem((Tc, 2 * HC), bf16), wT=vmem((G, STATE, Tc), bf16),
        values=vmem((Tc, W), bf16), S2=vmem((2 * STATE, W), bf16),
        rr=vmem((G, R, 2 * STATE), bf16), ww=vmem((R, 2 * HC), bf16), yf=vmem((R, W), f32),
        xsend=vmem((z_n, RC, W), f32), xr=vmem((z_n, RC, W), f32),
        zsend=vmem((z_n, RC, W), f32), zr=vmem((z_n, RC, W), f32),
        mixed=vmem((RC, W), f32), starts=vmem((RC, W), f32), carried=vmem((RC, W), f32),
        normed=vmem((RC, W), bf16), nrm=vmem((2, chips, RC, W), bf16),
        pt=vmem((tp, R, blk), f32), pr=vmem((R, blk), f32),
        hid=vmem((n, tp, R, blk), bf16), feat=vmem((R, n * tp * blk), bf16),
        logit=vmem((R, hw.shape[1]), f32), stat=vmem((8, R), f32), every=vmem((total, 8, R), f32),
        oww=vmem(ow.shape, bf16), hww=vmem(hw.shape, bf16),
        own=dma((18,)), core_send=dma((5,)), core_recv=dma((5,)),
        edge_send=dma((2, 3)), edge_recv=dma((3,)),
        r_send=dma((chips,)), r_recv=dma((chips,)), pd_send=dma((chips,)), pd_recv=dma((chips,)),
        x_send=dma((z_n,)), x_recv=dma((z_n,)), z_send=dma((z_n,)), z_recv=dma((z_n,)),
        res_send=dma((n,)), res_recv=dma((n,)), t_send=dma(()), t_recv=dma(()),
        st_send=dma((total,)), st_recv=dma((total,)),
    )
    many = [("gather1", [dma((z_n,))] * 4 + [dma((2, z_n))] * 2)]
    many.append(("gather2", [dma((z_n,))] * 4 + [dma((2, z_n))] * 2 + [dma((4, z_n))] * 2))
    names = list(inputs) + ["out_a", "out_b"] + list(scratch)
    groups = [(name, len(sems)) for name, sems in many]
    extra = [sem for _, sems in many for sem in sems]

    def run(*refs):
        plain, rest = list(refs[: len(names)]), list(refs[len(names) :])
        for _, size in groups:
            plain.append(tuple(rest[:size]))
            rest = rest[size:]
        one_kernel(n, tp, names + [name for name, _ in groups], *plain)

    out = jax.ShapeDtypeStruct((1, R), f32)
    a, b = pl.pallas_call(
        run,
        out_shape=(out, out),
        in_specs=[ANY] * len(inputs),
        out_specs=(VMEM, VMEM),
        scratch_shapes=list(scratch.values()) + extra,
        compiler_params=pltpu.CompilerParams(
            collective_id=5, has_side_effects=True, vmem_limit_bytes=58 * 1024 * 1024
        ),
    )(*inputs.values())
    return a[0], b[0]


def body(
    inner_input,
    gate_input,
    state_inputs,
    step_size,
    resets,
    decay_rate,
    skip_gain,
    conv_inner,
    conv_state,
    norm_gain,
    out_weight,
    residual,
    final_gain,
    head_weight,
    scored,
    targets,
    policy_logprob,
):
    f32 = jnp.float32
    n, tp = lax.axis_size("ctx"), lax.axis_size("tp")
    c, t = lax.axis_index("ctx"), lax.axis_index("tp")
    if n % 4 == 0 and tp == 2 and (state_inputs.shape[2] // STATE) % 2 == 0:
        return fused(
            n, tp, inner_input, gate_input, state_inputs, step_size, resets, decay_rate, skip_gain,
            conv_inner, conv_state, norm_gain, out_weight, residual, final_gain, head_weight,
            scored, targets, policy_logprob,
        )
    taps = conv_inner.shape[0]
    rows_here = inner_input.shape[0]
    q_count = state_inputs.shape[2] // STATE
    z_count = n // q_count
    z, q = c // q_count, c % q_count
    picked_rows = scored.shape[0]
    local_rows = scored - c * rows_here
    here = jnp.arange(rows_here, dtype=jnp.int32)
    pick = (local_rows[:, None] == here[None, :]).astype(jnp.bfloat16)
    gate_rows = jnp.dot(pick, gate_input, preferred_element_type=f32).astype(jnp.bfloat16)
    res_rows = jnp.dot(pick, residual, preferred_element_type=f32).astype(jnp.bfloat16)
    meta = jnp.zeros((8, rows_here), f32)
    meta = meta.at[0].set(resets.astype(f32))
    meta = meta.at[1, :picked_rows].set(local_rows.astype(f32))
    xs, ss, ds, gs, ms, x_edge, s_edge, m_edge, res_all = spread(
        n, tp, q_count, inner_input, state_inputs, step_size, gate_rows, meta, res_rows
    )
    tokens = q_count * rows_here
    width = xs.shape[2]
    heads = ds.shape[1]
    rows = q_count * picked_rows
    gate = gs.reshape(rows, width)
    flags = ms[:, 0].reshape(tokens)
    spots = ms[:, 1, :picked_rows] + (jnp.arange(q_count) * rows_here).astype(f32)[:, None]
    spots = spots.reshape(rows, 1).astype(jnp.int32)
    margin = taps - 1
    f_tail = jnp.where(z > 0, m_edge[0, rows_here - margin :], 0.0)
    clear = 1.0 - jnp.concatenate([f_tail, flags])
    keeping = [jnp.ones((tokens,), f32)]
    for offset in range(1, taps):
        keeping.append(keeping[-1] * clear[margin - offset + 1 : margin - offset + 1 + tokens])
    keeps = jnp.pad(jnp.stack(keeping), ((0, -taps % 8), (0, 0)))
    normed = middle(
        xs, x_edge, ss, s_edge, keeps, ds, jnp.broadcast_to(flags[None], (8, tokens)), spots, gate,
        conv_inner, conv_state, decay_rate.reshape(q_count, heads, 1),
        skip_gain.reshape(q_count, 1, heads), norm_gain[None], q_count, z_count,
    )
    res = res_all.reshape(z_count * rows, -1)
    return tail(
        normed, out_weight, head_weight, res, final_gain, targets, policy_logprob,
        n, tp, q_count, z_count,
    )


def solution(mesh):
    return jax.shard_map(
        body,
        mesh=mesh,
        in_specs=(
            P("ctx", "tp"),
            P("ctx", "tp"),
            P(None, "ctx", "tp"),
            P("tp", "ctx"),
            P("ctx"),
            P("tp"),
            P("tp"),
            P(None, "tp"),
            P(None, None, "tp"),
            P("tp"),
            P("tp", "ctx"),
            P("ctx", "tp"),
            P(),
            P(None, ("ctx", "tp")),
            P("ctx"),
            P(),
            P(),
        ),
        out_specs=(P(), P()),
        check_vma=False,
    )
```

```python
import functools
import jax
import jax.numpy as jnp
from jax import lax
from jax.experimental import pallas as pl
from jax.experimental.pallas import tpu as pltpu
from jax.sharding import PartitionSpec as P

HEAD_DIM = 64
STATE = 128
EDGE = 16
LEVELS = 32767.0
TINY = 1e-30

epsilon = 1e-05
precise = lax.Precision.HIGHEST
MESH = pl.DeviceIdType.MESH
VMEM = pl.BlockSpec(memory_space=pltpu.VMEM)
ANY = pl.BlockSpec(memory_space=pl.ANY)


def remote(src, dst, send, recv, device):
    return pltpu.make_async_remote_copy(
        src_ref=src, dst_ref=dst, send_sem=send, recv_sem=recv, device_id=device, device_id_type=MESH
    )


def greet(devices):
    barrier = pltpu.get_barrier_semaphore()
    for device in devices:
        pl.semaphore_signal(barrier, inc=1, device_id=device, device_id_type=MESH)
    pl.semaphore_wait(barrier, len(devices))


def spread_kernel(n, tp, q_count, z_count, x_ref, s_ref, d_ref, g_ref, m_ref, r_ref,
                  xo, so, do, go, mo, xh, sh, mh, ro,
                  send, recv, own, edge_send, edge_recv, res_send, res_recv):
    c, t = lax.axis_index("ctx"), lax.axis_index("tp")
    z, q = c // q_count, c % q_count
    total = n * tp
    me = c * tp + t
    barrier = pltpu.get_barrier_semaphore()

    def hello(k, carry):
        other = (me + k) % total
        pl.semaphore_signal(
            barrier, inc=1, device_id=(other // tp, other % tp), device_id_type=MESH
        )
        return carry

    lax.fori_loop(1, total, hello, 0)
    pl.semaphore_wait(barrier, total - 1)
    width = xo.shape[2]
    heads = do.shape[1]
    rows = x_ref.shape[0]

    def cols(ref, k, size):
        return ref.at[:, pl.ds(pl.multiple_of(k * size, 128), size)]

    def parts(k):
        return (
            cols(x_ref, k, width),
            s_ref.at[:, :, pl.ds(pl.multiple_of(k * STATE, 128), STATE)],
            d_ref.at[pl.ds(pl.multiple_of(k * heads, 8), heads), :],
            cols(g_ref, k, width),
            m_ref,
        )

    def slots(k):
        return (xo.at[k], so.at[k], do.at[k], go.at[k], mo.at[k])

    started = []
    tail = pl.ds(rows - EDGE, EDGE)
    next_z = jnp.minimum(z + 1, z_count - 1)

    def edges(k, dst_c):
        wide = pl.ds(pl.multiple_of(k * width, 128), width)
        thin = pl.ds(pl.multiple_of(k * STATE, 128), STATE)
        triple = ((x_ref.at[tail, wide], xh), (s_ref.at[:, tail, thin], sh), (m_ref, mh))
        return [
            remote(a, b, edge_send.at[k, i], edge_recv.at[i], (dst_c, t))
            for i, (a, b) in enumerate(triple)
        ]

    sends_edge = (q == q_count - 1) & (z < z_count - 1)
    gets_edge = z > 0
    if z_count > 1:
        @pl.when(sends_edge)
        def _():
            for k in range(q_count):
                for copy in edges(k, (z + 1) * q_count + k):
                    copy.start()

    for d in range(1, q_count):
        k = (q + d) % q_count
        for i, (a, b) in enumerate(zip(parts(k), slots(q))):
            copy = remote(a, b, send.at[d - 1, i], recv.at[d - 1, i], (z * q_count + k, t))
            copy.start()
            started.append(copy)
    per = n // tp

    def res_copy(j, to_t):
        return remote(
            r_ref.at[j], ro.at[c],
            res_send.at[j * tp + to_t], res_recv.at[c], (t * per + j, to_t)
        )

    for j in range(per):
        for to_t in range(tp):
            mine = (t * per + j == c) & (to_t == t)

            @pl.when(jnp.logical_not(mine))
            def _():
                res_copy(j, to_t).start()

            @pl.when(mine)
            def _():
                pltpu.make_async_copy(r_ref.at[j], ro.at[c], res_recv.at[c]).start()
    locals_ = [
        pltpu.make_async_copy(a, b, own.at[i]) for i, (a, b) in enumerate(zip(parts(q), slots(q)))
    ]
    for copy in locals_:
        copy.start()
    for copy in locals_:
        copy.wait()
    for j in range(per):
        for to_t in range(tp):
            mine = (t * per + j == c) & (to_t == t)

            @pl.when(jnp.logical_not(mine))
            def _():
                res_copy(j, to_t).wait_send()
    for k in range(n):
        pltpu.make_async_copy(ro.at[k], ro.at[k], res_recv.at[k]).wait()
    for copy in started:
        copy.wait_send()
    for d in range(1, q_count):
        k = (q + q_count - d) % q_count
        for i, (a, b) in enumerate(zip(parts(q), slots(k))):
            remote(a, b, send.at[d - 1, i], recv.at[d - 1, i], (z * q_count + k, t)).wait_recv()
    if z_count > 1:
        @pl.when(sends_edge)
        def _():
            for k in range(q_count):
                for copy in edges(k, (z + 1) * q_count + k):
                    copy.wait_send()

        @pl.when(gets_edge)
        def _():
            for i, ref in enumerate((xh, sh, mh)):
                pltpu.make_async_copy(ref, ref, edge_recv.at[i]).wait()


def spread(n, tp, q_count, x, s, d, g, m, r):
    z_count = n // q_count
    rows, all_width = x.shape
    width = all_width // q_count
    heads = d.shape[0] // q_count
    block = r.shape[1] * tp // n
    r = r.reshape(r.shape[0], n // tp, block).transpose(1, 0, 2)
    shape = jax.ShapeDtypeStruct
    outs = (
        shape((q_count, rows, width), x.dtype),
        shape((q_count, 2, rows, STATE), s.dtype),
        shape((q_count, heads, rows), d.dtype),
        shape((q_count, g.shape[0], width), g.dtype),
        shape((q_count,) + m.shape, m.dtype),
        shape((EDGE, width), x.dtype),
        shape((2, EDGE, STATE), s.dtype),
        shape(m.shape, m.dtype),
        shape((n,) + r.shape[1:], r.dtype),
    )
    dma = pltpu.SemaphoreType.DMA
    peers = max(q_count - 1, 1)
    return pl.pallas_call(
        functools.partial(spread_kernel, n, tp, q_count, z_count),
        out_shape=outs,
        in_specs=[ANY, ANY, ANY, VMEM, VMEM, VMEM],
        out_specs=[VMEM] * len(outs),
        scratch_shapes=[
            dma((peers, 5)), dma((peers, 5)), dma((5,)), dma((q_count, 3)), dma((3,)),
            dma((n,)), dma((n,)),
        ],
        compiler_params=pltpu.CompilerParams(collective_id=0, has_side_effects=True),
    )(x, s, d, g, m, r)


def staged(kernel, skip, count, shapes):
    def run(*refs):
        ins, rest, held, sems = (
            refs[:count], refs[count : -len(shapes) - 1], refs[-len(shapes) - 1 : -1], refs[-1]
        )
        held = iter(held)
        views, copies = [], []
        for i, ref in enumerate(ins):
            if i in skip:
                views.append(ref)
                continue
            local = next(held)
            copy = pltpu.make_async_copy(ref, local, sems.at[len(copies)])
            copy.start()
            copies.append(copy)
            views.append(local)
        for copy in copies:
            copy.wait()
        kernel(*views, *rest)

    extra = [pltpu.VMEM(a.shape, a.dtype) for a in shapes]
    return run, extra + [pltpu.SemaphoreType.DMA((len(shapes),))]


def mid_kernel(q_count, z_count, x_ref, xe_ref, s_ref, se_ref, k_ref, d_ref, f_ref, spot_ref,
               gate_ref, tx_ref, ts_ref, rate_ref, skip_ref, gain_ref, out,
               pad_x, pad_s, values, writes, reads, mine_r, all_r, y, far, pd, far_pd, mixed, carried,
               r_send, r_recv, y_send, y_recv, p_send, p_recv):
    f32, bf16 = jnp.float32, jnp.bfloat16
    c, t = lax.axis_index("ctx"), lax.axis_index("tp")
    z, q = c // q_count, c % q_count
    barrier = pltpu.get_barrier_semaphore()

    def peer(d):
        return (((z + d) % z_count) * q_count + q, t)

    for d in range(1, z_count):
        pl.semaphore_signal(barrier, inc=1, device_id=peer(d), device_id_type=MESH)
    tokens, width = values.shape
    piece = tokens // q_count
    heads = d_ref.shape[1]
    rows = mine_r.shape[0]
    taps = tx_ref.shape[0]
    has_edge = (z > 0).astype(f32)
    keep = k_ref[...].T

    def filtered(pad, kernel, start, target):
        total = jnp.zeros((piece, pad.shape[1]), f32)
        for off in range(taps):
            total = total + (
                keep[start : start + piece, off : off + 1]
                * kernel[off : off + 1]
                * pad[EDGE - off + start : EDGE - off + start + piece, :]
            )
        target[start : start + piece, :] = jax.nn.silu(total).astype(bf16)

    thin = pl.ds(pl.multiple_of(q * STATE, 128), STATE)
    for which, target in ((1, reads), (0, writes)):
        edge = se_ref[which].astype(f32)
        pad_s[:EDGE, :] = jnp.where(has_edge > 0.0, edge, 0.0)
        for k in range(q_count):
            pad_s[EDGE + k * piece : EDGE + (k + 1) * piece, :] = s_ref[k, which].astype(f32)
        kernel = ts_ref[which, :, thin]
        for k in range(q_count):
            filtered(pad_s, kernel, k * piece, target)
    spots = spot_ref[...]
    lanes = lax.broadcasted_iota(jnp.int32, (rows, tokens), 1)
    pick_f = jnp.where(spots == lanes, 1.0, 0.0)
    pick = pick_f.astype(bf16)
    mine_r[...] = jnp.dot(pick, reads[...], preferred_element_type=f32).astype(bf16)
    pl.semaphore_wait(barrier, z_count - 1)
    sent = []
    for d in range(1, z_count):
        copy = remote(mine_r, all_r.at[z], r_send.at[d], r_recv.at[d], peer(d))
        copy.start()
        sent.append(copy)
    all_r[z] = mine_r[...]
    wide = pl.ds(pl.multiple_of(q * width, 128), width)
    kernel_x = tx_ref[:, wide]
    pad_x[:EDGE, :] = jnp.where(has_edge > 0.0, xe_ref[...].astype(f32), 0.0)
    for k in range(q_count):
        pad_x[EDGE + k * piece : EDGE + (k + 1) * piece, :] = x_ref[k].astype(f32)
    for k in range(q_count):
        filtered(pad_x, kernel_x, k * piece, values)
    steps = jnp.concatenate([d_ref[k] for k in range(q_count)], axis=1)
    lower = jnp.where(
        lax.broadcasted_iota(jnp.int32, (tokens, tokens), 0)
        <= lax.broadcasted_iota(jnp.int32, (tokens, tokens), 1),
        1.0, 0.0,
    )
    runs = jnp.concatenate([-rate_ref[q] * steps, f_ref[...]], axis=0)
    sums = jnp.dot(runs, lower, precision=precise, preferred_element_type=f32)
    cumulated = sums[:heads]
    segment = sums[heads : heads + 1]
    at_rows = lax.dot_general(
        pick_f, sums, (((1,), (1,)), ((), ())), precision=precise, preferred_element_type=f32
    )
    row_cum = at_rows[:, :heads]
    row_seg = at_rows[:, heads : heads + 1]
    last = cumulated[:, tokens - 1 : tokens]
    last_seg = segment[:, tokens - 1 : tokens]
    to_end = jnp.exp(last - cumulated) * jnp.where(segment == last_seg, 1.0, 0.0) * steps
    spread_heads = jnp.where(
        lax.broadcasted_iota(jnp.int32, (heads, width), 0)
        == lax.broadcasted_iota(jnp.int32, (heads, width), 1) // HEAD_DIM,
        1.0, 0.0,
    )

    def widen(a):
        return jnp.dot(a, spread_heads, precision=precise, preferred_element_type=f32)

    plane = jnp.broadcast_to(jnp.exp(last) * jnp.where(last_seg == 0.0, 1.0, 0.0), (heads, 128))
    pd[...] = widen(plane.T[:8])
    weighted = values[...].astype(f32) * widen(to_end.T)
    state = jnp.dot(
        writes[...].astype(f32).T, weighted, precision=precise, preferred_element_type=f32
    )
    for d in range(1, z_count):
        here = all_r.at[(z + z_count - d) % z_count]
        remote(mine_r, here, r_send.at[d], r_recv.at[d], peer(d)).wait_recv()
    for k in range(z_count):
        y[k] = jnp.dot(
            all_r[k].astype(f32), state, precision=precise, preferred_element_type=f32
        )

    def outgoing(d):
        return (
            remote(y.at[(z + d) % z_count], far.at[z], y_send.at[d], y_recv.at[d], peer(d)),
            remote(pd, far_pd.at[z], p_send.at[d], p_recv.at[d], peer(d)),
        )

    for d in range(1, z_count):
        @pl.when(z + d < z_count)
        def _():
            for copy in outgoing(d):
                copy.start()
    scores = lax.dot_general(
        mine_r[...], writes[...], (((1,), (1,)), ((), ())), preferred_element_type=f32
    )
    causal = (spots >= lanes) & (row_seg == segment)
    half = lax.broadcasted_iota(jnp.int32, (rows, 2 * HEAD_DIM), 1) < HEAD_DIM
    for pair in range(heads // 2):
        mixes = []
        for h in (2 * pair, 2 * pair + 1):
            gaps = row_cum[:, h : h + 1] - cumulated[h : h + 1]
            decay = jnp.where(causal, jnp.exp(jnp.where(causal, gaps, 0.0)), 0.0)
            mixes.append(scores * decay * steps[h : h + 1])
        span = slice(pair * 2 * HEAD_DIM, (pair + 1) * 2 * HEAD_DIM)
        product = jnp.dot(
            jnp.concatenate(mixes, axis=0), values[:, span].astype(f32),
            precision=precise, preferred_element_type=f32,
        )
        mixed[:, span] = jnp.where(half, product[:rows], product[rows:])
    own_values = jnp.dot(pick, values[...], preferred_element_type=f32)
    from_start = jnp.exp(row_cum) * jnp.where(row_seg == 0.0, 1.0, 0.0)
    factors = widen(
        jnp.concatenate([from_start, jnp.broadcast_to(skip_ref[q], (8, heads))], axis=0)
    )
    gate = jax.nn.silu(gate_ref[...].astype(f32))
    carried[...] = jnp.zeros((rows, width), f32)
    for d in range(z_count - 1, 0, -1):
        @pl.when(z - d >= 0)
        def _():
            k = z - d + jnp.where(z - d < 0, z_count, 0)
            here, there = far.at[k], far_pd.at[k]
            remote(here, here, y_send.at[d], y_recv.at[d], peer(d)).wait_recv()
            remote(there, there, p_send.at[d], p_recv.at[d], peer(d)).wait_recv()
            carried[...] = carried[...] * far_pd[k][0:1] + far[k]
    gated = (
        mixed[...] + carried[...] * factors[:rows] + factors[rows : rows + 1] * own_values
    ) * gate
    scale = lax.rsqrt(jnp.mean(gated * gated, axis=1, keepdims=True) + epsilon)
    out[...] = (gated * scale * gain_ref[:, wide]).astype(bf16)
    for copy in sent:
        copy.wait_send()
    for d in range(1, z_count):
        @pl.when(z + d < z_count)
        def _():
            for copy in outgoing(d):
                copy.wait_send()


def middle(xs, x_edge, ss, s_edge, keeps, steps, flags, spots, gate, taps_x, taps_s, rate, skip, gain,
           q_count, z_count):
    f32, bf16 = jnp.float32, jnp.bfloat16
    tokens = steps.shape[0] * steps.shape[2]
    rows, width = gate.shape
    operands = (
        xs, x_edge, ss, s_edge, keeps, steps, flags, spots, gate, taps_x, taps_s, rate, skip, gain
    )
    run, extra = staged(
        functools.partial(mid_kernel, q_count, z_count), (), len(operands), operands
    )
    dma, vmem = pltpu.SemaphoreType.DMA, pltpu.VMEM
    return pl.pallas_call(
        run,
        out_shape=jax.ShapeDtypeStruct((rows, width), bf16),
        in_specs=[ANY] * len(operands),
        out_specs=VMEM,
        scratch_shapes=[
            vmem((EDGE + tokens, width), f32),
            vmem((EDGE + tokens, STATE), f32),
            vmem((tokens, width), bf16),
            vmem((tokens, STATE), bf16),
            vmem((tokens, STATE), bf16),
            vmem((rows, STATE), bf16),
            vmem((z_count, rows, STATE), bf16),
            vmem((z_count, rows, width), f32),
            vmem((z_count, rows, width), f32),
            vmem((8, width), f32),
            vmem((z_count, 8, width), f32),
            vmem((rows, width), f32),
            vmem((rows, width), f32),
        ] + [dma((z_count,))] * 6 + extra,
        compiler_params=pltpu.CompilerParams(
            collective_id=1, has_side_effects=True, vmem_limit_bytes=58 * 1024 * 1024
        ),
    )(*operands)


def tail_kernel(n, tp, q_count, z_count, n_ref, ow_ref, hw_ref, r_ref, g_ref, t_ref, p_ref, out,
                ow, hw, nrm, both, hid, feat, logit, stat, every,
                own, tp_send, tp_recv, st_send, st_recv, *gather_sems):
    c, t = lax.axis_index("ctx"), lax.axis_index("tp")
    z, q = c // q_count, c % q_count
    total = n * tp
    me = c * tp + t
    get_ow = pltpu.make_async_copy(ow_ref, ow, own.at[0])
    get_hw = pltpu.make_async_copy(hw_ref, hw, own.at[1])
    barrier = pltpu.get_barrier_semaphore()

    def device(k):
        return (k // tp, k % tp)

    def hello(d, carry):
        pl.semaphore_signal(
            barrier, inc=1, device_id=device((me + d) % total), device_id_type=MESH
        )
        return carry

    lax.fori_loop(1, total, hello, 0)
    get_ow.start()
    get_hw.start()
    pl.semaphore_wait(barrier, total - 1)
    core_n = 2 if q_count % 2 == 0 else 1
    x_n = q_count // core_n
    x, core = q // core_n, q % core_n

    def at_x(k):
        return (z * q_count + k * core_n + core, t)

    at_core = (z * q_count + x * core_n + (core_n - 1) - core, t)

    def gathered(slot, mine, sems):
        z_send, z_recv, x_send, x_recv, c_send, c_recv = sems
        sent = []

        def push(copy):
            copy.start()
            sent.append(copy)

        def to_x(ref, dst, d):
            for e in range(1, x_n):
                push(remote(ref, dst, x_send.at[e - 1, d], x_recv.at[e - 1, d], at_x((x + e) % x_n)))

        def to_core(ref, dst, e, d):
            if core_n > 1:
                push(remote(ref, dst, c_send.at[e, d], c_recv.at[e, d], at_core))

        home = slot(q, z)
        for d in range(1, z_count):
            push(remote(mine, home, z_send.at[d], z_recv.at[d], (((z + d) % z_count) * q_count + q, t)))
        to_x(mine, home, 0)
        to_core(mine, home, 0, 0)
        for d in range(z_count):
            k = (z + z_count - d) % z_count
            if d:
                here = slot(q, k)
                remote(here, here, z_send.at[d], z_recv.at[d], at_core).wait_recv()
                to_x(here, here, d)
                to_core(here, here, 0, d)
            for e in range(1, x_n):
                here = slot(((x + x_n - e) % x_n) * core_n + core, k)
                remote(here, here, x_send.at[e - 1, d], x_recv.at[e - 1, d], at_core).wait_recv()
                to_core(here, here, e, d)
        if core_n > 1:
            for d in range(z_count):
                k = (z + z_count - d) % z_count
                for e in range(x_n):
                    here = slot(((x + x_n - e) % x_n) * core_n + 1 - core, k)
                    remote(here, here, c_send.at[e, d], c_recv.at[e, d], at_core).wait_recv()
        return sent

    rows = n_ref.shape[0]
    width = n_ref.shape[1]

    def normed_slot(a, b):
        return nrm.at[a, b]

    pending = gathered(normed_slot, n_ref, gather_sems[:6])
    nrm[q, z] = n_ref[...]
    get_ow.wait()
    partial = jnp.zeros(both.shape[1:], jnp.float32)
    for k in range(q_count):
        partial = partial + jnp.dot(
            nrm[k].reshape(z_count * rows, width),
            ow[k * width : (k + 1) * width, :],
            preferred_element_type=jnp.float32,
        )
    both[t] = partial
    tp_copies = []
    for d in range(1, tp):
        copy = remote(both.at[t], both.at[t], tp_send.at[d], tp_recv.at[d], (c, (t + d) % tp))
        copy.start()
        tp_copies.append(copy)
    for d in range(1, tp):
        here = both.at[(t + tp - d) % tp]
        remote(here, here, tp_send.at[d], tp_recv.at[d], (c, (t + d) % tp)).wait_recv()
    summed = both[0]
    for k in range(1, tp):
        summed = summed + both[k]
    hid[q, z] = (r_ref[...].astype(jnp.float32) + summed).astype(jnp.bfloat16)

    def hidden_slot(a, b):
        return hid.at[a, b]

    pending = pending + tp_copies + gathered(hidden_slot, hid.at[q, z], gather_sems[6:])
    block = hid.shape[3]
    all_rows = hid.shape[2]
    squares = jnp.zeros((all_rows, 1), jnp.float32)
    for k in range(z_count):
        for a in range(q_count):
            piece = hid[a, k].astype(jnp.float32)
            squares = squares + jnp.sum(piece * piece, axis=1, keepdims=True)
    inverse = lax.rsqrt(squares / (n * block) + epsilon)
    for k in range(z_count):
        for a in range(q_count):
            first = (k * q_count + a) * block
            span = slice(first, first + block)
            feat[:, span] = (
                hid[a, k].astype(jnp.float32) * inverse * g_ref[:, span]
            ).astype(jnp.bfloat16)
    get_hw.wait()
    vocab = hw.shape[1]
    tile = min(256, vocab)

    def one_tile(i, carry):
        cols = pl.ds(pl.multiple_of(i * tile, 128), tile)
        logit[:, cols] = jnp.dot(feat[...], hw[:, cols], preferred_element_type=jnp.float32)
        return carry

    lax.fori_loop(0, vocab // tile, one_tile, 0)
    values = logit[...]
    top = jnp.max(values, axis=1, keepdims=True)
    added = jnp.sum(jnp.exp(values - top), axis=1, keepdims=True)
    column = t_ref[...] - me * vocab
    places = lax.broadcasted_iota(jnp.int32, values.shape, 1)
    hit = jnp.sum(jnp.where(places == column, values, 0.0), axis=1, keepdims=True)
    lane = lax.broadcasted_iota(jnp.int32, (all_rows, 128), 1)
    packed = jnp.where(lane == 0, top, jnp.where(lane == 1, added, jnp.where(lane == 2, hit, 0.0)))
    turned = packed.T[:8]
    stat[...] = turned

    def go(d, carry):
        remote(
            stat, every.at[me], st_send.at[d], st_recv.at[d], device((me + d) % total)
        ).start()
        return carry

    lax.fori_loop(1, total, go, 0)
    every[me] = turned

    def done(d, carry):
        here = every.at[(me + total - d) % total]
        copy = remote(stat, here, st_send.at[d], st_recv.at[d], device((me + d) % total))
        copy.wait_send()
        copy.wait_recv()
        return carry

    lax.fori_loop(1, total, done, 0)
    for copy in pending:
        copy.wait_send()
    found = every[...]
    tops = found[:, 0, :]
    row_top = jnp.max(tops, axis=0, keepdims=True)
    full = jnp.sum(found[:, 1, :] * jnp.exp(tops - row_top), axis=0, keepdims=True)
    picked = jnp.sum(found[:, 2, :], axis=0, keepdims=True)
    log_prob = picked - row_top - jnp.log(full)
    out[0:1, :] = log_prob
    out[1:2, :] = 0.5 * jnp.square(log_prob - p_ref[...])


def tail(normed, out_weight, head_weight, res, gain, targets, policy, n, tp, q_count, z_count):
    dma = pltpu.SemaphoreType.DMA
    total = n * tp
    rows, width = normed.shape
    all_rows = z_count * rows
    block = out_weight.shape[1]
    core_n = 2 if q_count % 2 == 0 else 1
    x_n = q_count // core_n
    vmem = pltpu.VMEM
    bf16, f32 = jnp.bfloat16, jnp.float32
    e_n = max(x_n - 1, 1)
    sems = [
        dma((z_count,)), dma((z_count,)), dma((e_n, z_count)), dma((e_n, z_count)),
        dma((x_n, z_count)), dma((x_n, z_count)),
    ]
    operands = (
        normed, out_weight, head_weight, res, gain[None], targets[:, None], policy[None]
    )
    run, extra = staged(
        functools.partial(tail_kernel, n, tp, q_count, z_count), (1, 2), len(operands),
        operands[:1] + operands[3:],
    )
    result = pl.pallas_call(
        run,
        out_shape=jax.ShapeDtypeStruct((2, all_rows), f32),
        in_specs=[ANY] * len(operands),
        out_specs=VMEM,
        scratch_shapes=[
            vmem(out_weight.shape, bf16),
            vmem(head_weight.shape, bf16),
            vmem((q_count, z_count, rows, width), bf16),
            vmem((tp, all_rows, block), f32),
            vmem((q_count, z_count, all_rows, block), bf16),
            vmem((all_rows, n * block), bf16),
            vmem((all_rows, head_weight.shape[1]), f32),
            vmem((8, all_rows), f32),
            vmem((total, 8, all_rows), f32),
            dma((2,)), dma((tp,)), dma((tp,)), dma((total,)), dma((total,)),
        ] + sems + sems + extra,
        compiler_params=pltpu.CompilerParams(
            collective_id=3, has_side_effects=True, vmem_limit_bytes=58 * 1024 * 1024
        ),
    )(*operands)
    return result[0], result[1]


def halves(a):
    hi = a.astype(jnp.bfloat16)
    return hi, (a - hi.astype(jnp.float32)).astype(jnp.bfloat16)


def thirds(a):
    hi = a.astype(jnp.bfloat16)
    rest = a - hi.astype(jnp.float32)
    mid = rest.astype(jnp.bfloat16)
    return hi, mid, (rest - mid.astype(jnp.float32)).astype(jnp.bfloat16)


def column(row, first, count):
    lanes = row.shape[1]
    spot = lax.broadcasted_iota(jnp.int32, (count, lanes), 0) + first
    hit = lax.broadcasted_iota(jnp.int32, (count, lanes), 1) == spot
    return jnp.sum(jnp.where(hit, jnp.broadcast_to(row, (count, lanes)), 0.0), axis=1, keepdims=True)


def one_kernel(n, tp, *refs):
    names, refs = refs[0], refs[1:]
    r = dict(zip(names, refs))
    f32, bf16 = jnp.float32, jnp.bfloat16
    c, t = lax.axis_index("ctx"), lax.axis_index("tp")
    total = n * tp
    me = c * tp + t
    chips = n // 2
    z_n = chips // 2
    k, p = c % 2, c // 2
    x, z = p % 2, p // 2

    def dev(z_, x_, k_):
        return ((z_ * 2 + x_) * 2 + k_, t)

    core_peer, x_peer, y_peer = dev(z, x, 1 - k), dev(z, 1 - x, k), (c, 1 - t)
    T, C = r["x"].shape
    W = C // 2
    S = r["s"].shape[2] // 2
    G = S // STATE
    GW = W // G
    H = r["d"].shape[0]
    HC = H // 2
    Tc = 2 * T
    r8 = r["scored"].shape[0]
    RC = 2 * r8
    R = chips * RC
    taps = r["tx"].shape[0]
    blk = r["ow"].shape[1] // tp
    D = n * tp * blk
    V = r["hw"].shape[1]
    per = n // tp

    barrier = pltpu.get_barrier_semaphore()

    def hello(d, carry):
        other = (me + d) % total
        pl.semaphore_signal(
            barrier, inc=1, device_id=(other // tp, other % tp), device_id_type=MESH
        )
        return carry

    lax.fori_loop(1, total, hello, 0)

    def lanes(a, size):
        return pl.ds(pl.multiple_of(a * size, 128), size)

    local = {}

    def fetch(name, src, dst):
        copy = pltpu.make_async_copy(src, dst, r["own"].at[len(local)])
        local[name] = copy
        copy.start()

    def arrived(ref, sem):
        pltpu.make_async_copy(ref, ref, sem).wait()

    sent = []

    def push(copy, when=None):
        sent.append((copy, when))
        if when is None:
            copy.start()
        else:
            pl.when(when)(copy.start)

    fetch("resets", r["resets"], r["resv"])
    fetch("scored", r["scored"], r["spot"])
    fetch("s", r["s"].at[:, :, lanes(k, S)], r["sc"].at[k])
    fetch("ts", r["ts"].at[:, :, lanes(k, S)], r["tsv"])
    half_heads = pl.ds(pl.multiple_of(k * HC, 8), HC)
    fetch("d", r["d"].at[half_heads], r["dc"].at[k])
    fetch("rate", r["rate"], r["ratev"])
    fetch("x", r["x"].at[:, lanes(k, W)], r["xc"].at[k])
    fetch("tx", r["tx"].at[:, lanes(k, W)], r["txv"])
    fetch("g", r["g"], r["gv"])
    fetch("res", r["res"], r["rv"])
    fetch("skip", r["skip"], r["skipv"])
    fetch("gain", r["gain"].at[:, lanes(k, W)], r["gainv"])
    fetch("fg", r["fg"], r["fgv"])
    fetch("tgt", r["tgt"], r["tgtv"])
    fetch("pol", r["pol"], r["polv"])
    fetch("ow", r["ow"], r["oww"])

    first = p == 0

    @pl.when(first)
    def _():
        r["xh"][...] = jnp.zeros(r["xh"].shape, bf16)
        r["sh"][...] = jnp.zeros(r["sh"].shape, bf16)
        r["mh"][...] = jnp.zeros(r["mh"].shape, f32)

    local["resets"].wait()
    local["scored"].wait()
    lane8 = lax.broadcasted_iota(jnp.int32, (8, T), 1)
    row8 = lax.broadcasted_iota(jnp.int32, (8, T), 0)
    places = jnp.zeros((8, T), f32)
    for i in range(r8):
        places = jnp.where(lane8 == i, (r["spot"][i] - c * T).astype(f32), places)
    flags_here = jnp.broadcast_to(r["resv"][...].astype(f32), (8, T))
    r["meta"][...] = jnp.where(row8 == 0, flags_here, places)

    pl.semaphore_wait(barrier, total - 1)

    send, recv = r["core_send"], r["core_recv"]
    edge_send, edge_recv = r["edge_send"], r["edge_recv"]
    swap = (
        (r["s"].at[:, :, lanes(1 - k, S)], r["sc"].at[k]),
        (r["meta"], r["mc"].at[k]),
        (r["d"].at[pl.ds(pl.multiple_of((1 - k) * HC, 8), HC)], r["dc"].at[k]),
        (r["x"].at[:, lanes(1 - k, W)], r["xc"].at[k]),
    )
    for i, (a, b) in enumerate(swap):
        push(remote(a, b, send.at[i], recv.at[i], core_peer))
    last_core = (k == 1) & (p < chips - 1)
    tail = pl.ds(T - EDGE, EDGE)
    nxt = jnp.minimum(p + 1, chips - 1)
    for j in range(2):
        triple = (
            (r["s"].at[:, tail, j * S : (j + 1) * S], r["sh"]),
            (r["meta"], r["mh"]),
            (r["x"].at[tail, j * W : (j + 1) * W], r["xh"]),
        )
        for i, (a, b) in enumerate(triple):
            push(remote(a, b, edge_send.at[j, i], edge_recv.at[i], (nxt * 2 + j, t)), last_core)
    r["mc"][k] = r["meta"][...]

    def from_core(i, buf):
        arrived(buf.at[1 - k], recv.at[i])

    def from_edge(i, ref):
        @pl.when(jnp.logical_not(first))
        def _():
            arrived(ref, edge_recv.at[i])

    from_core(1, r["mc"])
    spots = jnp.concatenate(
        [column(r["mc"][j][1:2], 0, r8) + j * T for j in range(2)], axis=0
    ).astype(jnp.int32)
    lane_t = lax.broadcasted_iota(jnp.int32, (RC, Tc), 1)
    pick_f = jnp.where(spots == lane_t, 1.0, 0.0)
    pick = pick_f.astype(bf16)

    chip_flags = jnp.concatenate([r["mc"][0], r["mc"][1]], axis=1)
    local["d"].wait()
    local["rate"].wait()
    from_core(2, r["dc"])
    steps = jnp.concatenate([r["dc"][0], r["dc"][1]], axis=1)
    lower = jnp.where(
        lax.broadcasted_iota(jnp.int32, (Tc, Tc), 0) <= lax.broadcasted_iota(jnp.int32, (Tc, Tc), 1),
        1.0, 0.0,
    ).astype(bf16)
    rate_col = column(r["ratev"][...], k * HC, HC)
    runs = jnp.concatenate([-rate_col * steps, chip_flags], axis=0)
    sums3 = jnp.dot(jnp.concatenate(thirds(runs), axis=0), lower, preferred_element_type=f32)
    count = HC + 8
    sums = sums3[:count] + sums3[count : 2 * count] + sums3[2 * count :]
    cumulated = sums[:HC]
    segment = sums[HC : HC + 1]
    last = cumulated[:, Tc - 1 : Tc]
    last_seg = segment[:, Tc - 1 : Tc]
    plane = jnp.broadcast_to(jnp.exp(last) * jnp.where(last_seg == 0.0, 1.0, 0.0), (HC, 128))
    r["mine_pd"][...] = jnp.concatenate([plane.T[:8], jnp.zeros((8, 128 - HC), f32)], axis=1)
    for d in range(1, chips):
        push(remote(
            r["mine_pd"], r["all_pd"].at[p], r["pd_send"].at[d], r["pd_recv"].at[d],
            (((p + d) % chips) * 2 + k, t),
        ))
    r["all_pd"][p] = r["mine_pd"][...]
    at_rows = lax.dot_general(
        pick_f, sums, (((1,), (1,)), ((), ())), precision=precise, preferred_element_type=f32
    )
    row_cum = at_rows[:, :HC]
    row_seg = at_rows[:, HC : HC + 1]
    to_end = jnp.exp(last - cumulated) * jnp.where(segment == last_seg, 1.0, 0.0) * steps
    r["te"][...] = jnp.concatenate(halves(to_end.T), axis=1)
    local["g"].wait()
    local["res"].wait()
    own_pick = jnp.where(
        column(r["meta"][1:2], 0, r8) == lax.broadcasted_iota(jnp.int32, (r8, T), 1).astype(f32),
        1.0, 0.0,
    ).astype(bf16)
    r["gc"][k] = jnp.dot(
        own_pick, r["gv"][:, lanes(k, W)], preferred_element_type=f32
    ).astype(bf16)
    r["gsend"][...] = jnp.dot(
        own_pick, r["gv"][:, lanes(1 - k, W)], preferred_element_type=f32
    ).astype(bf16)
    push(remote(r["gsend"], r["gc"].at[k], send.at[4], recv.at[4], core_peer))
    res_rows = jnp.dot(own_pick, r["rv"][...], preferred_element_type=f32).astype(bf16)

    for j in range(per * tp):
        r["rsend"][j] = res_rows[:, j * blk : (j + 1) * blk]

    def res_copy(j, to_t):
        i = j * tp + to_t
        return remote(
            r["rsend"].at[i], r["ro"].at[c], r["res_send"].at[i], r["res_recv"].at[c],
            (t * per + j, to_t),
        )

    for j in range(per):
        for to_t in range(tp):
            mine = (t * per + j == c) & (to_t == t)
            push(res_copy(j, to_t), jnp.logical_not(mine))

            @pl.when(mine)
            def _():
                pltpu.make_async_copy(
                    r["rsend"].at[j * tp + to_t], r["ro"].at[c], r["res_recv"].at[c]
                ).start()

    from_edge(1, r["mh"])
    flags = jnp.concatenate([r["mh"][...], chip_flags], axis=1)
    clear = 1.0 - flags
    keeping = jnp.ones((8, 3 * T), f32)
    columns = [keeping]
    for off in range(1, taps):
        shifted = clear if off == 1 else pltpu.roll(clear, off - 1, 1)
        keeping = keeping * shifted
        columns.append(keeping)
    keep_rows = jnp.zeros((8, 3 * T), f32)
    row8w = lax.broadcasted_iota(jnp.int32, (8, 3 * T), 0)
    for off in range(taps):
        keep_rows = jnp.where(row8w == off, jnp.broadcast_to(columns[off][0:1], (8, 3 * T)), keep_rows)
    keep = keep_rows[:, T:].T
    for off in range(1, taps):
        r["kb"][off] = jnp.broadcast_to(keep[:, off : off + 1], (Tc, 128))
    wide_keep = [None] + [r["kb"].at[off] for off in range(1, taps)]

    def filtered(pad, kernel, start, size):
        width = pad.shape[1]
        acc = kernel[0:1] * pad[EDGE + start : EDGE + start + size, :]
        for off in range(1, taps):
            kept = wide_keep[off][start : start + size, :]
            kept = jnp.concatenate([kept] * (width // 128), axis=1)
            acc = acc + kept * (
                kernel[off : off + 1] * pad[EDGE - off + start : EDGE - off + start + size, :]
            )
        return jax.nn.silu(acc).astype(bf16)

    local["s"].wait()
    local["ts"].wait()
    from_core(0, r["sc"])
    from_edge(0, r["sh"])
    pad = r["pad"]
    band = 64
    for which, target in ((1, r["reads"]), (0, r["writes"])):
        for g in range(G):
            cols = slice(g * STATE, (g + 1) * STATE)
            pad_s = r["pad_s"]
            pad_s[:EDGE, :] = r["sh"][which, :, cols].astype(f32)
            for j in range(2):
                pad_s[EDGE + j * T : EDGE + (j + 1) * T, :] = r["sc"][j, which, :, cols].astype(f32)
            kernel = r["tsv"][which, :, cols]
            for b in range(Tc // band):
                target[b * band : (b + 1) * band, cols] = filtered(pad_s, kernel, b * band, band)
        if which == 1:
            r["mine_r"][...] = jnp.dot(
                pick, r["reads"][...], preferred_element_type=f32
            ).astype(bf16)
            for d in range(1, chips):
                push(remote(
                    r["mine_r"], r["all_r"].at[p], r["r_send"].at[d], r["r_recv"].at[d],
                    (((p + d) % chips) * 2 + k, t),
                ))
            r["all_r"][p] = r["mine_r"][...]

    for g in range(G):
        r["wT"][g] = r["writes"][:, g * STATE : (g + 1) * STATE].astype(f32).T.astype(bf16)

    chunk = 256

    def spread_cols(j, size, offset):
        head = lax.broadcasted_iota(jnp.int32, (size, chunk), 0) % (size // 2)
        lane = lax.broadcasted_iota(jnp.int32, (size, chunk), 1)
        return jnp.where(head == offset + (j * chunk + lane) // HEAD_DIM, 1.0, 0.0).astype(bf16)

    local["x"].wait()
    local["tx"].wait()
    from_core(3, r["xc"])
    from_edge(2, r["xh"])

    def conv_step(j, carry):
        cols = lanes(j, chunk)
        pad[:EDGE, :] = r["xh"][:, cols].astype(f32)
        for i in range(2):
            pad[EDGE + i * T : EDGE + (i + 1) * T, :] = r["xc"][i, :, cols].astype(f32)
        kernel = r["txv"][:, cols]
        for b in range(Tc // band):
            r["values"][b * band : (b + 1) * band, cols] = filtered(pad, kernel, b * band, band)
        grown = jnp.dot(r["te"][...], spread_cols(j, 2 * HC, 0), preferred_element_type=f32)
        hi, lo = halves(r["values"][:, cols].astype(f32) * grown)
        w_t = r["wT"][(j * chunk) // GW]
        state = jnp.dot(w_t, hi, preferred_element_type=f32) + jnp.dot(
            w_t, lo, preferred_element_type=f32
        )
        s_hi, s_lo = halves(state)
        r["S2"][:STATE, cols] = s_hi
        r["S2"][STATE:, cols] = s_lo
        return carry

    lax.fori_loop(0, W // chunk, conv_step, 0)

    fetch("hw", r["hw"], r["hww"])

    for d in range(1, chips):
        here = (p + chips - d) % chips
        arrived(r["all_r"].at[here], r["r_recv"].at[d])
        arrived(r["all_pd"].at[here], r["pd_recv"].at[d])
    for g in range(G):
        rows_g = r["all_r"][:, :, g * STATE : (g + 1) * STATE].reshape(R, STATE)
        r["rr"][g, :, :STATE] = rows_g
        r["rr"][g, :, STATE:] = rows_g
    run_w = jnp.ones((1, 128), f32)
    weights = []
    for d in range(chips):
        weights.append(jnp.broadcast_to(run_w, (RC, 128)))
        run_w = jnp.where(d > p, run_w * r["all_pd"][d][0:1], run_w)
    far = jnp.concatenate(weights, axis=0)[:, :HC]
    r["ww"][...] = jnp.concatenate(halves(far), axis=1)

    def y_step(j, carry):
        cols = lanes(j, chunk)
        y = jnp.dot(r["rr"][(j * chunk) // GW], r["S2"][:, cols], preferred_element_type=f32)
        grown = jnp.dot(r["ww"][...], spread_cols(j, 2 * HC, 0), preferred_element_type=f32)
        r["yf"][:, cols] = y * grown
        return carry

    lax.fori_loop(0, W // chunk, y_step, 0)

    def y_rows(zd, xd):
        return r["yf"][pl.ds(pl.multiple_of((zd * 2 + xd) * RC, 16), RC), :]

    def coded(a, wire, scale):
        most = jnp.max(jnp.abs(a), axis=1, keepdims=True)
        inverse = jnp.where(most > 0.0, LEVELS / jnp.maximum(most, TINY), 0.0)
        wire[...] = jnp.round(a * inverse).astype(jnp.int32).astype(jnp.int16)
        scale[...] = jnp.broadcast_to(most * (1.0 / LEVELS), (RC, 128))

    def decoded(wire, scale):
        return wire[...].astype(jnp.int32).astype(f32) * scale[:, :1]

    for zd in range(z_n - 1, -1, -1):
        goes = (zd > z) | ((zd == z) & (x == 0))

        @pl.when(goes)
        def _():
            coded(y_rows(zd, 1 - x), r["xsend"].at[zd], r["xsend_f"].at[zd])

        for i, (a, b) in enumerate(((r["xsend"], r["xr"]), (r["xsend_f"], r["xr_f"]))):
            push(
                remote(a.at[zd], b.at[zd], r["x_send"].at[i, zd], r["x_recv"].at[i, zd], x_peer),
                goes,
            )

    def from_x_peer(zd):
        for i, b in enumerate((r["xr"], r["xr_f"])):
            arrived(b.at[zd], r["x_recv"].at[i, zd])
        return decoded(r["xr"].at[zd], r["xr_f"].at[zd])

    mine_r = r["mine_r"][...]
    scores = [
        lax.dot_general(
            mine_r[:, g * STATE : (g + 1) * STATE], r["writes"][:, g * STATE : (g + 1) * STATE],
            (((1,), (1,)), ((), ())), preferred_element_type=f32,
        )
        for g in range(G)
    ]
    causal = (spots >= lane_t) & (row_seg == segment)
    quad = 4
    quad_w = quad * HEAD_DIM
    which_head = lax.broadcasted_iota(jnp.int32, (RC, quad_w), 1) // HEAD_DIM

    def within(q):
        mixes = []
        for i in range(quad):
            h = q * quad + i
            gaps = row_cum[:, h : h + 1] - cumulated[h : h + 1]
            decay = jnp.where(causal, jnp.exp(jnp.where(causal, gaps, 0.0)), 0.0)
            mixes.append(scores[h * HEAD_DIM // GW] * decay * steps[h : h + 1])
        both = jnp.concatenate(halves(jnp.concatenate(mixes, axis=0)), axis=0)
        span = slice(q * quad_w, (q + 1) * quad_w)
        product = jnp.dot(both, r["values"][:, span], preferred_element_type=f32)
        product = product[: quad * RC] + product[quad * RC :]
        out = product[:RC]
        for i in range(1, quad):
            out = jnp.where(which_head == i, product[i * RC : (i + 1) * RC], out)
        r["mixed"][:, span] = out

    quads = HC // quad
    for q in range(quads // 2):
        within(q)
    for zd in range(z_n - 1, 0, -1):
        goes = zd > z

        @pl.when(goes)
        def _():
            coded(y_rows(zd, x) + from_x_peer(zd), r["zsend"].at[zd], r["zsend_f"].at[zd])

        for i, (a, b) in enumerate(((r["zsend"], r["zr"]), (r["zsend_f"], r["zr_f"]))):
            push(
                remote(a.at[zd], b.at[z], r["z_send"].at[i, zd], r["z_recv"].at[i, z], dev(zd, x, k)),
                goes,
            )
    for q in range(quads // 2, quads):
        within(q)

    local["skip"].wait()
    local["gain"].wait()
    from_start = jnp.exp(row_cum) * jnp.where(row_seg == 0.0, 1.0, 0.0)
    starts = jnp.concatenate(halves(from_start), axis=1)
    skip3 = jnp.concatenate(
        [jnp.broadcast_to(a, (8, H)) for a in thirds(jnp.broadcast_to(r["skipv"][...], (8, H)))], axis=0
    )
    from_core(4, r["gc"])
    gate = jnp.concatenate([r["gc"][0].astype(f32), r["gc"][1].astype(f32)], axis=0)

    def widen_step(j, carry):
        cols = lanes(j, chunk)
        own_values = jnp.dot(pick, r["values"][:, cols], preferred_element_type=f32)
        head = lax.broadcasted_iota(jnp.int32, (H, chunk), 0)
        lane = lax.broadcasted_iota(jnp.int32, (H, chunk), 1)
        all_heads = jnp.where(head == k * HC + (j * chunk + lane) // HEAD_DIM, 1.0, 0.0).astype(bf16)
        grown = jnp.dot(skip3, all_heads, preferred_element_type=f32)
        skip_row = grown[0:1] + grown[8:9] + grown[16:17]
        r["mixed"][:, cols] = r["mixed"][:, cols] + skip_row * own_values
        r["starts"][:, cols] = jnp.dot(starts, spread_cols(j, 2 * HC, 0), preferred_element_type=f32)
        return carry

    lax.fori_loop(0, W // chunk, widen_step, 0)
    gate = jax.nn.silu(gate)

    carried = r["carried"]
    carried[...] = jnp.zeros((RC, W), f32)

    @pl.when(x == 1)
    def _():
        carried[...] = from_x_peer(z)

    for zs in range(z_n - 1):
        @pl.when(zs < z)
        def _():
            for i, b in enumerate((r["zr"], r["zr_f"])):
                arrived(b.at[zs], r["z_recv"].at[i, zs])
            carried[...] = carried[...] + decoded(r["zr"].at[zs], r["zr_f"].at[zs])

    gated = (r["mixed"][...] + carried[...] * r["starts"][...]) * gate
    for g in range(G):
        span = slice(g * GW, (g + 1) * GW)
        part = gated[:, span]
        scale = lax.rsqrt(jnp.mean(part * part, axis=1, keepdims=True) + epsilon)
        r["normed"][:, span] = (part * scale * r["gainv"][:, span]).astype(bf16)

    nrm = r["nrm"]
    mine = r["normed"]
    z_send, z_recv, x_send, x_recv, c_send, c_recv = r["gather1"]

    def slot(z_, x_, k_):
        return nrm.at[k_, z_ * 2 + x_]

    home = slot(z, x, k)
    for d in range(1, z_n):
        push(remote(mine, home, z_send.at[d], z_recv.at[z], dev((z + d) % z_n, x, k)))
    push(remote(mine, home, x_send.at[z], x_recv.at[z], x_peer))
    push(remote(mine, home, c_send.at[0, z], c_recv.at[0, z], core_peer))
    nrm[k, p] = mine[...]

    def from_x(zs):
        here = slot(zs, 1 - x, k)
        arrived(here, x_recv.at[zs])
        push(remote(here, here, c_send.at[1, zs], c_recv.at[1, zs], core_peer))

    for zs in range(z_n):
        here = slot(zs, x, k)
        away = zs != z

        @pl.when(away)
        def _():
            arrived(here, z_recv.at[zs])

        push(remote(here, here, x_send.at[zs], x_recv.at[zs], x_peer), away)
        push(remote(here, here, c_send.at[0, zs], c_recv.at[0, zs], core_peer), away)
        if zs:
            from_x(zs - 1)
    from_x(z_n - 1)
    for zs in range(z_n):
        for e, x_ in ((0, x), (1, 1 - x)):
            arrived(slot(zs, x_, 1 - k), c_recv.at[e, zs])
    local["ow"].wait()
    partial = jnp.zeros((R, tp * blk), f32)
    for j in range(2):
        partial = partial + jnp.dot(
            nrm[j].reshape(R, W), r["oww"][j * W : (j + 1) * W, :], preferred_element_type=f32
        )
    for j in range(tp):
        r["pt"][j] = partial[:, j * blk : (j + 1) * blk]
    push(remote(r["pt"].at[1 - t], r["pr"], r["t_send"], r["t_recv"], y_peer))
    for j in range(n):
        arrived(r["ro"].at[j], r["res_recv"].at[j])
    res_all = r["ro"][...].astype(f32).reshape(R, blk)
    arrived(r["pr"], r["t_recv"])
    hid = r["hid"]
    hid[c, t] = (res_all + (r["pt"][t] + r["pr"][...])).astype(bf16)

    z_send, z_recv, a_send, a_recv, b_send, b_recv, c_send, c_recv = r["gather2"]
    even = k == 0
    a0, b0 = jnp.where(even, t, x), jnp.where(even, x, t)

    def place(z_, a_, b_, k_):
        y_, x_ = jnp.where(k_ == 0, a_, b_), jnp.where(k_ == 0, b_, a_)
        return hid.at[(z_ * 2 + x_) * 2 + k_, y_]

    a_peer = (jnp.where(even, c, x_peer[0]), jnp.where(even, 1 - t, t))
    b_peer = (jnp.where(even, x_peer[0], c), jnp.where(even, t, 1 - t))

    def to_a(here, d):
        push(remote(here, here, a_send.at[d], a_recv.at[d], a_peer))

    diag = (x_peer[0], 1 - t)

    def to_diag(here, d):
        push(remote(here, here, b_send.at[1, d], b_recv.at[1, d], diag))

    def to_b(here, e, d):
        push(remote(here, here, b_send.at[e, d], b_recv.at[e, d], b_peer))

    def to_core(here, e, d):
        push(remote(here, here, c_send.at[e, d], c_recv.at[e, d], core_peer))

    home = place(z, a0, b0, k)
    for d in range(1, z_n):
        push(remote(home, home, z_send.at[d], z_recv.at[d], dev((z + d) % z_n, x, k)))
    to_diag(home, 0)
    to_a(home, 0)
    to_b(home, 0, 0)
    to_core(home, 0, 0)
    for d in range(1, z_n):
        here = place((z + z_n - d) % z_n, a0, b0, k)
        arrived(here, z_recv.at[d])
        to_diag(here, d)
        to_a(here, d)
        to_b(here, 0, d)
        to_core(here, 0, d)
    for d in range(z_n):
        here = place((z + z_n - d) % z_n, 1 - a0, b0, k)
        arrived(here, a_recv.at[d])
        to_core(here, 1, d)
    for d in range(z_n):
        here = place((z + z_n - d) % z_n, a0, 1 - b0, k)
        arrived(here, b_recv.at[0, d])
        to_core(here, 2, d)
    for d in range(z_n):
        here = place((z + z_n - d) % z_n, 1 - a0, 1 - b0, k)
        arrived(here, b_recv.at[1, d])
        to_core(here, 3, d)
    oa, ob = jnp.where(even, x, t), jnp.where(even, t, x)
    for d in range(z_n):
        from_z = (z + z_n - d) % z_n
        for e, (a_, b_) in enumerate(((oa, ob), (1 - oa, ob), (oa, 1 - ob), (1 - oa, 1 - ob))):
            arrived(place(from_z, a_, b_, 1 - k), c_recv.at[e, d])

    squares = jnp.zeros((R, 1), f32)
    for a in range(n):
        for b in range(tp):
            piece = hid[a, b].astype(f32)
            squares = squares + jnp.sum(piece * piece, axis=1, keepdims=True)
    inverse = lax.rsqrt(squares / D + epsilon)
    local["fg"].wait()
    feat = r["feat"]
    for a in range(n):
        for b in range(tp):
            start = (a * tp + b) * blk
            span = slice(start, start + blk)
            feat[:, span] = (hid[a, b].astype(f32) * inverse * r["fgv"][:, span]).astype(bf16)
    local["hw"].wait()
    tile = min(256, V)
    logit = r["logit"]

    def one_tile(i, carry):
        cols = lanes(i, tile)
        logit[:, cols] = jnp.dot(feat[...], r["hww"][:, cols], preferred_element_type=f32)
        return carry

    lax.fori_loop(0, V // tile, one_tile, 0)
    values = logit[...]
    top = jnp.max(values, axis=1, keepdims=True)
    added = jnp.sum(jnp.exp(values - top), axis=1, keepdims=True)
    local["tgt"].wait()
    local["pol"].wait()
    target = column(r["tgtv"][...].astype(f32), 0, R).astype(jnp.int32) - me * V
    hit = jnp.sum(
        jnp.where(lax.broadcasted_iota(jnp.int32, values.shape, 1) == target, values, 0.0),
        axis=1, keepdims=True,
    )
    lane = lax.broadcasted_iota(jnp.int32, (R, 128), 1)
    packed = jnp.where(lane == 0, top, jnp.where(lane == 1, added, jnp.where(lane == 2, hit, 0.0)))
    turned = packed.T[:4]
    stat, every = r["stat"], r["every"]
    stat[...] = turned
    st_send, st_recv = r["st_send"], r["st_recv"]

    def device(a):
        return (a // tp, a % tp)

    def go(d, carry):
        remote(
            stat, every.at[me], st_send.at[d], st_recv.at[d], device((me + d) % total)
        ).start()
        return carry

    lax.fori_loop(1, total, go, 0)
    every[me] = turned

    for copy, when in sent:
        if when is None:
            copy.wait_send()
        else:
            pl.when(when)(copy.wait_send)

    def done(d, carry):
        here = every.at[(me + total - d) % total]
        copy = remote(stat, here, st_send.at[d], st_recv.at[d], device((me + d) % total))
        copy.wait_send()
        copy.wait_recv()
        return carry

    lax.fori_loop(1, total, done, 0)
    found = every[...]
    tops = found[:, 0, :]
    row_top = jnp.max(tops, axis=0, keepdims=True)
    full = jnp.sum(found[:, 1, :] * jnp.exp(tops - row_top), axis=0, keepdims=True)
    picked = jnp.sum(found[:, 2, :], axis=0, keepdims=True)
    log_prob = picked - row_top - jnp.log(full)
    r["out_a"][...] = log_prob
    r["out_b"][...] = 0.5 * jnp.square(log_prob - r["polv"][...])


def fused(n, tp, x, g, s, d, resets, rate, skip, tx, ts, gain, ow, res, fg, hw, scored, tgt, pol):
    f32, bf16, i32, i16 = jnp.float32, jnp.bfloat16, jnp.int32, jnp.int16
    dma, vmem = pltpu.SemaphoreType.DMA, pltpu.VMEM
    chips = n // 2
    z_n = chips // 2
    T, C = x.shape
    W, Tc = C // 2, 2 * T
    S = s.shape[2] // 2
    G = S // STATE
    H = d.shape[0]
    HC = H // 2
    r8 = scored.shape[0]
    RC = 2 * r8
    R = chips * RC
    blk = ow.shape[1] // tp
    taps = tx.shape[0]
    total = n * tp
    inputs = dict(
        x=x, g=g, s=s, d=d, resets=resets[None], rate=rate[None], skip=skip[None], tx=tx, ts=ts,
        gain=gain[None], ow=ow, res=res, fg=fg[None], hw=hw, scored=scored, tgt=tgt[None], pol=pol[None],
    )
    scratch = dict(
        resv=vmem((1, T), i32), spot=pltpu.SMEM((r8,), i32), meta=vmem((8, T), f32),
        xc=vmem((2, T, W), bf16), xh=vmem((EDGE, W), bf16),
        sc=vmem((2, 2, T, S), bf16), sh=vmem((2, EDGE, S), bf16),
        dc=vmem((2, HC, T), f32), mc=vmem((2, 8, T), f32), mh=vmem((8, T), f32),
        gv=vmem(g.shape, bf16), rv=vmem(res.shape, bf16),
        gc=vmem((2, r8, W), bf16), gsend=vmem((r8, W), bf16),
        rsend=vmem((n, r8, blk), bf16), ro=vmem((n, r8, blk), bf16),
        txv=vmem((taps, W), f32), tsv=vmem((2, taps, S), f32), gainv=vmem((1, W), f32),
        ratev=vmem((1, H), f32), skipv=vmem((1, H), f32), fgv=vmem((1, n * tp * blk), f32),
        tgtv=vmem((1, R), i32), polv=vmem((1, R), f32),
        pad=vmem((EDGE + Tc, 256), f32), pad_s=vmem((EDGE + Tc, STATE), f32),
        kb=vmem((taps, Tc, 128), f32),
        reads=vmem((Tc, S), bf16), writes=vmem((Tc, S), bf16),
        mine_r=vmem((RC, S), bf16), all_r=vmem((chips, RC, S), bf16),
        mine_pd=vmem((8, 128), f32), all_pd=vmem((chips, 8, 128), f32),
        te=vmem((Tc, 2 * HC), bf16), wT=vmem((G, STATE, Tc), bf16),
        values=vmem((Tc, W), bf16), S2=vmem((2 * STATE, W), bf16),
        rr=vmem((G, R, 2 * STATE), bf16), ww=vmem((R, 2 * HC), bf16), yf=vmem((R, W), f32),
        xsend=vmem((z_n, RC, W), i16), xr=vmem((z_n, RC, W), i16),
        zsend=vmem((z_n, RC, W), i16), zr=vmem((z_n, RC, W), i16),
        xsend_f=vmem((z_n, RC, 128), f32), xr_f=vmem((z_n, RC, 128), f32),
        zsend_f=vmem((z_n, RC, 128), f32), zr_f=vmem((z_n, RC, 128), f32),
        mixed=vmem((RC, W), f32), starts=vmem((RC, W), f32), carried=vmem((RC, W), f32),
        normed=vmem((RC, W), bf16), nrm=vmem((2, chips, RC, W), bf16),
        pt=vmem((tp, R, blk), f32), pr=vmem((R, blk), f32),
        hid=vmem((n, tp, R, blk), bf16), feat=vmem((R, n * tp * blk), bf16),
        logit=vmem((R, hw.shape[1]), f32), stat=vmem((4, R), f32), every=vmem((total, 4, R), f32),
        oww=vmem(ow.shape, bf16), hww=vmem(hw.shape, bf16),
        own=dma((18,)), core_send=dma((5,)), core_recv=dma((5,)),
        edge_send=dma((2, 3)), edge_recv=dma((3,)),
        r_send=dma((chips,)), r_recv=dma((chips,)), pd_send=dma((chips,)), pd_recv=dma((chips,)),
        x_send=dma((2, z_n)), x_recv=dma((2, z_n)), z_send=dma((2, z_n)), z_recv=dma((2, z_n)),
        res_send=dma((n,)), res_recv=dma((n,)), t_send=dma(()), t_recv=dma(()),
        st_send=dma((total,)), st_recv=dma((total,)),
    )
    many = [("gather1", [dma((z_n,))] * 4 + [dma((2, z_n))] * 2)]
    many.append(("gather2", [dma((z_n,))] * 4 + [dma((2, z_n))] * 2 + [dma((4, z_n))] * 2))
    names = list(inputs) + ["out_a", "out_b"] + list(scratch)
    groups = [(name, len(sems)) for name, sems in many]
    extra = [sem for _, sems in many for sem in sems]

    def run(*refs):
        plain, rest = list(refs[: len(names)]), list(refs[len(names) :])
        for _, size in groups:
            plain.append(tuple(rest[:size]))
            rest = rest[size:]
        one_kernel(n, tp, names + [name for name, _ in groups], *plain)

    out = jax.ShapeDtypeStruct((1, R), f32)
    a, b = pl.pallas_call(
        run,
        out_shape=(out, out),
        in_specs=[ANY] * len(inputs),
        out_specs=(VMEM, VMEM),
        scratch_shapes=list(scratch.values()) + extra,
        compiler_params=pltpu.CompilerParams(
            collective_id=5, has_side_effects=True, vmem_limit_bytes=58 * 1024 * 1024
        ),
    )(*inputs.values())
    return a[0], b[0]


def body(
    inner_input,
    gate_input,
    state_inputs,
    step_size,
    resets,
    decay_rate,
    skip_gain,
    conv_inner,
    conv_state,
    norm_gain,
    out_weight,
    residual,
    final_gain,
    head_weight,
    scored,
    targets,
    policy_logprob,
):
    f32 = jnp.float32
    n, tp = lax.axis_size("ctx"), lax.axis_size("tp")
    c, t = lax.axis_index("ctx"), lax.axis_index("tp")
    if n % 4 == 0 and tp == 2 and (state_inputs.shape[2] // STATE) % 2 == 0:
        return fused(
            n, tp, inner_input, gate_input, state_inputs, step_size, resets, decay_rate, skip_gain,
            conv_inner, conv_state, norm_gain, out_weight, residual, final_gain, head_weight,
            scored, targets, policy_logprob,
        )
    taps = conv_inner.shape[0]
    rows_here = inner_input.shape[0]
    q_count = state_inputs.shape[2] // STATE
    z_count = n // q_count
    z, q = c // q_count, c % q_count
    picked_rows = scored.shape[0]
    local_rows = scored - c * rows_here
    here = jnp.arange(rows_here, dtype=jnp.int32)
    pick = (local_rows[:, None] == here[None, :]).astype(jnp.bfloat16)
    gate_rows = jnp.dot(pick, gate_input, preferred_element_type=f32).astype(jnp.bfloat16)
    res_rows = jnp.dot(pick, residual, preferred_element_type=f32).astype(jnp.bfloat16)
    meta = jnp.zeros((8, rows_here), f32)
    meta = meta.at[0].set(resets.astype(f32))
    meta = meta.at[1, :picked_rows].set(local_rows.astype(f32))
    xs, ss, ds, gs, ms, x_edge, s_edge, m_edge, res_all = spread(
        n, tp, q_count, inner_input, state_inputs, step_size, gate_rows, meta, res_rows
    )
    tokens = q_count * rows_here
    width = xs.shape[2]
    heads = ds.shape[1]
    rows = q_count * picked_rows
    gate = gs.reshape(rows, width)
    flags = ms[:, 0].reshape(tokens)
    spots = ms[:, 1, :picked_rows] + (jnp.arange(q_count) * rows_here).astype(f32)[:, None]
    spots = spots.reshape(rows, 1).astype(jnp.int32)
    margin = taps - 1
    f_tail = jnp.where(z > 0, m_edge[0, rows_here - margin :], 0.0)
    clear = 1.0 - jnp.concatenate([f_tail, flags])
    keeping = [jnp.ones((tokens,), f32)]
    for offset in range(1, taps):
        keeping.append(keeping[-1] * clear[margin - offset + 1 : margin - offset + 1 + tokens])
    keeps = jnp.pad(jnp.stack(keeping), ((0, -taps % 8), (0, 0)))
    normed = middle(
        xs, x_edge, ss, s_edge, keeps, ds, jnp.broadcast_to(flags[None], (8, tokens)), spots, gate,
        conv_inner, conv_state, decay_rate.reshape(q_count, heads, 1),
        skip_gain.reshape(q_count, 1, heads), norm_gain[None], q_count, z_count,
    )
    res = res_all.reshape(z_count * rows, -1)
    return tail(
        normed, out_weight, head_weight, res, final_gain, targets, policy_logprob,
        n, tp, q_count, z_count,
    )


def solution(mesh):
    return jax.shard_map(
        body,
        mesh=mesh,
        in_specs=(
            P("ctx", "tp"),
            P("ctx", "tp"),
            P(None, "ctx", "tp"),
            P("tp", "ctx"),
            P("ctx"),
            P("tp"),
            P("tp"),
            P(None, "tp"),
            P(None, None, "tp"),
            P("tp"),
            P("tp", "ctx"),
            P("ctx", "tp"),
            P(),
            P(None, ("ctx", "tp")),
            P("ctx"),
            P(),
            P(),
        ),
        out_specs=(P(), P()),
        check_vma=False,
    )
```

```python
import functools
import jax
import jax.numpy as jnp
from jax import lax
from jax.experimental import pallas as pl
from jax.experimental.pallas import tpu as pltpu
from jax.sharding import PartitionSpec as P

HEAD_DIM = 64
STATE = 128
EDGE = 16
LEVELS = 32767.0
TINY = 1e-30

epsilon = 1e-05
precise = lax.Precision.HIGHEST
MESH = pl.DeviceIdType.MESH
VMEM = pl.BlockSpec(memory_space=pltpu.VMEM)
ANY = pl.BlockSpec(memory_space=pl.ANY)


def remote(src, dst, send, recv, device):
    return pltpu.make_async_remote_copy(
        src_ref=src, dst_ref=dst, send_sem=send, recv_sem=recv, device_id=device, device_id_type=MESH
    )


def greet(devices):
    barrier = pltpu.get_barrier_semaphore()
    for device in devices:
        pl.semaphore_signal(barrier, inc=1, device_id=device, device_id_type=MESH)
    pl.semaphore_wait(barrier, len(devices))


def spread_kernel(n, tp, q_count, z_count, x_ref, s_ref, d_ref, g_ref, m_ref, r_ref,
                  xo, so, do, go, mo, xh, sh, mh, ro,
                  send, recv, own, edge_send, edge_recv, res_send, res_recv):
    c, t = lax.axis_index("ctx"), lax.axis_index("tp")
    z, q = c // q_count, c % q_count
    total = n * tp
    me = c * tp + t
    barrier = pltpu.get_barrier_semaphore()

    def hello(k, carry):
        other = (me + k) % total
        pl.semaphore_signal(
            barrier, inc=1, device_id=(other // tp, other % tp), device_id_type=MESH
        )
        return carry

    lax.fori_loop(1, total, hello, 0)
    pl.semaphore_wait(barrier, total - 1)
    width = xo.shape[2]
    heads = do.shape[1]
    rows = x_ref.shape[0]

    def cols(ref, k, size):
        return ref.at[:, pl.ds(pl.multiple_of(k * size, 128), size)]

    def parts(k):
        return (
            cols(x_ref, k, width),
            s_ref.at[:, :, pl.ds(pl.multiple_of(k * STATE, 128), STATE)],
            d_ref.at[pl.ds(pl.multiple_of(k * heads, 8), heads), :],
            cols(g_ref, k, width),
            m_ref,
        )

    def slots(k):
        return (xo.at[k], so.at[k], do.at[k], go.at[k], mo.at[k])

    started = []
    tail = pl.ds(rows - EDGE, EDGE)
    next_z = jnp.minimum(z + 1, z_count - 1)

    def edges(k, dst_c):
        wide = pl.ds(pl.multiple_of(k * width, 128), width)
        thin = pl.ds(pl.multiple_of(k * STATE, 128), STATE)
        triple = ((x_ref.at[tail, wide], xh), (s_ref.at[:, tail, thin], sh), (m_ref, mh))
        return [
            remote(a, b, edge_send.at[k, i], edge_recv.at[i], (dst_c, t))
            for i, (a, b) in enumerate(triple)
        ]

    sends_edge = (q == q_count - 1) & (z < z_count - 1)
    gets_edge = z > 0
    if z_count > 1:
        @pl.when(sends_edge)
        def _():
            for k in range(q_count):
                for copy in edges(k, (z + 1) * q_count + k):
                    copy.start()

    for d in range(1, q_count):
        k = (q + d) % q_count
        for i, (a, b) in enumerate(zip(parts(k), slots(q))):
            copy = remote(a, b, send.at[d - 1, i], recv.at[d - 1, i], (z * q_count + k, t))
            copy.start()
            started.append(copy)
    per = n // tp

    def res_copy(j, to_t):
        return remote(
            r_ref.at[j], ro.at[c],
            res_send.at[j * tp + to_t], res_recv.at[c], (t * per + j, to_t)
        )

    for j in range(per):
        for to_t in range(tp):
            mine = (t * per + j == c) & (to_t == t)

            @pl.when(jnp.logical_not(mine))
            def _():
                res_copy(j, to_t).start()

            @pl.when(mine)
            def _():
                pltpu.make_async_copy(r_ref.at[j], ro.at[c], res_recv.at[c]).start()
    locals_ = [
        pltpu.make_async_copy(a, b, own.at[i]) for i, (a, b) in enumerate(zip(parts(q), slots(q)))
    ]
    for copy in locals_:
        copy.start()
    for copy in locals_:
        copy.wait()
    for j in range(per):
        for to_t in range(tp):
            mine = (t * per + j == c) & (to_t == t)

            @pl.when(jnp.logical_not(mine))
            def _():
                res_copy(j, to_t).wait_send()
    for k in range(n):
        pltpu.make_async_copy(ro.at[k], ro.at[k], res_recv.at[k]).wait()
    for copy in started:
        copy.wait_send()
    for d in range(1, q_count):
        k = (q + q_count - d) % q_count
        for i, (a, b) in enumerate(zip(parts(q), slots(k))):
            remote(a, b, send.at[d - 1, i], recv.at[d - 1, i], (z * q_count + k, t)).wait_recv()
    if z_count > 1:
        @pl.when(sends_edge)
        def _():
            for k in range(q_count):
                for copy in edges(k, (z + 1) * q_count + k):
                    copy.wait_send()

        @pl.when(gets_edge)
        def _():
            for i, ref in enumerate((xh, sh, mh)):
                pltpu.make_async_copy(ref, ref, edge_recv.at[i]).wait()


def spread(n, tp, q_count, x, s, d, g, m, r):
    z_count = n // q_count
    rows, all_width = x.shape
    width = all_width // q_count
    heads = d.shape[0] // q_count
    block = r.shape[1] * tp // n
    r = r.reshape(r.shape[0], n // tp, block).transpose(1, 0, 2)
    shape = jax.ShapeDtypeStruct
    outs = (
        shape((q_count, rows, width), x.dtype),
        shape((q_count, 2, rows, STATE), s.dtype),
        shape((q_count, heads, rows), d.dtype),
        shape((q_count, g.shape[0], width), g.dtype),
        shape((q_count,) + m.shape, m.dtype),
        shape((EDGE, width), x.dtype),
        shape((2, EDGE, STATE), s.dtype),
        shape(m.shape, m.dtype),
        shape((n,) + r.shape[1:], r.dtype),
    )
    dma = pltpu.SemaphoreType.DMA
    peers = max(q_count - 1, 1)
    return pl.pallas_call(
        functools.partial(spread_kernel, n, tp, q_count, z_count),
        out_shape=outs,
        in_specs=[ANY, ANY, ANY, VMEM, VMEM, VMEM],
        out_specs=[VMEM] * len(outs),
        scratch_shapes=[
            dma((peers, 5)), dma((peers, 5)), dma((5,)), dma((q_count, 3)), dma((3,)),
            dma((n,)), dma((n,)),
        ],
        compiler_params=pltpu.CompilerParams(collective_id=0, has_side_effects=True),
    )(x, s, d, g, m, r)


def staged(kernel, skip, count, shapes):
    def run(*refs):
        ins, rest, held, sems = (
            refs[:count], refs[count : -len(shapes) - 1], refs[-len(shapes) - 1 : -1], refs[-1]
        )
        held = iter(held)
        views, copies = [], []
        for i, ref in enumerate(ins):
            if i in skip:
                views.append(ref)
                continue
            local = next(held)
            copy = pltpu.make_async_copy(ref, local, sems.at[len(copies)])
            copy.start()
            copies.append(copy)
            views.append(local)
        for copy in copies:
            copy.wait()
        kernel(*views, *rest)

    extra = [pltpu.VMEM(a.shape, a.dtype) for a in shapes]
    return run, extra + [pltpu.SemaphoreType.DMA((len(shapes),))]


def mid_kernel(q_count, z_count, x_ref, xe_ref, s_ref, se_ref, k_ref, d_ref, f_ref, spot_ref,
               gate_ref, tx_ref, ts_ref, rate_ref, skip_ref, gain_ref, out,
               pad_x, pad_s, values, writes, reads, mine_r, all_r, y, far, pd, far_pd, mixed, carried,
               r_send, r_recv, y_send, y_recv, p_send, p_recv):
    f32, bf16 = jnp.float32, jnp.bfloat16
    c, t = lax.axis_index("ctx"), lax.axis_index("tp")
    z, q = c // q_count, c % q_count
    barrier = pltpu.get_barrier_semaphore()

    def peer(d):
        return (((z + d) % z_count) * q_count + q, t)

    for d in range(1, z_count):
        pl.semaphore_signal(barrier, inc=1, device_id=peer(d), device_id_type=MESH)
    tokens, width = values.shape
    piece = tokens // q_count
    heads = d_ref.shape[1]
    rows = mine_r.shape[0]
    taps = tx_ref.shape[0]
    has_edge = (z > 0).astype(f32)
    keep = k_ref[...].T

    def filtered(pad, kernel, start, target):
        total = jnp.zeros((piece, pad.shape[1]), f32)
        for off in range(taps):
            total = total + (
                keep[start : start + piece, off : off + 1]
                * kernel[off : off + 1]
                * pad[EDGE - off + start : EDGE - off + start + piece, :]
            )
        target[start : start + piece, :] = jax.nn.silu(total).astype(bf16)

    thin = pl.ds(pl.multiple_of(q * STATE, 128), STATE)
    for which, target in ((1, reads), (0, writes)):
        edge = se_ref[which].astype(f32)
        pad_s[:EDGE, :] = jnp.where(has_edge > 0.0, edge, 0.0)
        for k in range(q_count):
            pad_s[EDGE + k * piece : EDGE + (k + 1) * piece, :] = s_ref[k, which].astype(f32)
        kernel = ts_ref[which, :, thin]
        for k in range(q_count):
            filtered(pad_s, kernel, k * piece, target)
    spots = spot_ref[...]
    lanes = lax.broadcasted_iota(jnp.int32, (rows, tokens), 1)
    pick_f = jnp.where(spots == lanes, 1.0, 0.0)
    pick = pick_f.astype(bf16)
    mine_r[...] = jnp.dot(pick, reads[...], preferred_element_type=f32).astype(bf16)
    pl.semaphore_wait(barrier, z_count - 1)
    sent = []
    for d in range(1, z_count):
        copy = remote(mine_r, all_r.at[z], r_send.at[d], r_recv.at[d], peer(d))
        copy.start()
        sent.append(copy)
    all_r[z] = mine_r[...]
    wide = pl.ds(pl.multiple_of(q * width, 128), width)
    kernel_x = tx_ref[:, wide]
    pad_x[:EDGE, :] = jnp.where(has_edge > 0.0, xe_ref[...].astype(f32), 0.0)
    for k in range(q_count):
        pad_x[EDGE + k * piece : EDGE + (k + 1) * piece, :] = x_ref[k].astype(f32)
    for k in range(q_count):
        filtered(pad_x, kernel_x, k * piece, values)
    steps = jnp.concatenate([d_ref[k] for k in range(q_count)], axis=1)
    lower = jnp.where(
        lax.broadcasted_iota(jnp.int32, (tokens, tokens), 0)
        <= lax.broadcasted_iota(jnp.int32, (tokens, tokens), 1),
        1.0, 0.0,
    )
    runs = jnp.concatenate([-rate_ref[q] * steps, f_ref[...]], axis=0)
    sums = jnp.dot(runs, lower, precision=precise, preferred_element_type=f32)
    cumulated = sums[:heads]
    segment = sums[heads : heads + 1]
    at_rows = lax.dot_general(
        pick_f, sums, (((1,), (1,)), ((), ())), precision=precise, preferred_element_type=f32
    )
    row_cum = at_rows[:, :heads]
    row_seg = at_rows[:, heads : heads + 1]
    last = cumulated[:, tokens - 1 : tokens]
    last_seg = segment[:, tokens - 1 : tokens]
    to_end = jnp.exp(last - cumulated) * jnp.where(segment == last_seg, 1.0, 0.0) * steps
    spread_heads = jnp.where(
        lax.broadcasted_iota(jnp.int32, (heads, width), 0)
        == lax.broadcasted_iota(jnp.int32, (heads, width), 1) // HEAD_DIM,
        1.0, 0.0,
    )

    def widen(a):
        return jnp.dot(a, spread_heads, precision=precise, preferred_element_type=f32)

    plane = jnp.broadcast_to(jnp.exp(last) * jnp.where(last_seg == 0.0, 1.0, 0.0), (heads, 128))
    pd[...] = widen(plane.T[:8])
    weighted = values[...].astype(f32) * widen(to_end.T)
    state = jnp.dot(
        writes[...].astype(f32).T, weighted, precision=precise, preferred_element_type=f32
    )
    for d in range(1, z_count):
        here = all_r.at[(z + z_count - d) % z_count]
        remote(mine_r, here, r_send.at[d], r_recv.at[d], peer(d)).wait_recv()
    for k in range(z_count):
        y[k] = jnp.dot(
            all_r[k].astype(f32), state, precision=precise, preferred_element_type=f32
        )

    def outgoing(d):
        return (
            remote(y.at[(z + d) % z_count], far.at[z], y_send.at[d], y_recv.at[d], peer(d)),
            remote(pd, far_pd.at[z], p_send.at[d], p_recv.at[d], peer(d)),
        )

    for d in range(1, z_count):
        @pl.when(z + d < z_count)
        def _():
            for copy in outgoing(d):
                copy.start()
    scores = lax.dot_general(
        mine_r[...], writes[...], (((1,), (1,)), ((), ())), preferred_element_type=f32
    )
    causal = (spots >= lanes) & (row_seg == segment)
    half = lax.broadcasted_iota(jnp.int32, (rows, 2 * HEAD_DIM), 1) < HEAD_DIM
    for pair in range(heads // 2):
        mixes = []
        for h in (2 * pair, 2 * pair + 1):
            gaps = row_cum[:, h : h + 1] - cumulated[h : h + 1]
            decay = jnp.where(causal, jnp.exp(jnp.where(causal, gaps, 0.0)), 0.0)
            mixes.append(scores * decay * steps[h : h + 1])
        span = slice(pair * 2 * HEAD_DIM, (pair + 1) * 2 * HEAD_DIM)
        product = jnp.dot(
            jnp.concatenate(mixes, axis=0), values[:, span].astype(f32),
            precision=precise, preferred_element_type=f32,
        )
        mixed[:, span] = jnp.where(half, product[:rows], product[rows:])
    own_values = jnp.dot(pick, values[...], preferred_element_type=f32)
    from_start = jnp.exp(row_cum) * jnp.where(row_seg == 0.0, 1.0, 0.0)
    factors = widen(
        jnp.concatenate([from_start, jnp.broadcast_to(skip_ref[q], (8, heads))], axis=0)
    )
    gate = jax.nn.silu(gate_ref[...].astype(f32))
    carried[...] = jnp.zeros((rows, width), f32)
    for d in range(z_count - 1, 0, -1):
        @pl.when(z - d >= 0)
        def _():
            k = z - d + jnp.where(z - d < 0, z_count, 0)
            here, there = far.at[k], far_pd.at[k]
            remote(here, here, y_send.at[d], y_recv.at[d], peer(d)).wait_recv()
            remote(there, there, p_send.at[d], p_recv.at[d], peer(d)).wait_recv()
            carried[...] = carried[...] * far_pd[k][0:1] + far[k]
    gated = (
        mixed[...] + carried[...] * factors[:rows] + factors[rows : rows + 1] * own_values
    ) * gate
    scale = lax.rsqrt(jnp.mean(gated * gated, axis=1, keepdims=True) + epsilon)
    out[...] = (gated * scale * gain_ref[:, wide]).astype(bf16)
    for copy in sent:
        copy.wait_send()
    for d in range(1, z_count):
        @pl.when(z + d < z_count)
        def _():
            for copy in outgoing(d):
                copy.wait_send()


def middle(xs, x_edge, ss, s_edge, keeps, steps, flags, spots, gate, taps_x, taps_s, rate, skip, gain,
           q_count, z_count):
    f32, bf16 = jnp.float32, jnp.bfloat16
    tokens = steps.shape[0] * steps.shape[2]
    rows, width = gate.shape
    operands = (
        xs, x_edge, ss, s_edge, keeps, steps, flags, spots, gate, taps_x, taps_s, rate, skip, gain
    )
    run, extra = staged(
        functools.partial(mid_kernel, q_count, z_count), (), len(operands), operands
    )
    dma, vmem = pltpu.SemaphoreType.DMA, pltpu.VMEM
    return pl.pallas_call(
        run,
        out_shape=jax.ShapeDtypeStruct((rows, width), bf16),
        in_specs=[ANY] * len(operands),
        out_specs=VMEM,
        scratch_shapes=[
            vmem((EDGE + tokens, width), f32),
            vmem((EDGE + tokens, STATE), f32),
            vmem((tokens, width), bf16),
            vmem((tokens, STATE), bf16),
            vmem((tokens, STATE), bf16),
            vmem((rows, STATE), bf16),
            vmem((z_count, rows, STATE), bf16),
            vmem((z_count, rows, width), f32),
            vmem((z_count, rows, width), f32),
            vmem((8, width), f32),
            vmem((z_count, 8, width), f32),
            vmem((rows, width), f32),
            vmem((rows, width), f32),
        ] + [dma((z_count,))] * 6 + extra,
        compiler_params=pltpu.CompilerParams(
            collective_id=1, has_side_effects=True, vmem_limit_bytes=58 * 1024 * 1024
        ),
    )(*operands)


def tail_kernel(n, tp, q_count, z_count, n_ref, ow_ref, hw_ref, r_ref, g_ref, t_ref, p_ref, out,
                ow, hw, nrm, both, hid, feat, logit, stat, every,
                own, tp_send, tp_recv, st_send, st_recv, *gather_sems):
    c, t = lax.axis_index("ctx"), lax.axis_index("tp")
    z, q = c // q_count, c % q_count
    total = n * tp
    me = c * tp + t
    get_ow = pltpu.make_async_copy(ow_ref, ow, own.at[0])
    get_hw = pltpu.make_async_copy(hw_ref, hw, own.at[1])
    barrier = pltpu.get_barrier_semaphore()

    def device(k):
        return (k // tp, k % tp)

    def hello(d, carry):
        pl.semaphore_signal(
            barrier, inc=1, device_id=device((me + d) % total), device_id_type=MESH
        )
        return carry

    lax.fori_loop(1, total, hello, 0)
    get_ow.start()
    get_hw.start()
    pl.semaphore_wait(barrier, total - 1)
    core_n = 2 if q_count % 2 == 0 else 1
    x_n = q_count // core_n
    x, core = q // core_n, q % core_n

    def at_x(k):
        return (z * q_count + k * core_n + core, t)

    at_core = (z * q_count + x * core_n + (core_n - 1) - core, t)

    def gathered(slot, mine, sems):
        z_send, z_recv, x_send, x_recv, c_send, c_recv = sems
        sent = []

        def push(copy):
            copy.start()
            sent.append(copy)

        def to_x(ref, dst, d):
            for e in range(1, x_n):
                push(remote(ref, dst, x_send.at[e - 1, d], x_recv.at[e - 1, d], at_x((x + e) % x_n)))

        def to_core(ref, dst, e, d):
            if core_n > 1:
                push(remote(ref, dst, c_send.at[e, d], c_recv.at[e, d], at_core))

        home = slot(q, z)
        for d in range(1, z_count):
            push(remote(mine, home, z_send.at[d], z_recv.at[d], (((z + d) % z_count) * q_count + q, t)))
        to_x(mine, home, 0)
        to_core(mine, home, 0, 0)
        for d in range(z_count):
            k = (z + z_count - d) % z_count
            if d:
                here = slot(q, k)
                remote(here, here, z_send.at[d], z_recv.at[d], at_core).wait_recv()
                to_x(here, here, d)
                to_core(here, here, 0, d)
            for e in range(1, x_n):
                here = slot(((x + x_n - e) % x_n) * core_n + core, k)
                remote(here, here, x_send.at[e - 1, d], x_recv.at[e - 1, d], at_core).wait_recv()
                to_core(here, here, e, d)
        if core_n > 1:
            for d in range(z_count):
                k = (z + z_count - d) % z_count
                for e in range(x_n):
                    here = slot(((x + x_n - e) % x_n) * core_n + 1 - core, k)
                    remote(here, here, c_send.at[e, d], c_recv.at[e, d], at_core).wait_recv()
        return sent

    rows = n_ref.shape[0]
    width = n_ref.shape[1]

    def normed_slot(a, b):
        return nrm.at[a, b]

    pending = gathered(normed_slot, n_ref, gather_sems[:6])
    nrm[q, z] = n_ref[...]
    get_ow.wait()
    partial = jnp.zeros(both.shape[1:], jnp.float32)
    for k in range(q_count):
        partial = partial + jnp.dot(
            nrm[k].reshape(z_count * rows, width),
            ow[k * width : (k + 1) * width, :],
            preferred_element_type=jnp.float32,
        )
    both[t] = partial
    tp_copies = []
    for d in range(1, tp):
        copy = remote(both.at[t], both.at[t], tp_send.at[d], tp_recv.at[d], (c, (t + d) % tp))
        copy.start()
        tp_copies.append(copy)
    for d in range(1, tp):
        here = both.at[(t + tp - d) % tp]
        remote(here, here, tp_send.at[d], tp_recv.at[d], (c, (t + d) % tp)).wait_recv()
    summed = both[0]
    for k in range(1, tp):
        summed = summed + both[k]
    hid[q, z] = (r_ref[...].astype(jnp.float32) + summed).astype(jnp.bfloat16)

    def hidden_slot(a, b):
        return hid.at[a, b]

    pending = pending + tp_copies + gathered(hidden_slot, hid.at[q, z], gather_sems[6:])
    block = hid.shape[3]
    all_rows = hid.shape[2]
    squares = jnp.zeros((all_rows, 1), jnp.float32)
    for k in range(z_count):
        for a in range(q_count):
            piece = hid[a, k].astype(jnp.float32)
            squares = squares + jnp.sum(piece * piece, axis=1, keepdims=True)
    inverse = lax.rsqrt(squares / (n * block) + epsilon)
    for k in range(z_count):
        for a in range(q_count):
            first = (k * q_count + a) * block
            span = slice(first, first + block)
            feat[:, span] = (
                hid[a, k].astype(jnp.float32) * inverse * g_ref[:, span]
            ).astype(jnp.bfloat16)
    get_hw.wait()
    vocab = hw.shape[1]
    tile = min(256, vocab)

    def one_tile(i, carry):
        cols = pl.ds(pl.multiple_of(i * tile, 128), tile)
        logit[:, cols] = jnp.dot(feat[...], hw[:, cols], preferred_element_type=jnp.float32)
        return carry

    lax.fori_loop(0, vocab // tile, one_tile, 0)
    values = logit[...]
    top = jnp.max(values, axis=1, keepdims=True)
    added = jnp.sum(jnp.exp(values - top), axis=1, keepdims=True)
    column = t_ref[...] - me * vocab
    places = lax.broadcasted_iota(jnp.int32, values.shape, 1)
    hit = jnp.sum(jnp.where(places == column, values, 0.0), axis=1, keepdims=True)
    lane = lax.broadcasted_iota(jnp.int32, (all_rows, 128), 1)
    packed = jnp.where(lane == 0, top, jnp.where(lane == 1, added, jnp.where(lane == 2, hit, 0.0)))
    turned = packed.T[:8]
    stat[...] = turned

    def go(d, carry):
        remote(
            stat, every.at[me], st_send.at[d], st_recv.at[d], device((me + d) % total)
        ).start()
        return carry

    lax.fori_loop(1, total, go, 0)
    every[me] = turned

    def done(d, carry):
        here = every.at[(me + total - d) % total]
        copy = remote(stat, here, st_send.at[d], st_recv.at[d], device((me + d) % total))
        copy.wait_send()
        copy.wait_recv()
        return carry

    lax.fori_loop(1, total, done, 0)
    for copy in pending:
        copy.wait_send()
    found = every[...]
    tops = found[:, 0, :]
    row_top = jnp.max(tops, axis=0, keepdims=True)
    full = jnp.sum(found[:, 1, :] * jnp.exp(tops - row_top), axis=0, keepdims=True)
    picked = jnp.sum(found[:, 2, :], axis=0, keepdims=True)
    log_prob = picked - row_top - jnp.log(full)
    out[0:1, :] = log_prob
    out[1:2, :] = 0.5 * jnp.square(log_prob - p_ref[...])


def tail(normed, out_weight, head_weight, res, gain, targets, policy, n, tp, q_count, z_count):
    dma = pltpu.SemaphoreType.DMA
    total = n * tp
    rows, width = normed.shape
    all_rows = z_count * rows
    block = out_weight.shape[1]
    core_n = 2 if q_count % 2 == 0 else 1
    x_n = q_count // core_n
    vmem = pltpu.VMEM
    bf16, f32 = jnp.bfloat16, jnp.float32
    e_n = max(x_n - 1, 1)
    sems = [
        dma((z_count,)), dma((z_count,)), dma((e_n, z_count)), dma((e_n, z_count)),
        dma((x_n, z_count)), dma((x_n, z_count)),
    ]
    operands = (
        normed, out_weight, head_weight, res, gain[None], targets[:, None], policy[None]
    )
    run, extra = staged(
        functools.partial(tail_kernel, n, tp, q_count, z_count), (1, 2), len(operands),
        operands[:1] + operands[3:],
    )
    result = pl.pallas_call(
        run,
        out_shape=jax.ShapeDtypeStruct((2, all_rows), f32),
        in_specs=[ANY] * len(operands),
        out_specs=VMEM,
        scratch_shapes=[
            vmem(out_weight.shape, bf16),
            vmem(head_weight.shape, bf16),
            vmem((q_count, z_count, rows, width), bf16),
            vmem((tp, all_rows, block), f32),
            vmem((q_count, z_count, all_rows, block), bf16),
            vmem((all_rows, n * block), bf16),
            vmem((all_rows, head_weight.shape[1]), f32),
            vmem((8, all_rows), f32),
            vmem((total, 8, all_rows), f32),
            dma((2,)), dma((tp,)), dma((tp,)), dma((total,)), dma((total,)),
        ] + sems + sems + extra,
        compiler_params=pltpu.CompilerParams(
            collective_id=3, has_side_effects=True, vmem_limit_bytes=58 * 1024 * 1024
        ),
    )(*operands)
    return result[0], result[1]


def halves(a):
    hi = a.astype(jnp.bfloat16)
    return hi, (a - hi.astype(jnp.float32)).astype(jnp.bfloat16)


def thirds(a):
    hi = a.astype(jnp.bfloat16)
    rest = a - hi.astype(jnp.float32)
    mid = rest.astype(jnp.bfloat16)
    return hi, mid, (rest - mid.astype(jnp.float32)).astype(jnp.bfloat16)


def column(row, first, count):
    lanes = row.shape[1]
    spot = lax.broadcasted_iota(jnp.int32, (count, lanes), 0) + first
    hit = lax.broadcasted_iota(jnp.int32, (count, lanes), 1) == spot
    return jnp.sum(jnp.where(hit, jnp.broadcast_to(row, (count, lanes)), 0.0), axis=1, keepdims=True)


def one_kernel(n, tp, *refs):
    names, refs = refs[0], refs[1:]
    r = dict(zip(names, refs))
    f32, bf16 = jnp.float32, jnp.bfloat16
    c, t = lax.axis_index("ctx"), lax.axis_index("tp")
    total = n * tp
    me = c * tp + t
    chips = n // 2
    z_n = chips // 2
    k, p = c % 2, c // 2
    x, z = p % 2, p // 2

    def dev(z_, x_, k_):
        return ((z_ * 2 + x_) * 2 + k_, t)

    core_peer, x_peer, y_peer = dev(z, x, 1 - k), dev(z, 1 - x, k), (c, 1 - t)
    T, C = r["x"].shape
    W = C // 2
    S = r["s"].shape[2] // 2
    G = S // STATE
    GW = W // G
    H = r["d"].shape[0]
    HC = H // 2
    Tc = 2 * T
    r8 = r["scored"].shape[0]
    RC = 2 * r8
    R = chips * RC
    taps = r["tx"].shape[0]
    blk = r["ow"].shape[1] // tp
    D = n * tp * blk
    V = r["hw"].shape[1]
    per = n // tp

    barrier = pltpu.get_barrier_semaphore()

    plane_peers = [
        (((z * 2 + (x + a) % 2) * 2 + (k + b) % 2), (t + e) % tp)
        for a in range(2) for b in range(2) for e in range(tp) if a + b + e
    ]
    z_peers = [dev((z + d) % z_n, x, k) for d in range(1, z_n)]

    def greet_one(sem, device):
        pl.semaphore_signal(sem, inc=1, device_id=device, device_id_type=MESH)

    for device in plane_peers + z_peers:
        greet_one(barrier, device)
    sends_up = (x == 1) & (k == 1) & (z < z_n - 1)

    @pl.when((x == 0) & (z > 0))
    def _():
        greet_one(barrier, dev(z - 1, 1, 1))

    def lanes(a, size):
        return pl.ds(pl.multiple_of(a * size, 128), size)

    local = {}

    def fetch(name, src, dst):
        copy = pltpu.make_async_copy(src, dst, r["own"].at[len(local)])
        local[name] = copy
        copy.start()

    def arrived(ref, sem):
        pltpu.make_async_copy(ref, ref, sem).wait()

    sent = []

    def push(copy, when=None):
        sent.append((copy, when))
        if when is None:
            copy.start()
        else:
            pl.when(when)(copy.start)

    fetch("resets", r["resets"], r["resv"])
    fetch("scored", r["scored"], r["spot"])
    fetch("s", r["s"].at[:, :, lanes(k, S)], r["sc"].at[k])
    fetch("ts", r["ts"].at[:, :, lanes(k, S)], r["tsv"])
    half_heads = pl.ds(pl.multiple_of(k * HC, 8), HC)
    fetch("d", r["d"].at[half_heads], r["dc"].at[k])
    fetch("rate", r["rate"], r["ratev"])
    fetch("x", r["x"].at[:, lanes(k, W)], r["xc"].at[k])
    fetch("tx", r["tx"].at[:, lanes(k, W)], r["txv"])
    fetch("g", r["g"], r["gv"])
    fetch("res", r["res"], r["rv"])
    fetch("skip", r["skip"], r["skipv"])
    fetch("gain", r["gain"].at[:, lanes(k, W)], r["gainv"])
    fetch("fg", r["fg"], r["fgv"])
    fetch("tgt", r["tgt"], r["tgtv"])
    fetch("pol", r["pol"], r["polv"])
    fetch("ow", r["ow"], r["oww"])

    first = p == 0

    @pl.when(first)
    def _():
        r["xh"][...] = jnp.zeros(r["xh"].shape, bf16)
        r["sh"][...] = jnp.zeros(r["sh"].shape, bf16)
        r["mh"][...] = jnp.zeros(r["mh"].shape, f32)

    local["resets"].wait()
    local["scored"].wait()
    lane8 = lax.broadcasted_iota(jnp.int32, (8, T), 1)
    row8 = lax.broadcasted_iota(jnp.int32, (8, T), 0)
    places = jnp.zeros((8, T), f32)
    for i in range(r8):
        places = jnp.where(lane8 == i, (r["spot"][i] - c * T).astype(f32), places)
    flags_here = jnp.broadcast_to(r["resv"][...].astype(f32), (8, T))
    r["meta"][...] = jnp.where(row8 == 0, flags_here, places)

    pl.semaphore_wait(barrier, len(plane_peers) + len(z_peers) + jnp.where(sends_up, 2, 0))
    for device in plane_peers:
        greet_one(r["ready"], device)

    send, recv = r["core_send"], r["core_recv"]
    edge_send, edge_recv = r["edge_send"], r["edge_recv"]
    swap = (
        (r["s"].at[:, :, lanes(1 - k, S)], r["sc"].at[k]),
        (r["meta"], r["mc"].at[k]),
        (r["d"].at[pl.ds(pl.multiple_of((1 - k) * HC, 8), HC)], r["dc"].at[k]),
        (r["x"].at[:, lanes(1 - k, W)], r["xc"].at[k]),
    )
    for i, (a, b) in enumerate(swap):
        push(remote(a, b, send.at[i], recv.at[i], core_peer))
    last_core = (k == 1) & (p < chips - 1)
    tail = pl.ds(T - EDGE, EDGE)
    nxt = jnp.minimum(p + 1, chips - 1)
    for j in range(2):
        triple = (
            (r["s"].at[:, tail, j * S : (j + 1) * S], r["sh"]),
            (r["meta"], r["mh"]),
            (r["x"].at[tail, j * W : (j + 1) * W], r["xh"]),
        )
        for i, (a, b) in enumerate(triple):
            push(remote(a, b, edge_send.at[j, i], edge_recv.at[i], (nxt * 2 + j, t)), last_core)
    r["mc"][k] = r["meta"][...]

    def from_core(i, buf):
        arrived(buf.at[1 - k], recv.at[i])

    def from_edge(i, ref):
        @pl.when(jnp.logical_not(first))
        def _():
            arrived(ref, edge_recv.at[i])

    from_core(1, r["mc"])
    spots = jnp.concatenate(
        [column(r["mc"][j][1:2], 0, r8) + j * T for j in range(2)], axis=0
    ).astype(jnp.int32)
    lane_t = lax.broadcasted_iota(jnp.int32, (RC, Tc), 1)
    pick_f = jnp.where(spots == lane_t, 1.0, 0.0)
    pick = pick_f.astype(bf16)

    chip_flags = jnp.concatenate([r["mc"][0], r["mc"][1]], axis=1)
    local["d"].wait()
    local["rate"].wait()
    from_core(2, r["dc"])
    steps = jnp.concatenate([r["dc"][0], r["dc"][1]], axis=1)
    lower = jnp.where(
        lax.broadcasted_iota(jnp.int32, (Tc, Tc), 0) <= lax.broadcasted_iota(jnp.int32, (Tc, Tc), 1),
        1.0, 0.0,
    ).astype(bf16)
    rate_col = column(r["ratev"][...], k * HC, HC)
    runs = jnp.concatenate([-rate_col * steps, chip_flags], axis=0)
    sums3 = jnp.dot(jnp.concatenate(thirds(runs), axis=0), lower, preferred_element_type=f32)
    count = HC + 8
    sums = sums3[:count] + sums3[count : 2 * count] + sums3[2 * count :]
    cumulated = sums[:HC]
    segment = sums[HC : HC + 1]
    last = cumulated[:, Tc - 1 : Tc]
    last_seg = segment[:, Tc - 1 : Tc]
    plane = jnp.broadcast_to(jnp.exp(last) * jnp.where(last_seg == 0.0, 1.0, 0.0), (HC, 128))
    r["mine_pd"][...] = jnp.concatenate([plane.T[:8], jnp.zeros((8, 128 - HC), f32)], axis=1)
    pl.semaphore_wait(r["ready"], len(plane_peers))
    for d in range(1, chips):
        remote(
            r["mine_pd"], r["all_pd"].at[p], r["pd_send"], r["pd_recv"],
            (((p + d) % chips) * 2 + k, t),
        ).start()
    r["all_pd"][p] = r["mine_pd"][...]
    at_rows = lax.dot_general(
        pick_f, sums, (((1,), (1,)), ((), ())), precision=precise, preferred_element_type=f32
    )
    row_cum = at_rows[:, :HC]
    row_seg = at_rows[:, HC : HC + 1]
    to_end = jnp.exp(last - cumulated) * jnp.where(segment == last_seg, 1.0, 0.0) * steps
    r["te"][...] = jnp.concatenate(halves(to_end.T), axis=1)
    local["g"].wait()
    local["res"].wait()
    own_pick = jnp.where(
        column(r["meta"][1:2], 0, r8) == lax.broadcasted_iota(jnp.int32, (r8, T), 1).astype(f32),
        1.0, 0.0,
    ).astype(bf16)
    r["gc"][k] = jnp.dot(
        own_pick, r["gv"][:, lanes(k, W)], preferred_element_type=f32
    ).astype(bf16)
    r["gsend"][...] = jnp.dot(
        own_pick, r["gv"][:, lanes(1 - k, W)], preferred_element_type=f32
    ).astype(bf16)
    push(remote(r["gsend"], r["gc"].at[k], send.at[4], recv.at[4], core_peer))
    res_rows = jnp.dot(own_pick, r["rv"][...], preferred_element_type=f32).astype(bf16)

    for j in range(per * tp):
        r["rsend"][j] = res_rows[:, j * blk : (j + 1) * blk]

    def res_copy(j, to_t):
        i = j * tp + to_t
        return remote(
            r["rsend"].at[i], r["ro"].at[c], r["res_send"], r["res_recv"],
            (t * per + j, to_t),
        )

    for j in range(per):
        for to_t in range(tp):
            mine = (t * per + j == c) & (to_t == t)
            pl.when(jnp.logical_not(mine))(res_copy(j, to_t).start)

            @pl.when(mine)
            def _():
                pltpu.make_async_copy(
                    r["rsend"].at[j * tp + to_t], r["ro"].at[c], r["res_recv"]
                ).start()

    from_edge(1, r["mh"])
    flags = jnp.concatenate([r["mh"][...], chip_flags], axis=1)
    clear = 1.0 - flags
    keeping = jnp.ones((8, 3 * T), f32)
    columns = [keeping]
    for off in range(1, taps):
        shifted = clear if off == 1 else pltpu.roll(clear, off - 1, 1)
        keeping = keeping * shifted
        columns.append(keeping)
    keep_rows = jnp.zeros((8, 3 * T), f32)
    row8w = lax.broadcasted_iota(jnp.int32, (8, 3 * T), 0)
    for off in range(taps):
        keep_rows = jnp.where(row8w == off, jnp.broadcast_to(columns[off][0:1], (8, 3 * T)), keep_rows)
    keep = keep_rows[:, T:].T
    for off in range(1, taps):
        r["kb"][off] = jnp.broadcast_to(keep[:, off : off + 1], (Tc, 128))
    wide_keep = [None] + [r["kb"].at[off] for off in range(1, taps)]

    def filtered(pad, kernel, start, size):
        width = pad.shape[1]
        acc = kernel[0:1] * pad[EDGE + start : EDGE + start + size, :]
        for off in range(1, taps):
            kept = wide_keep[off][start : start + size, :]
            kept = jnp.concatenate([kept] * (width // 128), axis=1)
            acc = acc + kept * (
                kernel[off : off + 1] * pad[EDGE - off + start : EDGE - off + start + size, :]
            )
        return jax.nn.silu(acc).astype(bf16)

    local["s"].wait()
    local["ts"].wait()
    from_core(0, r["sc"])
    from_edge(0, r["sh"])
    pad = r["pad"]
    band = 64
    for which, target in ((1, r["reads"]), (0, r["writes"])):
        for g in range(G):
            cols = slice(g * STATE, (g + 1) * STATE)
            pad_s = r["pad_s"]
            pad_s[:EDGE, :] = r["sh"][which, :, cols].astype(f32)
            for j in range(2):
                pad_s[EDGE + j * T : EDGE + (j + 1) * T, :] = r["sc"][j, which, :, cols].astype(f32)
            kernel = r["tsv"][which, :, cols]
            for b in range(Tc // band):
                target[b * band : (b + 1) * band, cols] = filtered(pad_s, kernel, b * band, band)
        if which == 1:
            r["mine_r"][...] = jnp.dot(
                pick, r["reads"][...], preferred_element_type=f32
            ).astype(bf16)
            for d in range(1, chips):
                remote(
                    r["mine_r"], r["all_r"].at[p], r["r_send"], r["r_recv"],
                    (((p + d) % chips) * 2 + k, t),
                ).start()
            r["all_r"][p] = r["mine_r"][...]

    for g in range(G):
        r["wT"][g] = r["writes"][:, g * STATE : (g + 1) * STATE].astype(f32).T.astype(bf16)

    chunk = 256

    def spread_cols(j, size, offset):
        head = lax.broadcasted_iota(jnp.int32, (size, chunk), 0) % (size // 2)
        lane = lax.broadcasted_iota(jnp.int32, (size, chunk), 1)
        return jnp.where(head == offset + (j * chunk + lane) // HEAD_DIM, 1.0, 0.0).astype(bf16)

    local["x"].wait()
    local["tx"].wait()
    from_core(3, r["xc"])
    from_edge(2, r["xh"])

    def conv_step(j, carry):
        cols = lanes(j, chunk)
        pad[:EDGE, :] = r["xh"][:, cols].astype(f32)
        for i in range(2):
            pad[EDGE + i * T : EDGE + (i + 1) * T, :] = r["xc"][i, :, cols].astype(f32)
        kernel = r["txv"][:, cols]
        for b in range(Tc // band):
            r["values"][b * band : (b + 1) * band, cols] = filtered(pad, kernel, b * band, band)
        grown = jnp.dot(r["te"][...], spread_cols(j, 2 * HC, 0), preferred_element_type=f32)
        hi, lo = halves(r["values"][:, cols].astype(f32) * grown)
        w_t = r["wT"][(j * chunk) // GW]
        state = jnp.dot(w_t, hi, preferred_element_type=f32) + jnp.dot(
            w_t, lo, preferred_element_type=f32
        )
        s_hi, s_lo = halves(state)
        r["S2"][:STATE, cols] = s_hi
        r["S2"][STATE:, cols] = s_lo
        return carry

    lax.fori_loop(0, W // chunk, conv_step, 0)

    fetch("hw", r["hw"], r["hww"])

    others = pl.ds(0, chips - 1)
    arrived(r["all_r"].at[others], r["r_recv"])
    arrived(r["all_pd"].at[others], r["pd_recv"])
    arrived(r["all_r"].at[others], r["r_send"])
    arrived(r["all_pd"].at[others], r["pd_send"])
    for g in range(G):
        rows_g = r["all_r"][:, :, g * STATE : (g + 1) * STATE].reshape(R, STATE)
        r["rr"][g, :, :STATE] = rows_g
        r["rr"][g, :, STATE:] = rows_g
    run_w = jnp.ones((1, 128), f32)
    weights = []
    for d in range(chips):
        weights.append(jnp.broadcast_to(run_w, (RC, 128)))
        run_w = jnp.where(d > p, run_w * r["all_pd"][d][0:1], run_w)
    far = jnp.concatenate(weights, axis=0)[:, :HC]
    r["ww"][...] = jnp.concatenate(halves(far), axis=1)

    def y_step(j, carry):
        cols = lanes(j, chunk)
        y = jnp.dot(r["rr"][(j * chunk) // GW], r["S2"][:, cols], preferred_element_type=f32)
        grown = jnp.dot(r["ww"][...], spread_cols(j, 2 * HC, 0), preferred_element_type=f32)
        r["yf"][:, cols] = y * grown
        return carry

    lax.fori_loop(0, W // chunk, y_step, 0)

    def y_rows(zd, xd):
        return r["yf"][pl.ds(pl.multiple_of((zd * 2 + xd) * RC, 16), RC), :]

    def coded(a, wire, scale):
        most = jnp.max(jnp.abs(a), axis=1, keepdims=True)
        inverse = jnp.where(most > 0.0, LEVELS / jnp.maximum(most, TINY), 0.0)
        wire[...] = jnp.round(a * inverse).astype(jnp.int32).astype(jnp.int16)
        scale[...] = jnp.broadcast_to(most * (1.0 / LEVELS), (RC, 128))

    def decoded(wire, scale):
        return wire[...].astype(jnp.int32).astype(f32) * scale[:, :1]

    for zd in range(z_n - 1, -1, -1):
        goes = (zd > z) | ((zd == z) & (x == 0))

        @pl.when(goes)
        def _():
            coded(y_rows(zd, 1 - x), r["xsend"].at[zd], r["xsend_f"].at[zd])

        for i, (a, b) in enumerate(((r["xsend"], r["xr"]), (r["xsend_f"], r["xr_f"]))):
            push(
                remote(a.at[zd], b.at[zd], r["x_send"].at[i, zd], r["x_recv"].at[i, zd], x_peer),
                goes,
            )

    def from_x_peer(zd):
        for i, b in enumerate((r["xr"], r["xr_f"])):
            arrived(b.at[zd], r["x_recv"].at[i, zd])
        return decoded(r["xr"].at[zd], r["xr_f"].at[zd])

    mine_r = r["mine_r"][...]
    scores = [
        lax.dot_general(
            mine_r[:, g * STATE : (g + 1) * STATE], r["writes"][:, g * STATE : (g + 1) * STATE],
            (((1,), (1,)), ((), ())), preferred_element_type=f32,
        )
        for g in range(G)
    ]
    causal = (spots >= lane_t) & (row_seg == segment)
    quad = 4
    quad_w = quad * HEAD_DIM
    which_head = lax.broadcasted_iota(jnp.int32, (RC, quad_w), 1) // HEAD_DIM

    def within(q):
        mixes = []
        for i in range(quad):
            h = q * quad + i
            gaps = row_cum[:, h : h + 1] - cumulated[h : h + 1]
            decay = jnp.where(causal, jnp.exp(jnp.where(causal, gaps, 0.0)), 0.0)
            mixes.append(scores[h * HEAD_DIM // GW] * decay * steps[h : h + 1])
        both = jnp.concatenate(halves(jnp.concatenate(mixes, axis=0)), axis=0)
        span = slice(q * quad_w, (q + 1) * quad_w)
        product = jnp.dot(both, r["values"][:, span], preferred_element_type=f32)
        product = product[: quad * RC] + product[quad * RC :]
        out = product[:RC]
        for i in range(1, quad):
            out = jnp.where(which_head == i, product[i * RC : (i + 1) * RC], out)
        r["mixed"][:, span] = out

    quads = HC // quad
    for q in range(quads // 2):
        within(q)
    for zd in range(z_n - 1, 0, -1):
        goes = zd > z

        @pl.when(goes)
        def _():
            coded(y_rows(zd, x) + from_x_peer(zd), r["zsend"].at[zd], r["zsend_f"].at[zd])

        for i, (a, b) in enumerate(((r["zsend"], r["zr"]), (r["zsend_f"], r["zr_f"]))):
            push(
                remote(a.at[zd], b.at[z], r["z_send"].at[i, zd], r["z_recv"].at[i, z], dev(zd, x, k)),
                goes,
            )
    for q in range(quads // 2, quads):
        within(q)

    local["skip"].wait()
    local["gain"].wait()
    from_start = jnp.exp(row_cum) * jnp.where(row_seg == 0.0, 1.0, 0.0)
    starts = jnp.concatenate(halves(from_start), axis=1)
    skip3 = jnp.concatenate(
        [jnp.broadcast_to(a, (8, H)) for a in thirds(jnp.broadcast_to(r["skipv"][...], (8, H)))], axis=0
    )
    from_core(4, r["gc"])
    gate = jnp.concatenate([r["gc"][0].astype(f32), r["gc"][1].astype(f32)], axis=0)

    def widen_step(j, carry):
        cols = lanes(j, chunk)
        own_values = jnp.dot(pick, r["values"][:, cols], preferred_element_type=f32)
        head = lax.broadcasted_iota(jnp.int32, (H, chunk), 0)
        lane = lax.broadcasted_iota(jnp.int32, (H, chunk), 1)
        all_heads = jnp.where(head == k * HC + (j * chunk + lane) // HEAD_DIM, 1.0, 0.0).astype(bf16)
        grown = jnp.dot(skip3, all_heads, preferred_element_type=f32)
        skip_row = grown[0:1] + grown[8:9] + grown[16:17]
        r["mixed"][:, cols] = r["mixed"][:, cols] + skip_row * own_values
        r["starts"][:, cols] = jnp.dot(starts, spread_cols(j, 2 * HC, 0), preferred_element_type=f32)
        return carry

    lax.fori_loop(0, W // chunk, widen_step, 0)
    gate = jax.nn.silu(gate)

    carried = r["carried"]
    carried[...] = jnp.zeros((RC, W), f32)

    @pl.when(x == 1)
    def _():
        carried[...] = from_x_peer(z)

    for zs in range(z_n - 1):
        @pl.when(zs < z)
        def _():
            for i, b in enumerate((r["zr"], r["zr_f"])):
                arrived(b.at[zs], r["z_recv"].at[i, zs])
            carried[...] = carried[...] + decoded(r["zr"].at[zs], r["zr_f"].at[zs])

    gated = (r["mixed"][...] + carried[...] * r["starts"][...]) * gate
    for g in range(G):
        span = slice(g * GW, (g + 1) * GW)
        part = gated[:, span]
        scale = lax.rsqrt(jnp.mean(part * part, axis=1, keepdims=True) + epsilon)
        r["normed"][:, span] = (part * scale * r["gainv"][:, span]).astype(bf16)

    nrm = r["nrm"]
    mine = r["normed"]
    z_recv, x_recv, c_recv = r["gather1"]
    g_send = r["g_send"]

    def slot(z_, x_, k_):
        return nrm.at[k_ * chips + z_ * 2 + x_]

    def go1(a, b, sem, device):
        remote(a, b, g_send.at[0], sem, device).start()

    home = slot(z, x, k)
    for d in range(1, z_n):
        go1(mine, home, z_recv.at[z], dev((z + d) % z_n, x, k))
    go1(mine, home, x_recv.at[z], x_peer)
    go1(mine, home, c_recv.at[0, z], core_peer)
    nrm[k * chips + p] = mine[...]
    for zs in range(z_n):
        @pl.when(zs != z)
        def _():
            here = slot(zs, x, k)
            arrived(here, z_recv.at[zs])
            go1(here, here, x_recv.at[zs], x_peer)
            go1(here, here, c_recv.at[0, zs], core_peer)

    for zs in range(z_n):
        here = slot(zs, 1 - x, k)
        arrived(here, x_recv.at[zs])
        go1(here, here, c_recv.at[1, zs], core_peer)
    for zs in range(z_n):
        for e, x_ in ((0, x), (1, 1 - x)):
            arrived(slot(zs, x_, 1 - k), c_recv.at[e, zs])
    arrived(nrm.at[pl.ds(0, 2 * chips - 1)], g_send.at[0])
    local["ow"].wait()
    partial = jnp.zeros((R, tp * blk), f32)
    for j in range(2):
        partial = partial + jnp.dot(
            nrm[j * chips : (j + 1) * chips].reshape(R, W), r["oww"][j * W : (j + 1) * W, :], preferred_element_type=f32
        )
    for j in range(tp):
        r["pt"][j] = partial[:, j * blk : (j + 1) * blk]
    push(remote(r["pt"].at[1 - t], r["pr"], r["t_send"], r["t_recv"], y_peer))
    arrived(r["ro"], r["res_recv"])
    in_half = (c >= t * per) & (c < (t + 1) * per)

    @pl.when(in_half)
    def _():
        arrived(r["rsend"].at[pl.ds(0, n - 1)], r["res_send"])

    @pl.when(jnp.logical_not(in_half))
    def _():
        arrived(r["rsend"], r["res_send"])

    res_all = r["ro"][...].astype(f32).reshape(R, blk)
    arrived(r["pr"], r["t_recv"])
    hid = r["hid"]
    hid[me] = (res_all + (r["pt"][t] + r["pr"][...])).astype(bf16)

    z_recv, a_recv, b_recv, c_recv = r["gather2"]
    even = k == 0
    a0, b0 = jnp.where(even, t, x), jnp.where(even, x, t)

    def place(z_, a_, b_, k_):
        y_, x_ = jnp.where(k_ == 0, a_, b_), jnp.where(k_ == 0, b_, a_)
        return hid.at[((z_ * 2 + x_) * 2 + k_) * tp + y_]

    a_peer = (jnp.where(even, c, x_peer[0]), jnp.where(even, 1 - t, t))
    b_peer = (jnp.where(even, x_peer[0], c), jnp.where(even, t, 1 - t))

    def go2(here, sem, device):
        remote(here, here, g_send.at[1], sem, device).start()

    def to_a(here, d):
        go2(here, a_recv.at[d], a_peer)

    diag = (x_peer[0], 1 - t)

    def to_diag(here, d):
        go2(here, b_recv.at[1, d], diag)

    def to_b(here, e, d):
        go2(here, b_recv.at[e, d], b_peer)

    def to_core(here, e, d):
        go2(here, c_recv.at[e, d], core_peer)

    home = place(z, a0, b0, k)
    for d in range(1, z_n):
        go2(home, z_recv.at[d], dev((z + d) % z_n, x, k))
    to_diag(home, 0)
    to_a(home, 0)
    to_b(home, 0, 0)
    to_core(home, 0, 0)
    for d in range(1, z_n):
        here = place((z + z_n - d) % z_n, a0, b0, k)
        arrived(here, z_recv.at[d])
        to_diag(here, d)
        to_a(here, d)
        to_b(here, 0, d)
        to_core(here, 0, d)
    for d in range(z_n):
        here = place((z + z_n - d) % z_n, 1 - a0, b0, k)
        arrived(here, a_recv.at[d])
        to_core(here, 1, d)
    for d in range(z_n):
        here = place((z + z_n - d) % z_n, a0, 1 - b0, k)
        arrived(here, b_recv.at[0, d])
        to_core(here, 2, d)
    for d in range(z_n):
        here = place((z + z_n - d) % z_n, 1 - a0, 1 - b0, k)
        arrived(here, b_recv.at[1, d])
        to_core(here, 3, d)
    oa, ob = jnp.where(even, x, t), jnp.where(even, t, x)
    for d in range(z_n):
        from_z = (z + z_n - d) % z_n
        for e, (a_, b_) in enumerate(((oa, ob), (1 - oa, ob), (oa, 1 - ob), (1 - oa, 1 - ob))):
            arrived(place(from_z, a_, b_, 1 - k), c_recv.at[e, d])

    arrived(hid.at[pl.ds(0, total - 1)], g_send.at[1])
    squares = jnp.zeros((R, 1), f32)
    for a in range(n):
        for b in range(tp):
            piece = hid[a * tp + b].astype(f32)
            squares = squares + jnp.sum(piece * piece, axis=1, keepdims=True)
    inverse = lax.rsqrt(squares / D + epsilon)
    local["fg"].wait()
    feat = r["feat"]
    for a in range(n):
        for b in range(tp):
            start = (a * tp + b) * blk
            span = slice(start, start + blk)
            feat[:, span] = (hid[a * tp + b].astype(f32) * inverse * r["fgv"][:, span]).astype(bf16)
    local["hw"].wait()
    tile = min(256, V)
    logit = r["logit"]

    def one_tile(i, carry):
        cols = lanes(i, tile)
        logit[:, cols] = jnp.dot(feat[...], r["hww"][:, cols], preferred_element_type=f32)
        return carry

    lax.fori_loop(0, V // tile, one_tile, 0)
    values = logit[...]
    top = jnp.max(values, axis=1, keepdims=True)
    added = jnp.sum(jnp.exp(values - top), axis=1, keepdims=True)
    local["tgt"].wait()
    local["pol"].wait()
    target = column(r["tgtv"][...].astype(f32), 0, R).astype(jnp.int32) - me * V
    hit = jnp.sum(
        jnp.where(lax.broadcasted_iota(jnp.int32, values.shape, 1) == target, values, 0.0),
        axis=1, keepdims=True,
    )
    lane = lax.broadcasted_iota(jnp.int32, (R, 128), 1)
    packed = jnp.where(lane == 0, top, jnp.where(lane == 1, added, jnp.where(lane == 2, hit, 0.0)))
    turned = packed.T[:4]
    stat, every = r["stat"], r["every"]
    stat[...] = turned
    st_send, st_recv = r["st_send"], r["st_recv"]

    def device(a):
        return (a // tp, a % tp)

    def go(d, carry):
        remote(stat, every.at[me], st_send, st_recv, device((me + d) % total)).start()
        return carry

    lax.fori_loop(1, total, go, 0)
    every[me] = turned

    for copy, when in sent:
        if when is None:
            copy.wait_send()
        else:
            pl.when(when)(copy.wait_send)
    rest = every.at[pl.ds(0, total - 1)]
    arrived(rest, st_send)
    arrived(rest, st_recv)
    found = every[...]
    tops = found[:, 0, :]
    row_top = jnp.max(tops, axis=0, keepdims=True)
    full = jnp.sum(found[:, 1, :] * jnp.exp(tops - row_top), axis=0, keepdims=True)
    picked = jnp.sum(found[:, 2, :], axis=0, keepdims=True)
    log_prob = picked - row_top - jnp.log(full)
    r["out"][0:1, :] = log_prob
    r["out"][1:2, :] = 0.5 * jnp.square(log_prob - r["polv"][...])


def fused(n, tp, x, g, s, d, resets, rate, skip, tx, ts, gain, ow, res, fg, hw, scored, tgt, pol):
    f32, bf16, i32, i16 = jnp.float32, jnp.bfloat16, jnp.int32, jnp.int16
    dma, vmem = pltpu.SemaphoreType.DMA, pltpu.VMEM
    chips = n // 2
    z_n = chips // 2
    T, C = x.shape
    W, Tc = C // 2, 2 * T
    S = s.shape[2] // 2
    G = S // STATE
    H = d.shape[0]
    HC = H // 2
    r8 = scored.shape[0]
    RC = 2 * r8
    R = chips * RC
    blk = ow.shape[1] // tp
    taps = tx.shape[0]
    total = n * tp
    inputs = dict(
        x=x, g=g, s=s, d=d, resets=resets[None], rate=rate[None], skip=skip[None], tx=tx, ts=ts,
        gain=gain[None], ow=ow, res=res, fg=fg[None], hw=hw, scored=scored, tgt=tgt[None], pol=pol[None],
    )
    scratch = dict(
        resv=vmem((1, T), i32), spot=pltpu.SMEM((r8,), i32), meta=vmem((8, T), f32),
        xc=vmem((2, T, W), bf16), xh=vmem((EDGE, W), bf16),
        sc=vmem((2, 2, T, S), bf16), sh=vmem((2, EDGE, S), bf16),
        dc=vmem((2, HC, T), f32), mc=vmem((2, 8, T), f32), mh=vmem((8, T), f32),
        gv=vmem(g.shape, bf16), rv=vmem(res.shape, bf16),
        gc=vmem((2, r8, W), bf16), gsend=vmem((r8, W), bf16),
        rsend=vmem((n, r8, blk), bf16), ro=vmem((n, r8, blk), bf16),
        txv=vmem((taps, W), f32), tsv=vmem((2, taps, S), f32), gainv=vmem((1, W), f32),
        ratev=vmem((1, H), f32), skipv=vmem((1, H), f32), fgv=vmem((1, n * tp * blk), f32),
        tgtv=vmem((1, R), i32), polv=vmem((1, R), f32),
        pad=vmem((EDGE + Tc, 256), f32), pad_s=vmem((EDGE + Tc, STATE), f32),
        kb=vmem((taps, Tc, 128), f32),
        reads=vmem((Tc, S), bf16), writes=vmem((Tc, S), bf16),
        mine_r=vmem((RC, S), bf16), all_r=vmem((chips, RC, S), bf16),
        mine_pd=vmem((8, 128), f32), all_pd=vmem((chips, 8, 128), f32),
        te=vmem((Tc, 2 * HC), bf16), wT=vmem((G, STATE, Tc), bf16),
        values=vmem((Tc, W), bf16), S2=vmem((2 * STATE, W), bf16),
        rr=vmem((G, R, 2 * STATE), bf16), ww=vmem((R, 2 * HC), bf16), yf=vmem((R, W), f32),
        xsend=vmem((z_n, RC, W), i16), xr=vmem((z_n, RC, W), i16),
        zsend=vmem((z_n, RC, W), i16), zr=vmem((z_n, RC, W), i16),
        xsend_f=vmem((z_n, RC, 128), f32), xr_f=vmem((z_n, RC, 128), f32),
        zsend_f=vmem((z_n, RC, 128), f32), zr_f=vmem((z_n, RC, 128), f32),
        mixed=vmem((RC, W), f32), starts=vmem((RC, W), f32), carried=vmem((RC, W), f32),
        normed=vmem((RC, W), bf16), nrm=vmem((2 * chips, RC, W), bf16),
        pt=vmem((tp, R, blk), f32), pr=vmem((R, blk), f32),
        hid=vmem((total, R, blk), bf16), feat=vmem((R, n * tp * blk), bf16),
        logit=vmem((R, hw.shape[1]), f32), stat=vmem((4, R), f32), every=vmem((total, 4, R), f32),
        oww=vmem(ow.shape, bf16), hww=vmem(hw.shape, bf16),
        own=dma((18,)), core_send=dma((5,)), core_recv=dma((5,)),
        edge_send=dma((2, 3)), edge_recv=dma((3,)),
        r_send=dma(()), r_recv=dma(()), pd_send=dma(()), pd_recv=dma(()),
        x_send=dma((2, z_n)), x_recv=dma((2, z_n)), z_send=dma((2, z_n)), z_recv=dma((2, z_n)),
        res_send=dma(()), res_recv=dma(()), g_send=dma((2,)), t_send=dma(()), t_recv=dma(()),
        st_send=dma(()), st_recv=dma(()), ready=pltpu.SemaphoreType.REGULAR,
    )
    many = [("gather1", [dma((z_n,))] * 2 + [dma((2, z_n))])]
    many.append(("gather2", [dma((z_n,))] * 2 + [dma((2, z_n)), dma((4, z_n))]))
    names = list(inputs) + ["out"] + list(scratch)
    groups = [(name, len(sems)) for name, sems in many]
    extra = [sem for _, sems in many for sem in sems]

    def run(*refs):
        plain, rest = list(refs[: len(names)]), list(refs[len(names) :])
        for _, size in groups:
            plain.append(tuple(rest[:size]))
            rest = rest[size:]
        one_kernel(n, tp, names + [name for name, _ in groups], *plain)

    both = pl.pallas_call(
        run,
        out_shape=jax.ShapeDtypeStruct((2, R), f32),
        in_specs=[ANY] * len(inputs),
        out_specs=VMEM,
        scratch_shapes=list(scratch.values()) + extra,
        compiler_params=pltpu.CompilerParams(
            collective_id=5, has_side_effects=True, vmem_limit_bytes=58 * 1024 * 1024
        ),
    )(*inputs.values())
    return both[0], both[1]


def body(
    inner_input,
    gate_input,
    state_inputs,
    step_size,
    resets,
    decay_rate,
    skip_gain,
    conv_inner,
    conv_state,
    norm_gain,
    out_weight,
    residual,
    final_gain,
    head_weight,
    scored,
    targets,
    policy_logprob,
):
    f32 = jnp.float32
    n, tp = lax.axis_size("ctx"), lax.axis_size("tp")
    c, t = lax.axis_index("ctx"), lax.axis_index("tp")
    if n % 4 == 0 and tp == 2 and (state_inputs.shape[2] // STATE) % 2 == 0:
        return fused(
            n, tp, inner_input, gate_input, state_inputs, step_size, resets, decay_rate, skip_gain,
            conv_inner, conv_state, norm_gain, out_weight, residual, final_gain, head_weight,
            scored, targets, policy_logprob,
        )
    taps = conv_inner.shape[0]
    rows_here = inner_input.shape[0]
    q_count = state_inputs.shape[2] // STATE
    z_count = n // q_count
    z, q = c // q_count, c % q_count
    picked_rows = scored.shape[0]
    local_rows = scored - c * rows_here
    here = jnp.arange(rows_here, dtype=jnp.int32)
    pick = (local_rows[:, None] == here[None, :]).astype(jnp.bfloat16)
    gate_rows = jnp.dot(pick, gate_input, preferred_element_type=f32).astype(jnp.bfloat16)
    res_rows = jnp.dot(pick, residual, preferred_element_type=f32).astype(jnp.bfloat16)
    meta = jnp.zeros((8, rows_here), f32)
    meta = meta.at[0].set(resets.astype(f32))
    meta = meta.at[1, :picked_rows].set(local_rows.astype(f32))
    xs, ss, ds, gs, ms, x_edge, s_edge, m_edge, res_all = spread(
        n, tp, q_count, inner_input, state_inputs, step_size, gate_rows, meta, res_rows
    )
    tokens = q_count * rows_here
    width = xs.shape[2]
    heads = ds.shape[1]
    rows = q_count * picked_rows
    gate = gs.reshape(rows, width)
    flags = ms[:, 0].reshape(tokens)
    spots = ms[:, 1, :picked_rows] + (jnp.arange(q_count) * rows_here).astype(f32)[:, None]
    spots = spots.reshape(rows, 1).astype(jnp.int32)
    margin = taps - 1
    f_tail = jnp.where(z > 0, m_edge[0, rows_here - margin :], 0.0)
    clear = 1.0 - jnp.concatenate([f_tail, flags])
    keeping = [jnp.ones((tokens,), f32)]
    for offset in range(1, taps):
        keeping.append(keeping[-1] * clear[margin - offset + 1 : margin - offset + 1 + tokens])
    keeps = jnp.pad(jnp.stack(keeping), ((0, -taps % 8), (0, 0)))
    normed = middle(
        xs, x_edge, ss, s_edge, keeps, ds, jnp.broadcast_to(flags[None], (8, tokens)), spots, gate,
        conv_inner, conv_state, decay_rate.reshape(q_count, heads, 1),
        skip_gain.reshape(q_count, 1, heads), norm_gain[None], q_count, z_count,
    )
    res = res_all.reshape(z_count * rows, -1)
    return tail(
        normed, out_weight, head_weight, res, final_gain, targets, policy_logprob,
        n, tp, q_count, z_count,
    )


def solution(mesh):
    return jax.shard_map(
        body,
        mesh=mesh,
        in_specs=(
            P("ctx", "tp"),
            P("ctx", "tp"),
            P(None, "ctx", "tp"),
            P("tp", "ctx"),
            P("ctx"),
            P("tp"),
            P("tp"),
            P(None, "tp"),
            P(None, None, "tp"),
            P("tp"),
            P("tp", "ctx"),
            P("ctx", "tp"),
            P(),
            P(None, ("ctx", "tp")),
            P("ctx"),
            P(),
            P(),
        ),
        out_specs=(P(), P()),
        check_vma=False,
    )
```

```python
import functools
import jax
import jax.numpy as jnp
from jax import lax
from jax.experimental import pallas as pl
from jax.experimental.pallas import tpu as pltpu
from jax.sharding import PartitionSpec as P

HEAD_DIM = 64
STATE = 128
EDGE = 16
LEVELS = 32767.0
TINY = 1e-30

epsilon = 1e-05
precise = lax.Precision.HIGHEST
MESH = pl.DeviceIdType.MESH
VMEM = pl.BlockSpec(memory_space=pltpu.VMEM)
ANY = pl.BlockSpec(memory_space=pl.ANY)


def remote(src, dst, send, recv, device):
    return pltpu.make_async_remote_copy(
        src_ref=src, dst_ref=dst, send_sem=send, recv_sem=recv, device_id=device, device_id_type=MESH
    )


def greet(devices):
    barrier = pltpu.get_barrier_semaphore()
    for device in devices:
        pl.semaphore_signal(barrier, inc=1, device_id=device, device_id_type=MESH)
    pl.semaphore_wait(barrier, len(devices))


def spread_kernel(n, tp, q_count, z_count, x_ref, s_ref, d_ref, g_ref, m_ref, r_ref,
                  xo, so, do, go, mo, xh, sh, mh, ro,
                  send, recv, own, edge_send, edge_recv, res_send, res_recv):
    c, t = lax.axis_index("ctx"), lax.axis_index("tp")
    z, q = c // q_count, c % q_count
    total = n * tp
    me = c * tp + t
    barrier = pltpu.get_barrier_semaphore()

    def hello(k, carry):
        other = (me + k) % total
        pl.semaphore_signal(
            barrier, inc=1, device_id=(other // tp, other % tp), device_id_type=MESH
        )
        return carry

    lax.fori_loop(1, total, hello, 0)
    pl.semaphore_wait(barrier, total - 1)
    width = xo.shape[2]
    heads = do.shape[1]
    rows = x_ref.shape[0]

    def cols(ref, k, size):
        return ref.at[:, pl.ds(pl.multiple_of(k * size, 128), size)]

    def parts(k):
        return (
            cols(x_ref, k, width),
            s_ref.at[:, :, pl.ds(pl.multiple_of(k * STATE, 128), STATE)],
            d_ref.at[pl.ds(pl.multiple_of(k * heads, 8), heads), :],
            cols(g_ref, k, width),
            m_ref,
        )

    def slots(k):
        return (xo.at[k], so.at[k], do.at[k], go.at[k], mo.at[k])

    started = []
    tail = pl.ds(rows - EDGE, EDGE)
    next_z = jnp.minimum(z + 1, z_count - 1)

    def edges(k, dst_c):
        wide = pl.ds(pl.multiple_of(k * width, 128), width)
        thin = pl.ds(pl.multiple_of(k * STATE, 128), STATE)
        triple = ((x_ref.at[tail, wide], xh), (s_ref.at[:, tail, thin], sh), (m_ref, mh))
        return [
            remote(a, b, edge_send.at[k, i], edge_recv.at[i], (dst_c, t))
            for i, (a, b) in enumerate(triple)
        ]

    sends_edge = (q == q_count - 1) & (z < z_count - 1)
    gets_edge = z > 0
    if z_count > 1:
        @pl.when(sends_edge)
        def _():
            for k in range(q_count):
                for copy in edges(k, (z + 1) * q_count + k):
                    copy.start()

    for d in range(1, q_count):
        k = (q + d) % q_count
        for i, (a, b) in enumerate(zip(parts(k), slots(q))):
            copy = remote(a, b, send.at[d - 1, i], recv.at[d - 1, i], (z * q_count + k, t))
            copy.start()
            started.append(copy)
    per = n // tp

    def res_copy(j, to_t):
        return remote(
            r_ref.at[j], ro.at[c],
            res_send.at[j * tp + to_t], res_recv.at[c], (t * per + j, to_t)
        )

    for j in range(per):
        for to_t in range(tp):
            mine = (t * per + j == c) & (to_t == t)

            @pl.when(jnp.logical_not(mine))
            def _():
                res_copy(j, to_t).start()

            @pl.when(mine)
            def _():
                pltpu.make_async_copy(r_ref.at[j], ro.at[c], res_recv.at[c]).start()
    locals_ = [
        pltpu.make_async_copy(a, b, own.at[i]) for i, (a, b) in enumerate(zip(parts(q), slots(q)))
    ]
    for copy in locals_:
        copy.start()
    for copy in locals_:
        copy.wait()
    for j in range(per):
        for to_t in range(tp):
            mine = (t * per + j == c) & (to_t == t)

            @pl.when(jnp.logical_not(mine))
            def _():
                res_copy(j, to_t).wait_send()
    for k in range(n):
        pltpu.make_async_copy(ro.at[k], ro.at[k], res_recv.at[k]).wait()
    for copy in started:
        copy.wait_send()
    for d in range(1, q_count):
        k = (q + q_count - d) % q_count
        for i, (a, b) in enumerate(zip(parts(q), slots(k))):
            remote(a, b, send.at[d - 1, i], recv.at[d - 1, i], (z * q_count + k, t)).wait_recv()
    if z_count > 1:
        @pl.when(sends_edge)
        def _():
            for k in range(q_count):
                for copy in edges(k, (z + 1) * q_count + k):
                    copy.wait_send()

        @pl.when(gets_edge)
        def _():
            for i, ref in enumerate((xh, sh, mh)):
                pltpu.make_async_copy(ref, ref, edge_recv.at[i]).wait()


def spread(n, tp, q_count, x, s, d, g, m, r):
    z_count = n // q_count
    rows, all_width = x.shape
    width = all_width // q_count
    heads = d.shape[0] // q_count
    block = r.shape[1] * tp // n
    r = r.reshape(r.shape[0], n // tp, block).transpose(1, 0, 2)
    shape = jax.ShapeDtypeStruct
    outs = (
        shape((q_count, rows, width), x.dtype),
        shape((q_count, 2, rows, STATE), s.dtype),
        shape((q_count, heads, rows), d.dtype),
        shape((q_count, g.shape[0], width), g.dtype),
        shape((q_count,) + m.shape, m.dtype),
        shape((EDGE, width), x.dtype),
        shape((2, EDGE, STATE), s.dtype),
        shape(m.shape, m.dtype),
        shape((n,) + r.shape[1:], r.dtype),
    )
    dma = pltpu.SemaphoreType.DMA
    peers = max(q_count - 1, 1)
    return pl.pallas_call(
        functools.partial(spread_kernel, n, tp, q_count, z_count),
        out_shape=outs,
        in_specs=[ANY, ANY, ANY, VMEM, VMEM, VMEM],
        out_specs=[VMEM] * len(outs),
        scratch_shapes=[
            dma((peers, 5)), dma((peers, 5)), dma((5,)), dma((q_count, 3)), dma((3,)),
            dma((n,)), dma((n,)),
        ],
        compiler_params=pltpu.CompilerParams(collective_id=0, has_side_effects=True),
    )(x, s, d, g, m, r)


def staged(kernel, skip, count, shapes):
    def run(*refs):
        ins, rest, held, sems = (
            refs[:count], refs[count : -len(shapes) - 1], refs[-len(shapes) - 1 : -1], refs[-1]
        )
        held = iter(held)
        views, copies = [], []
        for i, ref in enumerate(ins):
            if i in skip:
                views.append(ref)
                continue
            local = next(held)
            copy = pltpu.make_async_copy(ref, local, sems.at[len(copies)])
            copy.start()
            copies.append(copy)
            views.append(local)
        for copy in copies:
            copy.wait()
        kernel(*views, *rest)

    extra = [pltpu.VMEM(a.shape, a.dtype) for a in shapes]
    return run, extra + [pltpu.SemaphoreType.DMA((len(shapes),))]


def mid_kernel(q_count, z_count, x_ref, xe_ref, s_ref, se_ref, k_ref, d_ref, f_ref, spot_ref,
               gate_ref, tx_ref, ts_ref, rate_ref, skip_ref, gain_ref, out,
               pad_x, pad_s, values, writes, reads, mine_r, all_r, y, far, pd, far_pd, mixed, carried,
               r_send, r_recv, y_send, y_recv, p_send, p_recv):
    f32, bf16 = jnp.float32, jnp.bfloat16
    c, t = lax.axis_index("ctx"), lax.axis_index("tp")
    z, q = c // q_count, c % q_count
    barrier = pltpu.get_barrier_semaphore()

    def peer(d):
        return (((z + d) % z_count) * q_count + q, t)

    for d in range(1, z_count):
        pl.semaphore_signal(barrier, inc=1, device_id=peer(d), device_id_type=MESH)
    tokens, width = values.shape
    piece = tokens // q_count
    heads = d_ref.shape[1]
    rows = mine_r.shape[0]
    taps = tx_ref.shape[0]
    has_edge = (z > 0).astype(f32)
    keep = k_ref[...].T

    def filtered(pad, kernel, start, target):
        total = jnp.zeros((piece, pad.shape[1]), f32)
        for off in range(taps):
            total = total + (
                keep[start : start + piece, off : off + 1]
                * kernel[off : off + 1]
                * pad[EDGE - off + start : EDGE - off + start + piece, :]
            )
        target[start : start + piece, :] = jax.nn.silu(total).astype(bf16)

    thin = pl.ds(pl.multiple_of(q * STATE, 128), STATE)
    for which, target in ((1, reads), (0, writes)):
        edge = se_ref[which].astype(f32)
        pad_s[:EDGE, :] = jnp.where(has_edge > 0.0, edge, 0.0)
        for k in range(q_count):
            pad_s[EDGE + k * piece : EDGE + (k + 1) * piece, :] = s_ref[k, which].astype(f32)
        kernel = ts_ref[which, :, thin]
        for k in range(q_count):
            filtered(pad_s, kernel, k * piece, target)
    spots = spot_ref[...]
    lanes = lax.broadcasted_iota(jnp.int32, (rows, tokens), 1)
    pick_f = jnp.where(spots == lanes, 1.0, 0.0)
    pick = pick_f.astype(bf16)
    mine_r[...] = jnp.dot(pick, reads[...], preferred_element_type=f32).astype(bf16)
    pl.semaphore_wait(barrier, z_count - 1)
    sent = []
    for d in range(1, z_count):
        copy = remote(mine_r, all_r.at[z], r_send.at[d], r_recv.at[d], peer(d))
        copy.start()
        sent.append(copy)
    all_r[z] = mine_r[...]
    wide = pl.ds(pl.multiple_of(q * width, 128), width)
    kernel_x = tx_ref[:, wide]
    pad_x[:EDGE, :] = jnp.where(has_edge > 0.0, xe_ref[...].astype(f32), 0.0)
    for k in range(q_count):
        pad_x[EDGE + k * piece : EDGE + (k + 1) * piece, :] = x_ref[k].astype(f32)
    for k in range(q_count):
        filtered(pad_x, kernel_x, k * piece, values)
    steps = jnp.concatenate([d_ref[k] for k in range(q_count)], axis=1)
    lower = jnp.where(
        lax.broadcasted_iota(jnp.int32, (tokens, tokens), 0)
        <= lax.broadcasted_iota(jnp.int32, (tokens, tokens), 1),
        1.0, 0.0,
    )
    runs = jnp.concatenate([-rate_ref[q] * steps, f_ref[...]], axis=0)
    sums = jnp.dot(runs, lower, precision=precise, preferred_element_type=f32)
    cumulated = sums[:heads]
    segment = sums[heads : heads + 1]
    at_rows = lax.dot_general(
        pick_f, sums, (((1,), (1,)), ((), ())), precision=precise, preferred_element_type=f32
    )
    row_cum = at_rows[:, :heads]
    row_seg = at_rows[:, heads : heads + 1]
    last = cumulated[:, tokens - 1 : tokens]
    last_seg = segment[:, tokens - 1 : tokens]
    to_end = jnp.exp(last - cumulated) * jnp.where(segment == last_seg, 1.0, 0.0) * steps
    spread_heads = jnp.where(
        lax.broadcasted_iota(jnp.int32, (heads, width), 0)
        == lax.broadcasted_iota(jnp.int32, (heads, width), 1) // HEAD_DIM,
        1.0, 0.0,
    )

    def widen(a):
        return jnp.dot(a, spread_heads, precision=precise, preferred_element_type=f32)

    plane = jnp.broadcast_to(jnp.exp(last) * jnp.where(last_seg == 0.0, 1.0, 0.0), (heads, 128))
    pd[...] = widen(plane.T[:8])
    weighted = values[...].astype(f32) * widen(to_end.T)
    state = jnp.dot(
        writes[...].astype(f32).T, weighted, precision=precise, preferred_element_type=f32
    )
    for d in range(1, z_count):
        here = all_r.at[(z + z_count - d) % z_count]
        remote(mine_r, here, r_send.at[d], r_recv.at[d], peer(d)).wait_recv()
    for k in range(z_count):
        y[k] = jnp.dot(
            all_r[k].astype(f32), state, precision=precise, preferred_element_type=f32
        )

    def outgoing(d):
        return (
            remote(y.at[(z + d) % z_count], far.at[z], y_send.at[d], y_recv.at[d], peer(d)),
            remote(pd, far_pd.at[z], p_send.at[d], p_recv.at[d], peer(d)),
        )

    for d in range(1, z_count):
        @pl.when(z + d < z_count)
        def _():
            for copy in outgoing(d):
                copy.start()
    scores = lax.dot_general(
        mine_r[...], writes[...], (((1,), (1,)), ((), ())), preferred_element_type=f32
    )
    causal = (spots >= lanes) & (row_seg == segment)
    half = lax.broadcasted_iota(jnp.int32, (rows, 2 * HEAD_DIM), 1) < HEAD_DIM
    for pair in range(heads // 2):
        mixes = []
        for h in (2 * pair, 2 * pair + 1):
            gaps = row_cum[:, h : h + 1] - cumulated[h : h + 1]
            decay = jnp.where(causal, jnp.exp(jnp.where(causal, gaps, 0.0)), 0.0)
            mixes.append(scores * decay * steps[h : h + 1])
        span = slice(pair * 2 * HEAD_DIM, (pair + 1) * 2 * HEAD_DIM)
        product = jnp.dot(
            jnp.concatenate(mixes, axis=0), values[:, span].astype(f32),
            precision=precise, preferred_element_type=f32,
        )
        mixed[:, span] = jnp.where(half, product[:rows], product[rows:])
    own_values = jnp.dot(pick, values[...], preferred_element_type=f32)
    from_start = jnp.exp(row_cum) * jnp.where(row_seg == 0.0, 1.0, 0.0)
    factors = widen(
        jnp.concatenate([from_start, jnp.broadcast_to(skip_ref[q], (8, heads))], axis=0)
    )
    gate = jax.nn.silu(gate_ref[...].astype(f32))
    carried[...] = jnp.zeros((rows, width), f32)
    for d in range(z_count - 1, 0, -1):
        @pl.when(z - d >= 0)
        def _():
            k = z - d + jnp.where(z - d < 0, z_count, 0)
            here, there = far.at[k], far_pd.at[k]
            remote(here, here, y_send.at[d], y_recv.at[d], peer(d)).wait_recv()
            remote(there, there, p_send.at[d], p_recv.at[d], peer(d)).wait_recv()
            carried[...] = carried[...] * far_pd[k][0:1] + far[k]
    gated = (
        mixed[...] + carried[...] * factors[:rows] + factors[rows : rows + 1] * own_values
    ) * gate
    scale = lax.rsqrt(jnp.mean(gated * gated, axis=1, keepdims=True) + epsilon)
    out[...] = (gated * scale * gain_ref[:, wide]).astype(bf16)
    for copy in sent:
        copy.wait_send()
    for d in range(1, z_count):
        @pl.when(z + d < z_count)
        def _():
            for copy in outgoing(d):
                copy.wait_send()


def middle(xs, x_edge, ss, s_edge, keeps, steps, flags, spots, gate, taps_x, taps_s, rate, skip, gain,
           q_count, z_count):
    f32, bf16 = jnp.float32, jnp.bfloat16
    tokens = steps.shape[0] * steps.shape[2]
    rows, width = gate.shape
    operands = (
        xs, x_edge, ss, s_edge, keeps, steps, flags, spots, gate, taps_x, taps_s, rate, skip, gain
    )
    run, extra = staged(
        functools.partial(mid_kernel, q_count, z_count), (), len(operands), operands
    )
    dma, vmem = pltpu.SemaphoreType.DMA, pltpu.VMEM
    return pl.pallas_call(
        run,
        out_shape=jax.ShapeDtypeStruct((rows, width), bf16),
        in_specs=[ANY] * len(operands),
        out_specs=VMEM,
        scratch_shapes=[
            vmem((EDGE + tokens, width), f32),
            vmem((EDGE + tokens, STATE), f32),
            vmem((tokens, width), bf16),
            vmem((tokens, STATE), bf16),
            vmem((tokens, STATE), bf16),
            vmem((rows, STATE), bf16),
            vmem((z_count, rows, STATE), bf16),
            vmem((z_count, rows, width), f32),
            vmem((z_count, rows, width), f32),
            vmem((8, width), f32),
            vmem((z_count, 8, width), f32),
            vmem((rows, width), f32),
            vmem((rows, width), f32),
        ] + [dma((z_count,))] * 6 + extra,
        compiler_params=pltpu.CompilerParams(
            collective_id=1, has_side_effects=True, vmem_limit_bytes=58 * 1024 * 1024
        ),
    )(*operands)


def tail_kernel(n, tp, q_count, z_count, n_ref, ow_ref, hw_ref, r_ref, g_ref, t_ref, p_ref, out,
                ow, hw, nrm, both, hid, feat, logit, stat, every,
                own, tp_send, tp_recv, st_send, st_recv, *gather_sems):
    c, t = lax.axis_index("ctx"), lax.axis_index("tp")
    z, q = c // q_count, c % q_count
    total = n * tp
    me = c * tp + t
    get_ow = pltpu.make_async_copy(ow_ref, ow, own.at[0])
    get_hw = pltpu.make_async_copy(hw_ref, hw, own.at[1])
    barrier = pltpu.get_barrier_semaphore()

    def device(k):
        return (k // tp, k % tp)

    def hello(d, carry):
        pl.semaphore_signal(
            barrier, inc=1, device_id=device((me + d) % total), device_id_type=MESH
        )
        return carry

    lax.fori_loop(1, total, hello, 0)
    get_ow.start()
    get_hw.start()
    pl.semaphore_wait(barrier, total - 1)
    core_n = 2 if q_count % 2 == 0 else 1
    x_n = q_count // core_n
    x, core = q // core_n, q % core_n

    def at_x(k):
        return (z * q_count + k * core_n + core, t)

    at_core = (z * q_count + x * core_n + (core_n - 1) - core, t)

    def gathered(slot, mine, sems):
        z_send, z_recv, x_send, x_recv, c_send, c_recv = sems
        sent = []

        def push(copy):
            copy.start()
            sent.append(copy)

        def to_x(ref, dst, d):
            for e in range(1, x_n):
                push(remote(ref, dst, x_send.at[e - 1, d], x_recv.at[e - 1, d], at_x((x + e) % x_n)))

        def to_core(ref, dst, e, d):
            if core_n > 1:
                push(remote(ref, dst, c_send.at[e, d], c_recv.at[e, d], at_core))

        home = slot(q, z)
        for d in range(1, z_count):
            push(remote(mine, home, z_send.at[d], z_recv.at[d], (((z + d) % z_count) * q_count + q, t)))
        to_x(mine, home, 0)
        to_core(mine, home, 0, 0)
        for d in range(z_count):
            k = (z + z_count - d) % z_count
            if d:
                here = slot(q, k)
                remote(here, here, z_send.at[d], z_recv.at[d], at_core).wait_recv()
                to_x(here, here, d)
                to_core(here, here, 0, d)
            for e in range(1, x_n):
                here = slot(((x + x_n - e) % x_n) * core_n + core, k)
                remote(here, here, x_send.at[e - 1, d], x_recv.at[e - 1, d], at_core).wait_recv()
                to_core(here, here, e, d)
        if core_n > 1:
            for d in range(z_count):
                k = (z + z_count - d) % z_count
                for e in range(x_n):
                    here = slot(((x + x_n - e) % x_n) * core_n + 1 - core, k)
                    remote(here, here, c_send.at[e, d], c_recv.at[e, d], at_core).wait_recv()
        return sent

    rows = n_ref.shape[0]
    width = n_ref.shape[1]

    def normed_slot(a, b):
        return nrm.at[a, b]

    pending = gathered(normed_slot, n_ref, gather_sems[:6])
    nrm[q, z] = n_ref[...]
    get_ow.wait()
    partial = jnp.zeros(both.shape[1:], jnp.float32)
    for k in range(q_count):
        partial = partial + jnp.dot(
            nrm[k].reshape(z_count * rows, width),
            ow[k * width : (k + 1) * width, :],
            preferred_element_type=jnp.float32,
        )
    both[t] = partial
    tp_copies = []
    for d in range(1, tp):
        copy = remote(both.at[t], both.at[t], tp_send.at[d], tp_recv.at[d], (c, (t + d) % tp))
        copy.start()
        tp_copies.append(copy)
    for d in range(1, tp):
        here = both.at[(t + tp - d) % tp]
        remote(here, here, tp_send.at[d], tp_recv.at[d], (c, (t + d) % tp)).wait_recv()
    summed = both[0]
    for k in range(1, tp):
        summed = summed + both[k]
    hid[q, z] = (r_ref[...].astype(jnp.float32) + summed).astype(jnp.bfloat16)

    def hidden_slot(a, b):
        return hid.at[a, b]

    pending = pending + tp_copies + gathered(hidden_slot, hid.at[q, z], gather_sems[6:])
    block = hid.shape[3]
    all_rows = hid.shape[2]
    squares = jnp.zeros((all_rows, 1), jnp.float32)
    for k in range(z_count):
        for a in range(q_count):
            piece = hid[a, k].astype(jnp.float32)
            squares = squares + jnp.sum(piece * piece, axis=1, keepdims=True)
    inverse = lax.rsqrt(squares / (n * block) + epsilon)
    for k in range(z_count):
        for a in range(q_count):
            first = (k * q_count + a) * block
            span = slice(first, first + block)
            feat[:, span] = (
                hid[a, k].astype(jnp.float32) * inverse * g_ref[:, span]
            ).astype(jnp.bfloat16)
    get_hw.wait()
    vocab = hw.shape[1]
    tile = min(256, vocab)

    def one_tile(i, carry):
        cols = pl.ds(pl.multiple_of(i * tile, 128), tile)
        logit[:, cols] = jnp.dot(feat[...], hw[:, cols], preferred_element_type=jnp.float32)
        return carry

    lax.fori_loop(0, vocab // tile, one_tile, 0)
    values = logit[...]
    top = jnp.max(values, axis=1, keepdims=True)
    added = jnp.sum(jnp.exp(values - top), axis=1, keepdims=True)
    column = t_ref[...] - me * vocab
    places = lax.broadcasted_iota(jnp.int32, values.shape, 1)
    hit = jnp.sum(jnp.where(places == column, values, 0.0), axis=1, keepdims=True)
    lane = lax.broadcasted_iota(jnp.int32, (all_rows, 128), 1)
    packed = jnp.where(lane == 0, top, jnp.where(lane == 1, added, jnp.where(lane == 2, hit, 0.0)))
    turned = packed.T[:8]
    stat[...] = turned

    def go(d, carry):
        remote(
            stat, every.at[me], st_send.at[d], st_recv.at[d], device((me + d) % total)
        ).start()
        return carry

    lax.fori_loop(1, total, go, 0)
    every[me] = turned

    def done(d, carry):
        here = every.at[(me + total - d) % total]
        copy = remote(stat, here, st_send.at[d], st_recv.at[d], device((me + d) % total))
        copy.wait_send()
        copy.wait_recv()
        return carry

    lax.fori_loop(1, total, done, 0)
    for copy in pending:
        copy.wait_send()
    found = every[...]
    tops = found[:, 0, :]
    row_top = jnp.max(tops, axis=0, keepdims=True)
    full = jnp.sum(found[:, 1, :] * jnp.exp(tops - row_top), axis=0, keepdims=True)
    picked = jnp.sum(found[:, 2, :], axis=0, keepdims=True)
    log_prob = picked - row_top - jnp.log(full)
    out[0:1, :] = log_prob
    out[1:2, :] = 0.5 * jnp.square(log_prob - p_ref[...])


def tail(normed, out_weight, head_weight, res, gain, targets, policy, n, tp, q_count, z_count):
    dma = pltpu.SemaphoreType.DMA
    total = n * tp
    rows, width = normed.shape
    all_rows = z_count * rows
    block = out_weight.shape[1]
    core_n = 2 if q_count % 2 == 0 else 1
    x_n = q_count // core_n
    vmem = pltpu.VMEM
    bf16, f32 = jnp.bfloat16, jnp.float32
    e_n = max(x_n - 1, 1)
    sems = [
        dma((z_count,)), dma((z_count,)), dma((e_n, z_count)), dma((e_n, z_count)),
        dma((x_n, z_count)), dma((x_n, z_count)),
    ]
    operands = (
        normed, out_weight, head_weight, res, gain[None], targets[:, None], policy[None]
    )
    run, extra = staged(
        functools.partial(tail_kernel, n, tp, q_count, z_count), (1, 2), len(operands),
        operands[:1] + operands[3:],
    )
    result = pl.pallas_call(
        run,
        out_shape=jax.ShapeDtypeStruct((2, all_rows), f32),
        in_specs=[ANY] * len(operands),
        out_specs=VMEM,
        scratch_shapes=[
            vmem(out_weight.shape, bf16),
            vmem(head_weight.shape, bf16),
            vmem((q_count, z_count, rows, width), bf16),
            vmem((tp, all_rows, block), f32),
            vmem((q_count, z_count, all_rows, block), bf16),
            vmem((all_rows, n * block), bf16),
            vmem((all_rows, head_weight.shape[1]), f32),
            vmem((8, all_rows), f32),
            vmem((total, 8, all_rows), f32),
            dma((2,)), dma((tp,)), dma((tp,)), dma((total,)), dma((total,)),
        ] + sems + sems + extra,
        compiler_params=pltpu.CompilerParams(
            collective_id=3, has_side_effects=True, vmem_limit_bytes=58 * 1024 * 1024
        ),
    )(*operands)
    return result[0], result[1]


def halves(a):
    hi = a.astype(jnp.bfloat16)
    return hi, (a - hi.astype(jnp.float32)).astype(jnp.bfloat16)


def thirds(a):
    hi = a.astype(jnp.bfloat16)
    rest = a - hi.astype(jnp.float32)
    mid = rest.astype(jnp.bfloat16)
    return hi, mid, (rest - mid.astype(jnp.float32)).astype(jnp.bfloat16)


def column(row, first, count):
    lanes = row.shape[1]
    spot = lax.broadcasted_iota(jnp.int32, (count, lanes), 0) + first
    hit = lax.broadcasted_iota(jnp.int32, (count, lanes), 1) == spot
    return jnp.sum(jnp.where(hit, jnp.broadcast_to(row, (count, lanes)), 0.0), axis=1, keepdims=True)


def one_kernel(n, tp, *refs):
    names, refs = refs[0], refs[1:]
    r = dict(zip(names, refs))
    f32, bf16 = jnp.float32, jnp.bfloat16
    c, t = lax.axis_index("ctx"), lax.axis_index("tp")
    total = n * tp
    me = c * tp + t
    chips = n // 2
    z_n = chips // 2
    k, p = c % 2, c // 2
    x, z = p % 2, p // 2

    def dev(z_, x_, k_):
        return ((z_ * 2 + x_) * 2 + k_, t)

    core_peer, x_peer, y_peer = dev(z, x, 1 - k), dev(z, 1 - x, k), (c, 1 - t)
    T, C = r["x"].shape
    W = C // 2
    S = r["s"].shape[2] // 2
    G = S // STATE
    GW = W // G
    H = r["d"].shape[0]
    HC = H // 2
    Tc = 2 * T
    r8 = r["scored"].shape[0]
    RC = 2 * r8
    R = chips * RC
    taps = r["tx"].shape[0]
    blk = r["ow"].shape[1] // tp
    D = n * tp * blk
    V = r["hw"].shape[1]
    per = n // tp

    barrier = pltpu.get_barrier_semaphore()

    plane_peers = [
        (((z * 2 + (x + a) % 2) * 2 + (k + b) % 2), (t + e) % tp)
        for a in range(2) for b in range(2) for e in range(tp) if a + b + e
    ]
    z_peers = [dev((z + d) % z_n, x, k) for d in range(1, z_n)]

    def greet_one(sem, device):
        pl.semaphore_signal(sem, inc=1, device_id=device, device_id_type=MESH)

    for device in plane_peers + z_peers:
        greet_one(barrier, device)
    sends_up = (x == 1) & (k == 1) & (z < z_n - 1)

    @pl.when((x == 0) & (z > 0))
    def _():
        greet_one(barrier, dev(z - 1, 1, 1))

    def lanes(a, size):
        return pl.ds(pl.multiple_of(a * size, 128), size)

    local = {}

    def fetch(name, src, dst):
        copy = pltpu.make_async_copy(src, dst, r["own"].at[len(local)])
        local[name] = copy
        copy.start()

    def arrived(ref, sem):
        pltpu.make_async_copy(ref, ref, sem).wait()

    sent = []

    def push(copy, when=None):
        sent.append((copy, when))
        if when is None:
            copy.start()
        else:
            pl.when(when)(copy.start)

    fetch("resets", r["resets"], r["resv"])
    fetch("scored", r["scored"], r["spot"])
    fetch("g", r["g"], r["gv"])
    fetch("res", r["res"], r["rv"])
    fetch("s", r["s"].at[:, :, lanes(k, S)], r["sc"].at[k])
    fetch("ts", r["ts"].at[:, :, lanes(k, S)], r["tsv"])
    half_heads = pl.ds(pl.multiple_of(k * HC, 8), HC)
    fetch("d", r["d"].at[half_heads], r["dc"].at[k])
    fetch("rate", r["rate"], r["ratev"])
    fetch("x", r["x"].at[:, lanes(k, W)], r["xc"].at[k])
    fetch("tx", r["tx"].at[:, lanes(k, W)], r["txv"])
    fetch("skip", r["skip"], r["skipv"])
    fetch("gain", r["gain"].at[:, lanes(k, W)], r["gainv"])
    fetch("fg", r["fg"], r["fgv"])
    fetch("tgt", r["tgt"], r["tgtv"])
    fetch("pol", r["pol"], r["polv"])
    fetch("ow", r["ow"], r["oww"])

    first = p == 0

    @pl.when(first)
    def _():
        r["xh"][...] = jnp.zeros(r["xh"].shape, bf16)
        r["sh"][...] = jnp.zeros(r["sh"].shape, bf16)
        r["mh"][...] = jnp.zeros(r["mh"].shape, f32)

    local["resets"].wait()
    local["scored"].wait()
    lane8 = lax.broadcasted_iota(jnp.int32, (8, T), 1)
    row8 = lax.broadcasted_iota(jnp.int32, (8, T), 0)
    places = jnp.zeros((8, T), f32)
    for i in range(r8):
        places = jnp.where(lane8 == i, (r["spot"][i] - c * T).astype(f32), places)
    flags_here = jnp.broadcast_to(r["resv"][...].astype(f32), (8, T))
    r["meta"][...] = jnp.where(row8 == 0, flags_here, places)

    local["g"].wait()
    local["res"].wait()
    own_pick = jnp.where(
        column(r["meta"][1:2], 0, r8) == lax.broadcasted_iota(jnp.int32, (r8, T), 1).astype(f32),
        1.0, 0.0,
    ).astype(bf16)
    r["gc"][k] = jnp.dot(
        own_pick, r["gv"][:, lanes(k, W)], preferred_element_type=f32
    ).astype(bf16)
    r["gsend"][...] = jnp.dot(
        own_pick, r["gv"][:, lanes(1 - k, W)], preferred_element_type=f32
    ).astype(bf16)
    res_rows = jnp.dot(own_pick, r["rv"][...], preferred_element_type=f32).astype(bf16)

    for j in range(per * tp):
        r["rsend"][j] = res_rows[:, j * blk : (j + 1) * blk]

    pl.semaphore_wait(barrier, len(plane_peers) + len(z_peers) + jnp.where(sends_up, 2, 0))
    for device in plane_peers:
        greet_one(r["ready"], device)

    send, recv = r["core_send"], r["core_recv"]
    edge_send, edge_recv = r["edge_send"], r["edge_recv"]
    swap = (
        (r["s"].at[:, :, lanes(1 - k, S)], r["sc"].at[k]),
        (r["meta"], r["mc"].at[k]),
        (r["d"].at[pl.ds(pl.multiple_of((1 - k) * HC, 8), HC)], r["dc"].at[k]),
        (r["x"].at[:, lanes(1 - k, W)], r["xc"].at[k]),
    )
    for i, (a, b) in enumerate(swap):
        push(remote(a, b, send.at[i], recv.at[i], core_peer))
    last_core = (k == 1) & (p < chips - 1)
    tail = pl.ds(T - EDGE, EDGE)
    nxt = jnp.minimum(p + 1, chips - 1)
    for j in range(2):
        triple = (
            (r["s"].at[:, tail, j * S : (j + 1) * S], r["sh"]),
            (r["meta"], r["mh"]),
            (r["x"].at[tail, j * W : (j + 1) * W], r["xh"]),
        )
        for i, (a, b) in enumerate(triple):
            push(remote(a, b, edge_send.at[j, i], edge_recv.at[i], (nxt * 2 + j, t)), last_core)
    r["mc"][k] = r["meta"][...]

    def from_core(i, buf):
        arrived(buf.at[1 - k], recv.at[i])

    def from_edge(i, ref):
        @pl.when(jnp.logical_not(first))
        def _():
            arrived(ref, edge_recv.at[i])

    from_core(1, r["mc"])
    spots = jnp.concatenate(
        [column(r["mc"][j][1:2], 0, r8) + j * T for j in range(2)], axis=0
    ).astype(jnp.int32)
    lane_t = lax.broadcasted_iota(jnp.int32, (RC, Tc), 1)
    pick_f = jnp.where(spots == lane_t, 1.0, 0.0)
    pick = pick_f.astype(bf16)

    chip_flags = jnp.concatenate([r["mc"][0], r["mc"][1]], axis=1)
    local["d"].wait()
    local["rate"].wait()
    from_core(2, r["dc"])
    steps = jnp.concatenate([r["dc"][0], r["dc"][1]], axis=1)
    lower = jnp.where(
        lax.broadcasted_iota(jnp.int32, (Tc, Tc), 0) <= lax.broadcasted_iota(jnp.int32, (Tc, Tc), 1),
        1.0, 0.0,
    ).astype(bf16)
    rate_col = column(r["ratev"][...], k * HC, HC)
    runs = jnp.concatenate([-rate_col * steps, chip_flags], axis=0)
    sums3 = jnp.dot(jnp.concatenate(thirds(runs), axis=0), lower, preferred_element_type=f32)
    count = HC + 8
    sums = sums3[:count] + sums3[count : 2 * count] + sums3[2 * count :]
    cumulated = sums[:HC]
    segment = sums[HC : HC + 1]
    last = cumulated[:, Tc - 1 : Tc]
    last_seg = segment[:, Tc - 1 : Tc]
    plane = jnp.broadcast_to(jnp.exp(last) * jnp.where(last_seg == 0.0, 1.0, 0.0), (HC, 128))
    r["mine_pd"][...] = jnp.concatenate([plane.T[:8], jnp.zeros((8, 128 - HC), f32)], axis=1)
    pl.semaphore_wait(r["ready"], len(plane_peers))
    for d in range(1, chips):
        remote(
            r["mine_pd"], r["all_pd"].at[p], r["pd_send"], r["pd_recv"],
            (((p + d) % chips) * 2 + k, t),
        ).start()
    r["all_pd"][p] = r["mine_pd"][...]
    at_rows = lax.dot_general(
        pick_f, sums, (((1,), (1,)), ((), ())), precision=precise, preferred_element_type=f32
    )
    row_cum = at_rows[:, :HC]
    row_seg = at_rows[:, HC : HC + 1]
    to_end = jnp.exp(last - cumulated) * jnp.where(segment == last_seg, 1.0, 0.0) * steps
    r["te"][...] = jnp.concatenate(halves(to_end.T), axis=1)
    push(remote(r["gsend"], r["gc"].at[k], send.at[4], recv.at[4], core_peer))
    def res_copy(j, to_t):
        i = j * tp + to_t
        return remote(
            r["rsend"].at[i], r["ro"].at[c], r["res_send"], r["res_recv"],
            (t * per + j, to_t),
        )

    for j in range(per):
        for to_t in range(tp):
            mine = (t * per + j == c) & (to_t == t)
            pl.when(jnp.logical_not(mine))(res_copy(j, to_t).start)

            @pl.when(mine)
            def _():
                pltpu.make_async_copy(
                    r["rsend"].at[j * tp + to_t], r["ro"].at[c], r["res_recv"]
                ).start()

    from_edge(1, r["mh"])
    flags = jnp.concatenate([r["mh"][...], chip_flags], axis=1)
    clear = 1.0 - flags
    keeping = jnp.ones((8, 3 * T), f32)
    columns = [keeping]
    for off in range(1, taps):
        shifted = clear if off == 1 else pltpu.roll(clear, off - 1, 1)
        keeping = keeping * shifted
        columns.append(keeping)
    keep_rows = jnp.zeros((8, 3 * T), f32)
    row8w = lax.broadcasted_iota(jnp.int32, (8, 3 * T), 0)
    for off in range(taps):
        keep_rows = jnp.where(row8w == off, jnp.broadcast_to(columns[off][0:1], (8, 3 * T)), keep_rows)
    keep = keep_rows[:, T:].T
    for off in range(1, taps):
        r["kb"][off] = jnp.broadcast_to(keep[:, off : off + 1], (Tc, 128))
    wide_keep = [None] + [r["kb"].at[off] for off in range(1, taps)]

    def filtered(pad, kernel, start, size):
        width = pad.shape[1]
        acc = kernel[0:1] * pad[EDGE + start : EDGE + start + size, :]
        for off in range(1, taps):
            kept = wide_keep[off][start : start + size, :]
            kept = jnp.concatenate([kept] * (width // 128), axis=1)
            acc = acc + kept * (
                kernel[off : off + 1] * pad[EDGE - off + start : EDGE - off + start + size, :]
            )
        return jax.nn.silu(acc).astype(bf16)

    local["s"].wait()
    local["ts"].wait()
    from_core(0, r["sc"])
    from_edge(0, r["sh"])
    pad = r["pad"]
    band = 64
    for which, target in ((1, r["reads"]), (0, r["writes"])):
        for g in range(G):
            cols = slice(g * STATE, (g + 1) * STATE)
            pad_s = r["pad_s"]
            pad_s[:EDGE, :] = r["sh"][which, :, cols].astype(f32)
            for j in range(2):
                pad_s[EDGE + j * T : EDGE + (j + 1) * T, :] = r["sc"][j, which, :, cols].astype(f32)
            kernel = r["tsv"][which, :, cols]
            for b in range(Tc // band):
                target[b * band : (b + 1) * band, cols] = filtered(pad_s, kernel, b * band, band)
        if which == 1:
            r["mine_r"][...] = jnp.dot(
                pick, r["reads"][...], preferred_element_type=f32
            ).astype(bf16)
            for d in range(1, chips):
                remote(
                    r["mine_r"], r["all_r"].at[p], r["r_send"], r["r_recv"],
                    (((p + d) % chips) * 2 + k, t),
                ).start()
            r["all_r"][p] = r["mine_r"][...]

    for g in range(G):
        r["wT"][g] = r["writes"][:, g * STATE : (g + 1) * STATE].astype(f32).T.astype(bf16)

    chunk = 256

    def spread_cols(j, size, offset):
        head = lax.broadcasted_iota(jnp.int32, (size, chunk), 0) % (size // 2)
        lane = lax.broadcasted_iota(jnp.int32, (size, chunk), 1)
        return jnp.where(head == offset + (j * chunk + lane) // HEAD_DIM, 1.0, 0.0).astype(bf16)

    local["x"].wait()
    local["tx"].wait()
    from_core(3, r["xc"])
    from_edge(2, r["xh"])

    def conv_step(j, carry):
        cols = lanes(j, chunk)
        pad[:EDGE, :] = r["xh"][:, cols].astype(f32)
        for i in range(2):
            pad[EDGE + i * T : EDGE + (i + 1) * T, :] = r["xc"][i, :, cols].astype(f32)
        kernel = r["txv"][:, cols]
        for b in range(Tc // band):
            r["values"][b * band : (b + 1) * band, cols] = filtered(pad, kernel, b * band, band)
        grown = jnp.dot(r["te"][...], spread_cols(j, 2 * HC, 0), preferred_element_type=f32)
        hi, lo = halves(r["values"][:, cols].astype(f32) * grown)
        w_t = r["wT"][(j * chunk) // GW]
        state = jnp.dot(w_t, hi, preferred_element_type=f32) + jnp.dot(
            w_t, lo, preferred_element_type=f32
        )
        s_hi, s_lo = halves(state)
        r["S2"][:STATE, cols] = s_hi
        r["S2"][STATE:, cols] = s_lo
        return carry

    lax.fori_loop(0, W // chunk, conv_step, 0)

    fetch("hw", r["hw"], r["hww"])

    others = pl.ds(0, chips - 1)
    arrived(r["all_r"].at[others], r["r_recv"])
    arrived(r["all_pd"].at[others], r["pd_recv"])
    arrived(r["all_r"].at[others], r["r_send"])
    arrived(r["all_pd"].at[others], r["pd_send"])
    for g in range(G):
        rows_g = r["all_r"][:, :, g * STATE : (g + 1) * STATE].reshape(R, STATE)
        r["rr"][g, :, :STATE] = rows_g
        r["rr"][g, :, STATE:] = rows_g
    run_w = jnp.ones((1, 128), f32)
    weights = []
    for d in range(chips):
        weights.append(jnp.broadcast_to(run_w, (RC, 128)))
        run_w = jnp.where(d > p, run_w * r["all_pd"][d][0:1], run_w)
    far = jnp.concatenate(weights, axis=0)[:, :HC]
    r["ww"][...] = jnp.concatenate(halves(far), axis=1)

    def y_step(j, carry):
        cols = lanes(j, chunk)
        y = jnp.dot(r["rr"][(j * chunk) // GW], r["S2"][:, cols], preferred_element_type=f32)
        grown = jnp.dot(r["ww"][...], spread_cols(j, 2 * HC, 0), preferred_element_type=f32)
        r["yf"][:, cols] = y * grown
        return carry

    lax.fori_loop(0, W // chunk, y_step, 0)

    def y_rows(zd, xd):
        return r["yf"][pl.ds(pl.multiple_of((zd * 2 + xd) * RC, 16), RC), :]

    def coded(a, wire, scale):
        most = jnp.max(jnp.abs(a), axis=1, keepdims=True)
        inverse = jnp.where(most > 0.0, LEVELS / jnp.maximum(most, TINY), 0.0)
        wire[...] = jnp.round(a * inverse).astype(jnp.int32).astype(jnp.int16)
        scale[...] = jnp.broadcast_to(most * (1.0 / LEVELS), (RC, 128))

    def decoded(wire, scale):
        return wire[...].astype(jnp.int32).astype(f32) * scale[:, :1]

    for zd in range(z_n - 1, -1, -1):
        goes = (zd > z) | ((zd == z) & (x == 0))

        @pl.when(goes)
        def _():
            coded(y_rows(zd, 1 - x), r["xsend"].at[zd], r["xsend_f"].at[zd])

        for i, (a, b) in enumerate(((r["xsend"], r["xr"]), (r["xsend_f"], r["xr_f"]))):
            push(
                remote(a.at[zd], b.at[zd], r["x_send"].at[i, zd], r["x_recv"].at[i, zd], x_peer),
                goes,
            )

    def from_x_peer(zd):
        for i, b in enumerate((r["xr"], r["xr_f"])):
            arrived(b.at[zd], r["x_recv"].at[i, zd])
        return decoded(r["xr"].at[zd], r["xr_f"].at[zd])

    mine_r = r["mine_r"][...]
    scores = [
        lax.dot_general(
            mine_r[:, g * STATE : (g + 1) * STATE], r["writes"][:, g * STATE : (g + 1) * STATE],
            (((1,), (1,)), ((), ())), preferred_element_type=f32,
        )
        for g in range(G)
    ]
    causal = (spots >= lane_t) & (row_seg == segment)
    quad = 4
    quad_w = quad * HEAD_DIM
    which_head = lax.broadcasted_iota(jnp.int32, (RC, quad_w), 1) // HEAD_DIM

    def within(q):
        mixes = []
        for i in range(quad):
            h = q * quad + i
            gaps = row_cum[:, h : h + 1] - cumulated[h : h + 1]
            decay = jnp.where(causal, jnp.exp(jnp.where(causal, gaps, 0.0)), 0.0)
            mixes.append(scores[h * HEAD_DIM // GW] * decay * steps[h : h + 1])
        both = jnp.concatenate(halves(jnp.concatenate(mixes, axis=0)), axis=0)
        span = slice(q * quad_w, (q + 1) * quad_w)
        product = jnp.dot(both, r["values"][:, span], preferred_element_type=f32)
        product = product[: quad * RC] + product[quad * RC :]
        out = product[:RC]
        for i in range(1, quad):
            out = jnp.where(which_head == i, product[i * RC : (i + 1) * RC], out)
        r["mixed"][:, span] = out

    quads = HC // quad
    for q in range(quads // 2):
        within(q)
    for zd in range(z_n - 1, 0, -1):
        goes = zd > z

        @pl.when(goes)
        def _():
            coded(y_rows(zd, x) + from_x_peer(zd), r["zsend"].at[zd], r["zsend_f"].at[zd])

        for i, (a, b) in enumerate(((r["zsend"], r["zr"]), (r["zsend_f"], r["zr_f"]))):
            push(
                remote(a.at[zd], b.at[z], r["z_send"].at[i, zd], r["z_recv"].at[i, z], dev(zd, x, k)),
                goes,
            )
    for q in range(quads // 2, quads):
        within(q)

    local["skip"].wait()
    local["gain"].wait()
    from_start = jnp.exp(row_cum) * jnp.where(row_seg == 0.0, 1.0, 0.0)
    starts = jnp.concatenate(halves(from_start), axis=1)
    skip3 = jnp.concatenate(
        [jnp.broadcast_to(a, (8, H)) for a in thirds(jnp.broadcast_to(r["skipv"][...], (8, H)))], axis=0
    )
    from_core(4, r["gc"])
    gate = jnp.concatenate([r["gc"][0].astype(f32), r["gc"][1].astype(f32)], axis=0)

    def widen_step(j, carry):
        cols = lanes(j, chunk)
        own_values = jnp.dot(pick, r["values"][:, cols], preferred_element_type=f32)
        head = lax.broadcasted_iota(jnp.int32, (H, chunk), 0)
        lane = lax.broadcasted_iota(jnp.int32, (H, chunk), 1)
        all_heads = jnp.where(head == k * HC + (j * chunk + lane) // HEAD_DIM, 1.0, 0.0).astype(bf16)
        grown = jnp.dot(skip3, all_heads, preferred_element_type=f32)
        skip_row = grown[0:1] + grown[8:9] + grown[16:17]
        r["mixed"][:, cols] = r["mixed"][:, cols] + skip_row * own_values
        r["starts"][:, cols] = jnp.dot(starts, spread_cols(j, 2 * HC, 0), preferred_element_type=f32)
        return carry

    lax.fori_loop(0, W // chunk, widen_step, 0)
    gate = jax.nn.silu(gate)

    carried = r["carried"]
    carried[...] = jnp.zeros((RC, W), f32)

    @pl.when(x == 1)
    def _():
        carried[...] = from_x_peer(z)

    for zs in range(z_n - 1):
        @pl.when(zs < z)
        def _():
            for i, b in enumerate((r["zr"], r["zr_f"])):
                arrived(b.at[zs], r["z_recv"].at[i, zs])
            carried[...] = carried[...] + decoded(r["zr"].at[zs], r["zr_f"].at[zs])

    gated = (r["mixed"][...] + carried[...] * r["starts"][...]) * gate
    for g in range(G):
        span = slice(g * GW, (g + 1) * GW)
        part = gated[:, span]
        scale = lax.rsqrt(jnp.mean(part * part, axis=1, keepdims=True) + epsilon)
        r["normed"][:, span] = (part * scale * r["gainv"][:, span]).astype(bf16)

    nrm = r["nrm"]
    mine = r["normed"]
    z_recv, x_recv, c_recv = r["gather1"]
    g_send = r["g_send"]

    def slot(z_, x_, k_):
        return nrm.at[k_ * chips + z_ * 2 + x_]

    def go1(a, b, sem, device):
        remote(a, b, g_send.at[0], sem, device).start()

    home = slot(z, x, k)
    for d in range(1, z_n):
        go1(mine, home, z_recv.at[z], dev((z + d) % z_n, x, k))
    go1(mine, home, x_recv.at[z], x_peer)
    go1(mine, home, c_recv.at[0, z], core_peer)
    nrm[k * chips + p] = mine[...]
    for zs in range(z_n):
        @pl.when(zs != z)
        def _():
            here = slot(zs, x, k)
            arrived(here, z_recv.at[zs])
            go1(here, here, x_recv.at[zs], x_peer)
            go1(here, here, c_recv.at[0, zs], core_peer)

    for zs in range(z_n):
        here = slot(zs, 1 - x, k)
        arrived(here, x_recv.at[zs])
        go1(here, here, c_recv.at[1, zs], core_peer)
    for zs in range(z_n):
        for e, x_ in ((0, x), (1, 1 - x)):
            arrived(slot(zs, x_, 1 - k), c_recv.at[e, zs])
    arrived(nrm.at[pl.ds(0, 2 * chips - 1)], g_send.at[0])
    local["ow"].wait()
    partial = jnp.zeros((R, tp * blk), f32)
    for j in range(2):
        partial = partial + jnp.dot(
            nrm[j * chips : (j + 1) * chips].reshape(R, W), r["oww"][j * W : (j + 1) * W, :], preferred_element_type=f32
        )
    for j in range(tp):
        r["pt"][j] = partial[:, j * blk : (j + 1) * blk]
    push(remote(r["pt"].at[1 - t], r["pr"], r["t_send"], r["t_recv"], y_peer))
    arrived(r["ro"], r["res_recv"])
    in_half = (c >= t * per) & (c < (t + 1) * per)

    @pl.when(in_half)
    def _():
        arrived(r["rsend"].at[pl.ds(0, n - 1)], r["res_send"])

    @pl.when(jnp.logical_not(in_half))
    def _():
        arrived(r["rsend"], r["res_send"])

    res_all = r["ro"][...].astype(f32).reshape(R, blk)
    arrived(r["pr"], r["t_recv"])
    hid = r["hid"]
    hid_mine = (res_all + (r["pt"][t] + r["pr"][...])).astype(bf16)
    hid[me] = hid_mine
    wide_mine = hid_mine.astype(f32)
    sq_mine = jnp.sum(wide_mine * wide_mine, axis=1, keepdims=True)
    sq, sq_z, sq_p = r["sq"], r["sq_z"], r["sq_p"]
    sq[0] = jnp.broadcast_to(sq_mine, (R, 128)).T[:1]

    z_recv, a_recv, b_recv, c_recv = r["gather2"]
    even = k == 0
    a0, b0 = jnp.where(even, t, x), jnp.where(even, x, t)

    def place(z_, a_, b_, k_):
        y_, x_ = jnp.where(k_ == 0, a_, b_), jnp.where(k_ == 0, b_, a_)
        return hid.at[((z_ * 2 + x_) * 2 + k_) * tp + y_]

    a_peer = (jnp.where(even, c, x_peer[0]), jnp.where(even, 1 - t, t))
    b_peer = (jnp.where(even, x_peer[0], c), jnp.where(even, t, 1 - t))

    def go2(here, sem, device):
        remote(here, here, g_send.at[1], sem, device).start()

    def to_a(here, d):
        go2(here, a_recv.at[d], a_peer)

    diag = (x_peer[0], 1 - t)

    def to_diag(here, d):
        go2(here, b_recv.at[1, d], diag)

    def to_b(here, e, d):
        go2(here, b_recv.at[e, d], b_peer)

    def to_core(here, e, d):
        go2(here, c_recv.at[e, d], core_peer)

    for d in range(1, z_n):
        remote(
            sq.at[0], sq_z.at[z], r["sq_send"].at[0], r["sq_recv"].at[0], dev((z + d) % z_n, x, k)
        ).start()
    sq_z[z] = sq[0]
    home = place(z, a0, b0, k)
    for d in range(1, z_n):
        go2(home, z_recv.at[d], dev((z + d) % z_n, x, k))
    to_diag(home, 0)
    to_a(home, 0)
    to_b(home, 0, 0)
    to_core(home, 0, 0)
    arrived(sq_z.at[pl.ds(0, z_n - 1)], r["sq_recv"].at[0])
    column_sum = sq_z[0]
    for zs in range(1, z_n):
        column_sum = column_sum + sq_z[zs]
    sq[1] = column_sum
    in_plane = (x * 2 + k) * tp + t
    for device in plane_peers:
        remote(
            sq.at[1], sq_p.at[in_plane], r["sq_send"].at[1], r["sq_recv"].at[1], device
        ).start()
    sq_p[in_plane] = column_sum
    for d in range(1, z_n):
        here = place((z + z_n - d) % z_n, a0, b0, k)
        arrived(here, z_recv.at[d])
        to_diag(here, d)
        to_a(here, d)
        to_b(here, 0, d)
        to_core(here, 0, d)
    arrived(sq_p.at[pl.ds(0, len(plane_peers))], r["sq_recv"].at[1])
    squares = sq_p[0]
    for i in range(1, 4 * tp):
        squares = squares + sq_p[i]
    inverse_row = lax.rsqrt(squares / D + epsilon)
    inverse = jnp.broadcast_to(inverse_row, (128, R)).T
    local["fg"].wait()
    local["hw"].wait()
    logit, feat = r["logit"], r["feat"]
    oa, ob = jnp.where(even, x, t), jnp.where(even, t, x)
    tile = min(256, V)
    group = 4 * tp
    depth = group * blk

    def block(d):
        from_z = (z + z_n - d) % z_n
        for e, (a_, b_) in enumerate(((oa, ob), (1 - oa, ob), (oa, 1 - ob), (1 - oa, 1 - ob))):
            arrived(place(from_z, a_, b_, 1 - k), c_recv.at[e, d])
        for i in range(group):
            gain = r["fgv"][:, lanes(from_z * group + i, blk)]
            feat[:, i * blk : (i + 1) * blk] = (
                hid[from_z * group + i].astype(f32) * inverse[:, :blk] * gain
            ).astype(bf16)
        rows = pl.ds(pl.multiple_of(from_z * depth, depth), depth)

        def one_tile(i, carry):
            cols = lanes(i, tile)
            product = jnp.dot(feat[...], r["hww"][rows, cols], preferred_element_type=f32)
            logit[:, cols] = product if d == 0 else logit[:, cols] + product
            return carry

        lax.fori_loop(0, V // tile, one_tile, 0)

    for d in range(z_n):
        from_z = (z + z_n - d) % z_n
        here = place(from_z, 1 - a0, b0, k)
        arrived(here, a_recv.at[d])
        to_core(here, 1, d)
        here = place(from_z, a0, 1 - b0, k)
        arrived(here, b_recv.at[0, d])
        to_core(here, 2, d)
        here = place(from_z, 1 - a0, 1 - b0, k)
        arrived(here, b_recv.at[1, d])
        to_core(here, 3, d)
        if d:
            block(d - 1)
    block(z_n - 1)
    values = logit[...]
    top = jnp.max(values, axis=1, keepdims=True)
    added = jnp.sum(jnp.exp(values - top), axis=1, keepdims=True)
    local["tgt"].wait()
    local["pol"].wait()
    target = column(r["tgtv"][...].astype(f32), 0, R).astype(jnp.int32) - me * V
    hit = jnp.sum(
        jnp.where(lax.broadcasted_iota(jnp.int32, values.shape, 1) == target, values, 0.0),
        axis=1, keepdims=True,
    )
    lane = lax.broadcasted_iota(jnp.int32, (R, 128), 1)
    packed = jnp.where(lane == 0, top, jnp.where(lane == 1, added, jnp.where(lane == 2, hit, 0.0)))
    turned = packed.T[:4]
    stat, every = r["stat"], r["every"]
    stat[...] = turned
    st_send, st_recv = r["st_send"], r["st_recv"]

    def device(a):
        return (a // tp, a % tp)

    def go(d, carry):
        remote(stat, every.at[me], st_send, st_recv, device((me + d) % total)).start()
        return carry

    lax.fori_loop(1, total, go, 0)
    every[me] = turned

    for copy, when in sent:
        if when is None:
            copy.wait_send()
        else:
            pl.when(when)(copy.wait_send)
    arrived(hid.at[pl.ds(0, total - 1)], g_send.at[1])
    arrived(sq_z.at[pl.ds(0, z_n - 1)], r["sq_send"].at[0])
    arrived(sq_p.at[pl.ds(0, len(plane_peers))], r["sq_send"].at[1])
    rest = every.at[pl.ds(0, total - 1)]
    arrived(rest, st_send)
    arrived(rest, st_recv)
    found = every[...]
    tops = found[:, 0, :]
    row_top = jnp.max(tops, axis=0, keepdims=True)
    full = jnp.sum(found[:, 1, :] * jnp.exp(tops - row_top), axis=0, keepdims=True)
    picked = jnp.sum(found[:, 2, :], axis=0, keepdims=True)
    log_prob = picked - row_top - jnp.log(full)
    r["out"][0:1, :] = log_prob
    r["out"][1:2, :] = 0.5 * jnp.square(log_prob - r["polv"][...])


def fused(n, tp, x, g, s, d, resets, rate, skip, tx, ts, gain, ow, res, fg, hw, scored, tgt, pol):
    f32, bf16, i32, i16 = jnp.float32, jnp.bfloat16, jnp.int32, jnp.int16
    dma, vmem = pltpu.SemaphoreType.DMA, pltpu.VMEM
    chips = n // 2
    z_n = chips // 2
    T, C = x.shape
    W, Tc = C // 2, 2 * T
    S = s.shape[2] // 2
    G = S // STATE
    H = d.shape[0]
    HC = H // 2
    r8 = scored.shape[0]
    RC = 2 * r8
    R = chips * RC
    blk = ow.shape[1] // tp
    taps = tx.shape[0]
    total = n * tp
    inputs = dict(
        x=x, g=g, s=s, d=d, resets=resets[None], rate=rate[None], skip=skip[None], tx=tx, ts=ts,
        gain=gain[None], ow=ow, res=res, fg=fg[None], hw=hw, scored=scored, tgt=tgt[None], pol=pol[None],
    )
    scratch = dict(
        resv=vmem((1, T), i32), spot=pltpu.SMEM((r8,), i32), meta=vmem((8, T), f32),
        xc=vmem((2, T, W), bf16), xh=vmem((EDGE, W), bf16),
        sc=vmem((2, 2, T, S), bf16), sh=vmem((2, EDGE, S), bf16),
        dc=vmem((2, HC, T), f32), mc=vmem((2, 8, T), f32), mh=vmem((8, T), f32),
        gv=vmem(g.shape, bf16), rv=vmem(res.shape, bf16),
        gc=vmem((2, r8, W), bf16), gsend=vmem((r8, W), bf16),
        rsend=vmem((n, r8, blk), bf16), ro=vmem((n, r8, blk), bf16),
        txv=vmem((taps, W), f32), tsv=vmem((2, taps, S), f32), gainv=vmem((1, W), f32),
        ratev=vmem((1, H), f32), skipv=vmem((1, H), f32), fgv=vmem((1, n * tp * blk), f32),
        tgtv=vmem((1, R), i32), polv=vmem((1, R), f32),
        pad=vmem((EDGE + Tc, 256), f32), pad_s=vmem((EDGE + Tc, STATE), f32),
        kb=vmem((taps, Tc, 128), f32),
        reads=vmem((Tc, S), bf16), writes=vmem((Tc, S), bf16),
        mine_r=vmem((RC, S), bf16), all_r=vmem((chips, RC, S), bf16),
        mine_pd=vmem((8, 128), f32), all_pd=vmem((chips, 8, 128), f32),
        te=vmem((Tc, 2 * HC), bf16), wT=vmem((G, STATE, Tc), bf16),
        values=vmem((Tc, W), bf16), S2=vmem((2 * STATE, W), bf16),
        rr=vmem((G, R, 2 * STATE), bf16), ww=vmem((R, 2 * HC), bf16), yf=vmem((R, W), f32),
        xsend=vmem((z_n, RC, W), i16), xr=vmem((z_n, RC, W), i16),
        zsend=vmem((z_n, RC, W), i16), zr=vmem((z_n, RC, W), i16),
        xsend_f=vmem((z_n, RC, 128), f32), xr_f=vmem((z_n, RC, 128), f32),
        zsend_f=vmem((z_n, RC, 128), f32), zr_f=vmem((z_n, RC, 128), f32),
        mixed=vmem((RC, W), f32), starts=vmem((RC, W), f32), carried=vmem((RC, W), f32),
        normed=vmem((RC, W), bf16), nrm=vmem((2 * chips, RC, W), bf16),
        pt=vmem((tp, R, blk), f32), pr=vmem((R, blk), f32),
        hid=vmem((total, R, blk), bf16), feat=vmem((R, 4 * tp * blk), bf16), sq=vmem((2, 1, R), f32),
        sq_z=vmem((z_n, 1, R), f32), sq_p=vmem((4 * tp, 1, R), f32),
        logit=vmem((R, hw.shape[1]), f32), stat=vmem((4, R), f32), every=vmem((total, 4, R), f32),
        oww=vmem(ow.shape, bf16), hww=vmem(hw.shape, bf16),
        own=dma((18,)), core_send=dma((5,)), core_recv=dma((5,)),
        edge_send=dma((2, 3)), edge_recv=dma((3,)),
        r_send=dma(()), r_recv=dma(()), pd_send=dma(()), pd_recv=dma(()),
        x_send=dma((2, z_n)), x_recv=dma((2, z_n)), z_send=dma((2, z_n)), z_recv=dma((2, z_n)),
        res_send=dma(()), res_recv=dma(()), g_send=dma((2,)), sq_send=dma((2,)), sq_recv=dma((2,)), t_send=dma(()), t_recv=dma(()),
        st_send=dma(()), st_recv=dma(()), ready=pltpu.SemaphoreType.REGULAR,
    )
    many = [("gather1", [dma((z_n,))] * 2 + [dma((2, z_n))])]
    many.append(("gather2", [dma((z_n,))] * 2 + [dma((2, z_n)), dma((4, z_n))]))
    names = list(inputs) + ["out"] + list(scratch)
    groups = [(name, len(sems)) for name, sems in many]
    extra = [sem for _, sems in many for sem in sems]

    def run(*refs):
        plain, rest = list(refs[: len(names)]), list(refs[len(names) :])
        for _, size in groups:
            plain.append(tuple(rest[:size]))
            rest = rest[size:]
        one_kernel(n, tp, names + [name for name, _ in groups], *plain)

    both = pl.pallas_call(
        run,
        out_shape=jax.ShapeDtypeStruct((2, R), f32),
        in_specs=[ANY] * len(inputs),
        out_specs=VMEM,
        scratch_shapes=list(scratch.values()) + extra,
        compiler_params=pltpu.CompilerParams(
            collective_id=5, has_side_effects=True, vmem_limit_bytes=58 * 1024 * 1024
        ),
    )(*inputs.values())
    return both[0], both[1]


def body(
    inner_input,
    gate_input,
    state_inputs,
    step_size,
    resets,
    decay_rate,
    skip_gain,
    conv_inner,
    conv_state,
    norm_gain,
    out_weight,
    residual,
    final_gain,
    head_weight,
    scored,
    targets,
    policy_logprob,
):
    f32 = jnp.float32
    n, tp = lax.axis_size("ctx"), lax.axis_size("tp")
    c, t = lax.axis_index("ctx"), lax.axis_index("tp")
    groups_here, blk = state_inputs.shape[2] // STATE, out_weight.shape[1] // tp
    if n % 4 == 0 and tp == 2 and groups_here % 2 == 0 and blk == 128:
        return fused(
            n, tp, inner_input, gate_input, state_inputs, step_size, resets, decay_rate, skip_gain,
            conv_inner, conv_state, norm_gain, out_weight, residual, final_gain, head_weight,
            scored, targets, policy_logprob,
        )
    taps = conv_inner.shape[0]
    rows_here = inner_input.shape[0]
    q_count = state_inputs.shape[2] // STATE
    z_count = n // q_count
    z, q = c // q_count, c % q_count
    picked_rows = scored.shape[0]
    local_rows = scored - c * rows_here
    here = jnp.arange(rows_here, dtype=jnp.int32)
    pick = (local_rows[:, None] == here[None, :]).astype(jnp.bfloat16)
    gate_rows = jnp.dot(pick, gate_input, preferred_element_type=f32).astype(jnp.bfloat16)
    res_rows = jnp.dot(pick, residual, preferred_element_type=f32).astype(jnp.bfloat16)
    meta = jnp.zeros((8, rows_here), f32)
    meta = meta.at[0].set(resets.astype(f32))
    meta = meta.at[1, :picked_rows].set(local_rows.astype(f32))
    xs, ss, ds, gs, ms, x_edge, s_edge, m_edge, res_all = spread(
        n, tp, q_count, inner_input, state_inputs, step_size, gate_rows, meta, res_rows
    )
    tokens = q_count * rows_here
    width = xs.shape[2]
    heads = ds.shape[1]
    rows = q_count * picked_rows
    gate = gs.reshape(rows, width)
    flags = ms[:, 0].reshape(tokens)
    spots = ms[:, 1, :picked_rows] + (jnp.arange(q_count) * rows_here).astype(f32)[:, None]
    spots = spots.reshape(rows, 1).astype(jnp.int32)
    margin = taps - 1
    f_tail = jnp.where(z > 0, m_edge[0, rows_here - margin :], 0.0)
    clear = 1.0 - jnp.concatenate([f_tail, flags])
    keeping = [jnp.ones((tokens,), f32)]
    for offset in range(1, taps):
        keeping.append(keeping[-1] * clear[margin - offset + 1 : margin - offset + 1 + tokens])
    keeps = jnp.pad(jnp.stack(keeping), ((0, -taps % 8), (0, 0)))
    normed = middle(
        xs, x_edge, ss, s_edge, keeps, ds, jnp.broadcast_to(flags[None], (8, tokens)), spots, gate,
        conv_inner, conv_state, decay_rate.reshape(q_count, heads, 1),
        skip_gain.reshape(q_count, 1, heads), norm_gain[None], q_count, z_count,
    )
    res = res_all.reshape(z_count * rows, -1)
    return tail(
        normed, out_weight, head_weight, res, final_gain, targets, policy_logprob,
        n, tp, q_count, z_count,
    )


def solution(mesh):
    return jax.shard_map(
        body,
        mesh=mesh,
        in_specs=(
            P("ctx", "tp"),
            P("ctx", "tp"),
            P(None, "ctx", "tp"),
            P("tp", "ctx"),
            P("ctx"),
            P("tp"),
            P("tp"),
            P(None, "tp"),
            P(None, None, "tp"),
            P("tp"),
            P("tp", "ctx"),
            P("ctx", "tp"),
            P(),
            P(None, ("ctx", "tp")),
            P("ctx"),
            P(),
            P(),
        ),
        out_specs=(P(), P()),
        check_vma=False,
    )
```

```python
import functools
import jax
import jax.numpy as jnp
from jax import lax
from jax.experimental import pallas as pl
from jax.experimental.pallas import tpu as pltpu
from jax.sharding import PartitionSpec as P

HEAD_DIM = 64
STATE = 128
EDGE = 16
LEVELS = 32767.0
TINY = 1e-30

epsilon = 1e-05
precise = lax.Precision.HIGHEST
MESH = pl.DeviceIdType.MESH
VMEM = pl.BlockSpec(memory_space=pltpu.VMEM)
ANY = pl.BlockSpec(memory_space=pl.ANY)


def remote(src, dst, send, recv, device):
    return pltpu.make_async_remote_copy(
        src_ref=src, dst_ref=dst, send_sem=send, recv_sem=recv, device_id=device, device_id_type=MESH
    )


def greet(devices):
    barrier = pltpu.get_barrier_semaphore()
    for device in devices:
        pl.semaphore_signal(barrier, inc=1, device_id=device, device_id_type=MESH)
    pl.semaphore_wait(barrier, len(devices))


def spread_kernel(n, tp, q_count, z_count, x_ref, s_ref, d_ref, g_ref, m_ref, r_ref,
                  xo, so, do, go, mo, xh, sh, mh, ro,
                  send, recv, own, edge_send, edge_recv, res_send, res_recv):
    c, t = lax.axis_index("ctx"), lax.axis_index("tp")
    z, q = c // q_count, c % q_count
    total = n * tp
    me = c * tp + t
    barrier = pltpu.get_barrier_semaphore()

    def hello(k, carry):
        other = (me + k) % total
        pl.semaphore_signal(
            barrier, inc=1, device_id=(other // tp, other % tp), device_id_type=MESH
        )
        return carry

    lax.fori_loop(1, total, hello, 0)
    pl.semaphore_wait(barrier, total - 1)
    width = xo.shape[2]
    heads = do.shape[1]
    rows = x_ref.shape[0]

    def cols(ref, k, size):
        return ref.at[:, pl.ds(pl.multiple_of(k * size, 128), size)]

    def parts(k):
        return (
            cols(x_ref, k, width),
            s_ref.at[:, :, pl.ds(pl.multiple_of(k * STATE, 128), STATE)],
            d_ref.at[pl.ds(pl.multiple_of(k * heads, 8), heads), :],
            cols(g_ref, k, width),
            m_ref,
        )

    def slots(k):
        return (xo.at[k], so.at[k], do.at[k], go.at[k], mo.at[k])

    started = []
    tail = pl.ds(rows - EDGE, EDGE)
    next_z = jnp.minimum(z + 1, z_count - 1)

    def edges(k, dst_c):
        wide = pl.ds(pl.multiple_of(k * width, 128), width)
        thin = pl.ds(pl.multiple_of(k * STATE, 128), STATE)
        triple = ((x_ref.at[tail, wide], xh), (s_ref.at[:, tail, thin], sh), (m_ref, mh))
        return [
            remote(a, b, edge_send.at[k, i], edge_recv.at[i], (dst_c, t))
            for i, (a, b) in enumerate(triple)
        ]

    sends_edge = (q == q_count - 1) & (z < z_count - 1)
    gets_edge = z > 0
    if z_count > 1:
        @pl.when(sends_edge)
        def _():
            for k in range(q_count):
                for copy in edges(k, (z + 1) * q_count + k):
                    copy.start()

    for d in range(1, q_count):
        k = (q + d) % q_count
        for i, (a, b) in enumerate(zip(parts(k), slots(q))):
            copy = remote(a, b, send.at[d - 1, i], recv.at[d - 1, i], (z * q_count + k, t))
            copy.start()
            started.append(copy)
    per = n // tp

    def res_copy(j, to_t):
        return remote(
            r_ref.at[j], ro.at[c],
            res_send.at[j * tp + to_t], res_recv.at[c], (t * per + j, to_t)
        )

    for j in range(per):
        for to_t in range(tp):
            mine = (t * per + j == c) & (to_t == t)

            @pl.when(jnp.logical_not(mine))
            def _():
                res_copy(j, to_t).start()

            @pl.when(mine)
            def _():
                pltpu.make_async_copy(r_ref.at[j], ro.at[c], res_recv.at[c]).start()
    locals_ = [
        pltpu.make_async_copy(a, b, own.at[i]) for i, (a, b) in enumerate(zip(parts(q), slots(q)))
    ]
    for copy in locals_:
        copy.start()
    for copy in locals_:
        copy.wait()
    for j in range(per):
        for to_t in range(tp):
            mine = (t * per + j == c) & (to_t == t)

            @pl.when(jnp.logical_not(mine))
            def _():
                res_copy(j, to_t).wait_send()
    for k in range(n):
        pltpu.make_async_copy(ro.at[k], ro.at[k], res_recv.at[k]).wait()
    for copy in started:
        copy.wait_send()
    for d in range(1, q_count):
        k = (q + q_count - d) % q_count
        for i, (a, b) in enumerate(zip(parts(q), slots(k))):
            remote(a, b, send.at[d - 1, i], recv.at[d - 1, i], (z * q_count + k, t)).wait_recv()
    if z_count > 1:
        @pl.when(sends_edge)
        def _():
            for k in range(q_count):
                for copy in edges(k, (z + 1) * q_count + k):
                    copy.wait_send()

        @pl.when(gets_edge)
        def _():
            for i, ref in enumerate((xh, sh, mh)):
                pltpu.make_async_copy(ref, ref, edge_recv.at[i]).wait()


def spread(n, tp, q_count, x, s, d, g, m, r):
    z_count = n // q_count
    rows, all_width = x.shape
    width = all_width // q_count
    heads = d.shape[0] // q_count
    block = r.shape[1] * tp // n
    r = r.reshape(r.shape[0], n // tp, block).transpose(1, 0, 2)
    shape = jax.ShapeDtypeStruct
    outs = (
        shape((q_count, rows, width), x.dtype),
        shape((q_count, 2, rows, STATE), s.dtype),
        shape((q_count, heads, rows), d.dtype),
        shape((q_count, g.shape[0], width), g.dtype),
        shape((q_count,) + m.shape, m.dtype),
        shape((EDGE, width), x.dtype),
        shape((2, EDGE, STATE), s.dtype),
        shape(m.shape, m.dtype),
        shape((n,) + r.shape[1:], r.dtype),
    )
    dma = pltpu.SemaphoreType.DMA
    peers = max(q_count - 1, 1)
    return pl.pallas_call(
        functools.partial(spread_kernel, n, tp, q_count, z_count),
        out_shape=outs,
        in_specs=[ANY, ANY, ANY, VMEM, VMEM, VMEM],
        out_specs=[VMEM] * len(outs),
        scratch_shapes=[
            dma((peers, 5)), dma((peers, 5)), dma((5,)), dma((q_count, 3)), dma((3,)),
            dma((n,)), dma((n,)),
        ],
        compiler_params=pltpu.CompilerParams(collective_id=0, has_side_effects=True),
    )(x, s, d, g, m, r)


def staged(kernel, skip, count, shapes):
    def run(*refs):
        ins, rest, held, sems = (
            refs[:count], refs[count : -len(shapes) - 1], refs[-len(shapes) - 1 : -1], refs[-1]
        )
        held = iter(held)
        views, copies = [], []
        for i, ref in enumerate(ins):
            if i in skip:
                views.append(ref)
                continue
            local = next(held)
            copy = pltpu.make_async_copy(ref, local, sems.at[len(copies)])
            copy.start()
            copies.append(copy)
            views.append(local)
        for copy in copies:
            copy.wait()
        kernel(*views, *rest)

    extra = [pltpu.VMEM(a.shape, a.dtype) for a in shapes]
    return run, extra + [pltpu.SemaphoreType.DMA((len(shapes),))]


def mid_kernel(q_count, z_count, x_ref, xe_ref, s_ref, se_ref, k_ref, d_ref, f_ref, spot_ref,
               gate_ref, tx_ref, ts_ref, rate_ref, skip_ref, gain_ref, out,
               pad_x, pad_s, values, writes, reads, mine_r, all_r, y, far, pd, far_pd, mixed, carried,
               r_send, r_recv, y_send, y_recv, p_send, p_recv):
    f32, bf16 = jnp.float32, jnp.bfloat16
    c, t = lax.axis_index("ctx"), lax.axis_index("tp")
    z, q = c // q_count, c % q_count
    barrier = pltpu.get_barrier_semaphore()

    def peer(d):
        return (((z + d) % z_count) * q_count + q, t)

    for d in range(1, z_count):
        pl.semaphore_signal(barrier, inc=1, device_id=peer(d), device_id_type=MESH)
    tokens, width = values.shape
    piece = tokens // q_count
    heads = d_ref.shape[1]
    rows = mine_r.shape[0]
    taps = tx_ref.shape[0]
    has_edge = (z > 0).astype(f32)
    keep = k_ref[...].T

    def filtered(pad, kernel, start, target):
        total = jnp.zeros((piece, pad.shape[1]), f32)
        for off in range(taps):
            total = total + (
                keep[start : start + piece, off : off + 1]
                * kernel[off : off + 1]
                * pad[EDGE - off + start : EDGE - off + start + piece, :]
            )
        target[start : start + piece, :] = jax.nn.silu(total).astype(bf16)

    thin = pl.ds(pl.multiple_of(q * STATE, 128), STATE)
    for which, target in ((1, reads), (0, writes)):
        edge = se_ref[which].astype(f32)
        pad_s[:EDGE, :] = jnp.where(has_edge > 0.0, edge, 0.0)
        for k in range(q_count):
            pad_s[EDGE + k * piece : EDGE + (k + 1) * piece, :] = s_ref[k, which].astype(f32)
        kernel = ts_ref[which, :, thin]
        for k in range(q_count):
            filtered(pad_s, kernel, k * piece, target)
    spots = spot_ref[...]
    lanes = lax.broadcasted_iota(jnp.int32, (rows, tokens), 1)
    pick_f = jnp.where(spots == lanes, 1.0, 0.0)
    pick = pick_f.astype(bf16)
    mine_r[...] = jnp.dot(pick, reads[...], preferred_element_type=f32).astype(bf16)
    pl.semaphore_wait(barrier, z_count - 1)
    sent = []
    for d in range(1, z_count):
        copy = remote(mine_r, all_r.at[z], r_send.at[d], r_recv.at[d], peer(d))
        copy.start()
        sent.append(copy)
    all_r[z] = mine_r[...]
    wide = pl.ds(pl.multiple_of(q * width, 128), width)
    kernel_x = tx_ref[:, wide]
    pad_x[:EDGE, :] = jnp.where(has_edge > 0.0, xe_ref[...].astype(f32), 0.0)
    for k in range(q_count):
        pad_x[EDGE + k * piece : EDGE + (k + 1) * piece, :] = x_ref[k].astype(f32)
    for k in range(q_count):
        filtered(pad_x, kernel_x, k * piece, values)
    steps = jnp.concatenate([d_ref[k] for k in range(q_count)], axis=1)
    lower = jnp.where(
        lax.broadcasted_iota(jnp.int32, (tokens, tokens), 0)
        <= lax.broadcasted_iota(jnp.int32, (tokens, tokens), 1),
        1.0, 0.0,
    )
    runs = jnp.concatenate([-rate_ref[q] * steps, f_ref[...]], axis=0)
    sums = jnp.dot(runs, lower, precision=precise, preferred_element_type=f32)
    cumulated = sums[:heads]
    segment = sums[heads : heads + 1]
    at_rows = lax.dot_general(
        pick_f, sums, (((1,), (1,)), ((), ())), precision=precise, preferred_element_type=f32
    )
    row_cum = at_rows[:, :heads]
    row_seg = at_rows[:, heads : heads + 1]
    last = cumulated[:, tokens - 1 : tokens]
    last_seg = segment[:, tokens - 1 : tokens]
    to_end = jnp.exp(last - cumulated) * jnp.where(segment == last_seg, 1.0, 0.0) * steps
    spread_heads = jnp.where(
        lax.broadcasted_iota(jnp.int32, (heads, width), 0)
        == lax.broadcasted_iota(jnp.int32, (heads, width), 1) // HEAD_DIM,
        1.0, 0.0,
    )

    def widen(a):
        return jnp.dot(a, spread_heads, precision=precise, preferred_element_type=f32)

    plane = jnp.broadcast_to(jnp.exp(last) * jnp.where(last_seg == 0.0, 1.0, 0.0), (heads, 128))
    pd[...] = widen(plane.T[:8])
    weighted = values[...].astype(f32) * widen(to_end.T)
    state = jnp.dot(
        writes[...].astype(f32).T, weighted, precision=precise, preferred_element_type=f32
    )
    for d in range(1, z_count):
        here = all_r.at[(z + z_count - d) % z_count]
        remote(mine_r, here, r_send.at[d], r_recv.at[d], peer(d)).wait_recv()
    for k in range(z_count):
        y[k] = jnp.dot(
            all_r[k].astype(f32), state, precision=precise, preferred_element_type=f32
        )

    def outgoing(d):
        return (
            remote(y.at[(z + d) % z_count], far.at[z], y_send.at[d], y_recv.at[d], peer(d)),
            remote(pd, far_pd.at[z], p_send.at[d], p_recv.at[d], peer(d)),
        )

    for d in range(1, z_count):
        @pl.when(z + d < z_count)
        def _():
            for copy in outgoing(d):
                copy.start()
    scores = lax.dot_general(
        mine_r[...], writes[...], (((1,), (1,)), ((), ())), preferred_element_type=f32
    )
    causal = (spots >= lanes) & (row_seg == segment)
    half = lax.broadcasted_iota(jnp.int32, (rows, 2 * HEAD_DIM), 1) < HEAD_DIM
    for pair in range(heads // 2):
        mixes = []
        for h in (2 * pair, 2 * pair + 1):
            gaps = row_cum[:, h : h + 1] - cumulated[h : h + 1]
            decay = jnp.where(causal, jnp.exp(jnp.where(causal, gaps, 0.0)), 0.0)
            mixes.append(scores * decay * steps[h : h + 1])
        span = slice(pair * 2 * HEAD_DIM, (pair + 1) * 2 * HEAD_DIM)
        product = jnp.dot(
            jnp.concatenate(mixes, axis=0), values[:, span].astype(f32),
            precision=precise, preferred_element_type=f32,
        )
        mixed[:, span] = jnp.where(half, product[:rows], product[rows:])
    own_values = jnp.dot(pick, values[...], preferred_element_type=f32)
    from_start = jnp.exp(row_cum) * jnp.where(row_seg == 0.0, 1.0, 0.0)
    factors = widen(
        jnp.concatenate([from_start, jnp.broadcast_to(skip_ref[q], (8, heads))], axis=0)
    )
    gate = jax.nn.silu(gate_ref[...].astype(f32))
    carried[...] = jnp.zeros((rows, width), f32)
    for d in range(z_count - 1, 0, -1):
        @pl.when(z - d >= 0)
        def _():
            k = z - d + jnp.where(z - d < 0, z_count, 0)
            here, there = far.at[k], far_pd.at[k]
            remote(here, here, y_send.at[d], y_recv.at[d], peer(d)).wait_recv()
            remote(there, there, p_send.at[d], p_recv.at[d], peer(d)).wait_recv()
            carried[...] = carried[...] * far_pd[k][0:1] + far[k]
    gated = (
        mixed[...] + carried[...] * factors[:rows] + factors[rows : rows + 1] * own_values
    ) * gate
    scale = lax.rsqrt(jnp.mean(gated * gated, axis=1, keepdims=True) + epsilon)
    out[...] = (gated * scale * gain_ref[:, wide]).astype(bf16)
    for copy in sent:
        copy.wait_send()
    for d in range(1, z_count):
        @pl.when(z + d < z_count)
        def _():
            for copy in outgoing(d):
                copy.wait_send()


def middle(xs, x_edge, ss, s_edge, keeps, steps, flags, spots, gate, taps_x, taps_s, rate, skip, gain,
           q_count, z_count):
    f32, bf16 = jnp.float32, jnp.bfloat16
    tokens = steps.shape[0] * steps.shape[2]
    rows, width = gate.shape
    operands = (
        xs, x_edge, ss, s_edge, keeps, steps, flags, spots, gate, taps_x, taps_s, rate, skip, gain
    )
    run, extra = staged(
        functools.partial(mid_kernel, q_count, z_count), (), len(operands), operands
    )
    dma, vmem = pltpu.SemaphoreType.DMA, pltpu.VMEM
    return pl.pallas_call(
        run,
        out_shape=jax.ShapeDtypeStruct((rows, width), bf16),
        in_specs=[ANY] * len(operands),
        out_specs=VMEM,
        scratch_shapes=[
            vmem((EDGE + tokens, width), f32),
            vmem((EDGE + tokens, STATE), f32),
            vmem((tokens, width), bf16),
            vmem((tokens, STATE), bf16),
            vmem((tokens, STATE), bf16),
            vmem((rows, STATE), bf16),
            vmem((z_count, rows, STATE), bf16),
            vmem((z_count, rows, width), f32),
            vmem((z_count, rows, width), f32),
            vmem((8, width), f32),
            vmem((z_count, 8, width), f32),
            vmem((rows, width), f32),
            vmem((rows, width), f32),
        ] + [dma((z_count,))] * 6 + extra,
        compiler_params=pltpu.CompilerParams(
            collective_id=1, has_side_effects=True, vmem_limit_bytes=58 * 1024 * 1024
        ),
    )(*operands)


def tail_kernel(n, tp, q_count, z_count, n_ref, ow_ref, hw_ref, r_ref, g_ref, t_ref, p_ref, out,
                ow, hw, nrm, both, hid, feat, logit, stat, every,
                own, tp_send, tp_recv, st_send, st_recv, *gather_sems):
    c, t = lax.axis_index("ctx"), lax.axis_index("tp")
    z, q = c // q_count, c % q_count
    total = n * tp
    me = c * tp + t
    get_ow = pltpu.make_async_copy(ow_ref, ow, own.at[0])
    get_hw = pltpu.make_async_copy(hw_ref, hw, own.at[1])
    barrier = pltpu.get_barrier_semaphore()

    def device(k):
        return (k // tp, k % tp)

    def hello(d, carry):
        pl.semaphore_signal(
            barrier, inc=1, device_id=device((me + d) % total), device_id_type=MESH
        )
        return carry

    lax.fori_loop(1, total, hello, 0)
    get_ow.start()
    get_hw.start()
    pl.semaphore_wait(barrier, total - 1)
    core_n = 2 if q_count % 2 == 0 else 1
    x_n = q_count // core_n
    x, core = q // core_n, q % core_n

    def at_x(k):
        return (z * q_count + k * core_n + core, t)

    at_core = (z * q_count + x * core_n + (core_n - 1) - core, t)

    def gathered(slot, mine, sems):
        z_send, z_recv, x_send, x_recv, c_send, c_recv = sems
        sent = []

        def push(copy):
            copy.start()
            sent.append(copy)

        def to_x(ref, dst, d):
            for e in range(1, x_n):
                push(remote(ref, dst, x_send.at[e - 1, d], x_recv.at[e - 1, d], at_x((x + e) % x_n)))

        def to_core(ref, dst, e, d):
            if core_n > 1:
                push(remote(ref, dst, c_send.at[e, d], c_recv.at[e, d], at_core))

        home = slot(q, z)
        for d in range(1, z_count):
            push(remote(mine, home, z_send.at[d], z_recv.at[d], (((z + d) % z_count) * q_count + q, t)))
        to_x(mine, home, 0)
        to_core(mine, home, 0, 0)
        for d in range(z_count):
            k = (z + z_count - d) % z_count
            if d:
                here = slot(q, k)
                remote(here, here, z_send.at[d], z_recv.at[d], at_core).wait_recv()
                to_x(here, here, d)
                to_core(here, here, 0, d)
            for e in range(1, x_n):
                here = slot(((x + x_n - e) % x_n) * core_n + core, k)
                remote(here, here, x_send.at[e - 1, d], x_recv.at[e - 1, d], at_core).wait_recv()
                to_core(here, here, e, d)
        if core_n > 1:
            for d in range(z_count):
                k = (z + z_count - d) % z_count
                for e in range(x_n):
                    here = slot(((x + x_n - e) % x_n) * core_n + 1 - core, k)
                    remote(here, here, c_send.at[e, d], c_recv.at[e, d], at_core).wait_recv()
        return sent

    rows = n_ref.shape[0]
    width = n_ref.shape[1]

    def normed_slot(a, b):
        return nrm.at[a, b]

    pending = gathered(normed_slot, n_ref, gather_sems[:6])
    nrm[q, z] = n_ref[...]
    get_ow.wait()
    partial = jnp.zeros(both.shape[1:], jnp.float32)
    for k in range(q_count):
        partial = partial + jnp.dot(
            nrm[k].reshape(z_count * rows, width),
            ow[k * width : (k + 1) * width, :],
            preferred_element_type=jnp.float32,
        )
    both[t] = partial
    tp_copies = []
    for d in range(1, tp):
        copy = remote(both.at[t], both.at[t], tp_send.at[d], tp_recv.at[d], (c, (t + d) % tp))
        copy.start()
        tp_copies.append(copy)
    for d in range(1, tp):
        here = both.at[(t + tp - d) % tp]
        remote(here, here, tp_send.at[d], tp_recv.at[d], (c, (t + d) % tp)).wait_recv()
    summed = both[0]
    for k in range(1, tp):
        summed = summed + both[k]
    hid[q, z] = (r_ref[...].astype(jnp.float32) + summed).astype(jnp.bfloat16)

    def hidden_slot(a, b):
        return hid.at[a, b]

    pending = pending + tp_copies + gathered(hidden_slot, hid.at[q, z], gather_sems[6:])
    block = hid.shape[3]
    all_rows = hid.shape[2]
    squares = jnp.zeros((all_rows, 1), jnp.float32)
    for k in range(z_count):
        for a in range(q_count):
            piece = hid[a, k].astype(jnp.float32)
            squares = squares + jnp.sum(piece * piece, axis=1, keepdims=True)
    inverse = lax.rsqrt(squares / (n * block) + epsilon)
    for k in range(z_count):
        for a in range(q_count):
            first = (k * q_count + a) * block
            span = slice(first, first + block)
            feat[:, span] = (
                hid[a, k].astype(jnp.float32) * inverse * g_ref[:, span]
            ).astype(jnp.bfloat16)
    get_hw.wait()
    vocab = hw.shape[1]
    tile = min(256, vocab)

    def one_tile(i, carry):
        cols = pl.ds(pl.multiple_of(i * tile, 128), tile)
        logit[:, cols] = jnp.dot(feat[...], hw[:, cols], preferred_element_type=jnp.float32)
        return carry

    lax.fori_loop(0, vocab // tile, one_tile, 0)
    values = logit[...]
    top = jnp.max(values, axis=1, keepdims=True)
    added = jnp.sum(jnp.exp(values - top), axis=1, keepdims=True)
    column = t_ref[...] - me * vocab
    places = lax.broadcasted_iota(jnp.int32, values.shape, 1)
    hit = jnp.sum(jnp.where(places == column, values, 0.0), axis=1, keepdims=True)
    lane = lax.broadcasted_iota(jnp.int32, (all_rows, 128), 1)
    packed = jnp.where(lane == 0, top, jnp.where(lane == 1, added, jnp.where(lane == 2, hit, 0.0)))
    turned = packed.T[:8]
    stat[...] = turned

    def go(d, carry):
        remote(
            stat, every.at[me], st_send.at[d], st_recv.at[d], device((me + d) % total)
        ).start()
        return carry

    lax.fori_loop(1, total, go, 0)
    every[me] = turned

    def done(d, carry):
        here = every.at[(me + total - d) % total]
        copy = remote(stat, here, st_send.at[d], st_recv.at[d], device((me + d) % total))
        copy.wait_send()
        copy.wait_recv()
        return carry

    lax.fori_loop(1, total, done, 0)
    for copy in pending:
        copy.wait_send()
    found = every[...]
    tops = found[:, 0, :]
    row_top = jnp.max(tops, axis=0, keepdims=True)
    full = jnp.sum(found[:, 1, :] * jnp.exp(tops - row_top), axis=0, keepdims=True)
    picked = jnp.sum(found[:, 2, :], axis=0, keepdims=True)
    log_prob = picked - row_top - jnp.log(full)
    out[0:1, :] = log_prob
    out[1:2, :] = 0.5 * jnp.square(log_prob - p_ref[...])


def tail(normed, out_weight, head_weight, res, gain, targets, policy, n, tp, q_count, z_count):
    dma = pltpu.SemaphoreType.DMA
    total = n * tp
    rows, width = normed.shape
    all_rows = z_count * rows
    block = out_weight.shape[1]
    core_n = 2 if q_count % 2 == 0 else 1
    x_n = q_count // core_n
    vmem = pltpu.VMEM
    bf16, f32 = jnp.bfloat16, jnp.float32
    e_n = max(x_n - 1, 1)
    sems = [
        dma((z_count,)), dma((z_count,)), dma((e_n, z_count)), dma((e_n, z_count)),
        dma((x_n, z_count)), dma((x_n, z_count)),
    ]
    operands = (
        normed, out_weight, head_weight, res, gain[None], targets[:, None], policy[None]
    )
    run, extra = staged(
        functools.partial(tail_kernel, n, tp, q_count, z_count), (1, 2), len(operands),
        operands[:1] + operands[3:],
    )
    result = pl.pallas_call(
        run,
        out_shape=jax.ShapeDtypeStruct((2, all_rows), f32),
        in_specs=[ANY] * len(operands),
        out_specs=VMEM,
        scratch_shapes=[
            vmem(out_weight.shape, bf16),
            vmem(head_weight.shape, bf16),
            vmem((q_count, z_count, rows, width), bf16),
            vmem((tp, all_rows, block), f32),
            vmem((q_count, z_count, all_rows, block), bf16),
            vmem((all_rows, n * block), bf16),
            vmem((all_rows, head_weight.shape[1]), f32),
            vmem((8, all_rows), f32),
            vmem((total, 8, all_rows), f32),
            dma((2,)), dma((tp,)), dma((tp,)), dma((total,)), dma((total,)),
        ] + sems + sems + extra,
        compiler_params=pltpu.CompilerParams(
            collective_id=3, has_side_effects=True, vmem_limit_bytes=58 * 1024 * 1024
        ),
    )(*operands)
    return result[0], result[1]


def halves(a):
    hi = a.astype(jnp.bfloat16)
    return hi, (a - hi.astype(jnp.float32)).astype(jnp.bfloat16)


def thirds(a):
    hi = a.astype(jnp.bfloat16)
    rest = a - hi.astype(jnp.float32)
    mid = rest.astype(jnp.bfloat16)
    return hi, mid, (rest - mid.astype(jnp.float32)).astype(jnp.bfloat16)


def column(row, first, count):
    lanes = row.shape[1]
    spot = lax.broadcasted_iota(jnp.int32, (count, lanes), 0) + first
    hit = lax.broadcasted_iota(jnp.int32, (count, lanes), 1) == spot
    return jnp.sum(jnp.where(hit, jnp.broadcast_to(row, (count, lanes)), 0.0), axis=1, keepdims=True)


def one_kernel(n, tp, *refs):
    names, refs = refs[0], refs[1:]
    r = dict(zip(names, refs))
    f32, bf16 = jnp.float32, jnp.bfloat16
    c, t = lax.axis_index("ctx"), lax.axis_index("tp")
    total = n * tp
    me = c * tp + t
    chips = n // 2
    z_n = chips // 2
    k, p = c % 2, c // 2
    x, z = p % 2, p // 2

    def dev(z_, x_, k_):
        return ((z_ * 2 + x_) * 2 + k_, t)

    core_peer, x_peer, y_peer = dev(z, x, 1 - k), dev(z, 1 - x, k), (c, 1 - t)
    T, C = r["x"].shape
    W = C // 2
    S = r["s"].shape[2] // 2
    G = S // STATE
    GW = W // G
    H = r["d"].shape[0]
    HC = H // 2
    Tc = 2 * T
    r8 = r["scored"].shape[0]
    RC = 2 * r8
    R = chips * RC
    taps = r["tx"].shape[0]
    blk = r["ow"].shape[1] // tp
    D = n * tp * blk
    V = r["hw"].shape[1]
    per = n // tp

    barrier = pltpu.get_barrier_semaphore()

    plane_peers = [
        (((z * 2 + (x + a) % 2) * 2 + (k + b) % 2), (t + e) % tp)
        for a in range(2) for b in range(2) for e in range(tp) if a + b + e
    ]
    z_peers = [dev((z + d) % z_n, x, k) for d in range(1, z_n)]

    def greet_one(sem, device):
        pl.semaphore_signal(sem, inc=1, device_id=device, device_id_type=MESH)

    for device in plane_peers + z_peers:
        greet_one(barrier, device)
    sends_up = (x == 1) & (k == 1) & (z < z_n - 1)

    @pl.when((x == 0) & (z > 0))
    def _():
        greet_one(barrier, dev(z - 1, 1, 1))

    def lanes(a, size):
        return pl.ds(pl.multiple_of(a * size, 128), size)

    local = {}

    def fetch(name, src, dst):
        copy = pltpu.make_async_copy(src, dst, r["own"].at[len(local)])
        local[name] = copy
        copy.start()

    def arrived(ref, sem):
        pltpu.make_async_copy(ref, ref, sem).wait()

    sent = []

    def push(copy, when=None):
        sent.append((copy, when))
        if when is None:
            copy.start()
        else:
            pl.when(when)(copy.start)

    fetch("resets", r["resets"], r["resv"])
    fetch("scored", r["scored"], r["spot"])
    fetch("g", r["g"], r["gv"])
    fetch("res", r["res"], r["rv"])
    fetch("s", r["s"].at[:, :, lanes(k, S)], r["sc"].at[k])
    fetch("ts", r["ts"].at[:, :, lanes(k, S)], r["tsv"])
    half_heads = pl.ds(pl.multiple_of(k * HC, 8), HC)
    fetch("d", r["d"].at[half_heads], r["dc"].at[k])
    fetch("rate", r["rate"], r["ratev"])
    fetch("x", r["x"].at[:, lanes(k, W)], r["xc"].at[k])
    fetch("tx", r["tx"].at[:, lanes(k, W)], r["txv"])
    fetch("skip", r["skip"], r["skipv"])
    fetch("gain", r["gain"].at[:, lanes(k, W)], r["gainv"])
    fetch("fg", r["fg"], r["fgv"])
    fetch("tgt", r["tgt"], r["tgtv"])
    fetch("pol", r["pol"], r["polv"])
    fetch("ow", r["ow"], r["oww"])

    first = p == 0

    @pl.when(first)
    def _():
        r["xh"][...] = jnp.zeros(r["xh"].shape, bf16)
        r["sh"][...] = jnp.zeros(r["sh"].shape, bf16)
        r["mh"][...] = jnp.zeros(r["mh"].shape, f32)

    local["resets"].wait()
    local["scored"].wait()
    lane8 = lax.broadcasted_iota(jnp.int32, (8, T), 1)
    row8 = lax.broadcasted_iota(jnp.int32, (8, T), 0)
    places = jnp.zeros((8, T), f32)
    for i in range(r8):
        places = jnp.where(lane8 == i, (r["spot"][i] - c * T).astype(f32), places)
    flags_here = jnp.broadcast_to(r["resv"][...].astype(f32), (8, T))
    r["meta"][...] = jnp.where(row8 == 0, flags_here, places)

    local["g"].wait()
    local["res"].wait()
    own_pick = jnp.where(
        column(r["meta"][1:2], 0, r8) == lax.broadcasted_iota(jnp.int32, (r8, T), 1).astype(f32),
        1.0, 0.0,
    ).astype(bf16)
    r["gc"][k] = jnp.dot(
        own_pick, r["gv"][:, lanes(k, W)], preferred_element_type=f32
    ).astype(bf16)
    r["gsend"][...] = jnp.dot(
        own_pick, r["gv"][:, lanes(1 - k, W)], preferred_element_type=f32
    ).astype(bf16)
    res_rows = jnp.dot(own_pick, r["rv"][...], preferred_element_type=f32).astype(bf16)

    for j in range(per * tp):
        r["rsend"][j] = res_rows[:, j * blk : (j + 1) * blk]

    pl.semaphore_wait(barrier, len(plane_peers) + len(z_peers) + jnp.where(sends_up, 2, 0))
    for device in plane_peers:
        greet_one(r["ready"], device)

    send, recv = r["core_send"], r["core_recv"]
    edge_send, edge_recv = r["edge_send"], r["edge_recv"]
    swap = (
        (r["s"].at[:, :, lanes(1 - k, S)], r["sc"].at[k]),
        (r["meta"], r["mc"].at[k]),
        (r["d"].at[pl.ds(pl.multiple_of((1 - k) * HC, 8), HC)], r["dc"].at[k]),
        (r["x"].at[:, lanes(1 - k, W)], r["xc"].at[k]),
    )
    for i, (a, b) in enumerate(swap):
        push(remote(a, b, send.at[i], recv.at[i], core_peer))
    last_core = (k == 1) & (p < chips - 1)
    tail = pl.ds(T - EDGE, EDGE)
    nxt = jnp.minimum(p + 1, chips - 1)
    for j in range(2):
        triple = (
            (r["s"].at[:, tail, j * S : (j + 1) * S], r["sh"]),
            (r["meta"], r["mh"]),
            (r["x"].at[tail, j * W : (j + 1) * W], r["xh"]),
        )
        for i, (a, b) in enumerate(triple):
            push(remote(a, b, edge_send.at[j, i], edge_recv.at[i], (nxt * 2 + j, t)), last_core)
    r["mc"][k] = r["meta"][...]

    def from_core(i, buf):
        arrived(buf.at[1 - k], recv.at[i])

    def from_edge(i, ref):
        @pl.when(jnp.logical_not(first))
        def _():
            arrived(ref, edge_recv.at[i])

    from_core(1, r["mc"])
    spots = jnp.concatenate(
        [column(r["mc"][j][1:2], 0, r8) + j * T for j in range(2)], axis=0
    ).astype(jnp.int32)
    lane_t = lax.broadcasted_iota(jnp.int32, (RC, Tc), 1)
    pick_f = jnp.where(spots == lane_t, 1.0, 0.0)
    pick = pick_f.astype(bf16)

    chip_flags = jnp.concatenate([r["mc"][0], r["mc"][1]], axis=1)
    local["d"].wait()
    local["rate"].wait()
    from_core(2, r["dc"])
    steps = jnp.concatenate([r["dc"][0], r["dc"][1]], axis=1)
    lower = jnp.where(
        lax.broadcasted_iota(jnp.int32, (Tc, Tc), 0) <= lax.broadcasted_iota(jnp.int32, (Tc, Tc), 1),
        1.0, 0.0,
    ).astype(bf16)
    rate_col = column(r["ratev"][...], k * HC, HC)
    runs = jnp.concatenate([-rate_col * steps, chip_flags], axis=0)
    sums3 = jnp.dot(jnp.concatenate(thirds(runs), axis=0), lower, preferred_element_type=f32)
    count = HC + 8
    sums = sums3[:count] + sums3[count : 2 * count] + sums3[2 * count :]
    cumulated = sums[:HC]
    segment = sums[HC : HC + 1]
    last = cumulated[:, Tc - 1 : Tc]
    last_seg = segment[:, Tc - 1 : Tc]
    plane = jnp.broadcast_to(jnp.exp(last) * jnp.where(last_seg == 0.0, 1.0, 0.0), (HC, 128))
    r["mine_pd"][...] = jnp.concatenate([plane.T[:8], jnp.zeros((8, 128 - HC), f32)], axis=1)
    pl.semaphore_wait(r["ready"], len(plane_peers))
    for d in range(1, chips):
        remote(
            r["mine_pd"], r["all_pd"].at[p], r["pd_send"], r["pd_recv"],
            (((p + d) % chips) * 2 + k, t),
        ).start()
    r["all_pd"][p] = r["mine_pd"][...]
    at_rows = lax.dot_general(
        pick_f, sums, (((1,), (1,)), ((), ())), precision=precise, preferred_element_type=f32
    )
    row_cum = at_rows[:, :HC]
    row_seg = at_rows[:, HC : HC + 1]
    to_end = jnp.exp(last - cumulated) * jnp.where(segment == last_seg, 1.0, 0.0) * steps
    r["te"][...] = jnp.concatenate(halves(to_end.T), axis=1)
    push(remote(r["gsend"], r["gc"].at[k], send.at[4], recv.at[4], core_peer))
    def res_copy(j, to_t):
        i = j * tp + to_t
        return remote(
            r["rsend"].at[i], r["ro"].at[c], r["res_send"], r["res_recv"],
            (t * per + j, to_t),
        )

    for j in range(per):
        for to_t in range(tp):
            mine = (t * per + j == c) & (to_t == t)
            pl.when(jnp.logical_not(mine))(res_copy(j, to_t).start)

            @pl.when(mine)
            def _():
                pltpu.make_async_copy(
                    r["rsend"].at[j * tp + to_t], r["ro"].at[c], r["res_recv"]
                ).start()

    from_edge(1, r["mh"])
    flags = jnp.concatenate([r["mh"][...], chip_flags], axis=1)
    clear = 1.0 - flags
    keeping = jnp.ones((8, 3 * T), f32)
    columns = [keeping]
    for off in range(1, taps):
        shifted = clear if off == 1 else pltpu.roll(clear, off - 1, 1)
        keeping = keeping * shifted
        columns.append(keeping)
    keep_rows = jnp.zeros((8, 3 * T), f32)
    row8w = lax.broadcasted_iota(jnp.int32, (8, 3 * T), 0)
    for off in range(taps):
        keep_rows = jnp.where(row8w == off, jnp.broadcast_to(columns[off][0:1], (8, 3 * T)), keep_rows)
    keep = keep_rows[:, T:].T
    for off in range(1, taps):
        r["kb"][off] = jnp.broadcast_to(keep[:, off : off + 1], (Tc, 128))
    wide_keep = [None] + [r["kb"].at[off] for off in range(1, taps)]

    def filtered(pad, kernel, start, size):
        width = pad.shape[1]
        acc = kernel[0:1] * pad[EDGE + start : EDGE + start + size, :]
        for off in range(1, taps):
            kept = wide_keep[off][start : start + size, :]
            kept = jnp.concatenate([kept] * (width // 128), axis=1)
            acc = acc + kept * (
                kernel[off : off + 1] * pad[EDGE - off + start : EDGE - off + start + size, :]
            )
        return jax.nn.silu(acc).astype(bf16)

    local["s"].wait()
    local["ts"].wait()
    from_core(0, r["sc"])
    from_edge(0, r["sh"])
    pad = r["pad"]
    band = 64
    for which, target in ((1, r["reads"]), (0, r["writes"])):
        for g in range(G):
            cols = slice(g * STATE, (g + 1) * STATE)
            pad_s = r["pad_s"]
            pad_s[:EDGE, :] = r["sh"][which, :, cols].astype(f32)
            for j in range(2):
                pad_s[EDGE + j * T : EDGE + (j + 1) * T, :] = r["sc"][j, which, :, cols].astype(f32)
            kernel = r["tsv"][which, :, cols]
            for b in range(Tc // band):
                target[b * band : (b + 1) * band, cols] = filtered(pad_s, kernel, b * band, band)
        if which == 1:
            r["mine_r"][...] = jnp.dot(
                pick, r["reads"][...], preferred_element_type=f32
            ).astype(bf16)
            for d in range(1, chips):
                remote(
                    r["mine_r"], r["all_r"].at[p], r["r_send"], r["r_recv"],
                    (((p + d) % chips) * 2 + k, t),
                ).start()
            r["all_r"][p] = r["mine_r"][...]

    for g in range(G):
        r["wT"][g] = r["writes"][:, g * STATE : (g + 1) * STATE].astype(f32).T.astype(bf16)

    chunk = min(1024, GW)

    def spread_cols(j, size, offset):
        head = lax.broadcasted_iota(jnp.int32, (size, chunk), 0) % (size // 2)
        lane = lax.broadcasted_iota(jnp.int32, (size, chunk), 1)
        return jnp.where(head == offset + (j * chunk + lane) // HEAD_DIM, 1.0, 0.0).astype(bf16)

    local["x"].wait()
    local["tx"].wait()
    from_core(3, r["xc"])
    from_edge(2, r["xh"])

    def conv_step(j, carry):
        cols = lanes(j, chunk)
        pad[:EDGE, :] = r["xh"][:, cols].astype(f32)
        for i in range(2):
            pad[EDGE + i * T : EDGE + (i + 1) * T, :] = r["xc"][i, :, cols].astype(f32)
        kernel = r["txv"][:, cols]
        for b in range(Tc // band):
            r["values"][b * band : (b + 1) * band, cols] = filtered(pad, kernel, b * band, band)
        grown = jnp.dot(r["te"][...], spread_cols(j, 2 * HC, 0), preferred_element_type=f32)
        hi, lo = halves(r["values"][:, cols].astype(f32) * grown)
        w_t = r["wT"][(j * chunk) // GW]
        state = jnp.dot(w_t, hi, preferred_element_type=f32) + jnp.dot(
            w_t, lo, preferred_element_type=f32
        )
        s_hi, s_lo = halves(state)
        r["S2"][:STATE, cols] = s_hi
        r["S2"][STATE:, cols] = s_lo
        return carry

    lax.fori_loop(0, W // chunk, conv_step, 0)

    fetch("hw", r["hw"], r["hww"])

    others = pl.ds(0, chips - 1)
    arrived(r["all_r"].at[others], r["r_recv"])
    arrived(r["all_pd"].at[others], r["pd_recv"])
    arrived(r["all_r"].at[others], r["r_send"])
    arrived(r["all_pd"].at[others], r["pd_send"])
    for g in range(G):
        rows_g = r["all_r"][:, :, g * STATE : (g + 1) * STATE].reshape(R, STATE)
        r["rr"][g, :, :STATE] = rows_g
        r["rr"][g, :, STATE:] = rows_g
    run_w = jnp.ones((1, 128), f32)
    weights = []
    for d in range(chips):
        weights.append(jnp.broadcast_to(run_w, (RC, 128)))
        run_w = jnp.where(d > p, run_w * r["all_pd"][d][0:1], run_w)
    far = jnp.concatenate(weights, axis=0)[:, :HC]
    r["ww"][...] = jnp.concatenate(halves(far), axis=1)

    def y_step(j, carry):
        cols = lanes(j, chunk)
        y = jnp.dot(r["rr"][(j * chunk) // GW], r["S2"][:, cols], preferred_element_type=f32)
        grown = jnp.dot(r["ww"][...], spread_cols(j, 2 * HC, 0), preferred_element_type=f32)
        r["yf"][:, cols] = y * grown
        return carry

    lax.fori_loop(0, W // chunk, y_step, 0)

    def y_rows(zd, xd):
        return r["yf"][pl.ds(pl.multiple_of((zd * 2 + xd) * RC, 16), RC), :]

    def coded(a, wire, scale):
        most = jnp.max(jnp.abs(a), axis=1, keepdims=True)
        inverse = jnp.where(most > 0.0, LEVELS / jnp.maximum(most, TINY), 0.0)
        wire[...] = jnp.round(a * inverse).astype(jnp.int32).astype(jnp.int16)
        scale[...] = jnp.broadcast_to(most * (1.0 / LEVELS), (RC, 128))

    def decoded(wire, scale):
        return wire[...].astype(jnp.int32).astype(f32) * scale[:, :1]

    for zd in range(z_n - 1, -1, -1):
        goes = (zd > z) | ((zd == z) & (x == 0))

        @pl.when(goes)
        def _():
            coded(y_rows(zd, 1 - x), r["xsend"].at[zd], r["xsend_f"].at[zd])

        for i, (a, b) in enumerate(((r["xsend"], r["xr"]), (r["xsend_f"], r["xr_f"]))):
            push(
                remote(a.at[zd], b.at[zd], r["x_send"].at[i, zd], r["x_recv"].at[i, zd], x_peer),
                goes,
            )

    def from_x_peer(zd):
        for i, b in enumerate((r["xr"], r["xr_f"])):
            arrived(b.at[zd], r["x_recv"].at[i, zd])
        return decoded(r["xr"].at[zd], r["xr_f"].at[zd])

    mine_r = r["mine_r"][...]
    scores = [
        lax.dot_general(
            mine_r[:, g * STATE : (g + 1) * STATE], r["writes"][:, g * STATE : (g + 1) * STATE],
            (((1,), (1,)), ((), ())), preferred_element_type=f32,
        )
        for g in range(G)
    ]
    causal = (spots >= lane_t) & (row_seg == segment)
    quad = 4
    quad_w = quad * HEAD_DIM
    which_head = lax.broadcasted_iota(jnp.int32, (RC, quad_w), 1) // HEAD_DIM

    def within(q):
        mixes = []
        for i in range(quad):
            h = q * quad + i
            gaps = row_cum[:, h : h + 1] - cumulated[h : h + 1]
            decay = jnp.where(causal, jnp.exp(jnp.where(causal, gaps, 0.0)), 0.0)
            mixes.append(scores[h * HEAD_DIM // GW] * decay * steps[h : h + 1])
        both = jnp.concatenate(halves(jnp.concatenate(mixes, axis=0)), axis=0)
        span = slice(q * quad_w, (q + 1) * quad_w)
        product = jnp.dot(both, r["values"][:, span], preferred_element_type=f32)
        product = product[: quad * RC] + product[quad * RC :]
        out = product[:RC]
        for i in range(1, quad):
            out = jnp.where(which_head == i, product[i * RC : (i + 1) * RC], out)
        r["mixed"][:, span] = out

    quads = HC // quad
    for q in range(quads // 2):
        within(q)
    for zd in range(z_n - 1, 0, -1):
        goes = zd > z

        @pl.when(goes)
        def _():
            coded(y_rows(zd, x) + from_x_peer(zd), r["zsend"].at[zd], r["zsend_f"].at[zd])

        for i, (a, b) in enumerate(((r["zsend"], r["zr"]), (r["zsend_f"], r["zr_f"]))):
            push(
                remote(a.at[zd], b.at[z], r["z_send"].at[i, zd], r["z_recv"].at[i, z], dev(zd, x, k)),
                goes,
            )
    for q in range(quads // 2, quads):
        within(q)

    local["skip"].wait()
    local["gain"].wait()
    from_start = jnp.exp(row_cum) * jnp.where(row_seg == 0.0, 1.0, 0.0)
    starts = jnp.concatenate(halves(from_start), axis=1)
    skip3 = jnp.concatenate(
        [jnp.broadcast_to(a, (8, H)) for a in thirds(jnp.broadcast_to(r["skipv"][...], (8, H)))], axis=0
    )
    from_core(4, r["gc"])
    gate = jnp.concatenate([r["gc"][0].astype(f32), r["gc"][1].astype(f32)], axis=0)

    def widen_step(j, carry):
        cols = lanes(j, chunk)
        own_values = jnp.dot(pick, r["values"][:, cols], preferred_element_type=f32)
        head = lax.broadcasted_iota(jnp.int32, (H, chunk), 0)
        lane = lax.broadcasted_iota(jnp.int32, (H, chunk), 1)
        all_heads = jnp.where(head == k * HC + (j * chunk + lane) // HEAD_DIM, 1.0, 0.0).astype(bf16)
        grown = jnp.dot(skip3, all_heads, preferred_element_type=f32)
        skip_row = grown[0:1] + grown[8:9] + grown[16:17]
        r["mixed"][:, cols] = r["mixed"][:, cols] + skip_row * own_values
        r["starts"][:, cols] = jnp.dot(starts, spread_cols(j, 2 * HC, 0), preferred_element_type=f32)
        return carry

    lax.fori_loop(0, W // chunk, widen_step, 0)
    gate = jax.nn.silu(gate)

    carried = r["carried"]
    carried[...] = jnp.zeros((RC, W), f32)

    @pl.when(x == 1)
    def _():
        carried[...] = from_x_peer(z)

    for zs in range(z_n - 1):
        @pl.when(zs < z)
        def _():
            for i, b in enumerate((r["zr"], r["zr_f"])):
                arrived(b.at[zs], r["z_recv"].at[i, zs])
            carried[...] = carried[...] + decoded(r["zr"].at[zs], r["zr_f"].at[zs])

    gated = (r["mixed"][...] + carried[...] * r["starts"][...]) * gate
    for g in range(G):
        span = slice(g * GW, (g + 1) * GW)
        part = gated[:, span]
        scale = lax.rsqrt(jnp.mean(part * part, axis=1, keepdims=True) + epsilon)
        r["normed"][:, span] = (part * scale * r["gainv"][:, span]).astype(bf16)

    nrm = r["nrm"]
    mine = r["normed"]
    z_recv, x_recv, c_recv = r["gather1"]
    g_send = r["g_send"]

    def slot(z_, x_, k_):
        return nrm.at[k_ * chips + z_ * 2 + x_]

    def go1(a, b, sem, device):
        remote(a, b, g_send.at[0], sem, device).start()

    home = slot(z, x, k)
    for d in range(1, z_n):
        go1(mine, home, z_recv.at[z], dev((z + d) % z_n, x, k))
    go1(mine, home, x_recv.at[z], x_peer)
    go1(mine, home, c_recv.at[0, z], core_peer)
    nrm[k * chips + p] = mine[...]
    for zs in range(z_n):
        @pl.when(zs != z)
        def _():
            here = slot(zs, x, k)
            arrived(here, z_recv.at[zs])
            go1(here, here, x_recv.at[zs], x_peer)
            go1(here, here, c_recv.at[0, zs], core_peer)

    for zs in range(z_n):
        here = slot(zs, 1 - x, k)
        arrived(here, x_recv.at[zs])
        go1(here, here, c_recv.at[1, zs], core_peer)
    for zs in range(z_n):
        for e, x_ in ((0, x), (1, 1 - x)):
            arrived(slot(zs, x_, 1 - k), c_recv.at[e, zs])
    arrived(nrm.at[pl.ds(0, 2 * chips - 1)], g_send.at[0])
    local["ow"].wait()
    partial = jnp.zeros((R, tp * blk), f32)
    for j in range(2):
        partial = partial + jnp.dot(
            nrm[j * chips : (j + 1) * chips].reshape(R, W), r["oww"][j * W : (j + 1) * W, :], preferred_element_type=f32
        )
    for j in range(tp):
        r["pt"][j] = partial[:, j * blk : (j + 1) * blk]
    push(remote(r["pt"].at[1 - t], r["pr"], r["t_send"], r["t_recv"], y_peer))
    arrived(r["ro"], r["res_recv"])
    in_half = (c >= t * per) & (c < (t + 1) * per)

    @pl.when(in_half)
    def _():
        arrived(r["rsend"].at[pl.ds(0, n - 1)], r["res_send"])

    @pl.when(jnp.logical_not(in_half))
    def _():
        arrived(r["rsend"], r["res_send"])

    res_all = r["ro"][...].astype(f32).reshape(R, blk)
    arrived(r["pr"], r["t_recv"])
    hid = r["hid"]
    hid_mine = (res_all + (r["pt"][t] + r["pr"][...])).astype(bf16)
    hid[me] = hid_mine
    wide_mine = hid_mine.astype(f32)
    sq_mine = jnp.sum(wide_mine * wide_mine, axis=1, keepdims=True)
    sq, sq_z, sq_p = r["sq"], r["sq_z"], r["sq_p"]
    sq[0] = jnp.broadcast_to(sq_mine, (R, 128)).T[:1]

    z_recv, a_recv, b_recv, c_recv = r["gather2"]
    even = k == 0
    a0, b0 = jnp.where(even, t, x), jnp.where(even, x, t)

    def place(z_, a_, b_, k_):
        y_, x_ = jnp.where(k_ == 0, a_, b_), jnp.where(k_ == 0, b_, a_)
        return hid.at[((z_ * 2 + x_) * 2 + k_) * tp + y_]

    a_peer = (jnp.where(even, c, x_peer[0]), jnp.where(even, 1 - t, t))
    b_peer = (jnp.where(even, x_peer[0], c), jnp.where(even, t, 1 - t))

    def go2(here, sem, device):
        remote(here, here, g_send.at[1], sem, device).start()

    def to_a(here, d):
        go2(here, a_recv.at[d], a_peer)

    diag = (x_peer[0], 1 - t)

    def to_diag(here, d):
        go2(here, b_recv.at[1, d], diag)

    def to_b(here, e, d):
        go2(here, b_recv.at[e, d], b_peer)

    def to_core(here, e, d):
        go2(here, c_recv.at[e, d], core_peer)

    for d in range(1, z_n):
        remote(
            sq.at[0], sq_z.at[z], r["sq_send"].at[0], r["sq_recv"].at[0], dev((z + d) % z_n, x, k)
        ).start()
    sq_z[z] = sq[0]
    home = place(z, a0, b0, k)
    for d in range(1, z_n):
        go2(home, z_recv.at[d], dev((z + d) % z_n, x, k))
    to_diag(home, 0)
    to_a(home, 0)
    to_b(home, 0, 0)
    to_core(home, 0, 0)
    arrived(sq_z.at[pl.ds(0, z_n - 1)], r["sq_recv"].at[0])
    column_sum = sq_z[0]
    for zs in range(1, z_n):
        column_sum = column_sum + sq_z[zs]
    sq[1] = column_sum
    in_plane = (x * 2 + k) * tp + t
    for device in plane_peers:
        remote(
            sq.at[1], sq_p.at[in_plane], r["sq_send"].at[1], r["sq_recv"].at[1], device
        ).start()
    sq_p[in_plane] = column_sum
    for d in range(1, z_n):
        here = place((z + z_n - d) % z_n, a0, b0, k)
        arrived(here, z_recv.at[d])
        to_diag(here, d)
        to_a(here, d)
        to_b(here, 0, d)
        to_core(here, 0, d)
    arrived(sq_p.at[pl.ds(0, len(plane_peers))], r["sq_recv"].at[1])
    squares = sq_p[0]
    for i in range(1, 4 * tp):
        squares = squares + sq_p[i]
    inverse_row = lax.rsqrt(squares / D + epsilon)
    inverse = jnp.broadcast_to(inverse_row, (128, R)).T
    local["fg"].wait()
    local["hw"].wait()
    logit, feat = r["logit"], r["feat"]
    oa, ob = jnp.where(even, x, t), jnp.where(even, t, x)
    tile = min(1024, V)
    group = 4 * tp
    depth = group * blk

    def block(d):
        from_z = (z + z_n - d) % z_n
        for e, (a_, b_) in enumerate(((oa, ob), (1 - oa, ob), (oa, 1 - ob), (1 - oa, 1 - ob))):
            arrived(place(from_z, a_, b_, 1 - k), c_recv.at[e, d])
        for i in range(group):
            gain = r["fgv"][:, lanes(from_z * group + i, blk)]
            feat[:, i * blk : (i + 1) * blk] = (
                hid[from_z * group + i].astype(f32) * inverse[:, :blk] * gain
            ).astype(bf16)
        rows = pl.ds(pl.multiple_of(from_z * depth, depth), depth)

        def one_tile(i, carry):
            cols = lanes(i, tile)
            product = jnp.dot(feat[...], r["hww"][rows, cols], preferred_element_type=f32)
            logit[:, cols] = product if d == 0 else logit[:, cols] + product
            return carry

        lax.fori_loop(0, V // tile, one_tile, 0)

    for d in range(z_n):
        from_z = (z + z_n - d) % z_n
        here = place(from_z, 1 - a0, b0, k)
        arrived(here, a_recv.at[d])
        to_core(here, 1, d)
        here = place(from_z, a0, 1 - b0, k)
        arrived(here, b_recv.at[0, d])
        to_core(here, 2, d)
        here = place(from_z, 1 - a0, 1 - b0, k)
        arrived(here, b_recv.at[1, d])
        to_core(here, 3, d)
        if d:
            block(d - 1)
    block(z_n - 1)
    values = logit[...]
    top = jnp.max(values, axis=1, keepdims=True)
    added = jnp.sum(jnp.exp(values - top), axis=1, keepdims=True)
    local["tgt"].wait()
    local["pol"].wait()
    target = column(r["tgtv"][...].astype(f32), 0, R).astype(jnp.int32) - me * V
    hit = jnp.sum(
        jnp.where(lax.broadcasted_iota(jnp.int32, values.shape, 1) == target, values, 0.0),
        axis=1, keepdims=True,
    )
    lane = lax.broadcasted_iota(jnp.int32, (R, 128), 1)
    packed = jnp.where(lane == 0, top, jnp.where(lane == 1, added, jnp.where(lane == 2, hit, 0.0)))
    turned = packed.T[:4]
    stat, every = r["stat"], r["every"]
    stat[...] = turned
    st_send, st_recv = r["st_send"], r["st_recv"]

    def device(a):
        return (a // tp, a % tp)

    def go(d, carry):
        remote(stat, every.at[me], st_send, st_recv, device((me + d) % total)).start()
        return carry

    lax.fori_loop(1, total, go, 0)
    every[me] = turned

    for copy, when in sent:
        if when is None:
            copy.wait_send()
        else:
            pl.when(when)(copy.wait_send)
    arrived(hid.at[pl.ds(0, total - 1)], g_send.at[1])
    arrived(sq_z.at[pl.ds(0, z_n - 1)], r["sq_send"].at[0])
    arrived(sq_p.at[pl.ds(0, len(plane_peers))], r["sq_send"].at[1])
    rest = every.at[pl.ds(0, total - 1)]
    arrived(rest, st_send)
    arrived(rest, st_recv)
    found = every[...]
    tops = found[:, 0, :]
    row_top = jnp.max(tops, axis=0, keepdims=True)
    full = jnp.sum(found[:, 1, :] * jnp.exp(tops - row_top), axis=0, keepdims=True)
    picked = jnp.sum(found[:, 2, :], axis=0, keepdims=True)
    log_prob = picked - row_top - jnp.log(full)
    r["out"][0:1, :] = log_prob
    r["out"][1:2, :] = 0.5 * jnp.square(log_prob - r["polv"][...])


def fused(n, tp, x, g, s, d, resets, rate, skip, tx, ts, gain, ow, res, fg, hw, scored, tgt, pol):
    f32, bf16, i32, i16 = jnp.float32, jnp.bfloat16, jnp.int32, jnp.int16
    dma, vmem = pltpu.SemaphoreType.DMA, pltpu.VMEM
    chips = n // 2
    z_n = chips // 2
    T, C = x.shape
    W, Tc = C // 2, 2 * T
    S = s.shape[2] // 2
    G = S // STATE
    H = d.shape[0]
    HC = H // 2
    r8 = scored.shape[0]
    RC = 2 * r8
    R = chips * RC
    blk = ow.shape[1] // tp
    taps = tx.shape[0]
    total = n * tp
    inputs = dict(
        x=x, g=g, s=s, d=d, resets=resets[None], rate=rate[None], skip=skip[None], tx=tx, ts=ts,
        gain=gain[None], ow=ow, res=res, fg=fg[None], hw=hw, scored=scored, tgt=tgt[None], pol=pol[None],
    )
    scratch = dict(
        resv=vmem((1, T), i32), spot=pltpu.SMEM((r8,), i32), meta=vmem((8, T), f32),
        xc=vmem((2, T, W), bf16), xh=vmem((EDGE, W), bf16),
        sc=vmem((2, 2, T, S), bf16), sh=vmem((2, EDGE, S), bf16),
        dc=vmem((2, HC, T), f32), mc=vmem((2, 8, T), f32), mh=vmem((8, T), f32),
        gv=vmem(g.shape, bf16), rv=vmem(res.shape, bf16),
        gc=vmem((2, r8, W), bf16), gsend=vmem((r8, W), bf16),
        rsend=vmem((n, r8, blk), bf16), ro=vmem((n, r8, blk), bf16),
        txv=vmem((taps, W), f32), tsv=vmem((2, taps, S), f32), gainv=vmem((1, W), f32),
        ratev=vmem((1, H), f32), skipv=vmem((1, H), f32), fgv=vmem((1, n * tp * blk), f32),
        tgtv=vmem((1, R), i32), polv=vmem((1, R), f32),
        pad=vmem((EDGE + Tc, min(1024, W // G)), f32), pad_s=vmem((EDGE + Tc, STATE), f32),
        kb=vmem((taps, Tc, 128), f32),
        reads=vmem((Tc, S), bf16), writes=vmem((Tc, S), bf16),
        mine_r=vmem((RC, S), bf16), all_r=vmem((chips, RC, S), bf16),
        mine_pd=vmem((8, 128), f32), all_pd=vmem((chips, 8, 128), f32),
        te=vmem((Tc, 2 * HC), bf16), wT=vmem((G, STATE, Tc), bf16),
        values=vmem((Tc, W), bf16), S2=vmem((2 * STATE, W), bf16),
        rr=vmem((G, R, 2 * STATE), bf16), ww=vmem((R, 2 * HC), bf16), yf=vmem((R, W), f32),
        xsend=vmem((z_n, RC, W), i16), xr=vmem((z_n, RC, W), i16),
        zsend=vmem((z_n, RC, W), i16), zr=vmem((z_n, RC, W), i16),
        xsend_f=vmem((z_n, RC, 128), f32), xr_f=vmem((z_n, RC, 128), f32),
        zsend_f=vmem((z_n, RC, 128), f32), zr_f=vmem((z_n, RC, 128), f32),
        mixed=vmem((RC, W), f32), starts=vmem((RC, W), f32), carried=vmem((RC, W), f32),
        normed=vmem((RC, W), bf16), nrm=vmem((2 * chips, RC, W), bf16),
        pt=vmem((tp, R, blk), f32), pr=vmem((R, blk), f32),
        hid=vmem((total, R, blk), bf16), feat=vmem((R, 4 * tp * blk), bf16), sq=vmem((2, 1, R), f32),
        sq_z=vmem((z_n, 1, R), f32), sq_p=vmem((4 * tp, 1, R), f32),
        logit=vmem((R, hw.shape[1]), f32), stat=vmem((4, R), f32), every=vmem((total, 4, R), f32),
        oww=vmem(ow.shape, bf16), hww=vmem(hw.shape, bf16),
        own=dma((18,)), core_send=dma((5,)), core_recv=dma((5,)),
        edge_send=dma((2, 3)), edge_recv=dma((3,)),
        r_send=dma(()), r_recv=dma(()), pd_send=dma(()), pd_recv=dma(()),
        x_send=dma((2, z_n)), x_recv=dma((2, z_n)), z_send=dma((2, z_n)), z_recv=dma((2, z_n)),
        res_send=dma(()), res_recv=dma(()), g_send=dma((2,)), sq_send=dma((2,)), sq_recv=dma((2,)), t_send=dma(()), t_recv=dma(()),
        st_send=dma(()), st_recv=dma(()), ready=pltpu.SemaphoreType.REGULAR,
    )
    many = [("gather1", [dma((z_n,))] * 2 + [dma((2, z_n))])]
    many.append(("gather2", [dma((z_n,))] * 2 + [dma((2, z_n)), dma((4, z_n))]))
    names = list(inputs) + ["out"] + list(scratch)
    groups = [(name, len(sems)) for name, sems in many]
    extra = [sem for _, sems in many for sem in sems]

    def run(*refs):
        plain, rest = list(refs[: len(names)]), list(refs[len(names) :])
        for _, size in groups:
            plain.append(tuple(rest[:size]))
            rest = rest[size:]
        one_kernel(n, tp, names + [name for name, _ in groups], *plain)

    both = pl.pallas_call(
        run,
        out_shape=jax.ShapeDtypeStruct((2, R), f32),
        in_specs=[ANY] * len(inputs),
        out_specs=VMEM,
        scratch_shapes=list(scratch.values()) + extra,
        compiler_params=pltpu.CompilerParams(
            collective_id=5, has_side_effects=True, vmem_limit_bytes=58 * 1024 * 1024
        ),
    )(*inputs.values())
    return both[0], both[1]


def body(
    inner_input,
    gate_input,
    state_inputs,
    step_size,
    resets,
    decay_rate,
    skip_gain,
    conv_inner,
    conv_state,
    norm_gain,
    out_weight,
    residual,
    final_gain,
    head_weight,
    scored,
    targets,
    policy_logprob,
):
    f32 = jnp.float32
    n, tp = lax.axis_size("ctx"), lax.axis_size("tp")
    c, t = lax.axis_index("ctx"), lax.axis_index("tp")
    groups_here, blk = state_inputs.shape[2] // STATE, out_weight.shape[1] // tp
    if n % 4 == 0 and tp == 2 and groups_here % 2 == 0 and blk == 128:
        return fused(
            n, tp, inner_input, gate_input, state_inputs, step_size, resets, decay_rate, skip_gain,
            conv_inner, conv_state, norm_gain, out_weight, residual, final_gain, head_weight,
            scored, targets, policy_logprob,
        )
    taps = conv_inner.shape[0]
    rows_here = inner_input.shape[0]
    q_count = state_inputs.shape[2] // STATE
    z_count = n // q_count
    z, q = c // q_count, c % q_count
    picked_rows = scored.shape[0]
    local_rows = scored - c * rows_here
    here = jnp.arange(rows_here, dtype=jnp.int32)
    pick = (local_rows[:, None] == here[None, :]).astype(jnp.bfloat16)
    gate_rows = jnp.dot(pick, gate_input, preferred_element_type=f32).astype(jnp.bfloat16)
    res_rows = jnp.dot(pick, residual, preferred_element_type=f32).astype(jnp.bfloat16)
    meta = jnp.zeros((8, rows_here), f32)
    meta = meta.at[0].set(resets.astype(f32))
    meta = meta.at[1, :picked_rows].set(local_rows.astype(f32))
    xs, ss, ds, gs, ms, x_edge, s_edge, m_edge, res_all = spread(
        n, tp, q_count, inner_input, state_inputs, step_size, gate_rows, meta, res_rows
    )
    tokens = q_count * rows_here
    width = xs.shape[2]
    heads = ds.shape[1]
    rows = q_count * picked_rows
    gate = gs.reshape(rows, width)
    flags = ms[:, 0].reshape(tokens)
    spots = ms[:, 1, :picked_rows] + (jnp.arange(q_count) * rows_here).astype(f32)[:, None]
    spots = spots.reshape(rows, 1).astype(jnp.int32)
    margin = taps - 1
    f_tail = jnp.where(z > 0, m_edge[0, rows_here - margin :], 0.0)
    clear = 1.0 - jnp.concatenate([f_tail, flags])
    keeping = [jnp.ones((tokens,), f32)]
    for offset in range(1, taps):
        keeping.append(keeping[-1] * clear[margin - offset + 1 : margin - offset + 1 + tokens])
    keeps = jnp.pad(jnp.stack(keeping), ((0, -taps % 8), (0, 0)))
    normed = middle(
        xs, x_edge, ss, s_edge, keeps, ds, jnp.broadcast_to(flags[None], (8, tokens)), spots, gate,
        conv_inner, conv_state, decay_rate.reshape(q_count, heads, 1),
        skip_gain.reshape(q_count, 1, heads), norm_gain[None], q_count, z_count,
    )
    res = res_all.reshape(z_count * rows, -1)
    return tail(
        normed, out_weight, head_weight, res, final_gain, targets, policy_logprob,
        n, tp, q_count, z_count,
    )


def solution(mesh):
    return jax.shard_map(
        body,
        mesh=mesh,
        in_specs=(
            P("ctx", "tp"),
            P("ctx", "tp"),
            P(None, "ctx", "tp"),
            P("tp", "ctx"),
            P("ctx"),
            P("tp"),
            P("tp"),
            P(None, "tp"),
            P(None, None, "tp"),
            P("tp"),
            P("tp", "ctx"),
            P("ctx", "tp"),
            P(),
            P(None, ("ctx", "tp")),
            P("ctx"),
            P(),
            P(),
        ),
        out_specs=(P(), P()),
        check_vma=False,
    )
```

```python
import functools
import jax
import jax.numpy as jnp
from jax import lax
from jax.experimental import pallas as pl
from jax.experimental.pallas import tpu as pltpu
from jax.sharding import PartitionSpec as P

HEAD_DIM = 64
STATE = 128
EDGE = 16
LEVELS = 32767.0
TINY = 1e-30

epsilon = 1e-05
precise = lax.Precision.HIGHEST
MESH = pl.DeviceIdType.MESH
VMEM = pl.BlockSpec(memory_space=pltpu.VMEM)
ANY = pl.BlockSpec(memory_space=pl.ANY)


def remote(src, dst, send, recv, device):
    return pltpu.make_async_remote_copy(
        src_ref=src, dst_ref=dst, send_sem=send, recv_sem=recv, device_id=device, device_id_type=MESH
    )


def greet(devices):
    barrier = pltpu.get_barrier_semaphore()
    for device in devices:
        pl.semaphore_signal(barrier, inc=1, device_id=device, device_id_type=MESH)
    pl.semaphore_wait(barrier, len(devices))


def spread_kernel(n, tp, q_count, z_count, x_ref, s_ref, d_ref, g_ref, m_ref, r_ref,
                  xo, so, do, go, mo, xh, sh, mh, ro,
                  send, recv, own, edge_send, edge_recv, res_send, res_recv):
    c, t = lax.axis_index("ctx"), lax.axis_index("tp")
    z, q = c // q_count, c % q_count
    total = n * tp
    me = c * tp + t
    barrier = pltpu.get_barrier_semaphore()

    def hello(k, carry):
        other = (me + k) % total
        pl.semaphore_signal(
            barrier, inc=1, device_id=(other // tp, other % tp), device_id_type=MESH
        )
        return carry

    lax.fori_loop(1, total, hello, 0)
    pl.semaphore_wait(barrier, total - 1)
    width = xo.shape[2]
    heads = do.shape[1]
    rows = x_ref.shape[0]

    def cols(ref, k, size):
        return ref.at[:, pl.ds(pl.multiple_of(k * size, 128), size)]

    def parts(k):
        return (
            cols(x_ref, k, width),
            s_ref.at[:, :, pl.ds(pl.multiple_of(k * STATE, 128), STATE)],
            d_ref.at[pl.ds(pl.multiple_of(k * heads, 8), heads), :],
            cols(g_ref, k, width),
            m_ref,
        )

    def slots(k):
        return (xo.at[k], so.at[k], do.at[k], go.at[k], mo.at[k])

    started = []
    tail = pl.ds(rows - EDGE, EDGE)
    next_z = jnp.minimum(z + 1, z_count - 1)

    def edges(k, dst_c):
        wide = pl.ds(pl.multiple_of(k * width, 128), width)
        thin = pl.ds(pl.multiple_of(k * STATE, 128), STATE)
        triple = ((x_ref.at[tail, wide], xh), (s_ref.at[:, tail, thin], sh), (m_ref, mh))
        return [
            remote(a, b, edge_send.at[k, i], edge_recv.at[i], (dst_c, t))
            for i, (a, b) in enumerate(triple)
        ]

    sends_edge = (q == q_count - 1) & (z < z_count - 1)
    gets_edge = z > 0
    if z_count > 1:
        @pl.when(sends_edge)
        def _():
            for k in range(q_count):
                for copy in edges(k, (z + 1) * q_count + k):
                    copy.start()

    for d in range(1, q_count):
        k = (q + d) % q_count
        for i, (a, b) in enumerate(zip(parts(k), slots(q))):
            copy = remote(a, b, send.at[d - 1, i], recv.at[d - 1, i], (z * q_count + k, t))
            copy.start()
            started.append(copy)
    per = n // tp

    def res_copy(j, to_t):
        return remote(
            r_ref.at[j], ro.at[c],
            res_send.at[j * tp + to_t], res_recv.at[c], (t * per + j, to_t)
        )

    for j in range(per):
        for to_t in range(tp):
            mine = (t * per + j == c) & (to_t == t)

            @pl.when(jnp.logical_not(mine))
            def _():
                res_copy(j, to_t).start()

            @pl.when(mine)
            def _():
                pltpu.make_async_copy(r_ref.at[j], ro.at[c], res_recv.at[c]).start()
    locals_ = [
        pltpu.make_async_copy(a, b, own.at[i]) for i, (a, b) in enumerate(zip(parts(q), slots(q)))
    ]
    for copy in locals_:
        copy.start()
    for copy in locals_:
        copy.wait()
    for j in range(per):
        for to_t in range(tp):
            mine = (t * per + j == c) & (to_t == t)

            @pl.when(jnp.logical_not(mine))
            def _():
                res_copy(j, to_t).wait_send()
    for k in range(n):
        pltpu.make_async_copy(ro.at[k], ro.at[k], res_recv.at[k]).wait()
    for copy in started:
        copy.wait_send()
    for d in range(1, q_count):
        k = (q + q_count - d) % q_count
        for i, (a, b) in enumerate(zip(parts(q), slots(k))):
            remote(a, b, send.at[d - 1, i], recv.at[d - 1, i], (z * q_count + k, t)).wait_recv()
    if z_count > 1:
        @pl.when(sends_edge)
        def _():
            for k in range(q_count):
                for copy in edges(k, (z + 1) * q_count + k):
                    copy.wait_send()

        @pl.when(gets_edge)
        def _():
            for i, ref in enumerate((xh, sh, mh)):
                pltpu.make_async_copy(ref, ref, edge_recv.at[i]).wait()


def spread(n, tp, q_count, x, s, d, g, m, r):
    z_count = n // q_count
    rows, all_width = x.shape
    width = all_width // q_count
    heads = d.shape[0] // q_count
    block = r.shape[1] * tp // n
    r = r.reshape(r.shape[0], n // tp, block).transpose(1, 0, 2)
    shape = jax.ShapeDtypeStruct
    outs = (
        shape((q_count, rows, width), x.dtype),
        shape((q_count, 2, rows, STATE), s.dtype),
        shape((q_count, heads, rows), d.dtype),
        shape((q_count, g.shape[0], width), g.dtype),
        shape((q_count,) + m.shape, m.dtype),
        shape((EDGE, width), x.dtype),
        shape((2, EDGE, STATE), s.dtype),
        shape(m.shape, m.dtype),
        shape((n,) + r.shape[1:], r.dtype),
    )
    dma = pltpu.SemaphoreType.DMA
    peers = max(q_count - 1, 1)
    return pl.pallas_call(
        functools.partial(spread_kernel, n, tp, q_count, z_count),
        out_shape=outs,
        in_specs=[ANY, ANY, ANY, VMEM, VMEM, VMEM],
        out_specs=[VMEM] * len(outs),
        scratch_shapes=[
            dma((peers, 5)), dma((peers, 5)), dma((5,)), dma((q_count, 3)), dma((3,)),
            dma((n,)), dma((n,)),
        ],
        compiler_params=pltpu.CompilerParams(collective_id=0, has_side_effects=True),
    )(x, s, d, g, m, r)


def staged(kernel, skip, count, shapes):
    def run(*refs):
        ins, rest, held, sems = (
            refs[:count], refs[count : -len(shapes) - 1], refs[-len(shapes) - 1 : -1], refs[-1]
        )
        held = iter(held)
        views, copies = [], []
        for i, ref in enumerate(ins):
            if i in skip:
                views.append(ref)
                continue
            local = next(held)
            copy = pltpu.make_async_copy(ref, local, sems.at[len(copies)])
            copy.start()
            copies.append(copy)
            views.append(local)
        for copy in copies:
            copy.wait()
        kernel(*views, *rest)

    extra = [pltpu.VMEM(a.shape, a.dtype) for a in shapes]
    return run, extra + [pltpu.SemaphoreType.DMA((len(shapes),))]


def mid_kernel(q_count, z_count, x_ref, xe_ref, s_ref, se_ref, k_ref, d_ref, f_ref, spot_ref,
               gate_ref, tx_ref, ts_ref, rate_ref, skip_ref, gain_ref, out,
               pad_x, pad_s, values, writes, reads, mine_r, all_r, y, far, pd, far_pd, mixed, carried,
               r_send, r_recv, y_send, y_recv, p_send, p_recv):
    f32, bf16 = jnp.float32, jnp.bfloat16
    c, t = lax.axis_index("ctx"), lax.axis_index("tp")
    z, q = c // q_count, c % q_count
    barrier = pltpu.get_barrier_semaphore()

    def peer(d):
        return (((z + d) % z_count) * q_count + q, t)

    for d in range(1, z_count):
        pl.semaphore_signal(barrier, inc=1, device_id=peer(d), device_id_type=MESH)
    tokens, width = values.shape
    piece = tokens // q_count
    heads = d_ref.shape[1]
    rows = mine_r.shape[0]
    taps = tx_ref.shape[0]
    has_edge = (z > 0).astype(f32)
    keep = k_ref[...].T

    def filtered(pad, kernel, start, target):
        total = jnp.zeros((piece, pad.shape[1]), f32)
        for off in range(taps):
            total = total + (
                keep[start : start + piece, off : off + 1]
                * kernel[off : off + 1]
                * pad[EDGE - off + start : EDGE - off + start + piece, :]
            )
        target[start : start + piece, :] = jax.nn.silu(total).astype(bf16)

    thin = pl.ds(pl.multiple_of(q * STATE, 128), STATE)
    for which, target in ((1, reads), (0, writes)):
        edge = se_ref[which].astype(f32)
        pad_s[:EDGE, :] = jnp.where(has_edge > 0.0, edge, 0.0)
        for k in range(q_count):
            pad_s[EDGE + k * piece : EDGE + (k + 1) * piece, :] = s_ref[k, which].astype(f32)
        kernel = ts_ref[which, :, thin]
        for k in range(q_count):
            filtered(pad_s, kernel, k * piece, target)
    spots = spot_ref[...]
    lanes = lax.broadcasted_iota(jnp.int32, (rows, tokens), 1)
    pick_f = jnp.where(spots == lanes, 1.0, 0.0)
    pick = pick_f.astype(bf16)
    mine_r[...] = jnp.dot(pick, reads[...], preferred_element_type=f32).astype(bf16)
    pl.semaphore_wait(barrier, z_count - 1)
    sent = []
    for d in range(1, z_count):
        copy = remote(mine_r, all_r.at[z], r_send.at[d], r_recv.at[d], peer(d))
        copy.start()
        sent.append(copy)
    all_r[z] = mine_r[...]
    wide = pl.ds(pl.multiple_of(q * width, 128), width)
    kernel_x = tx_ref[:, wide]
    pad_x[:EDGE, :] = jnp.where(has_edge > 0.0, xe_ref[...].astype(f32), 0.0)
    for k in range(q_count):
        pad_x[EDGE + k * piece : EDGE + (k + 1) * piece, :] = x_ref[k].astype(f32)
    for k in range(q_count):
        filtered(pad_x, kernel_x, k * piece, values)
    steps = jnp.concatenate([d_ref[k] for k in range(q_count)], axis=1)
    lower = jnp.where(
        lax.broadcasted_iota(jnp.int32, (tokens, tokens), 0)
        <= lax.broadcasted_iota(jnp.int32, (tokens, tokens), 1),
        1.0, 0.0,
    )
    runs = jnp.concatenate([-rate_ref[q] * steps, f_ref[...]], axis=0)
    sums = jnp.dot(runs, lower, precision=precise, preferred_element_type=f32)
    cumulated = sums[:heads]
    segment = sums[heads : heads + 1]
    at_rows = lax.dot_general(
        pick_f, sums, (((1,), (1,)), ((), ())), precision=precise, preferred_element_type=f32
    )
    row_cum = at_rows[:, :heads]
    row_seg = at_rows[:, heads : heads + 1]
    last = cumulated[:, tokens - 1 : tokens]
    last_seg = segment[:, tokens - 1 : tokens]
    to_end = jnp.exp(last - cumulated) * jnp.where(segment == last_seg, 1.0, 0.0) * steps
    spread_heads = jnp.where(
        lax.broadcasted_iota(jnp.int32, (heads, width), 0)
        == lax.broadcasted_iota(jnp.int32, (heads, width), 1) // HEAD_DIM,
        1.0, 0.0,
    )

    def widen(a):
        return jnp.dot(a, spread_heads, precision=precise, preferred_element_type=f32)

    plane = jnp.broadcast_to(jnp.exp(last) * jnp.where(last_seg == 0.0, 1.0, 0.0), (heads, 128))
    pd[...] = widen(plane.T[:8])
    weighted = values[...].astype(f32) * widen(to_end.T)
    state = jnp.dot(
        writes[...].astype(f32).T, weighted, precision=precise, preferred_element_type=f32
    )
    for d in range(1, z_count):
        here = all_r.at[(z + z_count - d) % z_count]
        remote(mine_r, here, r_send.at[d], r_recv.at[d], peer(d)).wait_recv()
    for k in range(z_count):
        y[k] = jnp.dot(
            all_r[k].astype(f32), state, precision=precise, preferred_element_type=f32
        )

    def outgoing(d):
        return (
            remote(y.at[(z + d) % z_count], far.at[z], y_send.at[d], y_recv.at[d], peer(d)),
            remote(pd, far_pd.at[z], p_send.at[d], p_recv.at[d], peer(d)),
        )

    for d in range(1, z_count):
        @pl.when(z + d < z_count)
        def _():
            for copy in outgoing(d):
                copy.start()
    scores = lax.dot_general(
        mine_r[...], writes[...], (((1,), (1,)), ((), ())), preferred_element_type=f32
    )
    causal = (spots >= lanes) & (row_seg == segment)
    half = lax.broadcasted_iota(jnp.int32, (rows, 2 * HEAD_DIM), 1) < HEAD_DIM
    for pair in range(heads // 2):
        mixes = []
        for h in (2 * pair, 2 * pair + 1):
            gaps = row_cum[:, h : h + 1] - cumulated[h : h + 1]
            decay = jnp.where(causal, jnp.exp(jnp.where(causal, gaps, 0.0)), 0.0)
            mixes.append(scores * decay * steps[h : h + 1])
        span = slice(pair * 2 * HEAD_DIM, (pair + 1) * 2 * HEAD_DIM)
        product = jnp.dot(
            jnp.concatenate(mixes, axis=0), values[:, span].astype(f32),
            precision=precise, preferred_element_type=f32,
        )
        mixed[:, span] = jnp.where(half, product[:rows], product[rows:])
    own_values = jnp.dot(pick, values[...], preferred_element_type=f32)
    from_start = jnp.exp(row_cum) * jnp.where(row_seg == 0.0, 1.0, 0.0)
    factors = widen(
        jnp.concatenate([from_start, jnp.broadcast_to(skip_ref[q], (8, heads))], axis=0)
    )
    gate = jax.nn.silu(gate_ref[...].astype(f32))
    carried[...] = jnp.zeros((rows, width), f32)
    for d in range(z_count - 1, 0, -1):
        @pl.when(z - d >= 0)
        def _():
            k = z - d + jnp.where(z - d < 0, z_count, 0)
            here, there = far.at[k], far_pd.at[k]
            remote(here, here, y_send.at[d], y_recv.at[d], peer(d)).wait_recv()
            remote(there, there, p_send.at[d], p_recv.at[d], peer(d)).wait_recv()
            carried[...] = carried[...] * far_pd[k][0:1] + far[k]
    gated = (
        mixed[...] + carried[...] * factors[:rows] + factors[rows : rows + 1] * own_values
    ) * gate
    scale = lax.rsqrt(jnp.mean(gated * gated, axis=1, keepdims=True) + epsilon)
    out[...] = (gated * scale * gain_ref[:, wide]).astype(bf16)
    for copy in sent:
        copy.wait_send()
    for d in range(1, z_count):
        @pl.when(z + d < z_count)
        def _():
            for copy in outgoing(d):
                copy.wait_send()


def middle(xs, x_edge, ss, s_edge, keeps, steps, flags, spots, gate, taps_x, taps_s, rate, skip, gain,
           q_count, z_count):
    f32, bf16 = jnp.float32, jnp.bfloat16
    tokens = steps.shape[0] * steps.shape[2]
    rows, width = gate.shape
    operands = (
        xs, x_edge, ss, s_edge, keeps, steps, flags, spots, gate, taps_x, taps_s, rate, skip, gain
    )
    run, extra = staged(
        functools.partial(mid_kernel, q_count, z_count), (), len(operands), operands
    )
    dma, vmem = pltpu.SemaphoreType.DMA, pltpu.VMEM
    return pl.pallas_call(
        run,
        out_shape=jax.ShapeDtypeStruct((rows, width), bf16),
        in_specs=[ANY] * len(operands),
        out_specs=VMEM,
        scratch_shapes=[
            vmem((EDGE + tokens, width), f32),
            vmem((EDGE + tokens, STATE), f32),
            vmem((tokens, width), bf16),
            vmem((tokens, STATE), bf16),
            vmem((tokens, STATE), bf16),
            vmem((rows, STATE), bf16),
            vmem((z_count, rows, STATE), bf16),
            vmem((z_count, rows, width), f32),
            vmem((z_count, rows, width), f32),
            vmem((8, width), f32),
            vmem((z_count, 8, width), f32),
            vmem((rows, width), f32),
            vmem((rows, width), f32),
        ] + [dma((z_count,))] * 6 + extra,
        compiler_params=pltpu.CompilerParams(
            collective_id=1, has_side_effects=True, vmem_limit_bytes=58 * 1024 * 1024
        ),
    )(*operands)


def tail_kernel(n, tp, q_count, z_count, n_ref, ow_ref, hw_ref, r_ref, g_ref, t_ref, p_ref, out,
                ow, hw, nrm, both, hid, feat, logit, stat, every,
                own, tp_send, tp_recv, st_send, st_recv, *gather_sems):
    c, t = lax.axis_index("ctx"), lax.axis_index("tp")
    z, q = c // q_count, c % q_count
    total = n * tp
    me = c * tp + t
    get_ow = pltpu.make_async_copy(ow_ref, ow, own.at[0])
    get_hw = pltpu.make_async_copy(hw_ref, hw, own.at[1])
    barrier = pltpu.get_barrier_semaphore()

    def device(k):
        return (k // tp, k % tp)

    def hello(d, carry):
        pl.semaphore_signal(
            barrier, inc=1, device_id=device((me + d) % total), device_id_type=MESH
        )
        return carry

    lax.fori_loop(1, total, hello, 0)
    get_ow.start()
    get_hw.start()
    pl.semaphore_wait(barrier, total - 1)
    core_n = 2 if q_count % 2 == 0 else 1
    x_n = q_count // core_n
    x, core = q // core_n, q % core_n

    def at_x(k):
        return (z * q_count + k * core_n + core, t)

    at_core = (z * q_count + x * core_n + (core_n - 1) - core, t)

    def gathered(slot, mine, sems):
        z_send, z_recv, x_send, x_recv, c_send, c_recv = sems
        sent = []

        def push(copy):
            copy.start()
            sent.append(copy)

        def to_x(ref, dst, d):
            for e in range(1, x_n):
                push(remote(ref, dst, x_send.at[e - 1, d], x_recv.at[e - 1, d], at_x((x + e) % x_n)))

        def to_core(ref, dst, e, d):
            if core_n > 1:
                push(remote(ref, dst, c_send.at[e, d], c_recv.at[e, d], at_core))

        home = slot(q, z)
        for d in range(1, z_count):
            push(remote(mine, home, z_send.at[d], z_recv.at[d], (((z + d) % z_count) * q_count + q, t)))
        to_x(mine, home, 0)
        to_core(mine, home, 0, 0)
        for d in range(z_count):
            k = (z + z_count - d) % z_count
            if d:
                here = slot(q, k)
                remote(here, here, z_send.at[d], z_recv.at[d], at_core).wait_recv()
                to_x(here, here, d)
                to_core(here, here, 0, d)
            for e in range(1, x_n):
                here = slot(((x + x_n - e) % x_n) * core_n + core, k)
                remote(here, here, x_send.at[e - 1, d], x_recv.at[e - 1, d], at_core).wait_recv()
                to_core(here, here, e, d)
        if core_n > 1:
            for d in range(z_count):
                k = (z + z_count - d) % z_count
                for e in range(x_n):
                    here = slot(((x + x_n - e) % x_n) * core_n + 1 - core, k)
                    remote(here, here, c_send.at[e, d], c_recv.at[e, d], at_core).wait_recv()
        return sent

    rows = n_ref.shape[0]
    width = n_ref.shape[1]

    def normed_slot(a, b):
        return nrm.at[a, b]

    pending = gathered(normed_slot, n_ref, gather_sems[:6])
    nrm[q, z] = n_ref[...]
    get_ow.wait()
    partial = jnp.zeros(both.shape[1:], jnp.float32)
    for k in range(q_count):
        partial = partial + jnp.dot(
            nrm[k].reshape(z_count * rows, width),
            ow[k * width : (k + 1) * width, :],
            preferred_element_type=jnp.float32,
        )
    both[t] = partial
    tp_copies = []
    for d in range(1, tp):
        copy = remote(both.at[t], both.at[t], tp_send.at[d], tp_recv.at[d], (c, (t + d) % tp))
        copy.start()
        tp_copies.append(copy)
    for d in range(1, tp):
        here = both.at[(t + tp - d) % tp]
        remote(here, here, tp_send.at[d], tp_recv.at[d], (c, (t + d) % tp)).wait_recv()
    summed = both[0]
    for k in range(1, tp):
        summed = summed + both[k]
    hid[q, z] = (r_ref[...].astype(jnp.float32) + summed).astype(jnp.bfloat16)

    def hidden_slot(a, b):
        return hid.at[a, b]

    pending = pending + tp_copies + gathered(hidden_slot, hid.at[q, z], gather_sems[6:])
    block = hid.shape[3]
    all_rows = hid.shape[2]
    squares = jnp.zeros((all_rows, 1), jnp.float32)
    for k in range(z_count):
        for a in range(q_count):
            piece = hid[a, k].astype(jnp.float32)
            squares = squares + jnp.sum(piece * piece, axis=1, keepdims=True)
    inverse = lax.rsqrt(squares / (n * block) + epsilon)
    for k in range(z_count):
        for a in range(q_count):
            first = (k * q_count + a) * block
            span = slice(first, first + block)
            feat[:, span] = (
                hid[a, k].astype(jnp.float32) * inverse * g_ref[:, span]
            ).astype(jnp.bfloat16)
    get_hw.wait()
    vocab = hw.shape[1]
    tile = min(256, vocab)

    def one_tile(i, carry):
        cols = pl.ds(pl.multiple_of(i * tile, 128), tile)
        logit[:, cols] = jnp.dot(feat[...], hw[:, cols], preferred_element_type=jnp.float32)
        return carry

    lax.fori_loop(0, vocab // tile, one_tile, 0)
    values = logit[...]
    top = jnp.max(values, axis=1, keepdims=True)
    added = jnp.sum(jnp.exp(values - top), axis=1, keepdims=True)
    column = t_ref[...] - me * vocab
    places = lax.broadcasted_iota(jnp.int32, values.shape, 1)
    hit = jnp.sum(jnp.where(places == column, values, 0.0), axis=1, keepdims=True)
    lane = lax.broadcasted_iota(jnp.int32, (all_rows, 128), 1)
    packed = jnp.where(lane == 0, top, jnp.where(lane == 1, added, jnp.where(lane == 2, hit, 0.0)))
    turned = packed.T[:8]
    stat[...] = turned

    def go(d, carry):
        remote(
            stat, every.at[me], st_send.at[d], st_recv.at[d], device((me + d) % total)
        ).start()
        return carry

    lax.fori_loop(1, total, go, 0)
    every[me] = turned

    def done(d, carry):
        here = every.at[(me + total - d) % total]
        copy = remote(stat, here, st_send.at[d], st_recv.at[d], device((me + d) % total))
        copy.wait_send()
        copy.wait_recv()
        return carry

    lax.fori_loop(1, total, done, 0)
    for copy in pending:
        copy.wait_send()
    found = every[...]
    tops = found[:, 0, :]
    row_top = jnp.max(tops, axis=0, keepdims=True)
    full = jnp.sum(found[:, 1, :] * jnp.exp(tops - row_top), axis=0, keepdims=True)
    picked = jnp.sum(found[:, 2, :], axis=0, keepdims=True)
    log_prob = picked - row_top - jnp.log(full)
    out[0:1, :] = log_prob
    out[1:2, :] = 0.5 * jnp.square(log_prob - p_ref[...])


def tail(normed, out_weight, head_weight, res, gain, targets, policy, n, tp, q_count, z_count):
    dma = pltpu.SemaphoreType.DMA
    total = n * tp
    rows, width = normed.shape
    all_rows = z_count * rows
    block = out_weight.shape[1]
    core_n = 2 if q_count % 2 == 0 else 1
    x_n = q_count // core_n
    vmem = pltpu.VMEM
    bf16, f32 = jnp.bfloat16, jnp.float32
    e_n = max(x_n - 1, 1)
    sems = [
        dma((z_count,)), dma((z_count,)), dma((e_n, z_count)), dma((e_n, z_count)),
        dma((x_n, z_count)), dma((x_n, z_count)),
    ]
    operands = (
        normed, out_weight, head_weight, res, gain[None], targets[:, None], policy[None]
    )
    run, extra = staged(
        functools.partial(tail_kernel, n, tp, q_count, z_count), (1, 2), len(operands),
        operands[:1] + operands[3:],
    )
    result = pl.pallas_call(
        run,
        out_shape=jax.ShapeDtypeStruct((2, all_rows), f32),
        in_specs=[ANY] * len(operands),
        out_specs=VMEM,
        scratch_shapes=[
            vmem(out_weight.shape, bf16),
            vmem(head_weight.shape, bf16),
            vmem((q_count, z_count, rows, width), bf16),
            vmem((tp, all_rows, block), f32),
            vmem((q_count, z_count, all_rows, block), bf16),
            vmem((all_rows, n * block), bf16),
            vmem((all_rows, head_weight.shape[1]), f32),
            vmem((8, all_rows), f32),
            vmem((total, 8, all_rows), f32),
            dma((2,)), dma((tp,)), dma((tp,)), dma((total,)), dma((total,)),
        ] + sems + sems + extra,
        compiler_params=pltpu.CompilerParams(
            collective_id=3, has_side_effects=True, vmem_limit_bytes=58 * 1024 * 1024
        ),
    )(*operands)
    return result[0], result[1]


def halves(a):
    hi = a.astype(jnp.bfloat16)
    return hi, (a - hi.astype(jnp.float32)).astype(jnp.bfloat16)


def thirds(a):
    hi = a.astype(jnp.bfloat16)
    rest = a - hi.astype(jnp.float32)
    mid = rest.astype(jnp.bfloat16)
    return hi, mid, (rest - mid.astype(jnp.float32)).astype(jnp.bfloat16)


def column(row, first, count):
    lanes = row.shape[1]
    spot = lax.broadcasted_iota(jnp.int32, (count, lanes), 0) + first
    hit = lax.broadcasted_iota(jnp.int32, (count, lanes), 1) == spot
    return jnp.sum(jnp.where(hit, jnp.broadcast_to(row, (count, lanes)), 0.0), axis=1, keepdims=True)


def one_kernel(n, tp, *refs):
    names, refs = refs[0], refs[1:]
    r = dict(zip(names, refs))
    f32, bf16 = jnp.float32, jnp.bfloat16
    c, t = lax.axis_index("ctx"), lax.axis_index("tp")
    total = n * tp
    me = c * tp + t
    chips = n // 2
    z_n = chips // 2
    k, p = c % 2, c // 2
    x, z = p % 2, p // 2

    def dev(z_, x_, k_):
        return ((z_ * 2 + x_) * 2 + k_, t)

    core_peer, x_peer, y_peer = dev(z, x, 1 - k), dev(z, 1 - x, k), (c, 1 - t)
    T, C = r["x"].shape
    W = C // 2
    S = r["s"].shape[2] // 2
    G = S // STATE
    GW = W // G
    H = r["d"].shape[0]
    HC = H // 2
    Tc = 2 * T
    r8 = r["scored"].shape[0]
    RC = 2 * r8
    R = chips * RC
    taps = r["tx"].shape[0]
    blk = r["ow"].shape[1] // tp
    D = n * tp * blk
    V = r["hw"].shape[1]
    per = n // tp

    barrier = pltpu.get_barrier_semaphore()

    plane_peers = [
        (((z * 2 + (x + a) % 2) * 2 + (k + b) % 2), (t + e) % tp)
        for a in range(2) for b in range(2) for e in range(tp) if a + b + e
    ]
    z_peers = [dev((z + d) % z_n, x, k) for d in range(1, z_n)]

    def greet_one(sem, device):
        pl.semaphore_signal(sem, inc=1, device_id=device, device_id_type=MESH)

    for device in z_peers + plane_peers:
        greet_one(barrier, device)
    sends_up = (x == 1) & (k == 1) & (z < z_n - 1)

    @pl.when((x == 0) & (z > 0))
    def _():
        greet_one(barrier, dev(z - 1, 1, 1))

    def lanes(a, size):
        return pl.ds(pl.multiple_of(a * size, 128), size)

    local = {}

    def fetch(name, src, dst):
        copy = pltpu.make_async_copy(src, dst, r["own"].at[len(local)])
        local[name] = copy
        copy.start()

    def arrived(ref, sem):
        pltpu.make_async_copy(ref, ref, sem).wait()

    sent = []

    def push(copy, when=None):
        sent.append((copy, when))
        if when is None:
            copy.start()
        else:
            pl.when(when)(copy.start)

    fetch("resets", r["resets"], r["resv"])
    fetch("scored", r["scored"], r["spot"])
    fetch("g", r["g"], r["gv"])
    fetch("res", r["res"], r["rv"])
    fetch("s", r["s"].at[:, :, lanes(k, S)], r["sc"].at[k])
    fetch("ts", r["ts"].at[:, :, lanes(k, S)], r["tsv"])
    half_heads = pl.ds(pl.multiple_of(k * HC, 8), HC)
    fetch("d", r["d"].at[half_heads], r["dc"].at[k])
    fetch("rate", r["rate"], r["ratev"])
    fetch("x", r["x"].at[:, lanes(k, W)], r["xc"].at[k])
    fetch("tx", r["tx"].at[:, lanes(k, W)], r["txv"])
    fetch("skip", r["skip"], r["skipv"])
    fetch("gain", r["gain"].at[:, lanes(k, W)], r["gainv"])
    fetch("fg", r["fg"], r["fgv"])
    fetch("tgt", r["tgt"], r["tgtv"])
    fetch("pol", r["pol"], r["polv"])
    fetch("ow", r["ow"], r["oww"])

    first = p == 0

    @pl.when(first)
    def _():
        r["xh"][...] = jnp.zeros(r["xh"].shape, bf16)
        r["sh"][...] = jnp.zeros(r["sh"].shape, bf16)
        r["mh"][...] = jnp.zeros(r["mh"].shape, f32)

    local["resets"].wait()
    local["scored"].wait()
    lane8 = lax.broadcasted_iota(jnp.int32, (8, T), 1)
    row8 = lax.broadcasted_iota(jnp.int32, (8, T), 0)
    places = jnp.zeros((8, T), f32)
    for i in range(r8):
        places = jnp.where(lane8 == i, (r["spot"][i] - c * T).astype(f32), places)
    flags_here = jnp.broadcast_to(r["resv"][...].astype(f32), (8, T))
    r["meta"][...] = jnp.where(row8 == 0, flags_here, places)

    local["g"].wait()
    local["res"].wait()
    own_pick = jnp.where(
        column(r["meta"][1:2], 0, r8) == lax.broadcasted_iota(jnp.int32, (r8, T), 1).astype(f32),
        1.0, 0.0,
    ).astype(bf16)
    r["gc"][k] = jnp.dot(
        own_pick, r["gv"][:, lanes(k, W)], preferred_element_type=f32
    ).astype(bf16)
    r["gsend"][...] = jnp.dot(
        own_pick, r["gv"][:, lanes(1 - k, W)], preferred_element_type=f32
    ).astype(bf16)
    res_rows = jnp.dot(own_pick, r["rv"][...], preferred_element_type=f32).astype(bf16)

    for j in range(per * tp):
        r["rsend"][j] = res_rows[:, j * blk : (j + 1) * blk]

    pl.semaphore_wait(barrier, len(plane_peers) + len(z_peers) + jnp.where(sends_up, 2, 0))
    for device in plane_peers:
        greet_one(r["ready"], device)

    send, recv = r["core_send"], r["core_recv"]
    edge_send, edge_recv = r["edge_send"], r["edge_recv"]
    swap = (
        (r["s"].at[:, :, lanes(1 - k, S)], r["sc"].at[k]),
        (r["meta"], r["mc"].at[k]),
        (r["d"].at[pl.ds(pl.multiple_of((1 - k) * HC, 8), HC)], r["dc"].at[k]),
        (r["x"].at[:, lanes(1 - k, W)], r["xc"].at[k]),
    )
    for i, (a, b) in enumerate(swap):
        push(remote(a, b, send.at[i], recv.at[i], core_peer))
    last_core = (k == 1) & (p < chips - 1)
    tail = pl.ds(T - EDGE, EDGE)
    nxt = jnp.minimum(p + 1, chips - 1)
    for j in range(2):
        triple = (
            (r["s"].at[:, tail, j * S : (j + 1) * S], r["sh"]),
            (r["meta"], r["mh"]),
            (r["x"].at[tail, j * W : (j + 1) * W], r["xh"]),
        )
        for i, (a, b) in enumerate(triple):
            push(remote(a, b, edge_send.at[j, i], edge_recv.at[i], (nxt * 2 + j, t)), last_core)
    r["mc"][k] = r["meta"][...]

    def from_core(i, buf):
        arrived(buf.at[1 - k], recv.at[i])

    def from_edge(i, ref):
        @pl.when(jnp.logical_not(first))
        def _():
            arrived(ref, edge_recv.at[i])

    from_core(1, r["mc"])
    spots = jnp.concatenate(
        [column(r["mc"][j][1:2], 0, r8) + j * T for j in range(2)], axis=0
    ).astype(jnp.int32)
    lane_t = lax.broadcasted_iota(jnp.int32, (RC, Tc), 1)
    pick_f = jnp.where(spots == lane_t, 1.0, 0.0)
    pick = pick_f.astype(bf16)

    chip_flags = jnp.concatenate([r["mc"][0], r["mc"][1]], axis=1)
    local["d"].wait()
    local["rate"].wait()
    from_core(2, r["dc"])
    steps = jnp.concatenate([r["dc"][0], r["dc"][1]], axis=1)
    lower = jnp.where(
        lax.broadcasted_iota(jnp.int32, (Tc, Tc), 0) <= lax.broadcasted_iota(jnp.int32, (Tc, Tc), 1),
        1.0, 0.0,
    ).astype(bf16)
    rate_col = column(r["ratev"][...], k * HC, HC)
    runs = jnp.concatenate([-rate_col * steps, chip_flags], axis=0)
    sums3 = jnp.dot(jnp.concatenate(thirds(runs), axis=0), lower, preferred_element_type=f32)
    count = HC + 8
    sums = sums3[:count] + sums3[count : 2 * count] + sums3[2 * count :]
    cumulated = sums[:HC]
    segment = sums[HC : HC + 1]
    last = cumulated[:, Tc - 1 : Tc]
    last_seg = segment[:, Tc - 1 : Tc]
    plane = jnp.broadcast_to(jnp.exp(last) * jnp.where(last_seg == 0.0, 1.0, 0.0), (HC, 128))
    r["mine_pd"][...] = jnp.concatenate([plane.T[:8], jnp.zeros((8, 128 - HC), f32)], axis=1)
    pl.semaphore_wait(r["ready"], len(plane_peers))
    for d in range(1, chips):
        remote(
            r["mine_pd"], r["all_pd"].at[p], r["pd_send"], r["pd_recv"],
            (((p + d) % chips) * 2 + k, t),
        ).start()
    r["all_pd"][p] = r["mine_pd"][...]
    at_rows = lax.dot_general(
        pick_f, sums, (((1,), (1,)), ((), ())), precision=precise, preferred_element_type=f32
    )
    row_cum = at_rows[:, :HC]
    row_seg = at_rows[:, HC : HC + 1]
    to_end = jnp.exp(last - cumulated) * jnp.where(segment == last_seg, 1.0, 0.0) * steps
    r["te"][...] = jnp.concatenate(halves(to_end.T), axis=1)
    push(remote(r["gsend"], r["gc"].at[k], send.at[4], recv.at[4], core_peer))
    def res_copy(j, to_t):
        i = j * tp + to_t
        return remote(
            r["rsend"].at[i], r["ro"].at[c], r["res_send"], r["res_recv"],
            (t * per + j, to_t),
        )

    for j in range(per):
        for to_t in range(tp):
            mine = (t * per + j == c) & (to_t == t)
            pl.when(jnp.logical_not(mine))(res_copy(j, to_t).start)

            @pl.when(mine)
            def _():
                pltpu.make_async_copy(
                    r["rsend"].at[j * tp + to_t], r["ro"].at[c], r["res_recv"]
                ).start()

    from_edge(1, r["mh"])
    flags = jnp.concatenate([r["mh"][...], chip_flags], axis=1)
    clear = 1.0 - flags
    keeping = jnp.ones((8, 3 * T), f32)
    columns = [keeping]
    for off in range(1, taps):
        shifted = clear if off == 1 else pltpu.roll(clear, off - 1, 1)
        keeping = keeping * shifted
        columns.append(keeping)
    keep_rows = jnp.zeros((8, 3 * T), f32)
    row8w = lax.broadcasted_iota(jnp.int32, (8, 3 * T), 0)
    for off in range(taps):
        keep_rows = jnp.where(row8w == off, jnp.broadcast_to(columns[off][0:1], (8, 3 * T)), keep_rows)
    keep = keep_rows[:, T:].T
    for off in range(1, taps):
        r["kb"][off] = jnp.broadcast_to(keep[:, off : off + 1], (Tc, 128))
    wide_keep = [None] + [r["kb"].at[off] for off in range(1, taps)]

    def filtered(pad, kernel, start, size):
        width = pad.shape[1]
        acc = kernel[0:1] * pad[EDGE + start : EDGE + start + size, :]
        for off in range(1, taps):
            kept = wide_keep[off][start : start + size, :]
            kept = jnp.concatenate([kept] * (width // 128), axis=1)
            acc = acc + kept * (
                kernel[off : off + 1] * pad[EDGE - off + start : EDGE - off + start + size, :]
            )
        return jax.nn.silu(acc).astype(bf16)

    local["s"].wait()
    local["ts"].wait()
    from_core(0, r["sc"])
    from_edge(0, r["sh"])
    pad = r["pad"]
    band = 64
    for which, target in ((1, r["reads"]), (0, r["writes"])):
        for g in range(G):
            cols = slice(g * STATE, (g + 1) * STATE)
            pad_s = r["pad_s"]
            pad_s[:EDGE, :] = r["sh"][which, :, cols].astype(f32)
            for j in range(2):
                pad_s[EDGE + j * T : EDGE + (j + 1) * T, :] = r["sc"][j, which, :, cols].astype(f32)
            kernel = r["tsv"][which, :, cols]
            for b in range(Tc // band):
                target[b * band : (b + 1) * band, cols] = filtered(pad_s, kernel, b * band, band)
        if which == 1:
            r["mine_r"][...] = jnp.dot(
                pick, r["reads"][...], preferred_element_type=f32
            ).astype(bf16)
            for d in range(1, chips):
                remote(
                    r["mine_r"], r["all_r"].at[p], r["r_send"], r["r_recv"],
                    (((p + d) % chips) * 2 + k, t),
                ).start()
            r["all_r"][p] = r["mine_r"][...]

    for g in range(G):
        r["wT"][g] = r["writes"][:, g * STATE : (g + 1) * STATE].astype(f32).T.astype(bf16)

    chunk = min(1024, GW)

    def spread_cols(j, size, offset):
        head = lax.broadcasted_iota(jnp.int32, (size, chunk), 0) % (size // 2)
        lane = lax.broadcasted_iota(jnp.int32, (size, chunk), 1)
        return jnp.where(head == offset + (j * chunk + lane) // HEAD_DIM, 1.0, 0.0).astype(bf16)

    local["x"].wait()
    local["tx"].wait()
    from_core(3, r["xc"])
    from_edge(2, r["xh"])

    def conv_step(j, carry):
        cols = lanes(j, chunk)
        pad[:EDGE, :] = r["xh"][:, cols].astype(f32)
        for i in range(2):
            pad[EDGE + i * T : EDGE + (i + 1) * T, :] = r["xc"][i, :, cols].astype(f32)
        kernel = r["txv"][:, cols]
        for b in range(Tc // band):
            r["values"][b * band : (b + 1) * band, cols] = filtered(pad, kernel, b * band, band)
        grown = jnp.dot(r["te"][...], spread_cols(j, 2 * HC, 0), preferred_element_type=f32)
        hi, lo = halves(r["values"][:, cols].astype(f32) * grown)
        w_t = r["wT"][(j * chunk) // GW]
        state = jnp.dot(w_t, hi, preferred_element_type=f32) + jnp.dot(
            w_t, lo, preferred_element_type=f32
        )
        s_hi, s_lo = halves(state)
        r["S2"][:STATE, cols] = s_hi
        r["S2"][STATE:, cols] = s_lo
        return carry

    lax.fori_loop(0, W // chunk, conv_step, 0)

    fetch("hw", r["hw"], r["hww"])

    others = pl.ds(0, chips - 1)
    arrived(r["all_r"].at[others], r["r_recv"])
    arrived(r["all_pd"].at[others], r["pd_recv"])
    arrived(r["all_r"].at[others], r["r_send"])
    arrived(r["all_pd"].at[others], r["pd_send"])
    for g in range(G):
        rows_g = r["all_r"][:, :, g * STATE : (g + 1) * STATE].reshape(R, STATE)
        r["rr"][g, :, :STATE] = rows_g
        r["rr"][g, :, STATE:] = rows_g
    run_w = jnp.ones((1, 128), f32)
    weights = []
    for d in range(chips):
        weights.append(jnp.broadcast_to(run_w, (RC, 128)))
        run_w = jnp.where(d > p, run_w * r["all_pd"][d][0:1], run_w)
    far = jnp.concatenate(weights, axis=0)[:, :HC]
    r["ww"][...] = jnp.concatenate(halves(far), axis=1)

    def y_step(j, carry):
        cols = lanes(j, chunk)
        y = jnp.dot(r["rr"][(j * chunk) // GW], r["S2"][:, cols], preferred_element_type=f32)
        grown = jnp.dot(r["ww"][...], spread_cols(j, 2 * HC, 0), preferred_element_type=f32)
        r["yf"][:, cols] = y * grown
        return carry

    lax.fori_loop(0, W // chunk, y_step, 0)

    def y_rows(zd, xd):
        return r["yf"][pl.ds(pl.multiple_of((zd * 2 + xd) * RC, 16), RC), :]

    def coded(a, wire, scale):
        most = jnp.max(jnp.abs(a), axis=1, keepdims=True)
        inverse = jnp.where(most > 0.0, LEVELS / jnp.maximum(most, TINY), 0.0)
        wire[...] = jnp.round(a * inverse).astype(jnp.int32).astype(jnp.int16)
        scale[...] = jnp.broadcast_to(most * (1.0 / LEVELS), (RC, 128))

    def decoded(wire, scale):
        return wire[...].astype(jnp.int32).astype(f32) * scale[:, :1]

    for zd in range(z_n - 1, -1, -1):
        goes = (zd > z) | ((zd == z) & (x == 0))

        @pl.when(goes)
        def _():
            coded(y_rows(zd, 1 - x), r["xsend"].at[zd], r["xsend_f"].at[zd])

        for i, (a, b) in enumerate(((r["xsend"], r["xr"]), (r["xsend_f"], r["xr_f"]))):
            push(
                remote(a.at[zd], b.at[zd], r["x_send"].at[i, zd], r["x_recv"].at[i, zd], x_peer),
                goes,
            )

    def from_x_peer(zd):
        for i, b in enumerate((r["xr"], r["xr_f"])):
            arrived(b.at[zd], r["x_recv"].at[i, zd])
        return decoded(r["xr"].at[zd], r["xr_f"].at[zd])

    mine_r = r["mine_r"][...]
    scores = [
        lax.dot_general(
            mine_r[:, g * STATE : (g + 1) * STATE], r["writes"][:, g * STATE : (g + 1) * STATE],
            (((1,), (1,)), ((), ())), preferred_element_type=f32,
        )
        for g in range(G)
    ]
    causal = (spots >= lane_t) & (row_seg == segment)
    quad = 4
    quad_w = quad * HEAD_DIM
    which_head = lax.broadcasted_iota(jnp.int32, (RC, quad_w), 1) // HEAD_DIM

    def within(q):
        mixes = []
        for i in range(quad):
            h = q * quad + i
            gaps = row_cum[:, h : h + 1] - cumulated[h : h + 1]
            decay = jnp.where(causal, jnp.exp(jnp.where(causal, gaps, 0.0)), 0.0)
            mixes.append(scores[h * HEAD_DIM // GW] * decay * steps[h : h + 1])
        both = jnp.concatenate(halves(jnp.concatenate(mixes, axis=0)), axis=0)
        span = slice(q * quad_w, (q + 1) * quad_w)
        product = jnp.dot(both, r["values"][:, span], preferred_element_type=f32)
        product = product[: quad * RC] + product[quad * RC :]
        out = product[:RC]
        for i in range(1, quad):
            out = jnp.where(which_head == i, product[i * RC : (i + 1) * RC], out)
        r["mixed"][:, span] = out

    quads = HC // quad
    for q in range(quads // 2):
        within(q)
    for zd in range(z_n - 1, 0, -1):
        goes = zd > z

        @pl.when(goes)
        def _():
            coded(y_rows(zd, x) + from_x_peer(zd), r["zsend"].at[zd], r["zsend_f"].at[zd])

        for i, (a, b) in enumerate(((r["zsend"], r["zr"]), (r["zsend_f"], r["zr_f"]))):
            push(
                remote(a.at[zd], b.at[z], r["z_send"].at[i, zd], r["z_recv"].at[i, z], dev(zd, x, k)),
                goes,
            )
    for q in range(quads // 2, quads):
        within(q)

    local["skip"].wait()
    local["gain"].wait()
    from_start = jnp.exp(row_cum) * jnp.where(row_seg == 0.0, 1.0, 0.0)
    starts = jnp.concatenate(halves(from_start), axis=1)
    skip3 = jnp.concatenate(
        [jnp.broadcast_to(a, (8, H)) for a in thirds(jnp.broadcast_to(r["skipv"][...], (8, H)))], axis=0
    )
    from_core(4, r["gc"])
    gate = jnp.concatenate([r["gc"][0].astype(f32), r["gc"][1].astype(f32)], axis=0)

    def widen_step(j, carry):
        cols = lanes(j, chunk)
        own_values = jnp.dot(pick, r["values"][:, cols], preferred_element_type=f32)
        head = lax.broadcasted_iota(jnp.int32, (H, chunk), 0)
        lane = lax.broadcasted_iota(jnp.int32, (H, chunk), 1)
        all_heads = jnp.where(head == k * HC + (j * chunk + lane) // HEAD_DIM, 1.0, 0.0).astype(bf16)
        grown = jnp.dot(skip3, all_heads, preferred_element_type=f32)
        skip_row = grown[0:1] + grown[8:9] + grown[16:17]
        r["mixed"][:, cols] = r["mixed"][:, cols] + skip_row * own_values
        r["starts"][:, cols] = jnp.dot(starts, spread_cols(j, 2 * HC, 0), preferred_element_type=f32)
        return carry

    lax.fori_loop(0, W // chunk, widen_step, 0)
    gate = jax.nn.silu(gate)

    carried = r["carried"]
    carried[...] = jnp.zeros((RC, W), f32)

    @pl.when(x == 1)
    def _():
        carried[...] = from_x_peer(z)

    for zs in range(z_n - 1):
        @pl.when(zs < z)
        def _():
            for i, b in enumerate((r["zr"], r["zr_f"])):
                arrived(b.at[zs], r["z_recv"].at[i, zs])
            carried[...] = carried[...] + decoded(r["zr"].at[zs], r["zr_f"].at[zs])

    gated = (r["mixed"][...] + carried[...] * r["starts"][...]) * gate
    for g in range(G):
        span = slice(g * GW, (g + 1) * GW)
        part = gated[:, span]
        scale = lax.rsqrt(jnp.mean(part * part, axis=1, keepdims=True) + epsilon)
        r["normed"][:, span] = (part * scale * r["gainv"][:, span]).astype(bf16)

    nrm = r["nrm"]
    mine = r["normed"]
    z_recv, x_recv, c_recv = r["gather1"]
    g_send = r["g_send"]

    def slot(z_, x_, k_):
        return nrm.at[k_ * chips + z_ * 2 + x_]

    def go1(a, b, sem, device):
        remote(a, b, g_send.at[0], sem, device).start()

    home = slot(z, x, k)
    for d in range(1, z_n):
        go1(mine, home, z_recv.at[z], dev((z + d) % z_n, x, k))
    go1(mine, home, x_recv.at[z], x_peer)
    go1(mine, home, c_recv.at[0, z], core_peer)
    nrm[k * chips + p] = mine[...]
    for zs in range(z_n):
        @pl.when(zs != z)
        def _():
            here = slot(zs, x, k)
            arrived(here, z_recv.at[zs])
            go1(here, here, x_recv.at[zs], x_peer)
            go1(here, here, c_recv.at[0, zs], core_peer)

    for zs in range(z_n):
        here = slot(zs, 1 - x, k)
        arrived(here, x_recv.at[zs])
        go1(here, here, c_recv.at[1, zs], core_peer)
    for zs in range(z_n):
        for e, x_ in ((0, x), (1, 1 - x)):
            arrived(slot(zs, x_, 1 - k), c_recv.at[e, zs])
    arrived(nrm.at[pl.ds(0, 2 * chips - 1)], g_send.at[0])
    local["ow"].wait()
    partial = jnp.zeros((R, tp * blk), f32)
    for j in range(2):
        partial = partial + jnp.dot(
            nrm[j * chips : (j + 1) * chips].reshape(R, W), r["oww"][j * W : (j + 1) * W, :], preferred_element_type=f32
        )
    for j in range(tp):
        r["pt"][j] = partial[:, j * blk : (j + 1) * blk]
    push(remote(r["pt"].at[1 - t], r["pr"], r["t_send"], r["t_recv"], y_peer))
    arrived(r["ro"], r["res_recv"])
    in_half = (c >= t * per) & (c < (t + 1) * per)

    @pl.when(in_half)
    def _():
        arrived(r["rsend"].at[pl.ds(0, n - 1)], r["res_send"])

    @pl.when(jnp.logical_not(in_half))
    def _():
        arrived(r["rsend"], r["res_send"])

    res_all = r["ro"][...].astype(f32).reshape(R, blk)
    arrived(r["pr"], r["t_recv"])
    hid = r["hid"]
    hid_mine = (res_all + (r["pt"][t] + r["pr"][...])).astype(bf16)
    hid[me] = hid_mine
    wide_mine = hid_mine.astype(f32)
    sq_mine = jnp.sum(wide_mine * wide_mine, axis=1, keepdims=True)
    sq, sq_z, sq_p = r["sq"], r["sq_z"], r["sq_p"]
    sq[0] = jnp.broadcast_to(sq_mine, (R, 128)).T[:1]

    z_recv, a_recv, b_recv, c_recv = r["gather2"]
    even = k == 0
    a0, b0 = jnp.where(even, t, x), jnp.where(even, x, t)

    def place(z_, a_, b_, k_):
        y_, x_ = jnp.where(k_ == 0, a_, b_), jnp.where(k_ == 0, b_, a_)
        return hid.at[((z_ * 2 + x_) * 2 + k_) * tp + y_]

    a_peer = (jnp.where(even, c, x_peer[0]), jnp.where(even, 1 - t, t))
    b_peer = (jnp.where(even, x_peer[0], c), jnp.where(even, t, 1 - t))

    def go2(here, sem, device):
        remote(here, here, g_send.at[1], sem, device).start()

    def to_a(here, d):
        go2(here, a_recv.at[d], a_peer)

    diag = (x_peer[0], 1 - t)

    def to_diag(here, d):
        go2(here, b_recv.at[1, d], diag)

    def to_b(here, e, d):
        go2(here, b_recv.at[e, d], b_peer)

    def to_core(here, e, d):
        go2(here, c_recv.at[e, d], core_peer)

    for d in range(1, z_n):
        remote(
            sq.at[0], sq_z.at[z], r["sq_send"].at[0], r["sq_recv"].at[0], dev((z + d) % z_n, x, k)
        ).start()
    sq_z[z] = sq[0]
    home = place(z, a0, b0, k)
    for d in range(1, z_n):
        go2(home, z_recv.at[d], dev((z + d) % z_n, x, k))
    to_diag(home, 0)
    to_a(home, 0)
    to_b(home, 0, 0)
    to_core(home, 0, 0)
    arrived(sq_z.at[pl.ds(0, z_n - 1)], r["sq_recv"].at[0])
    column_sum = sq_z[0]
    for zs in range(1, z_n):
        column_sum = column_sum + sq_z[zs]
    sq[1] = column_sum
    in_plane = (x * 2 + k) * tp + t
    for device in plane_peers:
        remote(
            sq.at[1], sq_p.at[in_plane], r["sq_send"].at[1], r["sq_recv"].at[1], device
        ).start()
    sq_p[in_plane] = column_sum
    for d in range(1, z_n):
        here = place((z + z_n - d) % z_n, a0, b0, k)
        arrived(here, z_recv.at[d])
        to_diag(here, d)
        to_a(here, d)
        to_b(here, 0, d)
        to_core(here, 0, d)
    arrived(sq_p.at[pl.ds(0, len(plane_peers))], r["sq_recv"].at[1])
    squares = sq_p[0]
    for i in range(1, 4 * tp):
        squares = squares + sq_p[i]
    inverse_row = lax.rsqrt(squares / D + epsilon)
    inverse = jnp.broadcast_to(inverse_row, (128, R)).T
    local["fg"].wait()
    local["hw"].wait()
    logit, feat = r["logit"], r["feat"]
    oa, ob = jnp.where(even, x, t), jnp.where(even, t, x)
    tile = min(1024, V)
    group = 4 * tp
    depth = group * blk

    def block(d):
        from_z = (z + z_n - d) % z_n
        for e, (a_, b_) in enumerate(((oa, ob), (1 - oa, ob), (oa, 1 - ob), (1 - oa, 1 - ob))):
            arrived(place(from_z, a_, b_, 1 - k), c_recv.at[e, d])
        for i in range(group):
            gain = r["fgv"][:, lanes(from_z * group + i, blk)]
            feat[:, i * blk : (i + 1) * blk] = (
                hid[from_z * group + i].astype(f32) * inverse[:, :blk] * gain
            ).astype(bf16)
        rows = pl.ds(pl.multiple_of(from_z * depth, depth), depth)

        def one_tile(i, carry):
            cols = lanes(i, tile)
            product = jnp.dot(feat[...], r["hww"][rows, cols], preferred_element_type=f32)
            logit[:, cols] = product if d == 0 else logit[:, cols] + product
            return carry

        lax.fori_loop(0, V // tile, one_tile, 0)

    for d in range(z_n):
        from_z = (z + z_n - d) % z_n
        here = place(from_z, 1 - a0, b0, k)
        arrived(here, a_recv.at[d])
        to_core(here, 1, d)
        here = place(from_z, a0, 1 - b0, k)
        arrived(here, b_recv.at[0, d])
        to_core(here, 2, d)
        here = place(from_z, 1 - a0, 1 - b0, k)
        arrived(here, b_recv.at[1, d])
        to_core(here, 3, d)
        if d:
            block(d - 1)
    block(z_n - 1)
    values = logit[...]
    top = jnp.max(values, axis=1, keepdims=True)
    added = jnp.sum(jnp.exp(values - top), axis=1, keepdims=True)
    local["tgt"].wait()
    local["pol"].wait()
    target = column(r["tgtv"][...].astype(f32), 0, R).astype(jnp.int32) - me * V
    hit = jnp.sum(
        jnp.where(lax.broadcasted_iota(jnp.int32, values.shape, 1) == target, values, 0.0),
        axis=1, keepdims=True,
    )
    lane = lax.broadcasted_iota(jnp.int32, (R, 128), 1)
    packed = jnp.where(lane == 0, top, jnp.where(lane == 1, added, jnp.where(lane == 2, hit, 0.0)))
    turned = packed.T[:4]
    stat, every = r["stat"], r["every"]
    stat[...] = turned
    st_send, st_recv = r["st_send"], r["st_recv"]

    def device(a):
        return (a // tp, a % tp)

    def go(d, carry):
        remote(stat, every.at[me], st_send, st_recv, device((me + d) % total)).start()
        return carry

    lax.fori_loop(1, total, go, 0)
    every[me] = turned

    for copy, when in sent:
        if when is None:
            copy.wait_send()
        else:
            pl.when(when)(copy.wait_send)
    arrived(hid.at[pl.ds(0, total - 1)], g_send.at[1])
    arrived(sq_z.at[pl.ds(0, z_n - 1)], r["sq_send"].at[0])
    arrived(sq_p.at[pl.ds(0, len(plane_peers))], r["sq_send"].at[1])
    rest = every.at[pl.ds(0, total - 1)]
    arrived(rest, st_send)
    arrived(rest, st_recv)
    found = every[...]
    tops = found[:, 0, :]
    row_top = jnp.max(tops, axis=0, keepdims=True)
    full = jnp.sum(found[:, 1, :] * jnp.exp(tops - row_top), axis=0, keepdims=True)
    picked = jnp.sum(found[:, 2, :], axis=0, keepdims=True)
    log_prob = picked - row_top - jnp.log(full)
    r["out"][0:1, :] = log_prob
    r["out"][1:2, :] = 0.5 * jnp.square(log_prob - r["polv"][...])


def fused(n, tp, x, g, s, d, resets, rate, skip, tx, ts, gain, ow, res, fg, hw, scored, tgt, pol):
    f32, bf16, i32, i16 = jnp.float32, jnp.bfloat16, jnp.int32, jnp.int16
    dma, vmem = pltpu.SemaphoreType.DMA, pltpu.VMEM
    chips = n // 2
    z_n = chips // 2
    T, C = x.shape
    W, Tc = C // 2, 2 * T
    S = s.shape[2] // 2
    G = S // STATE
    H = d.shape[0]
    HC = H // 2
    r8 = scored.shape[0]
    RC = 2 * r8
    R = chips * RC
    blk = ow.shape[1] // tp
    taps = tx.shape[0]
    total = n * tp
    inputs = dict(
        x=x, g=g, s=s, d=d, resets=resets[None], rate=rate[None], skip=skip[None], tx=tx, ts=ts,
        gain=gain[None], ow=ow, res=res, fg=fg[None], hw=hw, scored=scored, tgt=tgt[None], pol=pol[None],
    )
    scratch = dict(
        resv=vmem((1, T), i32), spot=pltpu.SMEM((r8,), i32), meta=vmem((8, T), f32),
        xc=vmem((2, T, W), bf16), xh=vmem((EDGE, W), bf16),
        sc=vmem((2, 2, T, S), bf16), sh=vmem((2, EDGE, S), bf16),
        dc=vmem((2, HC, T), f32), mc=vmem((2, 8, T), f32), mh=vmem((8, T), f32),
        gv=vmem(g.shape, bf16), rv=vmem(res.shape, bf16),
        gc=vmem((2, r8, W), bf16), gsend=vmem((r8, W), bf16),
        rsend=vmem((n, r8, blk), bf16), ro=vmem((n, r8, blk), bf16),
        txv=vmem((taps, W), f32), tsv=vmem((2, taps, S), f32), gainv=vmem((1, W), f32),
        ratev=vmem((1, H), f32), skipv=vmem((1, H), f32), fgv=vmem((1, n * tp * blk), f32),
        tgtv=vmem((1, R), i32), polv=vmem((1, R), f32),
        pad=vmem((EDGE + Tc, min(1024, W // G)), f32), pad_s=vmem((EDGE + Tc, STATE), f32),
        kb=vmem((taps, Tc, 128), f32),
        reads=vmem((Tc, S), bf16), writes=vmem((Tc, S), bf16),
        mine_r=vmem((RC, S), bf16), all_r=vmem((chips, RC, S), bf16),
        mine_pd=vmem((8, 128), f32), all_pd=vmem((chips, 8, 128), f32),
        te=vmem((Tc, 2 * HC), bf16), wT=vmem((G, STATE, Tc), bf16),
        values=vmem((Tc, W), bf16), S2=vmem((2 * STATE, W), bf16),
        rr=vmem((G, R, 2 * STATE), bf16), ww=vmem((R, 2 * HC), bf16), yf=vmem((R, W), f32),
        xsend=vmem((z_n, RC, W), i16), xr=vmem((z_n, RC, W), i16),
        zsend=vmem((z_n, RC, W), i16), zr=vmem((z_n, RC, W), i16),
        xsend_f=vmem((z_n, RC, 128), f32), xr_f=vmem((z_n, RC, 128), f32),
        zsend_f=vmem((z_n, RC, 128), f32), zr_f=vmem((z_n, RC, 128), f32),
        mixed=vmem((RC, W), f32), starts=vmem((RC, W), f32), carried=vmem((RC, W), f32),
        normed=vmem((RC, W), bf16), nrm=vmem((2 * chips, RC, W), bf16),
        pt=vmem((tp, R, blk), f32), pr=vmem((R, blk), f32),
        hid=vmem((total, R, blk), bf16), feat=vmem((R, 4 * tp * blk), bf16), sq=vmem((2, 1, R), f32),
        sq_z=vmem((z_n, 1, R), f32), sq_p=vmem((4 * tp, 1, R), f32),
        logit=vmem((R, hw.shape[1]), f32), stat=vmem((4, R), f32), every=vmem((total, 4, R), f32),
        oww=vmem(ow.shape, bf16), hww=vmem(hw.shape, bf16),
        own=dma((18,)), core_send=dma((5,)), core_recv=dma((5,)),
        edge_send=dma((2, 3)), edge_recv=dma((3,)),
        r_send=dma(()), r_recv=dma(()), pd_send=dma(()), pd_recv=dma(()),
        x_send=dma((2, z_n)), x_recv=dma((2, z_n)), z_send=dma((2, z_n)), z_recv=dma((2, z_n)),
        res_send=dma(()), res_recv=dma(()), g_send=dma((2,)), sq_send=dma((2,)), sq_recv=dma((2,)), t_send=dma(()), t_recv=dma(()),
        st_send=dma(()), st_recv=dma(()), ready=pltpu.SemaphoreType.REGULAR,
    )
    many = [("gather1", [dma((z_n,))] * 2 + [dma((2, z_n))])]
    many.append(("gather2", [dma((z_n,))] * 2 + [dma((2, z_n)), dma((4, z_n))]))
    names = list(inputs) + ["out"] + list(scratch)
    groups = [(name, len(sems)) for name, sems in many]
    extra = [sem for _, sems in many for sem in sems]

    def run(*refs):
        plain, rest = list(refs[: len(names)]), list(refs[len(names) :])
        for _, size in groups:
            plain.append(tuple(rest[:size]))
            rest = rest[size:]
        one_kernel(n, tp, names + [name for name, _ in groups], *plain)

    both = pl.pallas_call(
        run,
        out_shape=jax.ShapeDtypeStruct((2, R), f32),
        in_specs=[ANY] * len(inputs),
        out_specs=VMEM,
        scratch_shapes=list(scratch.values()) + extra,
        compiler_params=pltpu.CompilerParams(
            collective_id=5, has_side_effects=True, vmem_limit_bytes=58 * 1024 * 1024
        ),
    )(*inputs.values())
    return both[0], both[1]


def body(
    inner_input,
    gate_input,
    state_inputs,
    step_size,
    resets,
    decay_rate,
    skip_gain,
    conv_inner,
    conv_state,
    norm_gain,
    out_weight,
    residual,
    final_gain,
    head_weight,
    scored,
    targets,
    policy_logprob,
):
    f32 = jnp.float32
    n, tp = lax.axis_size("ctx"), lax.axis_size("tp")
    c, t = lax.axis_index("ctx"), lax.axis_index("tp")
    groups_here, blk = state_inputs.shape[2] // STATE, out_weight.shape[1] // tp
    if n % 4 == 0 and tp == 2 and groups_here % 2 == 0 and blk == 128:
        return fused(
            n, tp, inner_input, gate_input, state_inputs, step_size, resets, decay_rate, skip_gain,
            conv_inner, conv_state, norm_gain, out_weight, residual, final_gain, head_weight,
            scored, targets, policy_logprob,
        )
    taps = conv_inner.shape[0]
    rows_here = inner_input.shape[0]
    q_count = state_inputs.shape[2] // STATE
    z_count = n // q_count
    z, q = c // q_count, c % q_count
    picked_rows = scored.shape[0]
    local_rows = scored - c * rows_here
    here = jnp.arange(rows_here, dtype=jnp.int32)
    pick = (local_rows[:, None] == here[None, :]).astype(jnp.bfloat16)
    gate_rows = jnp.dot(pick, gate_input, preferred_element_type=f32).astype(jnp.bfloat16)
    res_rows = jnp.dot(pick, residual, preferred_element_type=f32).astype(jnp.bfloat16)
    meta = jnp.zeros((8, rows_here), f32)
    meta = meta.at[0].set(resets.astype(f32))
    meta = meta.at[1, :picked_rows].set(local_rows.astype(f32))
    xs, ss, ds, gs, ms, x_edge, s_edge, m_edge, res_all = spread(
        n, tp, q_count, inner_input, state_inputs, step_size, gate_rows, meta, res_rows
    )
    tokens = q_count * rows_here
    width = xs.shape[2]
    heads = ds.shape[1]
    rows = q_count * picked_rows
    gate = gs.reshape(rows, width)
    flags = ms[:, 0].reshape(tokens)
    spots = ms[:, 1, :picked_rows] + (jnp.arange(q_count) * rows_here).astype(f32)[:, None]
    spots = spots.reshape(rows, 1).astype(jnp.int32)
    margin = taps - 1
    f_tail = jnp.where(z > 0, m_edge[0, rows_here - margin :], 0.0)
    clear = 1.0 - jnp.concatenate([f_tail, flags])
    keeping = [jnp.ones((tokens,), f32)]
    for offset in range(1, taps):
        keeping.append(keeping[-1] * clear[margin - offset + 1 : margin - offset + 1 + tokens])
    keeps = jnp.pad(jnp.stack(keeping), ((0, -taps % 8), (0, 0)))
    normed = middle(
        xs, x_edge, ss, s_edge, keeps, ds, jnp.broadcast_to(flags[None], (8, tokens)), spots, gate,
        conv_inner, conv_state, decay_rate.reshape(q_count, heads, 1),
        skip_gain.reshape(q_count, 1, heads), norm_gain[None], q_count, z_count,
    )
    res = res_all.reshape(z_count * rows, -1)
    return tail(
        normed, out_weight, head_weight, res, final_gain, targets, policy_logprob,
        n, tp, q_count, z_count,
    )


def solution(mesh):
    return jax.shard_map(
        body,
        mesh=mesh,
        in_specs=(
            P("ctx", "tp"),
            P("ctx", "tp"),
            P(None, "ctx", "tp"),
            P("tp", "ctx"),
            P("ctx"),
            P("tp"),
            P("tp"),
            P(None, "tp"),
            P(None, None, "tp"),
            P("tp"),
            P("tp", "ctx"),
            P("ctx", "tp"),
            P(),
            P(None, ("ctx", "tp")),
            P("ctx"),
            P(),
            P(),
        ),
        out_specs=(P(), P()),
        check_vma=False,
    )
```
